32 devices in a mesh: row: 8 (over z, x), col: 4 (over y, core).
Axes of the slice: x: 2, y: 2, z: 4, core: 2. Of those that a mesh axis runs over, the one named last changes fastest.
Arguments:
- start_vector: float32 [12288, 12288], P('row', 'col'), may hold values from -6 to 6, as said below
- ham_blocks: bfloat16 [384, 128, 128], P('row'), may hold values from -0.1875 to 0.1875
- diagonal: float32 [12288], replicated, may hold values from -1 to 1
- pair_lists: int32 [3, 8, 64], replicated, may hold values from 0 to 47, as said below
- pair_counts: int32 [8], replicated, may hold values from 16 to 64, as said below
- hot_blocks: int32 [8, 2], replicated, may hold values from 0 to 11, as said below
- selection: int32 [8, 8], replicated, may hold values from 0 to 1
Outputs:
- first_iterate: float32 [12288, 12288], P('row', 'col')
- second_iterate: float32 [12288, 12288], P('row', 'col')
The draws below stay inside these ranges and needn't reach their ends.
Inputs may be any that keep to these rules, and one draw needn't show every extreme that they name: start_vector is symmetric: entry (a, b) equals entry (b, a). `pair_lists`: component 0 is a tile (0 to 7), component 1 a block of a tile (0 to 11), component 2 a block id (0 to 47); slot k < 8 of every list has source tile k. `pair_counts`: some tile has all 64 slots live. `hot_blocks`: the 2 blocks of a tile are distinct.
All inputs are finite; a program needn't handle non-finite values.
Results may differ from the reference program's by a relative error of at most 0.0023.
Values may be sent and summed in bfloat16 or wider, within the bound.
A program may use at most 320 MiB of HBM per device.

```python
import jax
import jax.numpy as jnp
from jax import lax

N = 12288
BLK = 128
HOT = 2
NPAIR = 64
NHB = 48
NTILE = 8
BT = 12


def draw_start_vector(key, part):
    base = jax.random.normal(key, (N, N), jnp.float32)
    return jnp.clip((base + base.T) * 0.7071067811865476, -6.0, 6.0)


def draw_pair_lists(key, part):
    key_source, key_target, key_ham = jax.random.split(jax.random.fold_in(key, 11), 3)
    pair_shape = (NTILE, NPAIR)
    random_source = jax.random.randint(key_source, pair_shape, 0, NTILE)
    position = jnp.arange(NPAIR, dtype=jnp.int32)[None, :] + jnp.zeros((NTILE, 1), jnp.int32)
    source = jnp.where(position < NTILE, position, random_source)
    target = jax.random.randint(key_target, pair_shape, 0, BT)
    ham_ids = jax.random.randint(key_ham, pair_shape, 0, NHB)
    return jnp.stack([source, target, ham_ids]).astype(jnp.int32)


def draw_pair_counts(key, part):
    lowest = max(NTILE, NPAIR // 4)
    spread_size = NPAIR - lowest
    first_key, second_key, third_key = jax.random.split(jax.random.fold_in(key, 13), 3)
    first_draw = jax.random.randint(first_key, (NTILE,), 0, spread_size + 1)
    second_draw = jax.random.randint(second_key, (NTILE,), 0, spread_size + 1)
    drawn = lowest + first_draw * second_draw // max(spread_size, 1)
    busiest = jax.random.randint(third_key, (), 0, NTILE)
    return jnp.where(jnp.arange(NTILE) == busiest, NPAIR, drawn).astype(jnp.int32)


def draw_hot_blocks(key, part):
    scores = jax.random.randint(jax.random.fold_in(key, 17), (NTILE, BT), 0, 1 << 20) * BT + jnp.arange(BT, dtype=jnp.int32)[None, :]
    ordering = jnp.argsort(scores, axis=1)
    return ordering[:, :HOT].astype(jnp.int32)


def plant(result, stream_key, low, largest):
    longest = result.shape.index(max(result.shape))
    spots = []
    for shift in (0, 1):
        where = [jax.random.randint(jax.random.fold_in(stream_key, axis), (), 0, length) for axis, length in enumerate(result.shape)]
        where[longest] = (where[longest] + shift) % result.shape[longest]
        spots.append(tuple(where))
    return result.at[spots[0]].set(low).at[spots[1]].set(largest)


def block_scale(stream_key, shape, cuts, low, largest):
    loudness = 1.0
    for axis_at, blocks in cuts:
        heights = jax.random.uniform(jax.random.fold_in(jax.random.fold_in(stream_key, 6), axis_at), (blocks,), jnp.float32, low / len(cuts), largest / len(cuts))
        loudness = loudness * jnp.repeat(jnp.exp(heights), shape[axis_at] // blocks).reshape((-1,) + (1,) * (len(shape) - 1 - axis_at))
    return loudness


def centred(key, dims, deviation, most, cuts=(), kind=jnp.bfloat16):
    array = deviation * jax.random.normal(key, dims, jnp.float32)
    if cuts:
        array = array * block_scale(key, dims, cuts, -0.22, 0.18)
    return jnp.clip(array, -most, most).astype(kind)


def setup_inputs(seed: int = 0) -> dict:
    seeds = jax.random.split(jax.random.key(seed), 8)
    return {
        "start_vector": draw_start_vector(jax.random.fold_in(seeds[7], 71), 0),
        "ham_blocks": centred(seeds[1], (NTILE * NHB, BLK, BLK), (BLK * 8) ** -0.5, 0.1875, ((0, 8),)),
        "diagonal": jnp.clip(jax.random.uniform(seeds[2], (N,), jnp.float32, -1.0, 1.0), -1.0, 1.0),
        "pair_lists": draw_pair_lists(jax.random.fold_in(seeds[7], 71), 0),
        "pair_counts": draw_pair_counts(jax.random.fold_in(seeds[7], 71), 0),
        "hot_blocks": draw_hot_blocks(jax.random.fold_in(seeds[7], 71), 0),
        "selection": plant(jax.random.randint(seeds[6], (NTILE, NTILE), 0, HOT), jax.random.fold_in(seeds[6], 1), 0, HOT - 1).astype(jnp.int32),
    }


center = 0.25
half_width = 2.5


def operator(iterate, ham_blocks, diagonal, pair_lists, pair_counts, hot_blocks, selection):
    tile_rows = N // NTILE
    rounded = lax.optimization_barrier(iterate.astype(jnp.bfloat16)).astype(jnp.float32)
    ham_wide = ham_blocks.astype(jnp.float32)

    def update(flat_index, accumulated):
        target_tile = flat_index // NPAIR
        pair_index = flat_index % NPAIR
        source_tile = pair_lists[0, target_tile, pair_index]
        target_block = pair_lists[1, target_tile, pair_index]
        block_id = pair_lists[2, target_tile, pair_index]
        chosen = hot_blocks[source_tile, selection[target_tile, source_tile]]
        src_start = (source_tile * tile_rows + chosen * BLK).astype(jnp.int32)
        source = lax.dynamic_slice_in_dim(rounded, src_start, BLK, 0)
        ham_block = lax.dynamic_index_in_dim(ham_wide, (target_tile * NHB + block_id).astype(jnp.int32), 0, keepdims=False)
        product = jnp.dot(ham_block, source, preferred_element_type=jnp.float32)
        is_live = (pair_index < pair_counts[target_tile]).astype(jnp.float32)
        row_start = (target_tile * tile_rows + target_block * BLK).astype(jnp.int32)
        current = lax.dynamic_slice_in_dim(accumulated, row_start, BLK, 0)
        return lax.dynamic_update_slice_in_dim(accumulated, current + is_live * product, row_start, 0)

    one_side = lax.fori_loop(0, NTILE * NPAIR, update, jnp.zeros((N, N), jnp.float32))
    return one_side + one_side.T + (diagonal[:, None] + diagonal[None, :]) * iterate


def reference(start_vector, ham_blocks, diagonal, pair_lists, pair_counts, hot_blocks, selection):
    first_iterate = (operator(start_vector, ham_blocks, diagonal, pair_lists, pair_counts, hot_blocks, selection) - center * start_vector) / half_width
    second_iterate = 2.0 * (operator(first_iterate, ham_blocks, diagonal, pair_lists, pair_counts, hot_blocks, selection) - center * first_iterate) / half_width - start_vector
    return first_iterate, second_iterate
```

```python
import functools

import jax
import jax.numpy as jnp
from jax import lax
from jax.experimental import pallas as pl
from jax.experimental.pallas import tpu as pltpu
from jax.sharding import PartitionSpec as P

center = 0.25
half_width = 2.5
VMEM_LIMIT = 60 * 1024 * 1024
MESH = pl.DeviceIdType.MESH


def dense_kernel(transposed, tiles, pairs, counts, ham_ref, out_ref, acc):
    tile = tiles[pl.program_id(0)]
    tile_count = counts.shape[0]
    slots = pairs.shape[0] // (3 * tile_count)
    size = ham_ref.shape[-1]
    acc[...] = jnp.zeros_like(acc)

    def add(slot, carry):
        at = tile * slots + slot
        source = pl.multiple_of(pairs[at] * size, size)
        target = pl.multiple_of(pairs[tile_count * slots + at] * size, size)
        block = ham_ref[0, pairs[2 * tile_count * slots + at]].astype(jnp.float32)
        if transposed:
            acc[pl.ds(source, size), pl.ds(target, size)] += block.T
        else:
            acc[pl.ds(target, size), pl.ds(source, size)] += block
        return carry

    lax.fori_loop(0, counts[tile], add, 0)
    out_ref[0] = acc[...].astype(out_ref.dtype)


def dense(hams, tiles, pairs, counts, shape, transposed):
    grid_spec = pltpu.PrefetchScalarGridSpec(
        num_scalar_prefetch=3,
        grid=(hams.shape[0],),
        in_specs=[pl.BlockSpec((1,) + hams.shape[1:], lambda i, *_: (i, 0, 0, 0))],
        out_specs=pl.BlockSpec((1,) + shape, lambda i, *_: (i, 0, 0)),
        scratch_shapes=[pltpu.VMEM(shape, jnp.float32)],
    )
    return pl.pallas_call(
        functools.partial(dense_kernel, transposed),
        out_shape=jax.ShapeDtypeStruct((hams.shape[0],) + shape, jnp.bfloat16),
        grid_spec=grid_spec,
        compiler_params=pltpu.CompilerParams(vmem_limit_bytes=VMEM_LIMIT),
    )(tiles, pairs, counts, hams)


def pack_kernel(place, hot, xr_ref, xc_ref, rows_ref, cols_ref):
    rows_ref[0] = xr_ref[...].astype(rows_ref.dtype)
    cols_ref[0] = xc_ref[...].astype(cols_ref.dtype)


def pack(x, place, hot, row_count, ratio, size):
    height, width = x.shape
    hot_count = hot.shape[0] // row_count
    blocks = width // (ratio * size)
    part = width // ratio

    def row_block(n, place, hot):
        n = jnp.minimum(n, ratio * hot_count - 1)
        return (hot[place[0] * hot_count + n // ratio], n % ratio)

    def col_block(n, place, hot):
        n = jnp.minimum(n, ratio * hot_count - 1)
        tile, which = n // hot_count, n % hot_count
        return (0, tile * blocks + hot[(place[1] * ratio + tile) * hot_count + which])

    grid_spec = pltpu.PrefetchScalarGridSpec(
        num_scalar_prefetch=2,
        grid=(ratio * hot_count,),
        in_specs=[pl.BlockSpec((size, part), row_block), pl.BlockSpec((height, size), col_block)],
        out_specs=[
            pl.BlockSpec((1, size, part), lambda n, *_: (n // ratio, 0, n % ratio)),
            pl.BlockSpec((1, height, size), lambda n, *_: (n, 0, 0)),
        ],
    )
    return pl.pallas_call(
        pack_kernel,
        out_shape=[
            jax.ShapeDtypeStruct((hot_count, size, width), jnp.bfloat16),
            jax.ShapeDtypeStruct((ratio * hot_count, height, size), jnp.bfloat16),
        ],
        grid_spec=grid_spec,
    )(place, hot, x, x)


class Grid:
    def __init__(self, row_n, col_n):
        line = 1
        while 4 * line * line <= 2 * row_n:
            line *= 2
        self.line, self.lanes = line, row_n // line
        self.cores = 2 if col_n % 2 == 0 else 1
        self.chips = col_n // self.cores
        self.row_n, self.col_n = row_n, col_n
        row, col = lax.axis_index("row"), lax.axis_index("col")
        self.row, self.col = row, col
        self.at, self.lane = row // self.lanes, lax.rem(row, self.lanes)
        self.chip, self.core = col // self.cores, lax.rem(col, self.cores)

    def on_line(self, at):
        return (at * self.lanes + self.lane, self.col)

    def other_lane(self, step):
        return (self.at * self.lanes + lax.rem(self.lane + step, self.lanes), self.col)

    def other_chip(self, step):
        return (self.row, lax.rem(self.chip + step, self.chips) * self.cores + self.core)

    def other_core(self):
        return (self.row, self.chip * self.cores + lax.rem(self.core + 1, self.cores))


def remote(src, dst, send, recv, device):
    return pltpu.make_async_remote_copy(
        src_ref=src, dst_ref=dst, send_sem=send, recv_sem=recv, device_id=device, device_id_type=MESH)


def greet(g):
    barrier = pltpu.get_barrier_semaphore()
    up, down = g.at + 1 < g.line, g.at > 0

    def hello(device):
        pl.semaphore_signal(barrier, inc=1, device_id=device, device_id_type=MESH)

    @pl.when(up)
    def _():
        hello(g.on_line(g.at + 1))

    @pl.when(down)
    def _():
        hello(g.on_line(g.at - 1))

    for step in range(1, g.lanes):
        hello(g.other_lane(step))
    for step in range(1, g.chips):
        hello(g.other_chip(step))
    fixed = g.lanes - 1 + g.chips - 1
    if g.cores == 2:
        hello(g.other_core())
        fixed += 1
    pl.semaphore_wait(barrier, fixed + up.astype(jnp.int32) + down.astype(jnp.int32))


def exchange_kernel(row_n, col_n, pieces, with_ham, sel, rows_ref, cols_ref, *refs):
    g = Grid(row_n, col_n)
    if with_ham:
        ham_ref, s_out, c_out, h_out = refs[:4]
        refs = refs[4:]
    else:
        s_out, c_out = refs[:2]
        refs = refs[2:]
    held, lane_buf, own_buf, col_buf, own_sem, line_recv, up_send, down_send, lane_send, lane_recv = refs[:10]
    chip_send, chip_recv, core_send, core_recv = refs[10:14]
    if with_ham:
        ham_buf, ham_sem, ham_recv, ham_up, ham_down, ham_lane = refs[14:]
        ratio = row_n // col_n
        ham_rows = ham_ref.shape[0] // pieces
    hot_count, size = rows_ref.shape[0], rows_ref.shape[1]
    piece = size // pieces
    block_n = cols_ref.shape[0]
    line, lanes, at = g.line, g.lanes, g.at

    take = pltpu.make_async_copy(rows_ref, held.at[at], own_sem.at[0])
    take_cols = pltpu.make_async_copy(cols_ref, col_buf, own_sem.at[1])
    take.start()
    take_cols.start()
    if with_ham:
        take_ham = pltpu.make_async_copy(ham_ref, ham_buf, ham_sem.at[0])
        take_ham.start()
    greet(g)

    def chip_copy(step, b):
        slot = g.col * block_n + b
        return remote(cols_ref.at[b], c_out.at[slot], chip_send.at[step - 1, b], chip_recv.at[step - 1, b], g.other_chip(step))

    def chip_slot(step):
        return (lax.rem(g.chip - step + g.chips, g.chips) * g.cores + g.core) * block_n

    def core_copy(step, b):
        if step == 0:
            src, slot = cols_ref.at[b], g.col * block_n + b
        else:
            slot = chip_slot(step) + b
            src = c_out.at[slot]
        return remote(src, c_out.at[slot], core_send.at[step, b], core_recv.at[step, b], g.other_core())

    for b in range(block_n):
        for step in range(1, g.chips):
            chip_copy(step, b).start()
    if g.cores == 2:
        for b in range(block_n):
            core_copy(0, b).start()
    take.wait()
    take_cols.wait()
    put_cols = pltpu.make_async_copy(col_buf, c_out.at[pl.ds(g.col * block_n, block_n)], own_sem.at[1])
    put_cols.start()

    def part(slot, p):
        return held.at[slot, :, pl.ds(pl.multiple_of(p * piece, piece), piece), :]

    def up_copy(slot, p):
        return remote(part(slot, p), part(slot, p), up_send.at[slot, p], line_recv.at[slot, p], g.on_line(at + 1))

    def down_copy(slot, p):
        return remote(part(slot, p), part(slot, p), down_send.at[slot, p], line_recv.at[slot, p], g.on_line(at - 1))

    def lane_copy(step, slot, p):
        rows = pl.ds(pl.multiple_of(p * piece, piece), piece)
        return remote(
            lane_buf.at[step - 1, slot, rows, :], s_out.at[slot * lanes + g.lane, rows, :],
            lane_send.at[step - 1, slot, p], lane_recv.at[step - 1, slot, p], g.other_lane(step))

    def choose(target, source, slot, p, out):
        rows = pl.ds(pl.multiple_of(p * piece, piece), piece)
        which = sel[target * row_n + source]
        value = held[slot, 0, rows, :]
        for h in range(1, hot_count):
            value = jnp.where(which == h, held[slot, h, rows, :], value)
        out[slot, rows, :] = value

    def select(slot, p):
        source = slot * lanes + g.lane
        for step in range(1, lanes):
            choose(at * lanes + lax.rem(g.lane + step, lanes), source, slot, p, lane_buf.at[step - 1])
            lane_copy(step, slot, p).start()
        choose(g.row, source, slot, p, own_buf)

    if with_ham:
        def ham_part(ref, p):
            return ref.at[pl.ds(pl.multiple_of(p * ham_rows, ham_rows), ham_rows)]

        def ham_copies(i, p):
            part_of = ham_part(h_out.at[i], p)
            up = remote(part_of, part_of, ham_up.at[i, p], ham_recv.at[i, p], g.on_line(at + 1))
            down = remote(part_of, part_of, ham_down.at[i, p], ham_recv.at[i, p], g.on_line(at - 1))
            over = [remote(part_of, part_of, ham_lane.at[i, step - 1, p], ham_recv.at[i, p], g.other_lane(step))
                    for step in range(1, lanes)]
            return up, down, over

        def ham_place(i):
            tile = g.col * ratio + i
            return tile // lanes, lax.rem(tile, lanes)

        take_ham.wait()
        for i in range(ratio):
            home, home_lane = ham_place(i)

            @pl.when((home == at) & (home_lane == g.lane))
            def _():
                put = pltpu.make_async_copy(ham_buf, h_out.at[i], ham_sem.at[0])
                put.start()
                put.wait()

        def ham_sends(i, p, act):
            home, home_lane = ham_place(i)
            up, down, over = ham_copies(i, p)

            @pl.when(home_lane == g.lane)
            def _():
                @pl.when((at >= home) & (at + 1 < line))
                def _():
                    act(up)

                @pl.when((at <= home) & (at > 0))
                def _():
                    act(down)

                for copy in over:
                    act(copy)

    def advance(n, carry):
        s, p = n // pieces, lax.rem(n, pieces)
        below, above = at - s, at + s

        @pl.when(below >= 0)
        def _():
            @pl.when(s > 0)
            def _():
                up_copy(below, p).wait_recv()

            @pl.when(at + 1 < line)
            def _():
                up_copy(below, p).start()

        @pl.when(above < line)
        def _():
            @pl.when(s > 0)
            def _():
                down_copy(above, p).wait_recv()

            @pl.when(at > 0)
            def _():
                down_copy(above, p).start()

        if with_ham:
            for i in range(ratio):
                home, home_lane = ham_place(i)
                away = jnp.where(at >= home, at - home, home - at)

                @pl.when((home_lane == g.lane) & (away == s))
                def _():
                    @pl.when(s > 0)
                    def _():
                        ham_copies(i, p)[0].wait_recv()

                    ham_sends(i, p, lambda copy: copy.start())

        @pl.when(below >= 0)
        def _():
            select(below, p)

        @pl.when((above < line) & (s > 0))
        def _():
            select(above, p)

        return carry

    def columns(step):
        for b in range(block_n):
            slot = chip_slot(step) + b
            remote(cols_ref.at[b], c_out.at[slot], chip_send.at[step - 1, b], chip_recv.at[step - 1, b], g.other_chip(step)).wait_recv()
            if g.cores == 2:
                core_copy(step, b).start()

    lax.fori_loop(0, pieces * (line // 2), advance, 0)
    for step in range(1, g.chips):
        columns(step)
    lax.fori_loop(pieces * (line // 2), pieces * line, advance, 0)

    for slot in range(line):
        pltpu.make_async_copy(own_buf.at[slot], s_out.at[slot * lanes + g.lane], own_sem.at[2 + slot]).start()

    for slot in range(line):
        pltpu.make_async_copy(own_buf.at[slot], s_out.at[slot * lanes + g.lane], own_sem.at[2 + slot]).wait()
    put_cols.wait()

    def finish(n, carry):
        slot, p = n // pieces, lax.rem(n, pieces)

        @pl.when((slot <= at) & (at + 1 < line))
        def _():
            up_copy(slot, p).wait_send()

        @pl.when((slot >= at) & (at > 0))
        def _():
            down_copy(slot, p).wait_send()

        for step in range(1, lanes):
            lane_copy(step, slot, p).wait_send()
            came = slot * lanes + lax.rem(g.lane - step + lanes, lanes)
            rows = pl.ds(pl.multiple_of(p * piece, piece), piece)
            remote(lane_buf.at[step - 1, slot, rows, :], s_out.at[came, rows, :], lane_send.at[step - 1, slot, p],
                   lane_recv.at[step - 1, slot, p], g.other_lane(step)).wait_recv()
        return carry

    lax.fori_loop(0, line * pieces, finish, 0)
    for b in range(block_n):
        for step in range(1, g.chips):
            chip_copy(step, b).wait_send()
        if g.cores == 2:
            for step in range(g.chips):
                core_copy(step, b).wait_send()
                other = lax.rem(g.core + 1, g.cores)
                slot = (lax.rem(g.chip - step + g.chips, g.chips) * g.cores + other) * block_n + b
                remote(cols_ref.at[b], c_out.at[slot], core_send.at[step, b], core_recv.at[step, b], g.other_core()).wait_recv()
    if with_ham:
        for i in range(ratio):
            home, home_lane = ham_place(i)

            def settle(p, carry):
                ham_sends(i, p, lambda copy: copy.wait_send())

                @pl.when(home_lane != g.lane)
                def _():
                    ham_copies(i, p)[2][0].wait_recv()
                return carry

            lax.fori_loop(0, pieces, settle, 0)


def exchange(rows, cols, ham, sel, row_n, col_n, ident):
    hot_count, size, width = rows.shape
    block_n, height = cols.shape[:2]
    ratio = row_n // col_n
    pieces = 4
    with jax.named_scope("grid"):
        g = Grid(row_n, col_n)
    line, lanes, chips = g.line, g.lanes, g.chips
    dma = pltpu.SemaphoreType.DMA
    anywhere = pl.BlockSpec(memory_space=pl.ANY)
    out_shape = [
        jax.ShapeDtypeStruct((row_n, size, width), jnp.bfloat16),
        jax.ShapeDtypeStruct((col_n * block_n, height, size), jnp.bfloat16),
    ]
    scratch = [
        pltpu.VMEM((line, hot_count, size, width), jnp.bfloat16),
        pltpu.VMEM((max(lanes - 1, 1), line, size, width), jnp.bfloat16),
        pltpu.VMEM((line, size, width), jnp.bfloat16),
        pltpu.VMEM(cols.shape, jnp.bfloat16),
        dma((2 + line,)),
        dma((line, pieces)),
        dma((line, pieces)),
        dma((line, pieces)),
        dma((max(lanes - 1, 1), line, pieces)),
        dma((max(lanes - 1, 1), line, pieces)),
        dma((max(chips - 1, 1), block_n)),
        dma((max(chips - 1, 1), block_n)),
        dma((chips, block_n)),
        dma((chips, block_n)),
    ]
    args = [sel, rows, cols]
    if ham is not None:
        out_shape.append(jax.ShapeDtypeStruct((ratio,) + ham.shape, ham.dtype))
        scratch += [
            pltpu.VMEM(ham.shape, ham.dtype),
            dma((1,)),
            dma((ratio, pieces)),
            dma((ratio, pieces)),
            dma((ratio, pieces)),
            dma((ratio, max(lanes - 1, 1), pieces)),
        ]
        args.append(ham)
    return pl.pallas_call(
        functools.partial(exchange_kernel, row_n, col_n, pieces, ham is not None),
        out_shape=out_shape,
        in_specs=[pl.BlockSpec(memory_space=pltpu.SMEM)] + [anywhere] * (len(args) - 1),
        out_specs=[anywhere] * len(out_shape),
        scratch_shapes=scratch,
        compiler_params=pltpu.CompilerParams(collective_id=ident, has_side_effects=True, vmem_limit_bytes=VMEM_LIMIT),
    )(*args)


def filter_kernel(source_count, row_chunk, last, place, sel, wa_ref, s_ref, wb_ref, rd_ref, cd_ref, *refs):
    b_refs = refs[:source_count]
    rest = refs[source_count:]
    if last:
        x_ref, start_ref, out_ref = rest
    else:
        x_ref, out_ref = rest

    def chunk(i, carry):
        rows = pl.ds(pl.multiple_of(i * row_chunk, row_chunk), row_chunk)
        beta = jnp.concatenate([b[0, rows, :] for b in b_refs], axis=1)
        acc = jnp.dot(wa_ref[rows, :], s_ref[...], preferred_element_type=jnp.float32)
        acc = acc + jnp.dot(beta, wb_ref[0], preferred_element_type=jnp.float32)
        x = x_ref[rows, :]
        acc = acc + (rd_ref[rows, :] + cd_ref[...] - center) * x
        if last:
            out_ref[rows, :] = acc * (2.0 / half_width) - start_ref[rows, :]
        else:
            out_ref[rows, :] = acc * (1.0 / half_width)
        return carry

    lax.fori_loop(0, x_ref.shape[0] // row_chunk, chunk, 0)


def filter_step(place, sel, wa, s, wb, rd, cd, cols, x, start, row_n, ratio):
    height, width = x.shape
    size = cols.shape[-1]
    hot_count = cols.shape[0] // row_n
    tile_width = width // ratio
    stripe = 256 if tile_width % 256 == 0 else size
    per_tile = tile_width // stripe
    row_chunk = height // 3 if height % 384 == 0 else size
    last = start is not None

    def b_spec(q):
        return pl.BlockSpec(
            (1, height, size),
            lambda n, place, sel: (q * hot_count + sel[(place[1] * ratio + jnp.minimum(n // per_tile, ratio - 1)) * row_n + q], 0, 0))

    striped = pl.BlockSpec((height, stripe), lambda n, *_: (0, n))
    in_specs = [
        pl.BlockSpec(wa.shape, lambda n, *_: (0, 0)),
        pl.BlockSpec((s.shape[0], stripe), lambda n, *_: (0, n)),
        pl.BlockSpec((1, wb.shape[1], stripe), lambda n, *_: (n // per_tile, 0, n % per_tile)),
        pl.BlockSpec((height, 1), lambda n, *_: (0, 0)),
        pl.BlockSpec((1, stripe), lambda n, *_: (0, n)),
    ] + [b_spec(q) for q in range(row_n)] + [striped] * (2 if last else 1)
    args = [wa, s, wb, rd, cd] + [cols] * row_n + [x] + ([start] if last else [])
    grid_spec = pltpu.PrefetchScalarGridSpec(
        num_scalar_prefetch=2, grid=(width // stripe,), in_specs=in_specs, out_specs=striped)
    return pl.pallas_call(
        functools.partial(filter_kernel, row_n, row_chunk, last),
        out_shape=jax.ShapeDtypeStruct(x.shape, jnp.float32),
        grid_spec=grid_spec,
        compiler_params=pltpu.CompilerParams(vmem_limit_bytes=VMEM_LIMIT),
    )(place, sel, *args)


def body(start_vector, ham_blocks, diagonal, pair_lists, pair_counts, hot_blocks, selection):
    row_n = lax.axis_size("row")
    col_n = lax.axis_size("col")
    ratio = row_n // col_n
    height, width = start_vector.shape
    size = ham_blocks.shape[1]
    row_index = lax.axis_index("row")
    col_index = lax.axis_index("col")
    place = jnp.stack([row_index, col_index]).astype(jnp.int32)
    pairs = pair_lists.reshape(-1)
    hot = hot_blocks.reshape(-1)
    sel = selection.reshape(-1)
    rd = lax.dynamic_slice_in_dim(diagonal, row_index * height, height)[:, None]
    cd = lax.dynamic_slice_in_dim(diagonal, col_index * width, width)[None, :]
    depth = row_n * size

    rows, cols = pack(start_vector, place, hot, row_n, ratio, size)
    s, b, hams = exchange(rows, cols, ham_blocks, sel, row_n, col_n, 0)
    s = s.reshape(depth, width)
    wa = dense(ham_blocks[None], place[:1], pairs, pair_counts, (height, depth), False)[0]
    mirrors = (col_index * ratio + jnp.arange(ratio)).astype(jnp.int32)
    wb = dense(hams, mirrors, pairs, pair_counts, (depth, width // ratio), True)
    first = filter_step(place, sel, wa, s, wb, rd, cd, b, start_vector, None, row_n, ratio)
    rows, cols = pack(first, place, hot, row_n, ratio, size)
    s, b = exchange(rows, cols, None, sel, row_n, col_n, 1)
    second = filter_step(place, sel, wa, s.reshape(depth, width), wb, rd, cd, b, first, start_vector, row_n, ratio)
    return (first, second)


def solution(mesh):
    in_specs = (P("row", "col"), P("row", None, None), P(), P(), P(), P(), P())
    out_specs = (P("row", "col"), P("row", "col"))
    return jax.shard_map(body, mesh=mesh, in_specs=in_specs, out_specs=out_specs, check_vma=False)
```

```python
import functools

import jax
import jax.numpy as jnp
from jax import lax
from jax.experimental import pallas as pl
from jax.experimental.pallas import tpu as pltpu
from jax.sharding import PartitionSpec as P

center = 0.25
half_width = 2.5
VMEM_LIMIT = 60 * 1024 * 1024
MESH = pl.DeviceIdType.MESH


def dense_kernel(transposed, tiles, pairs, counts, ham_ref, out_ref, acc):
    tile = tiles[pl.program_id(0)]
    tile_count = counts.shape[0]
    slots = pairs.shape[0] // (3 * tile_count)
    size = ham_ref.shape[-1]
    acc[...] = jnp.zeros_like(acc)

    def add(slot, carry):
        at = tile * slots + slot
        source = pl.multiple_of(pairs[at] * size, size)
        target = pl.multiple_of(pairs[tile_count * slots + at] * size, size)
        block = ham_ref[0, pairs[2 * tile_count * slots + at]].astype(jnp.float32)
        if transposed:
            acc[pl.ds(source, size), pl.ds(target, size)] += block.T
        else:
            acc[pl.ds(target, size), pl.ds(source, size)] += block
        return carry

    lax.fori_loop(0, counts[tile], add, 0)
    out_ref[0] = acc[...].astype(out_ref.dtype)


def dense(hams, tiles, pairs, counts, shape, transposed):
    grid_spec = pltpu.PrefetchScalarGridSpec(
        num_scalar_prefetch=3,
        grid=(hams.shape[0],),
        in_specs=[pl.BlockSpec((1,) + hams.shape[1:], lambda i, *_: (i, 0, 0, 0))],
        out_specs=pl.BlockSpec((1,) + shape, lambda i, *_: (i, 0, 0)),
        scratch_shapes=[pltpu.VMEM(shape, jnp.float32)],
    )
    return pl.pallas_call(
        functools.partial(dense_kernel, transposed),
        out_shape=jax.ShapeDtypeStruct((hams.shape[0],) + shape, jnp.bfloat16),
        grid_spec=grid_spec,
        compiler_params=pltpu.CompilerParams(vmem_limit_bytes=VMEM_LIMIT),
    )(tiles, pairs, counts, hams)


def pack_kernel(place, hot, xr_ref, xc_ref, rows_ref, cols_ref):
    rows_ref[0] = xr_ref[...].astype(rows_ref.dtype)
    cols_ref[0] = xc_ref[...].astype(cols_ref.dtype)


def pack(x, place, hot, row_count, ratio, size):
    height, width = x.shape
    hot_count = hot.shape[0] // row_count
    blocks = width // (ratio * size)
    part = width // ratio

    def row_block(n, place, hot):
        n = jnp.minimum(n, ratio * hot_count - 1)
        return (hot[place[0] * hot_count + n // ratio], n % ratio)

    def col_block(n, place, hot):
        n = jnp.minimum(n, ratio * hot_count - 1)
        tile, which = n // hot_count, n % hot_count
        return (0, tile * blocks + hot[(place[1] * ratio + tile) * hot_count + which])

    grid_spec = pltpu.PrefetchScalarGridSpec(
        num_scalar_prefetch=2,
        grid=(ratio * hot_count,),
        in_specs=[pl.BlockSpec((size, part), row_block), pl.BlockSpec((height, size), col_block)],
        out_specs=[
            pl.BlockSpec((1, size, part), lambda n, *_: (n // ratio, 0, n % ratio)),
            pl.BlockSpec((1, height, size), lambda n, *_: (n, 0, 0)),
        ],
    )
    return pl.pallas_call(
        pack_kernel,
        out_shape=[
            jax.ShapeDtypeStruct((hot_count, size, width), jnp.bfloat16),
            jax.ShapeDtypeStruct((ratio * hot_count, height, size), jnp.bfloat16),
        ],
        grid_spec=grid_spec,
    )(place, hot, x, x)


def layout(row_n, col_n):
    line = 1
    while 4 * line * line <= 2 * row_n:
        line *= 2
    cores = 2 if col_n % 2 == 0 else 1
    return line, row_n // line, col_n // cores, cores


class Grid:
    def __init__(self, row_n, col_n):
        self.line, self.lanes, self.chips, self.cores = layout(row_n, col_n)
        self.row_n, self.col_n = row_n, col_n
        row, col = lax.axis_index("row"), lax.axis_index("col")
        self.row, self.col = row, col
        self.at, self.lane = row // self.lanes, lax.rem(row, self.lanes)
        self.chip, self.core = col // self.cores, lax.rem(col, self.cores)

    def on_line(self, at):
        return (at * self.lanes + self.lane, self.col)

    def other_lane(self, step):
        return (self.at * self.lanes + lax.rem(self.lane + step, self.lanes), self.col)

    def other_chip(self, step):
        return (self.row, lax.rem(self.chip + step, self.chips) * self.cores + self.core)

    def other_core(self):
        return (self.row, self.chip * self.cores + lax.rem(self.core + 1, self.cores))


def remote(src, dst, send, recv, device):
    return pltpu.make_async_remote_copy(
        src_ref=src, dst_ref=dst, send_sem=send, recv_sem=recv, device_id=device, device_id_type=MESH)


def greet(g):
    barrier = pltpu.get_barrier_semaphore()
    up, down = g.at + 1 < g.line, g.at > 0

    def hello(device):
        pl.semaphore_signal(barrier, inc=1, device_id=device, device_id_type=MESH)

    @pl.when(up)
    def _():
        hello(g.on_line(g.at + 1))

    @pl.when(down)
    def _():
        hello(g.on_line(g.at - 1))

    for step in range(1, g.lanes):
        hello(g.other_lane(step))
    for step in range(1, g.chips):
        hello(g.other_chip(step))
    fixed = g.lanes - 1 + g.chips - 1
    if g.cores == 2:
        hello(g.other_core())
        fixed += 1
    pl.semaphore_wait(barrier, fixed + up.astype(jnp.int32) + down.astype(jnp.int32))


def exchange_kernel(row_n, col_n, pieces, with_ham, ahead, sel, rows_ref, cols_ref, *refs):
    g = Grid(row_n, col_n)
    first_step = 2 if ahead else 1
    if ahead:
        below_ref, above_ref, chip_ref = refs[:3]
        refs = refs[3:]
    if with_ham:
        ham_ref, s_out, c_out, h_out = refs[:4]
        refs = refs[4:]
    else:
        s_out, c_out = refs[:2]
        refs = refs[2:]
    held, lane_buf, own_buf, col_buf, own_sem, line_recv, up_send, down_send, lane_send, lane_recv = refs[:10]
    chip_send, chip_recv, core_send, core_recv = refs[10:14]
    if with_ham:
        ham_buf, ham_sem, ham_recv, ham_up, ham_down, ham_lane = refs[14:]
        ratio = row_n // col_n
        ham_rows = ham_ref.shape[0] // pieces
    if ahead:
        ahead_buf, ahead_sem = refs[14:]
    hot_count, size = rows_ref.shape[0], rows_ref.shape[1]
    piece = size // pieces
    block_n = cols_ref.shape[0]
    line, lanes, at = g.line, g.lanes, g.at

    take = pltpu.make_async_copy(rows_ref, held.at[at], own_sem.at[0])
    take_cols = pltpu.make_async_copy(cols_ref, col_buf, own_sem.at[1])
    take.start()
    take_cols.start()
    if ahead:
        take_chip = pltpu.make_async_copy(chip_ref, ahead_buf, ahead_sem.at[2])
        take_chip.start()

        @pl.when(at > 0)
        def _():
            pltpu.make_async_copy(below_ref, held.at[at - 1], ahead_sem.at[0]).start()

        @pl.when(at + 1 < line)
        def _():
            pltpu.make_async_copy(above_ref, held.at[at + 1], ahead_sem.at[1]).start()

    if with_ham:
        take_ham = pltpu.make_async_copy(ham_ref, ham_buf, ham_sem.at[0])
        take_ham.start()
    greet(g)

    def chip_copy(step, b):
        slot = g.col * block_n + b
        return remote(cols_ref.at[b], c_out.at[slot], chip_send.at[step - 1, b], chip_recv.at[step - 1, b], g.other_chip(step))

    def chip_slot(step):
        return (lax.rem(g.chip - step + g.chips, g.chips) * g.cores + g.core) * block_n

    def core_copy(step, b):
        if step == 0:
            src, slot = cols_ref.at[b], g.col * block_n + b
        else:
            slot = chip_slot(step) + b
            src = chip_ref.at[b] if ahead and step == 1 else c_out.at[slot]
        return remote(src, c_out.at[slot], core_send.at[step, b], core_recv.at[step, b], g.other_core())

    for b in range(block_n):
        for step in range(first_step, g.chips):
            chip_copy(step, b).start()
    if g.cores == 2:
        for step in range(first_step):
            for b in range(block_n):
                core_copy(step, b).start()
    take.wait()
    take_cols.wait()
    if ahead:
        take_chip.wait()
        put_chip = pltpu.make_async_copy(ahead_buf, c_out.at[pl.ds(chip_slot(1), block_n)], ahead_sem.at[2])
        put_chip.start()

        @pl.when(at > 0)
        def _():
            pltpu.make_async_copy(below_ref, held.at[at - 1], ahead_sem.at[0]).wait()

        @pl.when(at + 1 < line)
        def _():
            pltpu.make_async_copy(above_ref, held.at[at + 1], ahead_sem.at[1]).wait()

    put_cols = pltpu.make_async_copy(col_buf, c_out.at[pl.ds(g.col * block_n, block_n)], own_sem.at[1])
    put_cols.start()

    def part(slot, p):
        return held.at[slot, :, pl.ds(pl.multiple_of(p * piece, piece), piece), :]

    def up_copy(slot, p):
        return remote(part(slot, p), part(slot, p), up_send.at[slot, p], line_recv.at[slot, p], g.on_line(at + 1))

    def down_copy(slot, p):
        return remote(part(slot, p), part(slot, p), down_send.at[slot, p], line_recv.at[slot, p], g.on_line(at - 1))

    def lane_copy(step, slot, p):
        rows = pl.ds(pl.multiple_of(p * piece, piece), piece)
        return remote(
            lane_buf.at[step - 1, slot, rows, :], s_out.at[slot * lanes + g.lane, rows, :],
            lane_send.at[step - 1, slot, p], lane_recv.at[step - 1, slot, p], g.other_lane(step))

    def choose(target, source, slot, p, out):
        rows = pl.ds(pl.multiple_of(p * piece, piece), piece)
        which = sel[target * row_n + source]
        value = held[slot, 0, rows, :]
        for h in range(1, hot_count):
            value = jnp.where(which == h, held[slot, h, rows, :], value)
        out[slot, rows, :] = value

    def select(slot, p):
        source = slot * lanes + g.lane
        for step in range(1, lanes):
            choose(at * lanes + lax.rem(g.lane + step, lanes), source, slot, p, lane_buf.at[step - 1])
            lane_copy(step, slot, p).start()
        choose(g.row, source, slot, p, own_buf)

    if with_ham:
        def ham_part(ref, p):
            return ref.at[pl.ds(pl.multiple_of(p * ham_rows, ham_rows), ham_rows)]

        def ham_copies(i, p):
            part_of = ham_part(h_out.at[i], p)
            up = remote(part_of, part_of, ham_up.at[i, p], ham_recv.at[i, p], g.on_line(at + 1))
            down = remote(part_of, part_of, ham_down.at[i, p], ham_recv.at[i, p], g.on_line(at - 1))
            over = [remote(part_of, part_of, ham_lane.at[i, step - 1, p], ham_recv.at[i, p], g.other_lane(step))
                    for step in range(1, lanes)]
            return up, down, over

        def ham_place(i):
            tile = g.col * ratio + i
            return tile // lanes, lax.rem(tile, lanes)

        take_ham.wait()
        for i in range(ratio):
            home, home_lane = ham_place(i)

            @pl.when((home == at) & (home_lane == g.lane))
            def _():
                put = pltpu.make_async_copy(ham_buf, h_out.at[i], ham_sem.at[0])
                put.start()
                put.wait()

        def ham_sends(i, p, act):
            home, home_lane = ham_place(i)
            up, down, over = ham_copies(i, p)

            @pl.when(home_lane == g.lane)
            def _():
                @pl.when((at >= home) & (at + 1 < line))
                def _():
                    act(up)

                @pl.when((at <= home) & (at > 0))
                def _():
                    act(down)

                for copy in over:
                    act(copy)

    def advance(n, carry):
        s, p = n // pieces, lax.rem(n, pieces)
        below, above = at - s, at + s

        @pl.when(below >= 0)
        def _():
            @pl.when(s >= first_step)
            def _():
                up_copy(below, p).wait_recv()

            @pl.when((at + 1 < line) & (s >= first_step - 1))
            def _():
                up_copy(below, p).start()

        @pl.when(above < line)
        def _():
            @pl.when(s >= first_step)
            def _():
                down_copy(above, p).wait_recv()

            @pl.when((at > 0) & (s >= first_step - 1))
            def _():
                down_copy(above, p).start()

        if with_ham:
            for i in range(ratio):
                home, home_lane = ham_place(i)
                away = jnp.where(at >= home, at - home, home - at)

                @pl.when((home_lane == g.lane) & (away == s))
                def _():
                    @pl.when(s > 0)
                    def _():
                        ham_copies(i, p)[0].wait_recv()

                    ham_sends(i, p, lambda copy: copy.start())

        @pl.when(below >= 0)
        def _():
            select(below, p)

        @pl.when((above < line) & (s > 0))
        def _():
            select(above, p)

        return carry

    def columns(step):
        for b in range(block_n):
            slot = chip_slot(step) + b
            remote(cols_ref.at[b], c_out.at[slot], chip_send.at[step - 1, b], chip_recv.at[step - 1, b], g.other_chip(step)).wait_recv()
            if g.cores == 2:
                core_copy(step, b).start()

    lax.fori_loop(0, pieces * (line // 2), advance, 0)
    for step in range(first_step, g.chips):
        columns(step)
    lax.fori_loop(pieces * (line // 2), pieces * line, advance, 0)

    for slot in range(line):
        pltpu.make_async_copy(own_buf.at[slot], s_out.at[slot * lanes + g.lane], own_sem.at[2 + slot]).start()

    for slot in range(line):
        pltpu.make_async_copy(own_buf.at[slot], s_out.at[slot * lanes + g.lane], own_sem.at[2 + slot]).wait()
    put_cols.wait()
    if ahead:
        put_chip.wait()

    def finish(n, carry):
        slot, p = n // pieces, lax.rem(n, pieces)

        @pl.when((slot <= at + 1 - first_step) & (at + 1 < line))
        def _():
            up_copy(slot, p).wait_send()

        @pl.when((slot >= at - 1 + first_step) & (at > 0))
        def _():
            down_copy(slot, p).wait_send()

        for step in range(1, lanes):
            lane_copy(step, slot, p).wait_send()
            came = slot * lanes + lax.rem(g.lane - step + lanes, lanes)
            rows = pl.ds(pl.multiple_of(p * piece, piece), piece)
            remote(lane_buf.at[step - 1, slot, rows, :], s_out.at[came, rows, :], lane_send.at[step - 1, slot, p],
                   lane_recv.at[step - 1, slot, p], g.other_lane(step)).wait_recv()
        return carry

    lax.fori_loop(0, line * pieces, finish, 0)
    for b in range(block_n):
        for step in range(first_step, g.chips):
            chip_copy(step, b).wait_send()
        if g.cores == 2:
            for step in range(g.chips):
                core_copy(step, b).wait_send()
                other = lax.rem(g.core + 1, g.cores)
                slot = (lax.rem(g.chip - step + g.chips, g.chips) * g.cores + other) * block_n + b
                remote(cols_ref.at[b], c_out.at[slot], core_send.at[step, b], core_recv.at[step, b], g.other_core()).wait_recv()
    if with_ham:
        for i in range(ratio):
            home, home_lane = ham_place(i)

            def settle(p, carry):
                ham_sends(i, p, lambda copy: copy.wait_send())

                @pl.when(home_lane != g.lane)
                def _():
                    ham_copies(i, p)[2][0].wait_recv()
                return carry

            lax.fori_loop(0, pieces, settle, 0)


def exchange(rows, cols, ham, ahead, sel, row_n, col_n, ident):
    hot_count, size, width = rows.shape
    block_n, height = cols.shape[:2]
    ratio = row_n // col_n
    pieces = 4
    line, lanes, chips, _ = layout(row_n, col_n)
    dma = pltpu.SemaphoreType.DMA
    anywhere = pl.BlockSpec(memory_space=pl.ANY)
    out_shape = [
        jax.ShapeDtypeStruct((row_n, size, width), jnp.bfloat16),
        jax.ShapeDtypeStruct((col_n * block_n, height, size), jnp.bfloat16),
    ]
    scratch = [
        pltpu.VMEM((line, hot_count, size, width), jnp.bfloat16),
        pltpu.VMEM((max(lanes - 1, 1), line, size, width), jnp.bfloat16),
        pltpu.VMEM((line, size, width), jnp.bfloat16),
        pltpu.VMEM(cols.shape, jnp.bfloat16),
        dma((2 + line,)),
        dma((line, pieces)),
        dma((line, pieces)),
        dma((line, pieces)),
        dma((max(lanes - 1, 1), line, pieces)),
        dma((max(lanes - 1, 1), line, pieces)),
        dma((max(chips - 1, 1), block_n)),
        dma((max(chips - 1, 1), block_n)),
        dma((chips, block_n)),
        dma((chips, block_n)),
    ]
    args = [sel, rows, cols]
    if ahead is not None:
        scratch += [pltpu.VMEM(cols.shape, jnp.bfloat16), dma((3,))]
        args += ahead
    if ham is not None:
        out_shape.append(jax.ShapeDtypeStruct((ratio,) + ham.shape, ham.dtype))
        scratch += [
            pltpu.VMEM(ham.shape, ham.dtype),
            dma((1,)),
            dma((ratio, pieces)),
            dma((ratio, pieces)),
            dma((ratio, pieces)),
            dma((ratio, max(lanes - 1, 1), pieces)),
        ]
        args.append(ham)
    return pl.pallas_call(
        functools.partial(exchange_kernel, row_n, col_n, pieces, ham is not None, ahead is not None),
        out_shape=out_shape,
        in_specs=[pl.BlockSpec(memory_space=pltpu.SMEM)] + [anywhere] * (len(args) - 1),
        out_specs=[anywhere] * len(out_shape),
        scratch_shapes=scratch,
        compiler_params=pltpu.CompilerParams(collective_id=ident, has_side_effects=True, vmem_limit_bytes=VMEM_LIMIT),
    )(*args)


def hot_kernel(row_n, hot_count, place, hot, sel, *refs):
    refs = list(refs)

    def some(count):
        taken = refs[:count]
        del refs[:count]
        return taken

    wide = lambda blocks: jnp.concatenate(blocks, axis=1)
    wa_hot, x_rows, rd_hot = some(hot_count), some(hot_count), some(hot_count)
    b_hot = [some(row_n) for _ in range(hot_count)]
    s_ref, wb_ref, cd_ref = some(3)
    wa_ref, rd_ref = some(2)
    b_refs = some(row_n)
    s_hot, wb_hot, x_cols, cd_hot = some(hot_count), some(hot_count), some(hot_count), some(hot_count)
    rows_ref, cols_ref = refs
    scale = 1.0 / half_width

    def dot(a, b):
        return jnp.dot(a, b, preferred_element_type=jnp.float32)

    size = rows_ref.shape[1]
    acc = dot(jnp.concatenate([w[...] for w in wa_hot], axis=0), s_ref[...])
    beta = jnp.concatenate([wide([b[0] for b in blocks]) for blocks in b_hot], axis=0)
    acc = acc + dot(beta, wb_ref[0])
    for h in range(hot_count):
        value = acc[h * size:(h + 1) * size] + (rd_hot[h][...] + cd_ref[...] - center) * x_rows[h][...]
        rows_ref[h] = (value * scale).astype(rows_ref.dtype)
    acc = dot(wa_ref[...], wide([s[...] for s in s_hot]))
    acc = acc + dot(wide([b[0] for b in b_refs]), wide([w[0] for w in wb_hot]))
    for h in range(hot_count):
        value = acc[:, h * size:(h + 1) * size] + (rd_ref[...] + cd_hot[h][...] - center) * x_cols[h][...]
        cols_ref[h] = (value * scale).astype(cols_ref.dtype)


def hot_step(place, hot, sel, wa, s, wb, rd, cd, cols, x, row_n, ratio):
    height, width = x.shape
    size = cols.shape[-1]
    hot_count = hot.shape[0] // row_n
    tile_width = width // ratio
    stripe = 256 if tile_width % 256 == 0 else size
    per_tile = tile_width // stripe
    blocks = tile_width // size
    depth = s.shape[0]

    def tile(n):
        return jnp.minimum(n // per_tile, ratio - 1)

    def hot_row(h, place, hot):
        return hot[place[0] * hot_count + h]

    def hot_col(h, n, place, hot):
        return hot[(place[1] * ratio + tile(n)) * hot_count + h]

    def source(q, n, place, sel):
        return q * hot_count + sel[(place[1] * ratio + tile(n)) * row_n + q]

    spec = pl.BlockSpec
    each = range(hot_count)
    in_specs = [spec((size, depth), lambda n, place, hot, sel, h=h: (hot_row(h, place, hot), 0)) for h in each]
    in_specs += [spec((size, stripe), lambda n, place, hot, sel, h=h: (hot_row(h, place, hot), n)) for h in each]
    in_specs += [spec((size, 1), lambda n, place, hot, sel, h=h: (hot_row(h, place, hot), 0)) for h in each]
    in_specs += [spec((1, size, size), lambda n, place, hot, sel, h=h, q=q: (source(q, n, place, sel), hot_row(h, place, hot), 0))
                 for h in each for q in range(row_n)]
    in_specs += [
        spec((depth, stripe), lambda n, *_: (0, n)),
        spec((1, depth, stripe), lambda n, *_: (n // per_tile, 0, n % per_tile)),
        spec((1, stripe), lambda n, *_: (0, n)),
        spec((stripe, depth), lambda n, *_: (n % per_tile, 0)),
        spec((stripe, 1), lambda n, *_: (n % per_tile, 0)),
    ]
    in_specs += [spec((1, stripe, size), lambda n, place, hot, sel, q=q: (source(q, n, place, sel), n % per_tile, 0)) for q in range(row_n)]
    in_specs += [spec((depth, size), lambda n, place, hot, sel, h=h: (0, tile(n) * blocks + hot_col(h, n, place, hot))) for h in each]
    in_specs += [spec((1, depth, size), lambda n, place, hot, sel, h=h: (tile(n), 0, hot_col(h, n, place, hot))) for h in each]
    in_specs += [spec((stripe, size), lambda n, place, hot, sel, h=h: (n % per_tile, tile(n) * blocks + hot_col(h, n, place, hot))) for h in each]
    in_specs += [spec((1, size), lambda n, place, hot, sel, h=h: (0, tile(n) * blocks + hot_col(h, n, place, hot))) for h in each]
    args = [wa] * hot_count + [x] * hot_count + [rd] * hot_count + [cols] * (hot_count * row_n)
    args += [s, wb, cd, wa, rd] + [cols] * row_n + [s] * hot_count + [wb] * hot_count + [x] * hot_count + [cd] * hot_count
    grid_spec = pltpu.PrefetchScalarGridSpec(
        num_scalar_prefetch=3,
        grid=(width // stripe,),
        in_specs=in_specs,
        out_specs=[
            spec((hot_count, size, stripe), lambda n, *_: (0, 0, n)),
            spec((hot_count, stripe, size), lambda n, *_: (n // per_tile, n % per_tile, 0)),
        ],
    )
    return pl.pallas_call(
        functools.partial(hot_kernel, row_n, hot_count),
        out_shape=[
            jax.ShapeDtypeStruct((hot_count, size, width), jnp.bfloat16),
            jax.ShapeDtypeStruct((ratio * hot_count, height, size), jnp.bfloat16),
        ],
        grid_spec=grid_spec,
        compiler_params=pltpu.CompilerParams(vmem_limit_bytes=VMEM_LIMIT),
    )(place, hot, sel, *args)


def first_hops(rows, cols, row_n, col_n):
    line, lanes, chips, cores = layout(row_n, col_n)
    upward = [(r, r + lanes) for r in range(row_n - lanes)]
    below = lax.ppermute(rows, "row", upward)
    above = lax.ppermute(rows, "row", [(b, a) for a, b in upward])
    turn = [(c, (c // cores + 1) % chips * cores + c % cores) for c in range(col_n)]
    return [below, above, lax.ppermute(cols, "col", turn)]


def filter_kernel(source_count, row_chunk, last, place, sel, wa_ref, s_ref, wb_ref, rd_ref, cd_ref, *refs):
    b_refs = refs[:source_count]
    rest = refs[source_count:]
    if last:
        x_ref, start_ref, out_ref = rest
    else:
        x_ref, out_ref = rest

    def chunk(i, carry):
        rows = pl.ds(pl.multiple_of(i * row_chunk, row_chunk), row_chunk)
        beta = jnp.concatenate([b[0, rows, :] for b in b_refs], axis=1)
        acc = jnp.dot(wa_ref[rows, :], s_ref[...], preferred_element_type=jnp.float32)
        acc = acc + jnp.dot(beta, wb_ref[0], preferred_element_type=jnp.float32)
        x = x_ref[rows, :]
        acc = acc + (rd_ref[rows, :] + cd_ref[...] - center) * x
        if last:
            out_ref[rows, :] = acc * (2.0 / half_width) - start_ref[rows, :]
        else:
            out_ref[rows, :] = acc * (1.0 / half_width)
        return carry

    lax.fori_loop(0, x_ref.shape[0] // row_chunk, chunk, 0)


def filter_step(place, sel, wa, s, wb, rd, cd, cols, x, start, row_n, ratio):
    height, width = x.shape
    size = cols.shape[-1]
    hot_count = cols.shape[0] // row_n
    tile_width = width // ratio
    stripe = 256 if tile_width % 256 == 0 else size
    per_tile = tile_width // stripe
    row_chunk = height // 3 if height % 384 == 0 else size
    last = start is not None

    def b_spec(q):
        return pl.BlockSpec(
            (1, height, size),
            lambda n, place, sel: (q * hot_count + sel[(place[1] * ratio + jnp.minimum(n // per_tile, ratio - 1)) * row_n + q], 0, 0))

    striped = pl.BlockSpec((height, stripe), lambda n, *_: (0, n))
    in_specs = [
        pl.BlockSpec(wa.shape, lambda n, *_: (0, 0)),
        pl.BlockSpec((s.shape[0], stripe), lambda n, *_: (0, n)),
        pl.BlockSpec((1, wb.shape[1], stripe), lambda n, *_: (n // per_tile, 0, n % per_tile)),
        pl.BlockSpec((height, 1), lambda n, *_: (0, 0)),
        pl.BlockSpec((1, stripe), lambda n, *_: (0, n)),
    ] + [b_spec(q) for q in range(row_n)] + [striped] * (2 if last else 1)
    args = [wa, s, wb, rd, cd] + [cols] * row_n + [x] + ([start] if last else [])
    grid_spec = pltpu.PrefetchScalarGridSpec(
        num_scalar_prefetch=2, grid=(width // stripe,), in_specs=in_specs, out_specs=striped)
    return pl.pallas_call(
        functools.partial(filter_kernel, row_n, row_chunk, last),
        out_shape=jax.ShapeDtypeStruct(x.shape, jnp.float32),
        grid_spec=grid_spec,
        cost_estimate=pl.CostEstimate(
            flops=4 * height * width * s.shape[0], bytes_accessed=4 * 3 * height * width, transcendentals=0),
        compiler_params=pltpu.CompilerParams(vmem_limit_bytes=VMEM_LIMIT),
    )(place, sel, *args)


def body(start_vector, ham_blocks, diagonal, pair_lists, pair_counts, hot_blocks, selection):
    row_n = lax.axis_size("row")
    col_n = lax.axis_size("col")
    ratio = row_n // col_n
    height, width = start_vector.shape
    size = ham_blocks.shape[1]
    row_index = lax.axis_index("row")
    col_index = lax.axis_index("col")
    place = jnp.stack([row_index, col_index]).astype(jnp.int32)
    pairs = pair_lists.reshape(-1)
    hot = hot_blocks.reshape(-1)
    sel = selection.reshape(-1)
    rd = lax.dynamic_slice_in_dim(diagonal, row_index * height, height)[:, None]
    cd = lax.dynamic_slice_in_dim(diagonal, col_index * width, width)[None, :]
    depth = row_n * size

    rows, cols = pack(start_vector, place, hot, row_n, ratio, size)
    s, b, hams = exchange(rows, cols, ham_blocks, None, sel, row_n, col_n, 0)
    s = s.reshape(depth, width)
    wa = dense(ham_blocks[None], place[:1], pairs, pair_counts, (height, depth), False)[0]
    mirrors = (col_index * ratio + jnp.arange(ratio)).astype(jnp.int32)
    wb = dense(hams, mirrors, pairs, pair_counts, (depth, width // ratio), True)
    rows, cols = hot_step(place, hot, sel, wa, s, wb, rd, cd, b, start_vector, row_n, ratio)
    ahead = first_hops(rows, cols, row_n, col_n)
    s, _ = lax.optimization_barrier((s, rows))
    first = filter_step(place, sel, wa, s, wb, rd, cd, b, start_vector, None, row_n, ratio)
    s, b = exchange(rows, cols, None, ahead, sel, row_n, col_n, 1)
    second = filter_step(place, sel, wa, s.reshape(depth, width), wb, rd, cd, b, first, start_vector, row_n, ratio)
    return (first, second)


def solution(mesh):
    in_specs = (P("row", "col"), P("row", None, None), P(), P(), P(), P(), P())
    out_specs = (P("row", "col"), P("row", "col"))
    return jax.shard_map(body, mesh=mesh, in_specs=in_specs, out_specs=out_specs, check_vma=False)
```

```python
import functools

import jax
import jax.numpy as jnp
from jax import lax
from jax.experimental import pallas as pl
from jax.experimental.pallas import tpu as pltpu
from jax.sharding import PartitionSpec as P

center = 0.25
half_width = 2.5
VMEM_LIMIT = 60 * 1024 * 1024
MESH = pl.DeviceIdType.MESH


def dense_kernel(transposed, tiles, pairs, counts, ham_ref, out_ref, acc):
    tile = tiles[pl.program_id(0)]
    tile_count = counts.shape[0]
    slots = pairs.shape[0] // (3 * tile_count)
    size = ham_ref.shape[-1]
    acc[...] = jnp.zeros_like(acc)

    def add(slot, carry):
        at = tile * slots + slot
        source = pl.multiple_of(pairs[at] * size, size)
        target = pl.multiple_of(pairs[tile_count * slots + at] * size, size)
        block = ham_ref[0, pairs[2 * tile_count * slots + at]].astype(jnp.float32)
        if transposed:
            acc[pl.ds(source, size), pl.ds(target, size)] += block.T
        else:
            acc[pl.ds(target, size), pl.ds(source, size)] += block
        return carry

    lax.fori_loop(0, counts[tile], add, 0)
    out_ref[0] = acc[...].astype(out_ref.dtype)


def dense(hams, tiles, pairs, counts, shape, transposed):
    grid_spec = pltpu.PrefetchScalarGridSpec(
        num_scalar_prefetch=3,
        grid=(hams.shape[0],),
        in_specs=[pl.BlockSpec((1,) + hams.shape[1:], lambda i, *_: (i, 0, 0, 0))],
        out_specs=pl.BlockSpec((1,) + shape, lambda i, *_: (i, 0, 0)),
        scratch_shapes=[pltpu.VMEM(shape, jnp.float32)],
    )
    return pl.pallas_call(
        functools.partial(dense_kernel, transposed),
        out_shape=jax.ShapeDtypeStruct((hams.shape[0],) + shape, jnp.bfloat16),
        grid_spec=grid_spec,
        compiler_params=pltpu.CompilerParams(vmem_limit_bytes=VMEM_LIMIT),
    )(tiles, pairs, counts, hams)


def pack_kernel(place, hot, xr_ref, xc_ref, rows_ref, cols_ref):
    rows_ref[0] = xr_ref[...].astype(rows_ref.dtype)
    cols_ref[0] = xc_ref[...].astype(cols_ref.dtype)


def pack(x, place, hot, row_count, ratio, size):
    height, width = x.shape
    hot_count = hot.shape[0] // row_count
    blocks = width // (ratio * size)
    part = width // ratio

    def row_block(n, place, hot):
        n = jnp.minimum(n, ratio * hot_count - 1)
        return (hot[place[0] * hot_count + n // ratio], n % ratio)

    def col_block(n, place, hot):
        n = jnp.minimum(n, ratio * hot_count - 1)
        tile, which = n // hot_count, n % hot_count
        return (0, tile * blocks + hot[(place[1] * ratio + tile) * hot_count + which])

    grid_spec = pltpu.PrefetchScalarGridSpec(
        num_scalar_prefetch=2,
        grid=(ratio * hot_count,),
        in_specs=[pl.BlockSpec((size, part), row_block), pl.BlockSpec((height, size), col_block)],
        out_specs=[
            pl.BlockSpec((1, size, part), lambda n, *_: (n // ratio, 0, n % ratio)),
            pl.BlockSpec((1, height, size), lambda n, *_: (n, 0, 0)),
        ],
    )
    return pl.pallas_call(
        pack_kernel,
        out_shape=[
            jax.ShapeDtypeStruct((hot_count, size, width), jnp.bfloat16),
            jax.ShapeDtypeStruct((ratio * hot_count, height, size), jnp.bfloat16),
        ],
        grid_spec=grid_spec,
    )(place, hot, x, x)


def layout(row_n, col_n):
    line = 1
    while 4 * line * line <= 2 * row_n:
        line *= 2
    cores = 2 if col_n % 2 == 0 else 1
    return line, row_n // line, col_n // cores, cores


class Grid:
    def __init__(self, row_n, col_n):
        self.line, self.lanes, self.chips, self.cores = layout(row_n, col_n)
        self.row_n, self.col_n = row_n, col_n
        row, col = lax.axis_index("row"), lax.axis_index("col")
        self.row, self.col = row, col
        self.at, self.lane = row // self.lanes, lax.rem(row, self.lanes)
        self.chip, self.core = col // self.cores, lax.rem(col, self.cores)

    def on_line(self, at):
        return (at * self.lanes + self.lane, self.col)

    def other_lane(self, step):
        return (self.at * self.lanes + lax.rem(self.lane + step, self.lanes), self.col)

    def other_chip(self, step):
        return (self.row, lax.rem(self.chip + step, self.chips) * self.cores + self.core)

    def other_core(self):
        return (self.row, self.chip * self.cores + lax.rem(self.core + 1, self.cores))


def remote(src, dst, send, recv, device):
    return pltpu.make_async_remote_copy(
        src_ref=src, dst_ref=dst, send_sem=send, recv_sem=recv, device_id=device, device_id_type=MESH)


def greet(g):
    barrier = pltpu.get_barrier_semaphore()
    up, down = g.at + 1 < g.line, g.at > 0

    def hello(device):
        pl.semaphore_signal(barrier, inc=1, device_id=device, device_id_type=MESH)

    @pl.when(up)
    def _():
        hello(g.on_line(g.at + 1))

    @pl.when(down)
    def _():
        hello(g.on_line(g.at - 1))

    for step in range(1, g.lanes):
        hello(g.other_lane(step))
    for step in range(1, g.chips):
        hello(g.other_chip(step))
    fixed = g.lanes - 1 + g.chips - 1
    if g.cores == 2:
        hello(g.other_core())
        fixed += 1
    pl.semaphore_wait(barrier, fixed + up.astype(jnp.int32) + down.astype(jnp.int32))


def exchange_kernel(row_n, col_n, pieces, with_ham, ahead, sel, rows_ref, cols_ref, *refs):
    g = Grid(row_n, col_n)
    refs = list(refs)

    def some(count):
        taken = refs[:count]
        del refs[:count]
        return taken

    first_step = 2 if ahead else 1
    if ahead:
        below_ref, above_ref, chip_ref = some(3)
    if with_ham:
        (ham_ref,) = some(1)
    s_out, c_out = some(2)
    if with_ham:
        (h_out,) = some(1)
    held, lane_buf, own_buf, col_buf, pair_buf, turn_buf, got, turned = some(8)
    own_sem, line_recv, up_send, down_send, lane_send, lane_recv = some(6)
    chip_send, chip_recv, core_send, core_recv, pair_sem, got_send, got_recv = some(7)
    if ahead:
        ahead_buf, ahead_sem = some(2)
    if with_ham:
        ham_buf, far_buf, ham_sem, ham_recv, ham_up, ham_down, ham_lane, far_recv, far_send, far_chip = some(10)
        ham_rows = ham_ref.shape[0] // pieces
    ratio = row_n // col_n
    hot_count, size = rows_ref.shape[0], rows_ref.shape[1]
    height = cols_ref.shape[1]
    piece = size // pieces
    block_n = cols_ref.shape[0]
    line, lanes, at = g.line, g.lanes, g.at

    home = (g.col * ratio) // lanes
    diag = at == home
    up_ok = (at + 1 < line) & ((home != line - 1) | (at + 1 != line - 1))
    down_ok = (at > 0) & ((home != 0) | (at - 1 != 0))
    deaf = diag & ((at == 0) | (at == line - 1))

    take = pltpu.make_async_copy(rows_ref, held.at[at], own_sem.at[0])
    take_cols = pltpu.make_async_copy(cols_ref, col_buf, own_sem.at[1])
    take.start()
    take_cols.start()
    if ahead:
        take_chip = pltpu.make_async_copy(chip_ref, ahead_buf, ahead_sem.at[2])
        take_chip.start()

        @pl.when(at > 0)
        def _():
            pltpu.make_async_copy(below_ref, held.at[at - 1], ahead_sem.at[0]).start()

        @pl.when(at + 1 < line)
        def _():
            pltpu.make_async_copy(above_ref, held.at[at + 1], ahead_sem.at[1]).start()

    if with_ham:
        take_ham = pltpu.make_async_copy(ham_ref, ham_buf, ham_sem.at[0])
        take_ham.start()
    greet(g)

    def chip_copy(step, b):
        slot = g.col * block_n + b
        return remote(cols_ref.at[b], c_out.at[slot], chip_send.at[step - 1, b], chip_recv.at[step - 1, b], g.other_chip(step))

    def chip_slot(step):
        return (lax.rem(g.chip - step + g.chips, g.chips) * g.cores + g.core) * block_n

    def core_copy(step, b):
        if step == 0:
            src, slot = cols_ref.at[b], g.col * block_n + b
        else:
            slot = chip_slot(step) + b
            src = chip_ref.at[b] if ahead and step == 1 else c_out.at[slot]
        return remote(src, c_out.at[slot], core_send.at[step, b], core_recv.at[step, b], g.other_core())

    for b in range(block_n):
        for step in range(first_step, g.chips):
            chip_copy(step, b).start()
    if g.cores == 2:
        for step in range(first_step):
            for b in range(block_n):
                core_copy(step, b).start()
    take.wait()
    take_cols.wait()
    if ahead:
        take_chip.wait()
        put_chip = pltpu.make_async_copy(ahead_buf, c_out.at[pl.ds(chip_slot(1), block_n)], ahead_sem.at[2])
        put_chip.start()

        @pl.when(at > 0)
        def _():
            pltpu.make_async_copy(below_ref, held.at[at - 1], ahead_sem.at[0]).wait()

        @pl.when(at + 1 < line)
        def _():
            pltpu.make_async_copy(above_ref, held.at[at + 1], ahead_sem.at[1]).wait()

    put_cols = pltpu.make_async_copy(col_buf, c_out.at[pl.ds(g.col * block_n, block_n)], own_sem.at[1])
    put_cols.start()

    def part(slot, p):
        return held.at[slot, :, pl.ds(pl.multiple_of(p * piece, piece), piece), :]

    def up_copy(slot, p):
        return remote(part(slot, p), part(slot, p), up_send.at[slot, p], line_recv.at[slot, p], g.on_line(at + 1))

    def down_copy(slot, p):
        return remote(part(slot, p), part(slot, p), down_send.at[slot, p], line_recv.at[slot, p], g.on_line(at - 1))

    def lane_copy(step, slot, p):
        rows = pl.ds(pl.multiple_of(p * piece, piece), piece)
        return remote(
            lane_buf.at[step - 1, slot, rows, :], s_out.at[slot * lanes + g.lane, rows, :],
            lane_send.at[step - 1, slot, p], lane_recv.at[step - 1, slot, p], g.other_lane(step))

    def pick(target, source, blocks):
        which = sel[target * row_n + source]
        value = blocks[0]
        for h in range(1, hot_count):
            value = jnp.where(which == h, blocks[h], value)
        return value

    def select(slot, p):
        source = slot * lanes + g.lane
        rows = pl.ds(pl.multiple_of(p * piece, piece), piece)
        blocks = [held[slot, h, rows, :] for h in range(hot_count)]
        for step in range(1, lanes):
            target = at * lanes + lax.rem(g.lane + step, lanes)
            lane_buf[step - 1, slot, rows, :] = pick(target, source, blocks)
            lane_copy(step, slot, p).start()
        own_buf[slot, rows, :] = pick(g.row, source, blocks)

    def tile_place(col, i):
        tile = col * ratio + i
        return tile // lanes, lax.rem(tile, lanes)

    detour = g.chips % 2 == 0 and g.chips > 1
    across = g.chips // 2
    end = jnp.where(2 * home < line, line - 1, 0)
    if with_ham:
        def ham_part(ref, p):
            return ref.at[pl.ds(pl.multiple_of(p * ham_rows, ham_rows), ham_rows)]

        def ham_copies(i, p):
            here = ham_part(h_out.at[i], p)
            up = remote(here, here, ham_up.at[i, p], ham_recv.at[i, p], g.on_line(at + 1))
            down = remote(here, here, ham_down.at[i, p], ham_recv.at[i, p], g.on_line(at - 1))
            over = [remote(here, here, ham_lane.at[i, step - 1, p], ham_recv.at[i, p], g.other_lane(step))
                    for step in range(1, lanes)]
            return up, down, over

        def ham_sends(i, p, act):
            _, home_lane = tile_place(g.col, i)
            up, down, over = ham_copies(i, p)
            skip = end if detour else line

            @pl.when(home_lane == g.lane)
            def _():
                @pl.when((at >= home) & (at + 1 < line) & (at + 1 != skip))
                def _():
                    act(up)

                @pl.when((at <= home) & (at > 0) & (at - 1 != skip))
                def _():
                    act(down)

                for copy in over:
                    act(copy)

        if detour:
            far_col = lax.rem(g.chip + across, g.chips) * g.cores + g.core
            far_home = (far_col * ratio) // lanes
            far_end = jnp.where(2 * far_home < line, line - 1, 0)
            rising = far_end > far_home
            far_away = jnp.where(rising, at - far_home, far_home - at)

            def far_copies(i, p):
                here = ham_part(far_buf, p)
                way = jnp.where(rising, at + 1, at - 1)
                on = remote(here, here, far_send.at[p], far_recv.at[p], g.on_line(way))
                chip = remote(here, ham_part(h_out.at[i], p), far_chip.at[p], ham_recv.at[i, p], g.other_chip(across))
                return on, chip

            def far_sends(i, p, act):
                _, far_lane = tile_place(far_col, i)
                on, chip = far_copies(i, p)

                @pl.when((far_lane == g.lane) & (far_away >= 0))
                def _():
                    @pl.when(at != far_end)
                    def _():
                        act(on)

                    @pl.when(at == far_end)
                    def _():
                        act(chip)

        take_ham.wait()
        for i in range(ratio):
            _, home_lane = tile_place(g.col, i)

            @pl.when((home == at) & (home_lane == g.lane))
            def _():
                put = pltpu.make_async_copy(ham_buf, h_out.at[i], ham_sem.at[0])
                put.start()
                put.wait()

            if detour:
                _, far_lane = tile_place(far_col, i)

                @pl.when((far_home == at) & (far_lane == g.lane))
                def _():
                    put = pltpu.make_async_copy(ham_ref, far_buf, ham_sem.at[0])
                    put.start()
                    put.wait()

        def ham_step(s, p):
            for i in range(ratio):
                _, home_lane = tile_place(g.col, i)
                away = jnp.where(at >= home, at - home, home - at)

                @pl.when((home_lane == g.lane) & (away == s))
                def _():
                    @pl.when(s > 0)
                    def _():
                        ham_copies(i, p)[0].wait_recv()

                    ham_sends(i, p, lambda copy: copy.start())

                if detour:
                    _, far_lane = tile_place(far_col, i)

                    @pl.when((far_lane == g.lane) & (far_away == s))
                    def _():
                        @pl.when(s > 0)
                        def _():
                            far_copies(i, p)[0].wait_recv()

                        far_sends(i, p, lambda copy: copy.start())

        def ham_start(p, carry):
            ham_step(0, p)
            return carry

        lax.fori_loop(0, pieces, ham_start, 0)

    def advance(n, carry):
        s, p = n // pieces, lax.rem(n, pieces)
        below, above = at - s, at + s
        hears_below = (below >= 0) & ((s == 0) | (deaf == False))
        hears_above = (above < line) & ((s == 0) | (deaf == False))

        @pl.when(hears_below)
        def _():
            @pl.when(s >= first_step)
            def _():
                up_copy(below, p).wait_recv()

            @pl.when(up_ok & (s >= first_step - 1))
            def _():
                up_copy(below, p).start()

        @pl.when(hears_above)
        def _():
            @pl.when(s >= first_step)
            def _():
                down_copy(above, p).wait_recv()

            @pl.when(down_ok & (s >= first_step - 1))
            def _():
                down_copy(above, p).start()

        if with_ham:
            @pl.when(s > 0)
            def _():
                ham_step(s, p)

        @pl.when(hears_below & (at != home))
        def _():
            select(below, p)

        @pl.when(hears_above & (s > 0) & (at != home))
        def _():
            select(above, p)

        return carry

    def columns(step):
        for b in range(block_n):
            slot = chip_slot(step) + b
            remote(cols_ref.at[b], c_out.at[slot], chip_send.at[step - 1, b], chip_recv.at[step - 1, b], g.other_chip(step)).wait_recv()
            if g.cores == 2:
                core_copy(step, b).start()

    def core_came(step, b):
        other = lax.rem(g.core + 1, g.cores)
        slot = (lax.rem(g.chip - step + g.chips, g.chips) * g.cores + other) * block_n + b
        return remote(cols_ref.at[b], c_out.at[slot], core_send.at[step, b], core_recv.at[step, b], g.other_core())

    def pair_copy(q, turn):
        return pltpu.make_async_copy(c_out.at[pl.ds(q * hot_count, hot_count)], pair_buf.at[turn], pair_sem.at[turn])

    def turn_copy(i, step, q):
        return remote(turn_buf.at[step - 1, q], got.at[i, q], got_send.at[step - 1, q], got_recv.at[i, q], g.other_lane(step))

    def hand_out(q, carry):
        turn = lax.rem(q, 2)

        @pl.when(q + 1 < row_n)
        def _():
            pair_copy(q + 1, 1 - turn).start()

        pair_copy(q, turn).wait()
        for i in range(ratio):
            _, home_lane = tile_place(g.col, i)

            @pl.when(home_lane == g.lane)
            def _():
                def rows_of(k, carry):
                    rows = pl.ds(pl.multiple_of(k * size, size), size)
                    blocks = [pair_buf[turn, h, rows, :] for h in range(hot_count)]
                    for step in range(1, lanes):
                        target = at * lanes + lax.rem(g.lane + step, lanes)
                        turn_buf[step - 1, q, rows, :] = pick(target, q, blocks)
                    got[i, q, rows, :] = pick(g.row, q, blocks)
                    return carry

                lax.fori_loop(0, height // size, rows_of, 0)
                for step in range(1, lanes):
                    turn_copy(i, step, q).start()
        return carry

    def turn_over(i, q):
        for k in range(height // size):
            block = got[i, q, k * size:(k + 1) * size, :].astype(jnp.float32)
            turned[q, :, i * height + k * size:i * height + (k + 1) * size] = block.T.astype(turned.dtype)

    def turn_own(q):
        for i in range(ratio):
            _, home_lane = tile_place(g.col, i)

            @pl.when(home_lane == g.lane)
            def _():
                turn_over(i, q)

    def turn_come(q, carry):
        for i in range(ratio):
            _, home_lane = tile_place(g.col, i)

            @pl.when(home_lane != g.lane)
            def _():
                turn_copy(i, 1, q).wait_recv()
                turn_over(i, q)
        pltpu.make_async_copy(turned.at[q], s_out.at[q], pair_sem.at[2 + q]).start()
        return carry

    half = pieces * (line // 2)
    per_step = -(-row_n // half)
    lax.fori_loop(0, half, advance, 0)
    for step in range(first_step, g.chips):
        columns(step)

    put_cols.wait()
    if ahead:
        put_chip.wait()
    if g.cores == 2:
        for step in range(g.chips):
            for b in range(block_n):
                core_came(step, b).wait_recv()

    @pl.when(diag)
    def _():
        pair_copy(0, 0).start()
        lax.fori_loop(0, row_n, hand_out, 0)

    def advance_late(n, carry):
        advance(n, carry)

        @pl.when(diag)
        def _():
            for u in range(per_step):
                q = (n - half) * per_step + u

                @pl.when(q < row_n)
                def _():
                    turn_own(q)
        return carry

    lax.fori_loop(half, 2 * half, advance_late, 0)

    @pl.when(diag)
    def _():
        lax.fori_loop(0, row_n, turn_come, 0)
        for q in range(row_n):
            pltpu.make_async_copy(turned.at[q], s_out.at[q], pair_sem.at[2 + q]).wait()

        def sent(q, carry):
            for i in range(ratio):
                _, home_lane = tile_place(g.col, i)

                @pl.when(home_lane == g.lane)
                def _():
                    for step in range(1, lanes):
                        turn_copy(i, step, q).wait_send()
            return carry

        lax.fori_loop(0, row_n, sent, 0)

    @pl.when(at != home)
    def _():
        for slot in range(line):
            pltpu.make_async_copy(own_buf.at[slot], s_out.at[slot * lanes + g.lane], own_sem.at[2 + slot]).start()
        for slot in range(line):
            pltpu.make_async_copy(own_buf.at[slot], s_out.at[slot * lanes + g.lane], own_sem.at[2 + slot]).wait()

    def finish(n, carry):
        slot, p = n // pieces, lax.rem(n, pieces)

        @pl.when((slot <= at + 1 - first_step) & up_ok)
        def _():
            up_copy(slot, p).wait_send()

        @pl.when((slot >= at - 1 + first_step) & down_ok)
        def _():
            down_copy(slot, p).wait_send()

        @pl.when(at != home)
        def _():
            for step in range(1, lanes):
                lane_copy(step, slot, p).wait_send()
                came = slot * lanes + lax.rem(g.lane - step + lanes, lanes)
                rows = pl.ds(pl.multiple_of(p * piece, piece), piece)
                remote(lane_buf.at[step - 1, slot, rows, :], s_out.at[came, rows, :], lane_send.at[step - 1, slot, p],
                       lane_recv.at[step - 1, slot, p], g.other_lane(step)).wait_recv()
        return carry

    lax.fori_loop(0, line * pieces, finish, 0)
    for b in range(block_n):
        for step in range(first_step, g.chips):
            chip_copy(step, b).wait_send()
        if g.cores == 2:
            for step in range(g.chips):
                core_copy(step, b).wait_send()
    if with_ham:
        for i in range(ratio):
            _, home_lane = tile_place(g.col, i)

            def settle(p, carry):
                ham_sends(i, p, lambda copy: copy.wait_send())
                if detour:
                    far_sends(i, p, lambda copy: copy.wait_send())

                @pl.when(home_lane != g.lane)
                def _():
                    ham_copies(i, p)[2][0].wait_recv()
                return carry

            lax.fori_loop(0, pieces, settle, 0)


def exchange(rows, cols, ham, ahead, sel, row_n, col_n, ident):
    hot_count, size, width = rows.shape
    block_n, height = cols.shape[:2]
    ratio = row_n // col_n
    pieces = 4
    line, lanes, chips, _ = layout(row_n, col_n)
    others = max(lanes - 1, 1)
    dma = pltpu.SemaphoreType.DMA
    vmem = lambda *shape: pltpu.VMEM(shape, jnp.bfloat16)
    anywhere = pl.BlockSpec(memory_space=pl.ANY)
    out_shape = [
        jax.ShapeDtypeStruct((row_n, size, width), jnp.bfloat16),
        jax.ShapeDtypeStruct((col_n * block_n, height, size), jnp.bfloat16),
    ]
    scratch = [
        vmem(line, hot_count, size, width),
        vmem(others, line, size, width),
        vmem(line, size, width),
        vmem(*cols.shape),
        vmem(2, hot_count, height, size),
        vmem(others, row_n, height, size),
        vmem(ratio, row_n, height, size),
        vmem(row_n, size, width),
        dma((2 + line,)),
        dma((line, pieces)),
        dma((line, pieces)),
        dma((line, pieces)),
        dma((others, line, pieces)),
        dma((others, line, pieces)),
        dma((max(chips - 1, 1), block_n)),
        dma((max(chips - 1, 1), block_n)),
        dma((chips, block_n)),
        dma((chips, block_n)),
        dma((2 + row_n,)),
        dma((others, row_n)),
        dma((ratio, row_n)),
    ]
    args = [sel, rows, cols]
    if ahead is not None:
        scratch += [vmem(*cols.shape), dma((3,))]
        args += ahead
    if ham is not None:
        out_shape.append(jax.ShapeDtypeStruct((ratio,) + ham.shape, ham.dtype))
        scratch += [
            pltpu.VMEM(ham.shape, ham.dtype),
            pltpu.VMEM(ham.shape, ham.dtype),
            dma((1,)),
            dma((ratio, pieces)),
            dma((ratio, pieces)),
            dma((ratio, pieces)),
            dma((ratio, others, pieces)),
            dma((pieces,)),
            dma((pieces,)),
            dma((pieces,)),
        ]
        args.append(ham)
    return pl.pallas_call(
        functools.partial(exchange_kernel, row_n, col_n, pieces, ham is not None, ahead is not None),
        out_shape=out_shape,
        in_specs=[pl.BlockSpec(memory_space=pltpu.SMEM)] + [anywhere] * (len(args) - 1),
        out_specs=[anywhere] * len(out_shape),
        scratch_shapes=scratch,
        compiler_params=pltpu.CompilerParams(collective_id=ident, has_side_effects=True, vmem_limit_bytes=VMEM_LIMIT),
    )(*args)


def hot_kernel(row_n, hot_count, place, hot, sel, *refs):
    refs = list(refs)

    def some(count):
        taken = refs[:count]
        del refs[:count]
        return taken

    wide = lambda blocks: jnp.concatenate(blocks, axis=1)
    wa_hot, x_rows, rd_hot = some(hot_count), some(hot_count), some(hot_count)
    b_hot = [some(row_n) for _ in range(hot_count)]
    s_ref, wb_ref, cd_ref = some(3)
    wa_ref, rd_ref = some(2)
    b_refs = some(row_n)
    s_hot, wb_hot, x_cols, cd_hot = some(hot_count), some(hot_count), some(hot_count), some(hot_count)
    rows_ref, cols_ref = refs
    scale = 1.0 / half_width

    def dot(a, b):
        return jnp.dot(a, b, preferred_element_type=jnp.float32)

    size = rows_ref.shape[1]
    acc = dot(jnp.concatenate([w[...] for w in wa_hot], axis=0), s_ref[...])
    beta = jnp.concatenate([wide([b[0] for b in blocks]) for blocks in b_hot], axis=0)
    acc = acc + dot(beta, wb_ref[0])
    for h in range(hot_count):
        value = acc[h * size:(h + 1) * size] + (rd_hot[h][...] + cd_ref[...] - center) * x_rows[h][...]
        rows_ref[h] = (value * scale).astype(rows_ref.dtype)
    acc = dot(wa_ref[...], wide([s[...] for s in s_hot]))
    acc = acc + dot(wide([b[0] for b in b_refs]), wide([w[0] for w in wb_hot]))
    for h in range(hot_count):
        value = acc[:, h * size:(h + 1) * size] + (rd_ref[...] + cd_hot[h][...] - center) * x_cols[h][...]
        cols_ref[h] = (value * scale).astype(cols_ref.dtype)


def hot_step(place, hot, sel, wa, s, wb, rd, cd, cols, x, row_n, ratio):
    height, width = x.shape
    size = cols.shape[-1]
    hot_count = hot.shape[0] // row_n
    tile_width = width // ratio
    stripe = tile_width // 2 if tile_width % 256 == 0 else size
    per_tile = tile_width // stripe
    blocks = tile_width // size
    depth = s.shape[0]

    def tile(n):
        return jnp.minimum(n // per_tile, ratio - 1)

    def hot_row(h, place, hot):
        return hot[place[0] * hot_count + h]

    def hot_col(h, n, place, hot):
        return hot[(place[1] * ratio + tile(n)) * hot_count + h]

    def source(q, n, place, sel):
        return q * hot_count + sel[(place[1] * ratio + tile(n)) * row_n + q]

    spec = pl.BlockSpec
    each = range(hot_count)
    in_specs = [spec((size, depth), lambda n, place, hot, sel, h=h: (hot_row(h, place, hot), 0)) for h in each]
    in_specs += [spec((size, stripe), lambda n, place, hot, sel, h=h: (hot_row(h, place, hot), n)) for h in each]
    in_specs += [spec((size, 1), lambda n, place, hot, sel, h=h: (hot_row(h, place, hot), 0)) for h in each]
    in_specs += [spec((1, size, size), lambda n, place, hot, sel, h=h, q=q: (source(q, n, place, sel), hot_row(h, place, hot), 0))
                 for h in each for q in range(row_n)]
    in_specs += [
        spec((depth, stripe), lambda n, *_: (0, n)),
        spec((1, depth, stripe), lambda n, *_: (n // per_tile, 0, n % per_tile)),
        spec((1, stripe), lambda n, *_: (0, n)),
        spec((stripe, depth), lambda n, *_: (n % per_tile, 0)),
        spec((stripe, 1), lambda n, *_: (n % per_tile, 0)),
    ]
    in_specs += [spec((1, stripe, size), lambda n, place, hot, sel, q=q: (source(q, n, place, sel), n % per_tile, 0)) for q in range(row_n)]
    in_specs += [spec((depth, size), lambda n, place, hot, sel, h=h: (0, tile(n) * blocks + hot_col(h, n, place, hot))) for h in each]
    in_specs += [spec((1, depth, size), lambda n, place, hot, sel, h=h: (tile(n), 0, hot_col(h, n, place, hot))) for h in each]
    in_specs += [spec((stripe, size), lambda n, place, hot, sel, h=h: (n % per_tile, tile(n) * blocks + hot_col(h, n, place, hot))) for h in each]
    in_specs += [spec((1, size), lambda n, place, hot, sel, h=h: (0, tile(n) * blocks + hot_col(h, n, place, hot))) for h in each]
    args = [wa] * hot_count + [x] * hot_count + [rd] * hot_count + [cols] * (hot_count * row_n)
    args += [s, wb, cd, wa, rd] + [cols] * row_n + [s] * hot_count + [wb] * hot_count + [x] * hot_count + [cd] * hot_count
    grid_spec = pltpu.PrefetchScalarGridSpec(
        num_scalar_prefetch=3,
        grid=(width // stripe,),
        in_specs=in_specs,
        out_specs=[
            spec((hot_count, size, stripe), lambda n, *_: (0, 0, n)),
            spec((hot_count, stripe, size), lambda n, *_: (n // per_tile, n % per_tile, 0)),
        ],
    )
    return pl.pallas_call(
        functools.partial(hot_kernel, row_n, hot_count),
        out_shape=[
            jax.ShapeDtypeStruct((hot_count, size, width), jnp.bfloat16),
            jax.ShapeDtypeStruct((ratio * hot_count, height, size), jnp.bfloat16),
        ],
        grid_spec=grid_spec,
        compiler_params=pltpu.CompilerParams(vmem_limit_bytes=VMEM_LIMIT),
    )(place, hot, sel, *args)


def first_hops(rows, cols, row_n, col_n):
    line, lanes, chips, cores = layout(row_n, col_n)
    upward = [(r, r + lanes) for r in range(row_n - lanes)]
    below = lax.ppermute(rows, "row", upward)
    above = lax.ppermute(rows, "row", [(b, a) for a, b in upward])
    turn = [(c, (c // cores + 1) % chips * cores + c % cores) for c in range(col_n)]
    return [below, above, lax.ppermute(cols, "col", turn)]


def filter_kernel(source_count, row_chunk, last, place, sel, wa_ref, s_ref, wb_ref, rd_ref, cd_ref, *refs):
    b_refs = refs[:source_count]
    rest = refs[source_count:]
    if last:
        x_ref, start_ref, out_ref = rest
    else:
        x_ref, out_ref = rest

    def chunk(i, carry):
        rows = pl.ds(pl.multiple_of(i * row_chunk, row_chunk), row_chunk)
        beta = jnp.concatenate([b[0, rows, :] for b in b_refs], axis=1)
        acc = jnp.dot(wa_ref[rows, :], s_ref[...], preferred_element_type=jnp.float32)
        acc = acc + jnp.dot(beta, wb_ref[0], preferred_element_type=jnp.float32)
        x = x_ref[rows, :]
        acc = acc + (rd_ref[rows, :] + cd_ref[...] - center) * x
        if last:
            out_ref[rows, :] = acc * (2.0 / half_width) - start_ref[rows, :]
        else:
            out_ref[rows, :] = acc * (1.0 / half_width)
        return carry

    lax.fori_loop(0, x_ref.shape[0] // row_chunk, chunk, 0)


def filter_step(place, sel, wa, s, wb, rd, cd, cols, x, start, row_n, ratio):
    height, width = x.shape
    size = cols.shape[-1]
    hot_count = cols.shape[0] // row_n
    tile_width = width // ratio
    stripe = next(n for n in (512, 384, 256, size) if tile_width % n == 0)
    per_tile = tile_width // stripe
    row_chunk = height // 2 if height % 256 == 0 else height
    last = start is not None

    def b_spec(q):
        return pl.BlockSpec(
            (1, height, size),
            lambda n, place, sel: (q * hot_count + sel[(place[1] * ratio + jnp.minimum(n // per_tile, ratio - 1)) * row_n + q], 0, 0))

    striped = pl.BlockSpec((height, stripe), lambda n, *_: (0, n))
    in_specs = [
        pl.BlockSpec(wa.shape, lambda n, *_: (0, 0)),
        pl.BlockSpec((s.shape[0], stripe), lambda n, *_: (0, n)),
        pl.BlockSpec((1, wb.shape[1], stripe), lambda n, *_: (n // per_tile, 0, n % per_tile)),
        pl.BlockSpec((height, 1), lambda n, *_: (0, 0)),
        pl.BlockSpec((1, stripe), lambda n, *_: (0, n)),
    ] + [b_spec(q) for q in range(row_n)] + [striped] * (2 if last else 1)
    args = [wa, s, wb, rd, cd] + [cols] * row_n + [x] + ([start] if last else [])
    grid_spec = pltpu.PrefetchScalarGridSpec(
        num_scalar_prefetch=2, grid=(width // stripe,), in_specs=in_specs, out_specs=striped)
    return pl.pallas_call(
        functools.partial(filter_kernel, row_n, row_chunk, last),
        out_shape=jax.ShapeDtypeStruct(x.shape, jnp.float32),
        grid_spec=grid_spec,
        cost_estimate=pl.CostEstimate(
            flops=4 * height * width * s.shape[0], bytes_accessed=4 * 3 * height * width, transcendentals=0),
        compiler_params=pltpu.CompilerParams(vmem_limit_bytes=VMEM_LIMIT),
    )(place, sel, *args)


def body(start_vector, ham_blocks, diagonal, pair_lists, pair_counts, hot_blocks, selection):
    row_n = lax.axis_size("row")
    col_n = lax.axis_size("col")
    ratio = row_n // col_n
    height, width = start_vector.shape
    size = ham_blocks.shape[1]
    row_index = lax.axis_index("row")
    col_index = lax.axis_index("col")
    place = jnp.stack([row_index, col_index]).astype(jnp.int32)
    pairs = pair_lists.reshape(-1)
    hot = hot_blocks.reshape(-1)
    sel = selection.reshape(-1)
    rd = lax.dynamic_slice_in_dim(diagonal, row_index * height, height)[:, None]
    cd = lax.dynamic_slice_in_dim(diagonal, col_index * width, width)[None, :]
    depth = row_n * size

    rows, cols = pack(start_vector, place, hot, row_n, ratio, size)
    s, b, hams = exchange(rows, cols, ham_blocks, None, sel, row_n, col_n, 0)
    s = s.reshape(depth, width)
    wa = dense(ham_blocks[None], place[:1], pairs, pair_counts, (height, depth), False)[0]
    mirrors = (col_index * ratio + jnp.arange(ratio)).astype(jnp.int32)
    wb = dense(hams, mirrors, pairs, pair_counts, (depth, width // ratio), True)
    rows, cols = hot_step(place, hot, sel, wa, s, wb, rd, cd, b, start_vector, row_n, ratio)
    ahead = first_hops(rows, cols, row_n, col_n)
    s, _ = lax.optimization_barrier((s, rows))
    first = filter_step(place, sel, wa, s, wb, rd, cd, b, start_vector, None, row_n, ratio)
    s, b = exchange(rows, cols, None, ahead, sel, row_n, col_n, 1)
    second = filter_step(place, sel, wa, s.reshape(depth, width), wb, rd, cd, b, first, start_vector, row_n, ratio)
    return (first, second)


def solution(mesh):
    in_specs = (P("row", "col"), P("row", None, None), P(), P(), P(), P(), P())
    out_specs = (P("row", "col"), P("row", "col"))
    return jax.shard_map(body, mesh=mesh, in_specs=in_specs, out_specs=out_specs, check_vma=False)
```

```python
import functools

import jax
import jax.numpy as jnp
from jax import lax
from jax.experimental import pallas as pl
from jax.experimental.pallas import tpu as pltpu
from jax.sharding import PartitionSpec as P

center = 0.25
half_width = 2.5
VMEM_LIMIT = 60 * 1024 * 1024
VMEM_MOST = 67043328
MESH = pl.DeviceIdType.MESH


def dense_kernel(transposed, tiles, pairs, counts, ham_ref, out_ref, acc):
    tile = tiles[pl.program_id(0)]
    tile_count = counts.shape[0]
    slots = pairs.shape[0] // (3 * tile_count)
    size = ham_ref.shape[-1]
    acc[...] = jnp.zeros_like(acc)

    def add(slot, carry):
        at = tile * slots + slot
        source = pl.multiple_of(pairs[at] * size, size)
        target = pl.multiple_of(pairs[tile_count * slots + at] * size, size)
        block = ham_ref[0, pairs[2 * tile_count * slots + at]].astype(jnp.float32)
        if transposed:
            acc[pl.ds(source, size), pl.ds(target, size)] += block.T
        else:
            acc[pl.ds(target, size), pl.ds(source, size)] += block
        return carry

    lax.fori_loop(0, counts[tile], add, 0)
    out_ref[0] = acc[...].astype(out_ref.dtype)


def dense(hams, tiles, pairs, counts, shape, transposed):
    grid_spec = pltpu.PrefetchScalarGridSpec(
        num_scalar_prefetch=3,
        grid=(hams.shape[0],),
        in_specs=[pl.BlockSpec((1,) + hams.shape[1:], lambda i, *_: (i, 0, 0, 0))],
        out_specs=pl.BlockSpec((1,) + shape, lambda i, *_: (i, 0, 0)),
        scratch_shapes=[pltpu.VMEM(shape, jnp.float32)],
    )
    return pl.pallas_call(
        functools.partial(dense_kernel, transposed),
        out_shape=jax.ShapeDtypeStruct((hams.shape[0],) + shape, jnp.bfloat16),
        grid_spec=grid_spec,
        compiler_params=pltpu.CompilerParams(vmem_limit_bytes=VMEM_LIMIT),
    )(tiles, pairs, counts, hams)


def pack_kernel(place, hot, xr_ref, xc_ref, rows_ref, cols_ref):
    rows_ref[0] = xr_ref[...].astype(rows_ref.dtype)
    cols_ref[0] = xc_ref[...].astype(cols_ref.dtype)


def pack(x, place, hot, row_count, ratio, size):
    height, width = x.shape
    hot_count = hot.shape[0] // row_count
    blocks = width // (ratio * size)
    part = width // ratio

    def row_block(n, place, hot):
        n = jnp.minimum(n, ratio * hot_count - 1)
        return (hot[place[0] * hot_count + n // ratio], n % ratio)

    def col_block(n, place, hot):
        n = jnp.minimum(n, ratio * hot_count - 1)
        tile, which = n // hot_count, n % hot_count
        return (0, tile * blocks + hot[(place[1] * ratio + tile) * hot_count + which])

    grid_spec = pltpu.PrefetchScalarGridSpec(
        num_scalar_prefetch=2,
        grid=(ratio * hot_count,),
        in_specs=[pl.BlockSpec((size, part), row_block), pl.BlockSpec((height, size), col_block)],
        out_specs=[
            pl.BlockSpec((1, size, part), lambda n, *_: (n // ratio, 0, n % ratio)),
            pl.BlockSpec((1, height, size), lambda n, *_: (n, 0, 0)),
        ],
    )
    return pl.pallas_call(
        pack_kernel,
        out_shape=[
            jax.ShapeDtypeStruct((hot_count, size, width), jnp.bfloat16),
            jax.ShapeDtypeStruct((ratio * hot_count, height, size), jnp.bfloat16),
        ],
        grid_spec=grid_spec,
    )(place, hot, x, x)


def layout(row_n, col_n):
    line = 1
    while 4 * line * line <= 2 * row_n:
        line *= 2
    cores = 2 if col_n % 2 == 0 else 1
    return line, row_n // line, col_n // cores, cores


class Grid:
    def __init__(self, row_n, col_n):
        self.line, self.lanes, self.chips, self.cores = layout(row_n, col_n)
        self.row_n, self.col_n = row_n, col_n
        row, col = lax.axis_index("row"), lax.axis_index("col")
        self.row, self.col = row, col
        self.at, self.lane = row // self.lanes, lax.rem(row, self.lanes)
        self.chip, self.core = col // self.cores, lax.rem(col, self.cores)

    def on_line(self, at):
        return (at * self.lanes + self.lane, self.col)

    def other_lane(self, step):
        return (self.at * self.lanes + lax.rem(self.lane + step, self.lanes), self.col)

    def other_chip(self, step):
        return (self.row, lax.rem(self.chip + step, self.chips) * self.cores + self.core)

    def other_core(self):
        return (self.row, self.chip * self.cores + lax.rem(self.core + 1, self.cores))


def remote(src, dst, send, recv, device):
    return pltpu.make_async_remote_copy(
        src_ref=src, dst_ref=dst, send_sem=send, recv_sem=recv, device_id=device, device_id_type=MESH)


def greet(g):
    barrier = pltpu.get_barrier_semaphore()
    up, down = g.at + 1 < g.line, g.at > 0

    def hello(device):
        pl.semaphore_signal(barrier, inc=1, device_id=device, device_id_type=MESH)

    @pl.when(up)
    def _():
        hello(g.on_line(g.at + 1))

    @pl.when(down)
    def _():
        hello(g.on_line(g.at - 1))

    for step in range(1, g.lanes):
        hello(g.other_lane(step))
    for step in range(1, g.chips):
        hello(g.other_chip(step))
    fixed = g.lanes - 1 + g.chips - 1
    if g.cores == 2:
        hello(g.other_core())
        fixed += 1
    pl.semaphore_wait(barrier, fixed + up.astype(jnp.int32) + down.astype(jnp.int32))


def late_slot(at, line):
    return jnp.where(2 * at < line, line - 1, 0)


def exchange_kernel(row_n, col_n, pieces, with_ham, fused, sel, rows_ref, cols_ref, *refs):
    g = Grid(row_n, col_n)
    refs = list(refs)

    def some(count):
        taken = refs[:count]
        del refs[:count]
        return taken

    first_step = 2 if fused else 1
    if fused:
        below_ref, above_ref, chip_ref, wa_hbm, wb_hbm, rd_ref, cd_ref, x_hbm, start_hbm, s_out, acc_out = some(11)
    else:
        ham_ref, s_out, c_out, h_out = some(4)
    held, lane_buf, turn_buf, s_all, c_all = some(5)
    own_sem, line_recv, up_send, down_send, lane_send, lane_recv = some(6)
    chip_send, chip_recv, core_send, core_recv, turn_send, turn_recv = some(6)
    if fused:
        acc, wa, wb, x_buf, start_buf, load_sem, x_sem, start_sem, acc_sem = some(9)
    else:
        ham_buf, far_buf, ham_sem, ham_recv, ham_up, ham_down, ham_lane, far_recv, far_send, far_chip = some(10)
        ham_rows = ham_ref.shape[0] // pieces
    ratio = row_n // col_n
    hot_count, size = rows_ref.shape[0], rows_ref.shape[1]
    height = cols_ref.shape[1]
    width = rows_ref.shape[2]
    piece = size // pieces
    block_n = cols_ref.shape[0]
    line, lanes, at = g.line, g.lanes, g.at

    home = (g.col * ratio) // lanes
    diag = at == home
    up_ok = (at + 1 < line) & ((home != line - 1) | (at + 1 != line - 1))
    down_ok = (at > 0) & ((home != 0) | (at - 1 != 0))
    deaf = diag & ((at == 0) | (at == line - 1))

    def chip_slot(step):
        return (lax.rem(g.chip - step + g.chips, g.chips) * g.cores + g.core) * block_n

    own_slot = g.col * block_n
    take = pltpu.make_async_copy(rows_ref, held.at[at], own_sem.at[0])
    take_cols = pltpu.make_async_copy(cols_ref, c_all.at[pl.ds(own_slot, block_n)], own_sem.at[1])
    take.start()
    take_cols.start()
    if fused:
        take_chip = pltpu.make_async_copy(chip_ref, c_all.at[pl.ds(chip_slot(1), block_n)], own_sem.at[2])
        take_chip.start()

        @pl.when(at > 0)
        def _():
            pltpu.make_async_copy(below_ref, held.at[at - 1], own_sem.at[3]).start()

        @pl.when(at + 1 < line)
        def _():
            pltpu.make_async_copy(above_ref, held.at[at + 1], own_sem.at[4]).start()
    else:
        take_ham = pltpu.make_async_copy(ham_ref, ham_buf, ham_sem.at[0])
        take_ham.start()
    greet(g)

    def chip_copy(step, b):
        return remote(cols_ref.at[b], c_all.at[own_slot + b], chip_send.at[step - 1, b], chip_recv.at[step - 1, b], g.other_chip(step))

    def core_copy(step, b):
        if step == 0:
            src, slot = cols_ref.at[b], own_slot + b
        else:
            slot = chip_slot(step) + b
            src = chip_ref.at[b] if fused and step == 1 else c_all.at[slot]
        return remote(src, c_all.at[slot], core_send.at[step, b], core_recv.at[step, b], g.other_core())

    for b in range(block_n):
        for step in range(first_step, g.chips):
            chip_copy(step, b).start()
    if g.cores == 2:
        for step in range(first_step):
            for b in range(block_n):
                core_copy(step, b).start()
    take.wait()
    if fused:
        @pl.when(at > 0)
        def _():
            pltpu.make_async_copy(below_ref, held.at[at - 1], own_sem.at[3]).wait()

        @pl.when(at + 1 < line)
        def _():
            pltpu.make_async_copy(above_ref, held.at[at + 1], own_sem.at[4]).wait()

    def part(slot, p):
        return held.at[slot, :, pl.ds(pl.multiple_of(p * piece, piece), piece), :]

    def up_copy(slot, p):
        return remote(part(slot, p), part(slot, p), up_send.at[slot, p], line_recv.at[slot, p], g.on_line(at + 1))

    def down_copy(slot, p):
        return remote(part(slot, p), part(slot, p), down_send.at[slot, p], line_recv.at[slot, p], g.on_line(at - 1))

    def s_rows(source, p):
        return pl.ds(pl.multiple_of(source * size + p * piece, piece), piece)

    def lane_copy(step, slot, p):
        rows = pl.ds(pl.multiple_of(p * piece, piece), piece)
        return remote(
            lane_buf.at[step - 1, slot, rows, :], s_all.at[s_rows(slot * lanes + g.lane, p), :],
            lane_send.at[step - 1, slot, p], lane_recv.at[step - 1, slot, p], g.other_lane(step))

    def lane_came(step, slot, p):
        rows = pl.ds(pl.multiple_of(p * piece, piece), piece)
        came = slot * lanes + lax.rem(g.lane - step + lanes, lanes)
        return remote(
            lane_buf.at[step - 1, slot, rows, :], s_all.at[s_rows(came, p), :],
            lane_send.at[step - 1, slot, p], lane_recv.at[step - 1, slot, p], g.other_lane(step))

    def pick(target, source, blocks):
        which = sel[target * row_n + source]
        value = blocks[0]
        for h in range(1, hot_count):
            value = jnp.where(which == h, blocks[h], value)
        return value

    def select(slot, p):
        source = slot * lanes + g.lane
        rows = pl.ds(pl.multiple_of(p * piece, piece), piece)
        blocks = [held[slot, h, rows, :] for h in range(hot_count)]
        for step in range(1, lanes):
            target = at * lanes + lax.rem(g.lane + step, lanes)
            lane_buf[step - 1, slot, rows, :] = pick(target, source, blocks)
            lane_copy(step, slot, p).start()
        s_all[s_rows(source, p), :] = pick(g.row, source, blocks)

    def tile_place(col, i):
        tile = col * ratio + i
        return tile // lanes, lax.rem(tile, lanes)

    detour = g.chips % 2 == 0 and g.chips > 1
    across = g.chips // 2
    end = jnp.where(2 * home < line, line - 1, 0)
    if not fused:
        def ham_part(ref, p):
            return ref.at[pl.ds(pl.multiple_of(p * ham_rows, ham_rows), ham_rows)]

        def ham_copies(i, p):
            here = ham_part(h_out.at[i], p)
            up = remote(here, here, ham_up.at[i, p], ham_recv.at[i, p], g.on_line(at + 1))
            down = remote(here, here, ham_down.at[i, p], ham_recv.at[i, p], g.on_line(at - 1))
            over = [remote(here, here, ham_lane.at[i, step - 1, p], ham_recv.at[i, p], g.other_lane(step))
                    for step in range(1, lanes)]
            return up, down, over

        def ham_sends(i, p, act):
            _, home_lane = tile_place(g.col, i)
            up, down, over = ham_copies(i, p)
            skip = end if detour else line

            @pl.when(home_lane == g.lane)
            def _():
                @pl.when((at >= home) & (at + 1 < line) & (at + 1 != skip))
                def _():
                    act(up)

                @pl.when((at <= home) & (at > 0) & (at - 1 != skip))
                def _():
                    act(down)

                for copy in over:
                    act(copy)

        if detour:
            far_col = lax.rem(g.chip + across, g.chips) * g.cores + g.core
            far_home = (far_col * ratio) // lanes
            far_end = jnp.where(2 * far_home < line, line - 1, 0)
            rising = far_end > far_home
            far_away = jnp.where(rising, at - far_home, far_home - at)

            def far_copies(i, p):
                here = ham_part(far_buf, p)
                way = jnp.where(rising, at + 1, at - 1)
                on = remote(here, here, far_send.at[p], far_recv.at[p], g.on_line(way))
                chip = remote(here, ham_part(h_out.at[i], p), far_chip.at[p], ham_recv.at[i, p], g.other_chip(across))
                return on, chip

            def far_sends(i, p, act):
                _, far_lane = tile_place(far_col, i)
                on, chip = far_copies(i, p)

                @pl.when((far_lane == g.lane) & (far_away >= 0))
                def _():
                    @pl.when(at != far_end)
                    def _():
                        act(on)

                    @pl.when(at == far_end)
                    def _():
                        act(chip)

        take_ham.wait()
        for i in range(ratio):
            _, home_lane = tile_place(g.col, i)

            @pl.when((home == at) & (home_lane == g.lane))
            def _():
                put = pltpu.make_async_copy(ham_buf, h_out.at[i], ham_sem.at[0])
                put.start()
                put.wait()

            if detour:
                _, far_lane = tile_place(far_col, i)

                @pl.when((far_home == at) & (far_lane == g.lane))
                def _():
                    put = pltpu.make_async_copy(ham_ref, far_buf, ham_sem.at[0])
                    put.start()
                    put.wait()

        def ham_step(s, p):
            for i in range(ratio):
                _, home_lane = tile_place(g.col, i)
                away = jnp.where(at >= home, at - home, home - at)

                @pl.when((home_lane == g.lane) & (away == s))
                def _():
                    @pl.when(s > 0)
                    def _():
                        ham_copies(i, p)[0].wait_recv()

                    ham_sends(i, p, lambda copy: copy.start())

                if detour:
                    _, far_lane = tile_place(far_col, i)

                    @pl.when((far_lane == g.lane) & (far_away == s))
                    def _():
                        @pl.when(s > 0)
                        def _():
                            far_copies(i, p)[0].wait_recv()

                        far_sends(i, p, lambda copy: copy.start())

        def ham_start(p, carry):
            ham_step(0, p)
            return carry

        lax.fori_loop(0, pieces, ham_start, 0)

    def hears(s):
        quiet = (s == 0) | (deaf == False)
        return (at - s >= 0) & quiet, (at + s < line) & quiet

    def relay(n, carry):
        s, p = n // pieces, lax.rem(n, pieces)
        hears_below, hears_above = hears(s)

        @pl.when(hears_below)
        def _():
            @pl.when(s >= first_step)
            def _():
                up_copy(at - s, p).wait_recv()

            @pl.when(up_ok & (s >= first_step - 1))
            def _():
                up_copy(at - s, p).start()

        @pl.when(hears_above)
        def _():
            @pl.when(s >= first_step)
            def _():
                down_copy(at + s, p).wait_recv()

            @pl.when(down_ok & (s >= first_step - 1))
            def _():
                down_copy(at + s, p).start()
        return carry

    def digest(n, carry):
        s, p = n // pieces, lax.rem(n, pieces)
        hears_below, hears_above = hears(s)

        @pl.when(hears_below & (at != home))
        def _():
            select(at - s, p)

        @pl.when(hears_above & (s > 0) & (at != home))
        def _():
            select(at + s, p)
        return carry

    def advance(n, carry):
        relay(n, carry)
        if not fused:
            s, p = n // pieces, lax.rem(n, pieces)

            @pl.when(s > 0)
            def _():
                ham_step(s, p)
        return digest(n, carry)

    def core_came(step, b):
        other = lax.rem(g.core + 1, g.cores)
        slot = (lax.rem(g.chip - step + g.chips, g.chips) * g.cores + other) * block_n + b
        return remote(cols_ref.at[b], c_all.at[slot], core_send.at[step, b], core_recv.at[step, b], g.other_core())

    def turn_copy(i, step, q):
        rows = pl.ds(pl.multiple_of(q * size, size), size)
        return remote(turn_buf.at[step - 1, q], s_all.at[rows, i * height:(i + 1) * height],
                      turn_send.at[step - 1, q], turn_recv.at[i, q], g.other_lane(step))

    def turn(q):
        rows = pl.ds(pl.multiple_of(q * size, size), size)
        for i in range(ratio):
            _, home_lane = tile_place(g.col, i)

            @pl.when(home_lane == g.lane)
            def _():
                for k in range(height // size):
                    strip = slice(k * size, (k + 1) * size)
                    blocks = [c_all[q * hot_count + h, strip, :] for h in range(hot_count)]
                    for step in range(1, lanes):
                        target = at * lanes + lax.rem(g.lane + step, lanes)
                        value = pick(target, q, blocks).astype(jnp.float32).T
                        turn_buf[step - 1, q, :, strip] = value.astype(turn_buf.dtype)
                    value = pick(g.row, q, blocks).astype(jnp.float32).T
                    s_all[rows, i * height + k * size:i * height + (k + 1) * size] = value.astype(s_all.dtype)
                for step in range(1, lanes):
                    turn_copy(i, step, q).start()

    def turns(act):
        def one(q, carry):
            for i in range(ratio):
                _, home_lane = tile_place(g.col, i)
                act(i, q, home_lane)
            return carry

        lax.fori_loop(0, row_n, one, 0)

    def turn_came(i, q, home_lane):
        @pl.when(home_lane != g.lane)
        def _():
            turn_copy(i, 1, q).wait_recv()

    def turn_sent(i, q, home_lane):
        @pl.when(home_lane == g.lane)
        def _():
            for step in range(1, lanes):
                turn_copy(i, step, q).wait_send()

    if fused:
        stripe = x_buf.shape[2]
        stripes = width // stripe
        per_tile = height // stripe
        rows_at_once = height // 2
        share = -(-stripes // pieces)
        late = late_slot(at, line)
        take_wa = pltpu.make_async_copy(wa_hbm, wa, load_sem.at[0])
        take_wb = pltpu.make_async_copy(wb_hbm, wb, load_sem.at[1])

        def band(n):
            return pl.ds(pl.multiple_of(n * stripe, stripe), stripe)

        def x_copy(n):
            return pltpu.make_async_copy(x_hbm.at[:, band(n)], x_buf.at[lax.rem(n, 2)], x_sem.at[lax.rem(n, 2)])

        def start_copy(n):
            return pltpu.make_async_copy(start_hbm.at[:, band(n)], start_buf.at[lax.rem(n, 2)], start_sem.at[lax.rem(n, 2)])

        def acc_copy(n):
            return pltpu.make_async_copy(acc.at[:, band(n)], acc_out.at[:, band(n)], acc_sem.at[n])

        def beta_side(n, carry):
            tile, inner = n // per_tile, lax.rem(n, per_tile)

            @pl.when(n + 1 < stripes)
            def _():
                x_copy(n + 1).start()
                start_copy(n + 1).start()

            x_copy(n).wait()
            start_copy(n).wait()
            slots = [q * hot_count + sel[(g.col * ratio + tile) * row_n + q] for q in range(row_n)]
            for k in range(2):
                rows = slice(k * rows_at_once, (k + 1) * rows_at_once)
                beta = jnp.concatenate([c_all[slots[q], rows, :] for q in range(row_n)], axis=1)
                value = jnp.dot(beta, wb[tile, :, band(inner)], preferred_element_type=jnp.float32)
                value = value + (rd_ref[rows, :] + cd_ref[:, band(n)] - center) * x_buf[lax.rem(n, 2), rows, :]
                acc[rows, band(n)] = value - start_buf[lax.rem(n, 2), rows, :] * (half_width / 2.0)
            return carry

        def alpha_side(n, carry):
            for k in range(2):
                rows = slice(k * rows_at_once, (k + 1) * rows_at_once)
                value = acc[rows, band(n)]
                for other in range(1, line):
                    slot = lax.rem(late + other, line)
                    depth = pl.ds(pl.multiple_of(slot * lanes * size, size), lanes * size)
                    value = value + jnp.dot(wa[rows, depth], s_all[depth, band(n)], preferred_element_type=jnp.float32)
                acc[rows, band(n)] = value
            acc_copy(n).start()
            return carry

        def some_stripes(work, turn_n):
            lax.fori_loop(turn_n * share, jnp.minimum(turn_n * share + share, stripes), work, 0)

    half = pieces * (line // 2)
    per_step = -(-row_n // pieces)
    if fused:
        lax.fori_loop(pieces, half, relay, 0)
        take_wa.start()
        take_wb.start()
        x_copy(0).start()
        start_copy(0).start()
        lax.fori_loop(0, half, digest, 0)
    else:
        lax.fori_loop(0, half, advance, 0)
    for step in range(first_step, g.chips):
        for b in range(block_n):
            slot = chip_slot(step) + b
            remote(cols_ref.at[b], c_all.at[slot], chip_send.at[step - 1, b], chip_recv.at[step - 1, b], g.other_chip(step)).wait_recv()
            if g.cores == 2:
                core_copy(step, b).start()

    take_cols.wait()
    if fused:
        take_chip.wait()
    if g.cores == 2:
        for step in range(g.chips):
            for b in range(block_n):
                core_came(step, b).wait_recv()
    if not fused:
        put_cols = pltpu.make_async_copy(c_all, c_out, own_sem.at[2])
        put_cols.start()
    else:
        take_wa.wait()
        take_wb.wait()

    def middle(n, carry):
        advance(n, carry)

        @pl.when(diag)
        def _():
            for u in range(per_step):
                q = (n - half) * per_step + u

                @pl.when(q < row_n)
                def _():
                    turn(q)
        if fused:
            some_stripes(beta_side, n - half)
        return carry

    def lanes_came(slot):
        def one(p, carry):
            for step in range(1, lanes):
                lane_came(step, slot, p).wait_recv()
            return carry

        @pl.when(at != home)
        def _():
            lax.fori_loop(0, pieces, one, 0)

    lax.fori_loop(half, half + pieces, middle, 0)
    if fused:
        for other in range(1, line):
            lanes_came(lax.rem(late + other, line))

        @pl.when(diag)
        def _():
            turns(turn_came)

        def ending(n, carry):
            advance(n, carry)
            some_stripes(alpha_side, n - half - pieces)
            return carry

        lax.fori_loop(half + pieces, pieces * line, ending, 0)
        lanes_came(late)
        put_s = pltpu.make_async_copy(s_all.at[pl.ds(pl.multiple_of(late * lanes * size, size), lanes * size), :], s_out, own_sem.at[5])
        put_s.start()
        put_s.wait()
        for n in range(stripes):
            acc_copy(n).wait()
    else:
        lax.fori_loop(half + pieces, pieces * line, advance, 0)
        for slot in range(line):
            lanes_came(slot)

        @pl.when(diag)
        def _():
            turns(turn_came)

        put_s = pltpu.make_async_copy(s_all, s_out, own_sem.at[5])
        put_s.start()
        put_s.wait()
        put_cols.wait()

    @pl.when(diag)
    def _():
        turns(turn_sent)

    def finish(n, carry):
        slot, p = n // pieces, lax.rem(n, pieces)

        @pl.when((slot <= at + 1 - first_step) & up_ok)
        def _():
            up_copy(slot, p).wait_send()

        @pl.when((slot >= at - 1 + first_step) & down_ok)
        def _():
            down_copy(slot, p).wait_send()

        @pl.when(at != home)
        def _():
            for step in range(1, lanes):
                lane_copy(step, slot, p).wait_send()
        return carry

    lax.fori_loop(0, line * pieces, finish, 0)
    for b in range(block_n):
        for step in range(first_step, g.chips):
            chip_copy(step, b).wait_send()
        if g.cores == 2:
            for step in range(g.chips):
                core_copy(step, b).wait_send()
    if not fused:
        for i in range(ratio):
            _, home_lane = tile_place(g.col, i)

            def settle(p, carry):
                ham_sends(i, p, lambda copy: copy.wait_send())
                if detour:
                    far_sends(i, p, lambda copy: copy.wait_send())

                @pl.when(home_lane != g.lane)
                def _():
                    ham_copies(i, p)[2][0].wait_recv()
                return carry

            lax.fori_loop(0, pieces, settle, 0)


def exchange(rows, cols, sel, row_n, col_n, ident, ham=None, ahead=None, product=None):
    hot_count, size, width = rows.shape
    block_n, height = cols.shape[:2]
    ratio = row_n // col_n
    pieces = 4
    fused = product is not None
    line, lanes, chips, _ = layout(row_n, col_n)
    others = max(lanes - 1, 1)
    dma = pltpu.SemaphoreType.DMA
    vmem = lambda *shape: pltpu.VMEM(shape, jnp.bfloat16)
    anywhere = pl.BlockSpec(memory_space=pl.ANY)
    whole = pl.BlockSpec(memory_space=pltpu.VMEM)
    scratch = [
        vmem(line, hot_count, size, width),
        vmem(others, line, size, width),
        vmem(others, row_n, size, height),
        vmem(row_n * size, width),
        vmem(col_n * block_n, height, size),
        dma((6,)),
        dma((line, pieces)),
        dma((line, pieces)),
        dma((line, pieces)),
        dma((others, line, pieces)),
        dma((others, line, pieces)),
        dma((max(chips - 1, 1), block_n)),
        dma((max(chips - 1, 1), block_n)),
        dma((chips, block_n)),
        dma((chips, block_n)),
        dma((others, row_n)),
        dma((ratio, row_n)),
    ]
    args = [sel, rows, cols]
    in_specs = [pl.BlockSpec(memory_space=pltpu.SMEM), anywhere, anywhere]
    if fused:
        wa, wb, rd, cd, x, start = product
        stripe = 256 if height % 256 == 0 else size
        args += list(ahead) + [wa, wb, rd, cd, x, start]
        in_specs += [anywhere] * 5 + [whole] * 2 + [anywhere] * 2
        out_shape = [
            jax.ShapeDtypeStruct((lanes * size, width), jnp.bfloat16),
            jax.ShapeDtypeStruct((height, width), jnp.float32),
        ]
        scratch += [
            pltpu.VMEM((height, width), jnp.float32),
            vmem(*wa.shape),
            vmem(*wb.shape),
            pltpu.VMEM((2, height, stripe), jnp.float32),
            pltpu.VMEM((2, height, stripe), jnp.float32),
            dma((2,)),
            dma((2,)),
            dma((2,)),
            dma((width // stripe,)),
        ]
    else:
        args.append(ham)
        in_specs.append(anywhere)
        out_shape = [
            jax.ShapeDtypeStruct((row_n * size, width), jnp.bfloat16),
            jax.ShapeDtypeStruct((col_n * block_n, height, size), jnp.bfloat16),
            jax.ShapeDtypeStruct((ratio,) + ham.shape, ham.dtype),
        ]
        scratch += [
            pltpu.VMEM(ham.shape, ham.dtype),
            pltpu.VMEM(ham.shape, ham.dtype),
            dma((1,)),
            dma((ratio, pieces)),
            dma((ratio, pieces)),
            dma((ratio, pieces)),
            dma((ratio, others, pieces)),
            dma((pieces,)),
            dma((pieces,)),
            dma((pieces,)),
        ]
    return pl.pallas_call(
        functools.partial(exchange_kernel, row_n, col_n, pieces, ham is not None, fused),
        out_shape=out_shape,
        in_specs=in_specs,
        out_specs=[anywhere] * len(out_shape),
        scratch_shapes=scratch,
        compiler_params=pltpu.CompilerParams(collective_id=ident, has_side_effects=True, vmem_limit_bytes=VMEM_MOST),
    )(*args)


def last_kernel(place, acc_ref, wa_ref, s_ref, out_ref):
    acc = acc_ref[...] + jnp.dot(wa_ref[...], s_ref[...], preferred_element_type=jnp.float32)
    out_ref[...] = acc * (2.0 / half_width)


def last_step(place, acc, wa, s, row_n, col_n):
    height, width = acc.shape
    depth = s.shape[0]
    line, lanes, _, _ = layout(row_n, col_n)
    stripe = 256 if width % 256 == 0 else width
    grid_spec = pltpu.PrefetchScalarGridSpec(
        num_scalar_prefetch=1,
        grid=(width // stripe,),
        in_specs=[
            pl.BlockSpec((height, stripe), lambda n, place: (0, n)),
            pl.BlockSpec((height, depth), lambda n, place: (0, late_slot(place[0] // lanes, line))),
            pl.BlockSpec((depth, stripe), lambda n, place: (0, n)),
        ],
        out_specs=pl.BlockSpec((height, stripe), lambda n, place: (0, n)),
    )
    return pl.pallas_call(
        last_kernel,
        out_shape=jax.ShapeDtypeStruct(acc.shape, jnp.float32),
        grid_spec=grid_spec,
        compiler_params=pltpu.CompilerParams(vmem_limit_bytes=VMEM_LIMIT),
    )(place, acc, wa, s)


def hot_kernel(row_n, hot_count, place, hot, sel, *refs):
    refs = list(refs)

    def some(count):
        taken = refs[:count]
        del refs[:count]
        return taken

    wide = lambda blocks: jnp.concatenate(blocks, axis=1)
    wa_hot, x_rows, rd_hot = some(hot_count), some(hot_count), some(hot_count)
    b_hot = [some(row_n) for _ in range(hot_count)]
    s_ref, wb_ref, cd_ref = some(3)
    wa_ref, rd_ref = some(2)
    b_refs = some(row_n)
    s_hot, wb_hot, x_cols, cd_hot = some(hot_count), some(hot_count), some(hot_count), some(hot_count)
    rows_ref, cols_ref = refs
    scale = 1.0 / half_width

    def dot(a, b):
        return jnp.dot(a, b, preferred_element_type=jnp.float32)

    size = rows_ref.shape[1]
    acc = dot(jnp.concatenate([w[...] for w in wa_hot], axis=0), s_ref[...])
    beta = jnp.concatenate([wide([b[0] for b in blocks]) for blocks in b_hot], axis=0)
    acc = acc + dot(beta, wb_ref[0])
    for h in range(hot_count):
        value = acc[h * size:(h + 1) * size] + (rd_hot[h][...] + cd_ref[...] - center) * x_rows[h][...]
        rows_ref[h] = (value * scale).astype(rows_ref.dtype)
    acc = dot(wa_ref[...], wide([s[...] for s in s_hot]))
    acc = acc + dot(wide([b[0] for b in b_refs]), wide([w[0] for w in wb_hot]))
    for h in range(hot_count):
        value = acc[:, h * size:(h + 1) * size] + (rd_ref[...] + cd_hot[h][...] - center) * x_cols[h][...]
        cols_ref[h] = (value * scale).astype(cols_ref.dtype)


def hot_step(place, hot, sel, wa, s, wb, rd, cd, cols, x, row_n, ratio):
    height, width = x.shape
    size = cols.shape[-1]
    hot_count = hot.shape[0] // row_n
    tile_width = width // ratio
    stripe = tile_width // 2 if tile_width % 256 == 0 else size
    per_tile = tile_width // stripe
    blocks = tile_width // size
    depth = s.shape[0]

    def tile(n):
        return jnp.minimum(n // per_tile, ratio - 1)

    def hot_row(h, place, hot):
        return hot[place[0] * hot_count + h]

    def hot_col(h, n, place, hot):
        return hot[(place[1] * ratio + tile(n)) * hot_count + h]

    def source(q, n, place, sel):
        return q * hot_count + sel[(place[1] * ratio + tile(n)) * row_n + q]

    spec = pl.BlockSpec
    each = range(hot_count)
    in_specs = [spec((size, depth), lambda n, place, hot, sel, h=h: (hot_row(h, place, hot), 0)) for h in each]
    in_specs += [spec((size, stripe), lambda n, place, hot, sel, h=h: (hot_row(h, place, hot), n)) for h in each]
    in_specs += [spec((size, 1), lambda n, place, hot, sel, h=h: (hot_row(h, place, hot), 0)) for h in each]
    in_specs += [spec((1, size, size), lambda n, place, hot, sel, h=h, q=q: (source(q, n, place, sel), hot_row(h, place, hot), 0))
                 for h in each for q in range(row_n)]
    in_specs += [
        spec((depth, stripe), lambda n, *_: (0, n)),
        spec((1, depth, stripe), lambda n, *_: (n // per_tile, 0, n % per_tile)),
        spec((1, stripe), lambda n, *_: (0, n)),
        spec((stripe, depth), lambda n, *_: (n % per_tile, 0)),
        spec((stripe, 1), lambda n, *_: (n % per_tile, 0)),
    ]
    in_specs += [spec((1, stripe, size), lambda n, place, hot, sel, q=q: (source(q, n, place, sel), n % per_tile, 0)) for q in range(row_n)]
    in_specs += [spec((depth, size), lambda n, place, hot, sel, h=h: (0, tile(n) * blocks + hot_col(h, n, place, hot))) for h in each]
    in_specs += [spec((1, depth, size), lambda n, place, hot, sel, h=h: (tile(n), 0, hot_col(h, n, place, hot))) for h in each]
    in_specs += [spec((stripe, size), lambda n, place, hot, sel, h=h: (n % per_tile, tile(n) * blocks + hot_col(h, n, place, hot))) for h in each]
    in_specs += [spec((1, size), lambda n, place, hot, sel, h=h: (0, tile(n) * blocks + hot_col(h, n, place, hot))) for h in each]
    args = [wa] * hot_count + [x] * hot_count + [rd] * hot_count + [cols] * (hot_count * row_n)
    args += [s, wb, cd, wa, rd] + [cols] * row_n + [s] * hot_count + [wb] * hot_count + [x] * hot_count + [cd] * hot_count
    grid_spec = pltpu.PrefetchScalarGridSpec(
        num_scalar_prefetch=3,
        grid=(width // stripe,),
        in_specs=in_specs,
        out_specs=[
            spec((hot_count, size, stripe), lambda n, *_: (0, 0, n)),
            spec((hot_count, stripe, size), lambda n, *_: (n // per_tile, n % per_tile, 0)),
        ],
    )
    return pl.pallas_call(
        functools.partial(hot_kernel, row_n, hot_count),
        out_shape=[
            jax.ShapeDtypeStruct((hot_count, size, width), jnp.bfloat16),
            jax.ShapeDtypeStruct((ratio * hot_count, height, size), jnp.bfloat16),
        ],
        grid_spec=grid_spec,
        compiler_params=pltpu.CompilerParams(vmem_limit_bytes=VMEM_LIMIT),
    )(place, hot, sel, *args)


def first_hops(rows, cols, row_n, col_n):
    line, lanes, chips, cores = layout(row_n, col_n)
    upward = [(r, r + lanes) for r in range(row_n - lanes)]
    below = lax.ppermute(rows, "row", upward)
    above = lax.ppermute(rows, "row", [(b, a) for a, b in upward])
    turn = [(c, (c // cores + 1) % chips * cores + c % cores) for c in range(col_n)]
    return [below, above, lax.ppermute(cols, "col", turn)]


def filter_kernel(source_count, row_chunk, place, sel, wa_ref, s_ref, wb_ref, rd_ref, cd_ref, *refs):
    b_refs = refs[:source_count]
    x_ref, out_ref = refs[source_count:]

    def chunk(i, carry):
        rows = pl.ds(pl.multiple_of(i * row_chunk, row_chunk), row_chunk)
        beta = jnp.concatenate([b[0, rows, :] for b in b_refs], axis=1)
        acc = jnp.dot(wa_ref[rows, :], s_ref[...], preferred_element_type=jnp.float32)
        acc = acc + jnp.dot(beta, wb_ref[0], preferred_element_type=jnp.float32)
        acc = acc + (rd_ref[rows, :] + cd_ref[...] - center) * x_ref[rows, :]
        out_ref[rows, :] = acc * (1.0 / half_width)
        return carry

    lax.fori_loop(0, x_ref.shape[0] // row_chunk, chunk, 0)


def filter_step(place, sel, wa, s, wb, rd, cd, cols, x, row_n, ratio):
    height, width = x.shape
    size = cols.shape[-1]
    hot_count = cols.shape[0] // row_n
    tile_width = width // ratio
    stripe = next(n for n in (512, 384, 256, size) if tile_width % n == 0)
    per_tile = tile_width // stripe
    row_chunk = height // 2 if height % 256 == 0 else height

    def b_spec(q):
        return pl.BlockSpec(
            (1, height, size),
            lambda n, place, sel: (q * hot_count + sel[(place[1] * ratio + jnp.minimum(n // per_tile, ratio - 1)) * row_n + q], 0, 0))

    striped = pl.BlockSpec((height, stripe), lambda n, *_: (0, n))
    in_specs = [
        pl.BlockSpec(wa.shape, lambda n, *_: (0, 0)),
        pl.BlockSpec((s.shape[0], stripe), lambda n, *_: (0, n)),
        pl.BlockSpec((1, wb.shape[1], stripe), lambda n, *_: (n // per_tile, 0, n % per_tile)),
        pl.BlockSpec((height, 1), lambda n, *_: (0, 0)),
        pl.BlockSpec((1, stripe), lambda n, *_: (0, n)),
    ] + [b_spec(q) for q in range(row_n)] + [striped]
    args = [wa, s, wb, rd, cd] + [cols] * row_n + [x]
    grid_spec = pltpu.PrefetchScalarGridSpec(
        num_scalar_prefetch=2, grid=(width // stripe,), in_specs=in_specs, out_specs=striped)
    return pl.pallas_call(
        functools.partial(filter_kernel, row_n, row_chunk),
        out_shape=jax.ShapeDtypeStruct(x.shape, jnp.float32),
        grid_spec=grid_spec,
        cost_estimate=pl.CostEstimate(
            flops=4 * height * width * s.shape[0], bytes_accessed=4 * 3 * height * width, transcendentals=0),
        compiler_params=pltpu.CompilerParams(vmem_limit_bytes=VMEM_LIMIT),
    )(place, sel, *args)


def body(start_vector, ham_blocks, diagonal, pair_lists, pair_counts, hot_blocks, selection):
    row_n = lax.axis_size("row")
    col_n = lax.axis_size("col")
    ratio = row_n // col_n
    height, width = start_vector.shape
    size = ham_blocks.shape[1]
    row_index = lax.axis_index("row")
    col_index = lax.axis_index("col")
    place = jnp.stack([row_index, col_index]).astype(jnp.int32)
    pairs = pair_lists.reshape(-1)
    hot = hot_blocks.reshape(-1)
    sel = selection.reshape(-1)
    rd = lax.dynamic_slice_in_dim(diagonal, row_index * height, height)[:, None]
    cd = lax.dynamic_slice_in_dim(diagonal, col_index * width, width)[None, :]
    depth = row_n * size

    rows, cols = pack(start_vector, place, hot, row_n, ratio, size)
    s, b, hams = exchange(rows, cols, sel, row_n, col_n, 0, ham=ham_blocks)
    wa = dense(ham_blocks[None], place[:1], pairs, pair_counts, (height, depth), False)[0]
    mirrors = (col_index * ratio + jnp.arange(ratio)).astype(jnp.int32)
    wb = dense(hams, mirrors, pairs, pair_counts, (depth, width // ratio), True)
    rows, cols = hot_step(place, hot, sel, wa, s, wb, rd, cd, b, start_vector, row_n, ratio)
    ahead = first_hops(rows, cols, row_n, col_n)
    s, _ = lax.optimization_barrier((s, rows))
    first = filter_step(place, sel, wa, s, wb, rd, cd, b, start_vector, row_n, ratio)
    s, acc = exchange(rows, cols, sel, row_n, col_n, 1, ahead=ahead, product=(wa, wb, rd, cd, first, start_vector))
    return (first, last_step(place, acc, wa, s, row_n, col_n))


def solution(mesh):
    in_specs = (P("row", "col"), P("row", None, None), P(), P(), P(), P(), P())
    out_specs = (P("row", "col"), P("row", "col"))
    return jax.shard_map(body, mesh=mesh, in_specs=in_specs, out_specs=out_specs, check_vma=False)
```

```python
import functools

import jax
import jax.numpy as jnp
from jax import lax
from jax.experimental import pallas as pl
from jax.experimental.pallas import tpu as pltpu
from jax.sharding import PartitionSpec as P

center = 0.25
half_width = 2.5
VMEM_LIMIT = 60 * 1024 * 1024
VMEM_MOST = 67043328
MESH = pl.DeviceIdType.MESH


def dense_kernel(tile_of, place, pairs, counts, ham_ref, out_ref, acc):
    tile = tile_of(place, pl.program_id(0))
    size = ham_ref.shape[-1]
    acc[...] = jnp.zeros_like(acc)

    def add(slot, carry):
        source = pl.multiple_of(pairs[0, tile, slot] * size, size)
        target = pl.multiple_of(pairs[1, tile, slot] * size, size)
        acc[pl.ds(target, size), pl.ds(source, size)] += ham_ref[0, pairs[2, tile, slot]].astype(jnp.float32)
        return carry

    lax.fori_loop(0, counts[tile], add, 0)
    out_ref[0] = acc[...].astype(out_ref.dtype)


def dense(hams, place, pairs, counts, shape, tile_of):
    grid_spec = pltpu.PrefetchScalarGridSpec(
        num_scalar_prefetch=3,
        grid=(hams.shape[0],),
        in_specs=[pl.BlockSpec((1,) + hams.shape[1:], lambda i, *_: (i, 0, 0, 0))],
        out_specs=pl.BlockSpec((1,) + shape, lambda i, *_: (i, 0, 0)),
        scratch_shapes=[pltpu.VMEM(shape, jnp.float32)],
    )
    return pl.pallas_call(
        functools.partial(dense_kernel, tile_of),
        out_shape=jax.ShapeDtypeStruct((hams.shape[0],) + shape, jnp.bfloat16),
        grid_spec=grid_spec,
        compiler_params=pltpu.CompilerParams(vmem_limit_bytes=VMEM_LIMIT),
    )(place, pairs, counts, hams)


def dot_t(a, b):
    return lax.dot_general(a, b, (((1,), (1,)), ((), ())), preferred_element_type=jnp.float32)


def pack_kernel(place, hot, xr_ref, xc_ref, rows_ref, cols_ref):
    rows_ref[0] = xr_ref[...].astype(rows_ref.dtype)
    cols_ref[0] = xc_ref[...].astype(cols_ref.dtype)


def pack(x, place, hot, row_count, ratio, size):
    height, width = x.shape
    hot_count = hot.shape[1]
    blocks = width // (ratio * size)
    part = width // ratio

    def row_block(n, place, hot):
        n = jnp.minimum(n, ratio * hot_count - 1)
        return (hot[place[0], n // ratio], n % ratio)

    def col_block(n, place, hot):
        n = jnp.minimum(n, ratio * hot_count - 1)
        tile, which = n // hot_count, n % hot_count
        return (0, tile * blocks + hot[place[1] * ratio + tile, which])

    grid_spec = pltpu.PrefetchScalarGridSpec(
        num_scalar_prefetch=2,
        grid=(ratio * hot_count,),
        in_specs=[pl.BlockSpec((size, part), row_block), pl.BlockSpec((height, size), col_block)],
        out_specs=[
            pl.BlockSpec((1, size, part), lambda n, *_: (n // ratio, 0, n % ratio)),
            pl.BlockSpec((1, height, size), lambda n, *_: (n, 0, 0)),
        ],
    )
    return pl.pallas_call(
        pack_kernel,
        out_shape=[
            jax.ShapeDtypeStruct((hot_count, size, width), jnp.bfloat16),
            jax.ShapeDtypeStruct((ratio * hot_count, height, size), jnp.bfloat16),
        ],
        grid_spec=grid_spec,
    )(place, hot, x, x)


def layout(row_n, col_n):
    line = 1
    while 4 * line * line <= 2 * row_n:
        line *= 2
    cores = 2 if col_n % 2 == 0 else 1
    return line, row_n // line, col_n // cores, cores


class Grid:
    def __init__(self, row_n, col_n):
        self.line, self.lanes, self.chips, self.cores = layout(row_n, col_n)
        self.row_n, self.col_n = row_n, col_n
        row, col = lax.axis_index("row"), lax.axis_index("col")
        self.row, self.col = row, col
        self.at, self.lane = row // self.lanes, lax.rem(row, self.lanes)
        self.chip, self.core = col // self.cores, lax.rem(col, self.cores)

    def on_line(self, at):
        return (at * self.lanes + self.lane, self.col)

    def other_lane(self, step):
        return (self.at * self.lanes + lax.rem(self.lane + step, self.lanes), self.col)

    def other_chip(self, step):
        return (self.row, lax.rem(self.chip + step, self.chips) * self.cores + self.core)

    def other_core(self):
        return (self.row, self.chip * self.cores + lax.rem(self.core + 1, self.cores))


def remote(src, dst, send, recv, device):
    return pltpu.make_async_remote_copy(
        src_ref=src, dst_ref=dst, send_sem=send, recv_sem=recv, device_id=device, device_id_type=MESH)


def greet(g):
    barrier = pltpu.get_barrier_semaphore()
    up, down = g.at + 1 < g.line, g.at > 0

    def hello(device):
        pl.semaphore_signal(barrier, inc=1, device_id=device, device_id_type=MESH)

    @pl.when(up)
    def _():
        hello(g.on_line(g.at + 1))

    @pl.when(down)
    def _():
        hello(g.on_line(g.at - 1))

    for step in range(1, g.lanes):
        hello(g.other_lane(step))
    for step in range(1, g.chips):
        hello(g.other_chip(step))
    fixed = g.lanes - 1 + g.chips - 1
    if g.cores == 2:
        hello(g.other_core())
        fixed += 1
    pl.semaphore_wait(barrier, fixed + up.astype(jnp.int32) + down.astype(jnp.int32))


def late_slot(at, line):
    return jnp.where(2 * at < line, line - 1, 0)


def exchange_kernel(row_n, col_n, pieces, with_ham, fused, sel, rows_ref, cols_ref, *refs):
    g = Grid(row_n, col_n)
    refs = list(refs)

    def some(count):
        taken = refs[:count]
        del refs[:count]
        return taken

    first_step = 2 if fused else 1
    if fused:
        below_ref, above_ref, chip_ref, wa_hbm, wb_hbm, rd_ref, cd_ref, x_hbm, start_hbm, s_out, acc_out = some(11)
    else:
        ham_ref, diag_ref, s_out, c_out, h_out, rd_out, cd_out = some(7)
    held, lane_buf, turn_buf, s_all, c_all = some(5)
    own_sem, line_recv, up_send, down_send, lane_send, lane_recv = some(6)
    chip_send, chip_recv, core_send, core_recv, turn_send, turn_recv = some(6)
    if fused:
        acc, wa, wb, x_buf, start_buf, via_buf, load_sem, x_sem, start_sem, acc_sem, via_send, via_recv = some(12)
    else:
        ham_buf, far_buf, ham_sem, ham_recv, ham_up, ham_down, ham_lane, far_recv, far_send, far_chip = some(10)
        ham_rows = ham_ref.shape[0] // pieces
    ratio = row_n // col_n
    hot_count, size = rows_ref.shape[0], rows_ref.shape[1]
    height = cols_ref.shape[1]
    width = rows_ref.shape[2]
    piece = size // pieces
    block_n = cols_ref.shape[0]
    line, lanes, at = g.line, g.lanes, g.at

    home = (g.col * ratio) // lanes
    diag = at == home
    up_ok = (at + 1 < line) & ((home != line - 1) | (at + 1 != line - 1))
    down_ok = (at > 0) & ((home != 0) | (at - 1 != 0))
    deaf = diag & ((at == 0) | (at == line - 1))

    def chip_slot(step):
        return (lax.rem(g.chip - step + g.chips, g.chips) * g.cores + g.core) * block_n

    own_slot = g.col * block_n
    take = pltpu.make_async_copy(rows_ref, held.at[at], own_sem.at[0])
    take_cols = pltpu.make_async_copy(cols_ref, c_all.at[pl.ds(own_slot, block_n)], own_sem.at[1])
    take.start()
    take_cols.start()
    if fused:
        take_chip = pltpu.make_async_copy(chip_ref, c_all.at[pl.ds(chip_slot(1), block_n)], own_sem.at[2])
        take_chip.start()

        @pl.when(at > 0)
        def _():
            pltpu.make_async_copy(below_ref, held.at[at - 1], own_sem.at[3]).start()

        @pl.when(at + 1 < line)
        def _():
            pltpu.make_async_copy(above_ref, held.at[at + 1], own_sem.at[4]).start()
    else:
        take_ham = pltpu.make_async_copy(ham_ref, ham_buf, ham_sem.at[0])
        take_ham.start()
    greet(g)

    def chip_copy(step, b):
        return remote(cols_ref.at[b], c_all.at[own_slot + b], chip_send.at[step - 1, b], chip_recv.at[step - 1, b], g.other_chip(step))

    def core_copy(step, b):
        if step == 0:
            src, slot = cols_ref.at[b], own_slot + b
        else:
            slot = chip_slot(step) + b
            src = chip_ref.at[b] if fused and step == 1 else c_all.at[slot]
        return remote(src, c_all.at[slot], core_send.at[step, b], core_recv.at[step, b], g.other_core())

    for b in range(block_n):
        for step in range(first_step, g.chips):
            chip_copy(step, b).start()
    if g.cores == 2:
        for step in range(first_step):
            for b in range(block_n):
                core_copy(step, b).start()
    take.wait()
    if fused:
        @pl.when(at > 0)
        def _():
            pltpu.make_async_copy(below_ref, held.at[at - 1], own_sem.at[3]).wait()

        @pl.when(at + 1 < line)
        def _():
            pltpu.make_async_copy(above_ref, held.at[at + 1], own_sem.at[4]).wait()

    def part(slot, p):
        return held.at[slot, :, pl.ds(pl.multiple_of(p * piece, piece), piece), :]

    def up_copy(slot, p):
        return remote(part(slot, p), part(slot, p), up_send.at[slot, p], line_recv.at[slot, p], g.on_line(at + 1))

    def down_copy(slot, p):
        return remote(part(slot, p), part(slot, p), down_send.at[slot, p], line_recv.at[slot, p], g.on_line(at - 1))

    def s_rows(source, p):
        return pl.ds(pl.multiple_of(source * size + p * piece, piece), piece)

    def lane_copy(step, slot, p):
        rows = pl.ds(pl.multiple_of(p * piece, piece), piece)
        return remote(
            lane_buf.at[step - 1, slot, rows, :], s_all.at[s_rows(slot * lanes + g.lane, p), :],
            lane_send.at[step - 1, slot, p], lane_recv.at[step - 1, slot, p], g.other_lane(step))

    def lane_came(step, slot, p):
        rows = pl.ds(pl.multiple_of(p * piece, piece), piece)
        came = slot * lanes + lax.rem(g.lane - step + lanes, lanes)
        return remote(
            lane_buf.at[step - 1, slot, rows, :], s_all.at[s_rows(came, p), :],
            lane_send.at[step - 1, slot, p], lane_recv.at[step - 1, slot, p], g.other_lane(step))

    def pick(target, source, blocks):
        which = sel[target, source]
        value = blocks[0]
        for h in range(1, hot_count):
            value = jnp.where(which == h, blocks[h], value)
        return value

    def select(slot, p):
        source = slot * lanes + g.lane
        rows = pl.ds(pl.multiple_of(p * piece, piece), piece)
        blocks = [held[slot, h, rows, :] for h in range(hot_count)]
        for step in range(1, lanes):
            target = at * lanes + lax.rem(g.lane + step, lanes)
            lane_buf[step - 1, slot, rows, :] = pick(target, source, blocks)
            lane_copy(step, slot, p).start()
        s_all[s_rows(source, p), :] = pick(g.row, source, blocks)

    def tile_place(col, i):
        tile = col * ratio + i
        return tile // lanes, lax.rem(tile, lanes)

    detour = g.chips % 2 == 0 and g.chips > 1
    across = g.chips // 2
    end = jnp.where(2 * home < line, line - 1, 0)
    if not fused:
        def ham_part(ref, p):
            return ref.at[pl.ds(pl.multiple_of(p * ham_rows, ham_rows), ham_rows)]

        def ham_copies(i, p):
            here = ham_part(h_out.at[i], p)
            up = remote(here, here, ham_up.at[i, p], ham_recv.at[i, p], g.on_line(at + 1))
            down = remote(here, here, ham_down.at[i, p], ham_recv.at[i, p], g.on_line(at - 1))
            over = [remote(here, here, ham_lane.at[i, step - 1, p], ham_recv.at[i, p], g.other_lane(step))
                    for step in range(1, lanes)]
            return up, down, over

        def ham_sends(i, p, act):
            _, home_lane = tile_place(g.col, i)
            up, down, over = ham_copies(i, p)
            skip = end if detour else line

            @pl.when(home_lane == g.lane)
            def _():
                @pl.when((at >= home) & (at + 1 < line) & (at + 1 != skip))
                def _():
                    act(up)

                @pl.when((at <= home) & (at > 0) & (at - 1 != skip))
                def _():
                    act(down)

                for copy in over:
                    act(copy)

        if detour:
            far_col = lax.rem(g.chip + across, g.chips) * g.cores + g.core
            far_home = (far_col * ratio) // lanes
            far_end = jnp.where(2 * far_home < line, line - 1, 0)
            rising = far_end > far_home
            far_away = jnp.where(rising, at - far_home, far_home - at)

            def far_copies(i, p):
                here = ham_part(far_buf, p)
                way = jnp.where(rising, at + 1, at - 1)
                on = remote(here, here, far_send.at[p], far_recv.at[p], g.on_line(way))
                chip = remote(here, ham_part(h_out.at[i], p), far_chip.at[p], ham_recv.at[i, p], g.other_chip(across))
                return on, chip

            def far_sends(i, p, act):
                _, far_lane = tile_place(far_col, i)
                on, chip = far_copies(i, p)

                @pl.when((far_lane == g.lane) & (far_away >= 0))
                def _():
                    @pl.when(at != far_end)
                    def _():
                        act(on)

                    @pl.when(at == far_end)
                    def _():
                        act(chip)

        take_ham.wait()
        for i in range(ratio):
            _, home_lane = tile_place(g.col, i)

            @pl.when((home == at) & (home_lane == g.lane))
            def _():
                put = pltpu.make_async_copy(ham_buf, h_out.at[i], ham_sem.at[0])
                put.start()
                put.wait()

            if detour:
                _, far_lane = tile_place(far_col, i)

                @pl.when((far_home == at) & (far_lane == g.lane))
                def _():
                    put = pltpu.make_async_copy(ham_ref, far_buf, ham_sem.at[0])
                    put.start()
                    put.wait()

        def ham_step(s, p):
            for i in range(ratio):
                _, home_lane = tile_place(g.col, i)
                away = jnp.where(at >= home, at - home, home - at)

                @pl.when((home_lane == g.lane) & (away == s))
                def _():
                    if s > 0:
                        ham_copies(i, p)[0].wait_recv()

                    ham_sends(i, p, lambda copy: copy.start())

                if detour:
                    _, far_lane = tile_place(far_col, i)

                    @pl.when((far_lane == g.lane) & (far_away == s))
                    def _():
                        if s > 0:
                            far_copies(i, p)[0].wait_recv()

                        far_sends(i, p, lambda copy: copy.start())

        def ham_start(p, carry):
            ham_step(0, p)
            return carry

        lax.fori_loop(0, pieces, ham_start, 0)

    if fused and detour and line > 2:
        climbs = end > home
        before = jnp.where(climbs, end - 1, end + 1)
        via_slot = jnp.where(climbs, end - 2, end + 2)
        leaves = at == before
        far_col = lax.rem(g.chip + across, g.chips) * g.cores + g.core
        far_home = (far_col * ratio) // lanes
        far_end = jnp.where(2 * far_home < line, line - 1, 0)
        far_before = jnp.where(far_end > far_home, far_end - 1, far_end + 1)
        far_slot = jnp.where(far_end > far_home, far_end - 2, far_end + 2)
        kept = pieces // 2

        def via_leave(p):
            return remote(part(via_slot, p), via_buf.at[p - kept], via_send.at[0, p - kept], via_recv.at[0, p - kept], g.other_chip(across))

        def via_pass(p):
            return remote(via_buf.at[p - kept], via_buf.at[p - kept], via_send.at[1, p - kept], via_recv.at[1, p - kept], g.on_line(far_end))

        def via_land(p):
            return remote(via_buf.at[p - kept], part(far_slot, p), via_send.at[2, p - kept], line_recv.at[far_slot, p], g.other_chip(across))

        def via_came(stage, p):
            there = g.other_chip(across) if stage == 0 else g.on_line(far_before)
            return remote(via_buf.at[p - kept], via_buf.at[p - kept], via_send.at[stage, p - kept], via_recv.at[stage, p - kept], there)

        def via_up(slot, p):
            return ((leaves & climbs & (slot == via_slot)) == False) | (p < kept)

        def via_down(slot, p):
            return ((leaves & (climbs == False) & (slot == via_slot)) == False) | (p < kept)
    else:
        leaves = None
        via_up = via_down = lambda slot, p: p >= 0

    def hears(s):
        quiet = (s == 0) | (deaf == False)
        return (at - s >= 0) & quiet, (at + s < line) & quiet

    def relay(n, carry):
        s, p = n // pieces, lax.rem(n, pieces)
        hears_below, hears_above = hears(s)

        @pl.when(hears_below)
        def _():
            @pl.when(s >= first_step)
            def _():
                up_copy(at - s, p).wait_recv()

            @pl.when(up_ok & (s >= first_step - 1) & via_up(at - s, p))
            def _():
                up_copy(at - s, p).start()

        @pl.when(hears_above)
        def _():
            @pl.when(s >= first_step)
            def _():
                down_copy(at + s, p).wait_recv()

            @pl.when(down_ok & (s >= first_step - 1) & via_down(at + s, p))
            def _():
                down_copy(at + s, p).start()
        return carry

    def digest(n, carry):
        s, p = n // pieces, lax.rem(n, pieces)
        hears_below, hears_above = hears(s)

        @pl.when(hears_below & (at != home))
        def _():
            select(at - s, p)

        @pl.when(hears_above & (s > 0) & (at != home))
        def _():
            select(at + s, p)
        return carry

    def advance(n, carry):
        relay(n, carry)
        if not fused:
            for s in range(1, line):
                first = pieces * min(s, 2) + pieces // 2 * max(s - 2, 0)

                @pl.when((n >= first) & (n < first + pieces // 2))
                def _():
                    for u in range(2):
                        ham_step(s, (n - first) * 2 + u)
        return digest(n, carry)

    def core_came(step, b):
        other = lax.rem(g.core + 1, g.cores)
        slot = (lax.rem(g.chip - step + g.chips, g.chips) * g.cores + other) * block_n + b
        return remote(cols_ref.at[b], c_all.at[slot], core_send.at[step, b], core_recv.at[step, b], g.other_core())

    def turn_copy(i, step, q):
        rows = pl.ds(pl.multiple_of(q * size, size), size)
        return remote(turn_buf.at[step - 1, q], s_all.at[rows, i * height:(i + 1) * height],
                      turn_send.at[step - 1, q], turn_recv.at[i, q], g.other_lane(step))

    def turn(q):
        rows = pl.ds(pl.multiple_of(q * size, size), size)
        for i in range(ratio):
            _, home_lane = tile_place(g.col, i)

            @pl.when(home_lane == g.lane)
            def _():
                for k in range(height // size):
                    strip = slice(k * size, (k + 1) * size)
                    blocks = [c_all[q * hot_count + h, strip, :] for h in range(hot_count)]
                    for step in range(1, lanes):
                        target = at * lanes + lax.rem(g.lane + step, lanes)
                        value = pick(target, q, blocks).astype(jnp.float32).T
                        turn_buf[step - 1, q, :, strip] = value.astype(turn_buf.dtype)
                    value = pick(g.row, q, blocks).astype(jnp.float32).T
                    s_all[rows, i * height + k * size:i * height + (k + 1) * size] = value.astype(s_all.dtype)
                for step in range(1, lanes):
                    turn_copy(i, step, q).start()

    def turns(act):
        def one(q, carry):
            for i in range(ratio):
                _, home_lane = tile_place(g.col, i)
                act(i, q, home_lane)
            return carry

        lax.fori_loop(0, row_n, one, 0)

    def turn_came(i, q, home_lane):
        @pl.when(home_lane != g.lane)
        def _():
            turn_copy(i, 1, q).wait_recv()

    def turn_sent(i, q, home_lane):
        @pl.when(home_lane == g.lane)
        def _():
            for step in range(1, lanes):
                turn_copy(i, step, q).wait_send()

    if fused:
        stripe = x_buf.shape[2]
        stripes = width // stripe
        per_tile = height // stripe
        rows_at_once = height // 2
        share = -(-stripes // pieces)
        late = late_slot(at, line)
        take_wa = pltpu.make_async_copy(wa_hbm, wa, load_sem.at[0])
        take_wb = pltpu.make_async_copy(wb_hbm, wb, load_sem.at[1])

        def band(n):
            return pl.ds(pl.multiple_of(n * stripe, stripe), stripe)

        def x_copy(n):
            return pltpu.make_async_copy(x_hbm.at[:, band(n)], x_buf.at[lax.rem(n, 2)], x_sem.at[lax.rem(n, 2)])

        def start_copy(n):
            return pltpu.make_async_copy(start_hbm.at[:, band(n)], start_buf.at[lax.rem(n, 2)], start_sem.at[lax.rem(n, 2)])

        def acc_copy(n):
            return pltpu.make_async_copy(acc.at[:, band(n)], acc_out.at[:, band(n)], acc_sem.at[n])

        def beta_side(n, carry):
            tile, inner = n // per_tile, lax.rem(n, per_tile)

            @pl.when(n + 1 < stripes)
            def _():
                x_copy(n + 1).start()
                start_copy(n + 1).start()

            x_copy(n).wait()
            start_copy(n).wait()
            slots = [q * hot_count + sel[g.col * ratio + tile, q] for q in range(row_n)]
            for k in range(2):
                rows = slice(k * rows_at_once, (k + 1) * rows_at_once)
                beta = jnp.concatenate([c_all[slots[q], rows, :] for q in range(row_n)], axis=1)
                value = dot_t(beta, wb[tile, band(inner), :])
                value = value + (rd_ref[rows, :] + cd_ref[:, band(n)] - center) * x_buf[lax.rem(n, 2), rows, :]
                acc[rows, band(n)] = value - start_buf[lax.rem(n, 2), rows, :] * (half_width / 2.0)
            return carry

        def alpha_side(n, carry):
            for k in range(2):
                rows = slice(k * rows_at_once, (k + 1) * rows_at_once)
                value = acc[rows, band(n)]
                for other in range(1, line):
                    slot = lax.rem(late + other, line)
                    depth = pl.ds(pl.multiple_of(slot * lanes * size, size), lanes * size)
                    value = value + jnp.dot(wa[rows, depth], s_all[depth, band(n)], preferred_element_type=jnp.float32)
                acc[rows, band(n)] = value
            acc_copy(n).start()
            return carry

        def some_stripes(work, turn_n):
            lax.fori_loop(turn_n * share, jnp.minimum(turn_n * share + share, stripes), work, 0)

    half = pieces * (line // 2)
    per_step = -(-row_n // pieces)
    if fused:
        if leaves is not None:
            @pl.when(leaves)
            def _():
                for p in range(kept, pieces):
                    via_leave(p).start()

        lax.fori_loop(pieces, half, relay, 0)
        take_wa.start()
        take_wb.start()
        x_copy(0).start()
        start_copy(0).start()
        lax.fori_loop(0, half, digest, 0)
    else:
        lax.fori_loop(0, half, advance, 0)
    for step in range(first_step, g.chips):
        for b in range(block_n):
            slot = chip_slot(step) + b
            remote(cols_ref.at[b], c_all.at[slot], chip_send.at[step - 1, b], chip_recv.at[step - 1, b], g.other_chip(step)).wait_recv()
            if g.cores == 2:
                core_copy(step, b).start()

    take_cols.wait()
    if fused:
        take_chip.wait()
    if g.cores == 2:
        for step in range(g.chips):
            for b in range(block_n):
                core_came(step, b).wait_recv()
    if not fused:
        cd_out[...] = diag_ref[:, pl.ds(pl.multiple_of(g.col * width, width), width)]
        for k in range(height // size):
            strip = diag_ref[:, pl.ds(pl.multiple_of(g.row * height + k * size, size), size)]
            rd_out[k * size:(k + 1) * size, :] = jnp.broadcast_to(strip, (size, size)).T[:, :1]
        put_cols = pltpu.make_async_copy(c_all, c_out, own_sem.at[2])
        put_cols.start()
    else:
        take_wa.wait()
        take_wb.wait()

    def middle(n, carry):
        if leaves is not None:
            @pl.when((n < half + 2) & (at == far_before))
            def _():
                p = kept + lax.rem(n - half, 2)
                via_came(0, p).wait_recv()
                via_pass(p).start()

            @pl.when((n >= half) & (n < half + 2) & (at == far_end))
            def _():
                p = kept + lax.rem(n - half, 2)
                via_came(1, p).wait_recv()
                via_land(p).start()

        advance(n, carry)

        @pl.when(diag)
        def _():
            for u in range(per_step):
                q = (n - half) * per_step + u

                @pl.when(q < row_n)
                def _():
                    turn(q)
        if fused:
            some_stripes(beta_side, n - half)
        return carry

    def lanes_came(slot):
        def one(p, carry):
            for step in range(1, lanes):
                lane_came(step, slot, p).wait_recv()
            return carry

        @pl.when(at != home)
        def _():
            lax.fori_loop(0, pieces, one, 0)

    lax.fori_loop(half, half + pieces, middle, 0)
    if fused:
        for other in range(1, line):
            lanes_came(lax.rem(late + other, line))

        @pl.when(diag)
        def _():
            turns(turn_came)

        def ending(n, carry):
            advance(n, carry)
            some_stripes(alpha_side, n - half - pieces)
            return carry

        lax.fori_loop(half + pieces, pieces * line, ending, 0)
        lanes_came(late)
        put_s = pltpu.make_async_copy(s_all.at[pl.ds(pl.multiple_of(late * lanes * size, size), lanes * size), :], s_out, own_sem.at[5])
        put_s.start()
        put_s.wait()
        for n in range(stripes):
            acc_copy(n).wait()
    else:
        lax.fori_loop(half + pieces, pieces * line, advance, 0)
        for slot in range(line):
            lanes_came(slot)

        @pl.when(diag)
        def _():
            turns(turn_came)

        put_s = pltpu.make_async_copy(s_all, s_out, own_sem.at[5])
        put_s.start()
        put_s.wait()
        put_cols.wait()

    @pl.when(diag)
    def _():
        turns(turn_sent)

    def finish(n, carry):
        slot, p = n // pieces, lax.rem(n, pieces)

        @pl.when((slot <= at + 1 - first_step) & up_ok & via_up(slot, p))
        def _():
            up_copy(slot, p).wait_send()

        @pl.when((slot >= at - 1 + first_step) & down_ok & via_down(slot, p))
        def _():
            down_copy(slot, p).wait_send()

        @pl.when(at != home)
        def _():
            for step in range(1, lanes):
                lane_copy(step, slot, p).wait_send()
        return carry

    lax.fori_loop(0, line * pieces, finish, 0)
    if leaves is not None:
        for p in range(kept, pieces):
            @pl.when(leaves)
            def _():
                via_leave(p).wait_send()

            @pl.when(at == far_before)
            def _():
                via_pass(p).wait_send()

            @pl.when(at == far_end)
            def _():
                via_land(p).wait_send()
    for b in range(block_n):
        for step in range(first_step, g.chips):
            chip_copy(step, b).wait_send()
        if g.cores == 2:
            for step in range(g.chips):
                core_copy(step, b).wait_send()
    if not fused:
        for i in range(ratio):
            _, home_lane = tile_place(g.col, i)

            def settle(p, carry):
                ham_sends(i, p, lambda copy: copy.wait_send())
                if detour:
                    far_sends(i, p, lambda copy: copy.wait_send())

                @pl.when(home_lane != g.lane)
                def _():
                    ham_copies(i, p)[2][0].wait_recv()
                return carry

            lax.fori_loop(0, pieces, settle, 0)


def exchange(rows, cols, sel, row_n, col_n, ident, ham=None, diagonal=None, ahead=None, product=None):
    hot_count, size, width = rows.shape
    block_n, height = cols.shape[:2]
    ratio = row_n // col_n
    pieces = 4
    fused = product is not None
    line, lanes, chips, _ = layout(row_n, col_n)
    others = max(lanes - 1, 1)
    dma = pltpu.SemaphoreType.DMA
    vmem = lambda *shape: pltpu.VMEM(shape, jnp.bfloat16)
    anywhere = pl.BlockSpec(memory_space=pl.ANY)
    whole = pl.BlockSpec(memory_space=pltpu.VMEM)
    scratch = [
        vmem(line, hot_count, size, width),
        vmem(others, line, size, width),
        vmem(others, row_n, size, height),
        vmem(row_n * size, width),
        vmem(col_n * block_n, height, size),
        dma((6,)),
        dma((line, pieces)),
        dma((line, pieces)),
        dma((line, pieces)),
        dma((others, line, pieces)),
        dma((others, line, pieces)),
        dma((max(chips - 1, 1), block_n)),
        dma((max(chips - 1, 1), block_n)),
        dma((chips, block_n)),
        dma((chips, block_n)),
        dma((others, row_n)),
        dma((ratio, row_n)),
    ]
    args = [sel, rows, cols]
    in_specs = [pl.BlockSpec(memory_space=pltpu.SMEM), anywhere, anywhere]
    if fused:
        wa, wb, rd, cd, x, start = product
        stripe = 256 if height % 256 == 0 else size
        args += list(ahead) + [wa, wb, rd, cd, x, start]
        in_specs += [anywhere] * 5 + [whole] * 2 + [anywhere] * 2
        out_shape = [
            jax.ShapeDtypeStruct((lanes * size, width), jnp.bfloat16),
            jax.ShapeDtypeStruct((height, width), jnp.float32),
        ]
        out_specs = [anywhere] * 2
        scratch += [
            pltpu.VMEM((height, width), jnp.float32),
            vmem(*wa.shape),
            vmem(*wb.shape),
            pltpu.VMEM((2, height, stripe), jnp.float32),
            pltpu.VMEM((2, height, stripe), jnp.float32),
            vmem(pieces - pieces // 2, hot_count, size // pieces, width),
            dma((2,)),
            dma((2,)),
            dma((2,)),
            dma((width // stripe,)),
            dma((3, pieces)),
            dma((3, pieces)),
        ]
    else:
        args += [ham, diagonal[None, :]]
        in_specs += [anywhere, whole]
        out_shape = [
            jax.ShapeDtypeStruct((row_n * size, width), jnp.bfloat16),
            jax.ShapeDtypeStruct((col_n * block_n, height, size), jnp.bfloat16),
            jax.ShapeDtypeStruct((ratio,) + ham.shape, ham.dtype),
            jax.ShapeDtypeStruct((height, 1), jnp.float32),
            jax.ShapeDtypeStruct((1, width), jnp.float32),
        ]
        out_specs = [anywhere] * 3 + [whole] * 2
        scratch += [
            pltpu.VMEM(ham.shape, ham.dtype),
            pltpu.VMEM(ham.shape, ham.dtype),
            dma((1,)),
            dma((ratio, pieces)),
            dma((ratio, pieces)),
            dma((ratio, pieces)),
            dma((ratio, others, pieces)),
            dma((pieces,)),
            dma((pieces,)),
            dma((pieces,)),
        ]
    return pl.pallas_call(
        functools.partial(exchange_kernel, row_n, col_n, pieces, ham is not None, fused),
        out_shape=out_shape,
        in_specs=in_specs,
        out_specs=out_specs,
        scratch_shapes=scratch,
        compiler_params=pltpu.CompilerParams(collective_id=ident, has_side_effects=True, vmem_limit_bytes=VMEM_MOST),
    )(*args)


def last_kernel(place, acc_ref, wa_ref, s_ref, out_ref):
    acc = acc_ref[...] + jnp.dot(wa_ref[...], s_ref[...], preferred_element_type=jnp.float32)
    out_ref[...] = acc * (2.0 / half_width)


def last_step(place, acc, wa, s, row_n, col_n):
    height, width = acc.shape
    depth = s.shape[0]
    line, lanes, _, _ = layout(row_n, col_n)
    stripe = next(n for n in (512, 384, 256, width) if width % n == 0)
    grid_spec = pltpu.PrefetchScalarGridSpec(
        num_scalar_prefetch=1,
        grid=(width // stripe,),
        in_specs=[
            pl.BlockSpec((height, stripe), lambda n, place: (0, n)),
            pl.BlockSpec((height, depth), lambda n, place: (0, late_slot(place[0] // lanes, line))),
            pl.BlockSpec((depth, stripe), lambda n, place: (0, n)),
        ],
        out_specs=pl.BlockSpec((height, stripe), lambda n, place: (0, n)),
    )
    return pl.pallas_call(
        last_kernel,
        out_shape=jax.ShapeDtypeStruct(acc.shape, jnp.float32),
        grid_spec=grid_spec,
        compiler_params=pltpu.CompilerParams(vmem_limit_bytes=VMEM_LIMIT),
    )(place, acc, wa, s)


def hot_kernel(row_n, hot_count, place, hot, sel, *refs):
    refs = list(refs)

    def some(count):
        taken = refs[:count]
        del refs[:count]
        return taken

    wide = lambda blocks: jnp.concatenate(blocks, axis=1)
    wa_hot, x_rows, rd_hot = some(hot_count), some(hot_count), some(hot_count)
    b_hot = [some(row_n) for _ in range(hot_count)]
    s_ref, wb_ref, cd_ref = some(3)
    wa_ref, rd_ref = some(2)
    b_refs = some(row_n)
    s_hot, wb_hot, x_cols, cd_hot = some(hot_count), some(hot_count), some(hot_count), some(hot_count)
    rows_ref, cols_ref = refs
    scale = 1.0 / half_width

    def dot(a, b):
        return jnp.dot(a, b, preferred_element_type=jnp.float32)

    size = rows_ref.shape[1]
    acc = dot(jnp.concatenate([w[...] for w in wa_hot], axis=0), s_ref[...])
    beta = jnp.concatenate([wide([b[0] for b in blocks]) for blocks in b_hot], axis=0)
    acc = acc + dot_t(beta, wb_ref[0])
    for h in range(hot_count):
        value = acc[h * size:(h + 1) * size] + (rd_hot[h][...] + cd_ref[...] - center) * x_rows[h][...]
        rows_ref[h] = (value * scale).astype(rows_ref.dtype)
    acc = dot(wa_ref[...], wide([s[...] for s in s_hot]))
    acc = acc + dot_t(wide([b[0] for b in b_refs]), jnp.concatenate([w[0] for w in wb_hot], axis=0))
    for h in range(hot_count):
        value = acc[:, h * size:(h + 1) * size] + (rd_ref[...] + cd_hot[h][...] - center) * x_cols[h][...]
        cols_ref[h] = (value * scale).astype(cols_ref.dtype)


def hot_step(place, hot, sel, wa, s, wb, rd, cd, cols, x, row_n, ratio):
    height, width = x.shape
    size = cols.shape[-1]
    hot_count = hot.shape[1]
    tile_width = width // ratio
    stripe = tile_width // 2 if tile_width % 256 == 0 else size
    per_tile = tile_width // stripe
    blocks = tile_width // size
    depth = s.shape[0]

    def tile(n):
        return jnp.minimum(n // per_tile, ratio - 1)

    def hot_row(h, place, hot):
        return hot[place[0], h]

    def hot_col(h, n, place, hot):
        return hot[place[1] * ratio + tile(n), h]

    def source(q, n, place, sel):
        return q * hot_count + sel[place[1] * ratio + tile(n), q]

    spec = pl.BlockSpec
    each = range(hot_count)
    in_specs = [spec((size, depth), lambda n, place, hot, sel, h=h: (hot_row(h, place, hot), 0)) for h in each]
    in_specs += [spec((size, stripe), lambda n, place, hot, sel, h=h: (hot_row(h, place, hot), n)) for h in each]
    in_specs += [spec((size, 1), lambda n, place, hot, sel, h=h: (hot_row(h, place, hot), 0)) for h in each]
    in_specs += [spec((1, size, size), lambda n, place, hot, sel, h=h, q=q: (source(q, n, place, sel), hot_row(h, place, hot), 0))
                 for h in each for q in range(row_n)]
    in_specs += [
        spec((depth, stripe), lambda n, *_: (0, n)),
        spec((1, stripe, depth), lambda n, *_: (n // per_tile, n % per_tile, 0)),
        spec((1, stripe), lambda n, *_: (0, n)),
        spec((stripe, depth), lambda n, *_: (n % per_tile, 0)),
        spec((stripe, 1), lambda n, *_: (n % per_tile, 0)),
    ]
    in_specs += [spec((1, stripe, size), lambda n, place, hot, sel, q=q: (source(q, n, place, sel), n % per_tile, 0)) for q in range(row_n)]
    in_specs += [spec((depth, size), lambda n, place, hot, sel, h=h: (0, tile(n) * blocks + hot_col(h, n, place, hot))) for h in each]
    in_specs += [spec((1, size, depth), lambda n, place, hot, sel, h=h: (tile(n), hot_col(h, n, place, hot), 0)) for h in each]
    in_specs += [spec((stripe, size), lambda n, place, hot, sel, h=h: (n % per_tile, tile(n) * blocks + hot_col(h, n, place, hot))) for h in each]
    in_specs += [spec((1, size), lambda n, place, hot, sel, h=h: (0, tile(n) * blocks + hot_col(h, n, place, hot))) for h in each]
    args = [wa] * hot_count + [x] * hot_count + [rd] * hot_count + [cols] * (hot_count * row_n)
    args += [s, wb, cd, wa, rd] + [cols] * row_n + [s] * hot_count + [wb] * hot_count + [x] * hot_count + [cd] * hot_count
    grid_spec = pltpu.PrefetchScalarGridSpec(
        num_scalar_prefetch=3,
        grid=(width // stripe,),
        in_specs=in_specs,
        out_specs=[
            spec((hot_count, size, stripe), lambda n, *_: (0, 0, n)),
            spec((hot_count, stripe, size), lambda n, *_: (n // per_tile, n % per_tile, 0)),
        ],
    )
    return pl.pallas_call(
        functools.partial(hot_kernel, row_n, hot_count),
        out_shape=[
            jax.ShapeDtypeStruct((hot_count, size, width), jnp.bfloat16),
            jax.ShapeDtypeStruct((ratio * hot_count, height, size), jnp.bfloat16),
        ],
        grid_spec=grid_spec,
        compiler_params=pltpu.CompilerParams(vmem_limit_bytes=VMEM_LIMIT),
    )(place, hot, sel, *args)


def first_hops(rows, cols, row_n, col_n):
    line, lanes, chips, cores = layout(row_n, col_n)
    upward = [(r, r + lanes) for r in range(row_n - lanes)]
    below = lax.ppermute(rows, "row", upward)
    above = lax.ppermute(rows, "row", [(b, a) for a, b in upward])
    turn = [(c, (c // cores + 1) % chips * cores + c % cores) for c in range(col_n)]
    return [below, above, lax.ppermute(cols, "col", turn)]


def filter_kernel(source_count, row_chunk, place, sel, wa_ref, s_ref, wb_ref, rd_ref, cd_ref, *refs):
    b_refs = refs[:source_count]
    x_ref, out_ref = refs[source_count:]

    def chunk(i, carry):
        rows = pl.ds(pl.multiple_of(i * row_chunk, row_chunk), row_chunk)
        beta = jnp.concatenate([b[0, rows, :] for b in b_refs], axis=1)
        acc = jnp.dot(wa_ref[rows, :], s_ref[...], preferred_element_type=jnp.float32)
        acc = acc + dot_t(beta, wb_ref[0])
        acc = acc + (rd_ref[rows, :] + cd_ref[...] - center) * x_ref[rows, :]
        out_ref[rows, :] = acc * (1.0 / half_width)
        return carry

    lax.fori_loop(0, x_ref.shape[0] // row_chunk, chunk, 0)


def filter_step(place, sel, wa, s, wb, rd, cd, cols, x, row_n, ratio):
    height, width = x.shape
    size = cols.shape[-1]
    hot_count = cols.shape[0] // row_n
    tile_width = width // ratio
    stripe = next(n for n in (512, 384, 256, size) if tile_width % n == 0)
    per_tile = tile_width // stripe
    row_chunk = height // 2 if height % 256 == 0 else height

    def b_spec(q):
        return pl.BlockSpec(
            (1, height, size),
            lambda n, place, sel: (q * hot_count + sel[place[1] * ratio + jnp.minimum(n // per_tile, ratio - 1), q], 0, 0))

    striped = pl.BlockSpec((height, stripe), lambda n, *_: (0, n))
    in_specs = [
        pl.BlockSpec(wa.shape, lambda n, *_: (0, 0)),
        pl.BlockSpec((s.shape[0], stripe), lambda n, *_: (0, n)),
        pl.BlockSpec((1, stripe, wb.shape[2]), lambda n, *_: (n // per_tile, n % per_tile, 0)),
        pl.BlockSpec((height, 1), lambda n, *_: (0, 0)),
        pl.BlockSpec((1, stripe), lambda n, *_: (0, n)),
    ] + [b_spec(q) for q in range(row_n)] + [striped]
    args = [wa, s, wb, rd, cd] + [cols] * row_n + [x]
    grid_spec = pltpu.PrefetchScalarGridSpec(
        num_scalar_prefetch=2, grid=(width // stripe,), in_specs=in_specs, out_specs=striped)
    return pl.pallas_call(
        functools.partial(filter_kernel, row_n, row_chunk),
        out_shape=jax.ShapeDtypeStruct(x.shape, jnp.float32),
        grid_spec=grid_spec,
        cost_estimate=pl.CostEstimate(
            flops=4 * height * width * s.shape[0], bytes_accessed=4 * 3 * height * width, transcendentals=0),
        compiler_params=pltpu.CompilerParams(vmem_limit_bytes=VMEM_LIMIT),
    )(place, sel, *args)


def body(start_vector, ham_blocks, diagonal, pair_lists, pair_counts, hot_blocks, selection):
    row_n = lax.axis_size("row")
    col_n = lax.axis_size("col")
    ratio = row_n // col_n
    height, width = start_vector.shape
    size = ham_blocks.shape[1]
    place = jnp.stack([lax.axis_index("row"), lax.axis_index("col")]).astype(jnp.int32)
    shape = (height, row_n * size)
    rows, cols = pack(start_vector, place, hot_blocks, row_n, ratio, size)
    s, b, hams, rd, cd = exchange(rows, cols, selection, row_n, col_n, 0, ham=ham_blocks, diagonal=diagonal)
    wa = dense(ham_blocks[None], place, pair_lists, pair_counts, shape, lambda place, i: place[0])[0]
    wb = dense(hams, place, pair_lists, pair_counts, shape, lambda place, i: place[1] * ratio + i)
    rows, cols = hot_step(place, hot_blocks, selection, wa, s, wb, rd, cd, b, start_vector, row_n, ratio)
    ahead = first_hops(rows, cols, row_n, col_n)
    s, _ = lax.optimization_barrier((s, rows))
    first = filter_step(place, selection, wa, s, wb, rd, cd, b, start_vector, row_n, ratio)
    s, acc = exchange(rows, cols, selection, row_n, col_n, 1, ahead=ahead, product=(wa, wb, rd, cd, first, start_vector))
    return (first, last_step(place, acc, wa, s, row_n, col_n))


def solution(mesh):
    in_specs = (P("row", "col"), P("row", None, None), P(), P(), P(), P(), P())
    out_specs = (P("row", "col"), P("row", "col"))
    return jax.shard_map(body, mesh=mesh, in_specs=in_specs, out_specs=out_specs, check_vma=False)
```

```python
import functools

import jax
import jax.numpy as jnp
from jax import lax
from jax.experimental import pallas as pl
from jax.experimental.pallas import tpu as pltpu
from jax.sharding import PartitionSpec as P

center = 0.25
half_width = 2.5
VMEM_LIMIT = 60 * 1024 * 1024
VMEM_MOST = 67043328
MESH = pl.DeviceIdType.MESH


def dense_kernel(tile_of, place, pairs, counts, ham_ref, out_ref, acc):
    tile = tile_of(place, pl.program_id(0))
    size = ham_ref.shape[-1]
    acc[...] = jnp.zeros_like(acc)

    def add(slot, carry):
        source = pl.multiple_of(pairs[0, tile, slot] * size, size)
        target = pl.multiple_of(pairs[1, tile, slot] * size, size)
        acc[pl.ds(target, size), pl.ds(source, size)] += ham_ref[0, pairs[2, tile, slot]].astype(jnp.float32)
        return carry

    lax.fori_loop(0, counts[tile], add, 0)
    out_ref[0] = acc[...].astype(out_ref.dtype)


def dense(hams, place, pairs, counts, shape, tile_of):
    grid_spec = pltpu.PrefetchScalarGridSpec(
        num_scalar_prefetch=3,
        grid=(hams.shape[0],),
        in_specs=[pl.BlockSpec((1,) + hams.shape[1:], lambda i, *_: (i, 0, 0, 0))],
        out_specs=pl.BlockSpec((1,) + shape, lambda i, *_: (i, 0, 0)),
        scratch_shapes=[pltpu.VMEM(shape, jnp.float32)],
    )
    return pl.pallas_call(
        functools.partial(dense_kernel, tile_of),
        out_shape=jax.ShapeDtypeStruct((hams.shape[0],) + shape, jnp.bfloat16),
        grid_spec=grid_spec,
        compiler_params=pltpu.CompilerParams(vmem_limit_bytes=VMEM_LIMIT),
    )(place, pairs, counts, hams)


def dot_t(a, b):
    return lax.dot_general(a, b, (((1,), (1,)), ((), ())), preferred_element_type=jnp.float32)


def pack_kernel(place, hot, xr_ref, xc_ref, rows_ref, cols_ref):
    rows_ref[0] = xr_ref[...].astype(rows_ref.dtype)
    cols_ref[0] = xc_ref[...].astype(cols_ref.dtype)


def pack(x, place, hot, row_count, ratio, size):
    height, width = x.shape
    hot_count = hot.shape[1]
    blocks = width // (ratio * size)
    part = width // ratio

    def row_block(n, place, hot):
        n = jnp.minimum(n, ratio * hot_count - 1)
        return (hot[place[0], n // ratio], n % ratio)

    def col_block(n, place, hot):
        n = jnp.minimum(n, ratio * hot_count - 1)
        tile, which = n // hot_count, n % hot_count
        return (0, tile * blocks + hot[place[1] * ratio + tile, which])

    grid_spec = pltpu.PrefetchScalarGridSpec(
        num_scalar_prefetch=2,
        grid=(ratio * hot_count,),
        in_specs=[pl.BlockSpec((size, part), row_block), pl.BlockSpec((height, size), col_block)],
        out_specs=[
            pl.BlockSpec((1, size, part), lambda n, *_: (n // ratio, 0, n % ratio)),
            pl.BlockSpec((1, height, size), lambda n, *_: (n, 0, 0)),
        ],
    )
    return pl.pallas_call(
        pack_kernel,
        out_shape=[
            jax.ShapeDtypeStruct((hot_count, size, width), jnp.bfloat16),
            jax.ShapeDtypeStruct((ratio * hot_count, height, size), jnp.bfloat16),
        ],
        grid_spec=grid_spec,
    )(place, hot, x, x)


def layout(row_n, col_n):
    line = 1
    while 4 * line * line <= 2 * row_n:
        line *= 2
    cores = 2 if col_n % 2 == 0 else 1
    return line, row_n // line, col_n // cores, cores


class Grid:
    def __init__(self, row_n, col_n):
        self.line, self.lanes, self.chips, self.cores = layout(row_n, col_n)
        self.row_n, self.col_n = row_n, col_n
        row, col = lax.axis_index("row"), lax.axis_index("col")
        self.row, self.col = row, col
        self.at, self.lane = row // self.lanes, lax.rem(row, self.lanes)
        self.chip, self.core = col // self.cores, lax.rem(col, self.cores)

    def on_line(self, at):
        return (at * self.lanes + self.lane, self.col)

    def other_lane(self, step):
        return (self.at * self.lanes + lax.rem(self.lane + step, self.lanes), self.col)

    def other_chip(self, step):
        return (self.row, lax.rem(self.chip + step, self.chips) * self.cores + self.core)

    def other_core(self):
        return (self.row, self.chip * self.cores + lax.rem(self.core + 1, self.cores))


def remote(src, dst, send, recv, device):
    return pltpu.make_async_remote_copy(
        src_ref=src, dst_ref=dst, send_sem=send, recv_sem=recv, device_id=device, device_id_type=MESH)


def greet(g):
    barrier = pltpu.get_barrier_semaphore()
    up, down = g.at + 1 < g.line, g.at > 0

    def hello(device):
        pl.semaphore_signal(barrier, inc=1, device_id=device, device_id_type=MESH)

    @pl.when(up)
    def _():
        hello(g.on_line(g.at + 1))

    @pl.when(down)
    def _():
        hello(g.on_line(g.at - 1))

    for step in range(1, g.lanes):
        hello(g.other_lane(step))
    for step in range(1, g.chips):
        hello(g.other_chip(step))
    fixed = g.lanes - 1 + g.chips - 1
    if g.cores == 2:
        hello(g.other_core())
        fixed += 1
    pl.semaphore_wait(barrier, fixed + up.astype(jnp.int32) + down.astype(jnp.int32))


def got_slots(row_n, col_n):
    _, lanes, _, _ = layout(row_n, col_n)
    ratio = row_n // col_n
    return ratio if lanes > ratio > 1 else 1


def late_slot(at, line):
    return jnp.where(2 * at < line, line - 1, 0)


def exchange_kernel(row_n, col_n, pieces, with_ham, fused, sel, rows_ref, cols_ref, *refs):
    g = Grid(row_n, col_n)
    refs = list(refs)

    def some(count):
        taken = refs[:count]
        del refs[:count]
        return taken

    first_step = 2 if fused else 1
    if fused:
        below_ref, above_ref, chip_ref, wa_hbm, wb_hbm, rd_ref, cd_ref, x_hbm, start_hbm, s_out, acc_out = some(11)
    else:
        ham_ref, diag_ref, s_out, c_out, h_out, rd_out, cd_out = some(7)
    held, lane_buf, turn_buf, s_all, c_all = some(5)
    own_sem, line_recv, up_send, down_send, lane_send, lane_recv = some(6)
    chip_send, chip_recv, core_send, core_recv, turn_send, turn_recv = some(6)
    if fused:
        acc, wa, wb_buf, x_buf, start_buf, via_buf, beta, st_buf, got, load_sem, wb_sem, x_sem, start_sem, acc_sem, via_send, via_recv = some(16)
    else:
        ham_buf, far_buf, ham_sem, ham_recv, ham_up, ham_down, ham_lane, far_recv, far_send, far_chip = some(10)
        ham_rows = ham_ref.shape[0] // pieces
    ratio = row_n // col_n
    hot_count, size = rows_ref.shape[0], rows_ref.shape[1]
    height = cols_ref.shape[1]
    width = rows_ref.shape[2]
    piece = size // pieces
    block_n = cols_ref.shape[0]
    line, lanes, at = g.line, g.lanes, g.at

    home = (g.col * ratio) // lanes
    diag = at == home
    up_ok = (at + 1 < line) & ((home != line - 1) | (at + 1 != line - 1))
    down_ok = (at > 0) & ((home != 0) | (at - 1 != 0))
    deaf = diag & ((at == 0) | (at == line - 1))

    def chip_slot(step):
        return (lax.rem(g.chip - step + g.chips, g.chips) * g.cores + g.core) * block_n

    own_slot = g.col * block_n
    take = pltpu.make_async_copy(rows_ref, held.at[at], own_sem.at[0])
    take_cols = pltpu.make_async_copy(cols_ref, c_all.at[pl.ds(own_slot, block_n)], own_sem.at[1])
    take.start()
    take_cols.start()
    if fused:
        take_chip = pltpu.make_async_copy(chip_ref, c_all.at[pl.ds(chip_slot(1), block_n)], own_sem.at[2])
        take_chip.start()

        @pl.when(at > 0)
        def _():
            pltpu.make_async_copy(below_ref, held.at[at - 1], own_sem.at[3]).start()

        @pl.when(at + 1 < line)
        def _():
            pltpu.make_async_copy(above_ref, held.at[at + 1], own_sem.at[4]).start()
    else:
        take_ham = pltpu.make_async_copy(ham_ref, ham_buf, ham_sem.at[0])
        take_ham.start()
    greet(g)

    def chip_copy(step, b):
        return remote(cols_ref.at[b], c_all.at[own_slot + b], chip_send.at[step - 1, b], chip_recv.at[step - 1, b], g.other_chip(step))

    def core_copy(step, b):
        if step == 0:
            src, slot = cols_ref.at[b], own_slot + b
        else:
            slot = chip_slot(step) + b
            src = chip_ref.at[b] if fused and step == 1 else c_all.at[slot]
        return remote(src, c_all.at[slot], core_send.at[step, b], core_recv.at[step, b], g.other_core())

    for b in range(block_n):
        for step in range(first_step, g.chips):
            chip_copy(step, b).start()
    if g.cores == 2:
        for step in range(first_step):
            for b in range(block_n):
                core_copy(step, b).start()
    take.wait()
    if fused:
        @pl.when(at > 0)
        def _():
            pltpu.make_async_copy(below_ref, held.at[at - 1], own_sem.at[3]).wait()

        @pl.when(at + 1 < line)
        def _():
            pltpu.make_async_copy(above_ref, held.at[at + 1], own_sem.at[4]).wait()

    def part(slot, p):
        return held.at[slot, :, pl.ds(pl.multiple_of(p * piece, piece), piece), :]

    def up_copy(slot, p):
        return remote(part(slot, p), part(slot, p), up_send.at[slot, p], line_recv.at[slot, p], g.on_line(at + 1))

    def down_copy(slot, p):
        return remote(part(slot, p), part(slot, p), down_send.at[slot, p], line_recv.at[slot, p], g.on_line(at - 1))

    def s_rows(source, p):
        return pl.ds(pl.multiple_of(source * size + p * piece, piece), piece)

    def lane_copy(step, slot, p):
        rows = pl.ds(pl.multiple_of(p * piece, piece), piece)
        return remote(
            lane_buf.at[step - 1, slot, rows, :], s_all.at[s_rows(slot * lanes + g.lane, p), :],
            lane_send.at[step - 1, slot, p], lane_recv.at[step - 1, slot, p], g.other_lane(step))

    def lane_came(step, slot, p):
        rows = pl.ds(pl.multiple_of(p * piece, piece), piece)
        came = slot * lanes + lax.rem(g.lane - step + lanes, lanes)
        return remote(
            lane_buf.at[step - 1, slot, rows, :], s_all.at[s_rows(came, p), :],
            lane_send.at[step - 1, slot, p], lane_recv.at[step - 1, slot, p], g.other_lane(step))

    def pick(target, source, blocks):
        which = sel[target, source]
        value = blocks[0]
        for h in range(1, hot_count):
            value = jnp.where(which == h, blocks[h], value)
        return value

    def select(slot, p):
        source = slot * lanes + g.lane
        rows = pl.ds(pl.multiple_of(p * piece, piece), piece)
        blocks = [held[slot, h, rows, :] for h in range(hot_count)]
        for step in range(1, lanes):
            target = at * lanes + lax.rem(g.lane + step, lanes)
            lane_buf[step - 1, slot, rows, :] = pick(target, source, blocks)
            lane_copy(step, slot, p).start()
        s_all[s_rows(source, p), :] = pick(g.row, source, blocks)

    def tile_place(col, i):
        tile = col * ratio + i
        return tile // lanes, lax.rem(tile, lanes)

    detour = g.chips % 2 == 0 and g.chips > 1
    across = g.chips // 2
    end = jnp.where(2 * home < line, line - 1, 0)
    if not fused:
        def ham_part(ref, p):
            return ref.at[pl.ds(pl.multiple_of(p * ham_rows, ham_rows), ham_rows)]

        def ham_copies(i, p):
            here = ham_part(h_out.at[i], p)
            up = remote(here, here, ham_up.at[i, p], ham_recv.at[i, p], g.on_line(at + 1))
            down = remote(here, here, ham_down.at[i, p], ham_recv.at[i, p], g.on_line(at - 1))
            over = [remote(here, here, ham_lane.at[i, step - 1, p], ham_recv.at[i, p], g.other_lane(step))
                    for step in range(1, lanes)]
            return up, down, over

        def ham_sends(i, p, act):
            _, home_lane = tile_place(g.col, i)
            up, down, over = ham_copies(i, p)
            skip = end if detour else line

            @pl.when(home_lane == g.lane)
            def _():
                @pl.when((at >= home) & (at + 1 < line) & (at + 1 != skip))
                def _():
                    act(up)

                @pl.when((at <= home) & (at > 0) & (at - 1 != skip))
                def _():
                    act(down)

                for copy in over:
                    act(copy)

        if detour:
            far_col = lax.rem(g.chip + across, g.chips) * g.cores + g.core
            far_home = (far_col * ratio) // lanes
            far_end = jnp.where(2 * far_home < line, line - 1, 0)
            rising = far_end > far_home
            far_away = jnp.where(rising, at - far_home, far_home - at)

            def far_copies(i, p):
                here = ham_part(far_buf, p)
                way = jnp.where(rising, at + 1, at - 1)
                on = remote(here, here, far_send.at[p], far_recv.at[p], g.on_line(way))
                chip = remote(here, ham_part(h_out.at[i], p), far_chip.at[p], ham_recv.at[i, p], g.other_chip(across))
                return on, chip

            def far_sends(i, p, act):
                _, far_lane = tile_place(far_col, i)
                on, chip = far_copies(i, p)

                @pl.when((far_lane == g.lane) & (far_away >= 0))
                def _():
                    @pl.when(at != far_end)
                    def _():
                        act(on)

                    @pl.when(at == far_end)
                    def _():
                        act(chip)

        take_ham.wait()
        for i in range(ratio):
            _, home_lane = tile_place(g.col, i)

            @pl.when((home == at) & (home_lane == g.lane))
            def _():
                put = pltpu.make_async_copy(ham_buf, h_out.at[i], ham_sem.at[0])
                put.start()
                put.wait()

            if detour:
                _, far_lane = tile_place(far_col, i)

                @pl.when((far_home == at) & (far_lane == g.lane))
                def _():
                    put = pltpu.make_async_copy(ham_ref, far_buf, ham_sem.at[0])
                    put.start()
                    put.wait()

        def near_step(s, p):
            for i in range(ratio):
                _, home_lane = tile_place(g.col, i)
                away = jnp.where(at >= home, at - home, home - at)

                @pl.when((home_lane == g.lane) & (away == s))
                def _():
                    if s > 0:
                        ham_copies(i, p)[0].wait_recv()

                    ham_sends(i, p, lambda copy: copy.start())

        def far_step(s, p):
            for i in range(ratio if detour else 0):
                _, far_lane = tile_place(far_col, i)

                @pl.when((far_lane == g.lane) & (far_away == s))
                def _():
                    if s > 0:
                        far_copies(i, p)[0].wait_recv()

                    far_sends(i, p, lambda copy: copy.start())

        def far_steps(s):
            def one(p, carry):
                far_step(s, p)
                return carry

            lax.fori_loop(0, pieces, one, 0)

        if detour:
            held_back = (far_away > 0) & (at != far_end)
            up_first = (held_back & rising) == False
            down_first = (held_back & (rising == False)) == False
        else:
            up_first = down_first = at >= 0

        def ham_start(p, carry):
            near_step(0, p)
            far_step(0, p)
            return carry

        def ham_next(p, carry):
            near_step(1, p)
            far_step(1, p)
            return carry

        lax.fori_loop(0, pieces, ham_start, 0)

    if fused and detour and line > 2:
        climbs = end > home
        before = jnp.where(climbs, end - 1, end + 1)
        via_slot = jnp.where(climbs, end - 2, end + 2)
        leaves = at == before
        far_col = lax.rem(g.chip + across, g.chips) * g.cores + g.core
        far_home = (far_col * ratio) // lanes
        far_end = jnp.where(2 * far_home < line, line - 1, 0)
        far_before = jnp.where(far_end > far_home, far_end - 1, far_end + 1)
        far_slot = jnp.where(far_end > far_home, far_end - 2, far_end + 2)
        kept = pieces // 2

        def via_leave(p):
            return remote(part(via_slot, p), via_buf.at[p - kept], via_send.at[0, p - kept], via_recv.at[0, p - kept], g.other_chip(across))

        def via_pass(p):
            return remote(via_buf.at[p - kept], via_buf.at[p - kept], via_send.at[1, p - kept], via_recv.at[1, p - kept], g.on_line(far_end))

        def via_land(p):
            return remote(via_buf.at[p - kept], part(far_slot, p), via_send.at[2, p - kept], line_recv.at[far_slot, p], g.other_chip(across))

        def via_came(stage, p):
            there = g.other_chip(across) if stage == 0 else g.on_line(far_before)
            return remote(via_buf.at[p - kept], via_buf.at[p - kept], via_send.at[stage, p - kept], via_recv.at[stage, p - kept], there)

        def via_up(slot, p):
            return ((leaves & climbs & (slot == via_slot)) == False) | (p < kept)

        def via_down(slot, p):
            return ((leaves & (climbs == False) & (slot == via_slot)) == False) | (p < kept)
    else:
        leaves = None
        via_up = via_down = lambda slot, p: p >= 0

    half = pieces * (line // 2)

    def hears(s):
        quiet = (s == 0) | (deaf == False)
        return (at - s >= 0) & quiet, (at + s < line) & quiet

    if fused:
        up_first = down_first = at >= 0

    def relay(n, carry):
        s, p = n // pieces, lax.rem(n, pieces)
        hears_below, hears_above = hears(s)

        @pl.when(hears_below)
        def _():
            @pl.when(s >= first_step)
            def _():
                up_copy(at - s, p).wait_recv()

            @pl.when(up_ok & (s >= first_step - 1) & via_up(at - s, p) & ((s > 0) | up_first))
            def _():
                up_copy(at - s, p).start()

        @pl.when(hears_above)
        def _():
            @pl.when(s >= first_step)
            def _():
                down_copy(at + s, p).wait_recv()

            @pl.when(down_ok & (s >= first_step - 1) & via_down(at + s, p) & ((s > 0) | down_first))
            def _():
                down_copy(at + s, p).start()
        return carry

    def digest(n, carry):
        s, p = n // pieces, lax.rem(n, pieces)
        hears_below, hears_above = hears(s)

        @pl.when(hears_below & (at != home))
        def _():
            select(at - s, p)

        @pl.when(hears_above & (s > 0) & (at != home))
        def _():
            select(at + s, p)
        return carry

    def advance(n, carry):
        relay(n, carry)
        if not fused:
            @pl.when((n >= half) & (n < half + pieces))
            def _():
                for s in range(2, line):
                    near_step(s, n - half)
        return digest(n, carry)

    def core_came(step, b):
        other = lax.rem(g.core + 1, g.cores)
        slot = (lax.rem(g.chip - step + g.chips, g.chips) * g.cores + other) * block_n + b
        return remote(cols_ref.at[b], c_all.at[slot], core_send.at[step, b], core_recv.at[step, b], g.other_core())

    def got_at(i):
        return i if got_slots(row_n, col_n) > 1 else 0

    def turn_copy(i, step, q):
        if fused:
            there = got.at[got_at(i), q]
        else:
            there = s_all.at[pl.ds(pl.multiple_of(q * size, size), size), i * height:(i + 1) * height]
        return remote(turn_buf.at[step - 1, q], there, turn_send.at[step - 1, q], turn_recv.at[i, q], g.other_lane(step))

    def turn(q):
        rows = pl.ds(pl.multiple_of(q * size, size), size)
        for i in range(ratio):
            _, home_lane = tile_place(g.col, i)

            @pl.when(home_lane == g.lane)
            def _():
                for k in range(height // size):
                    strip = slice(k * size, (k + 1) * size)
                    blocks = [c_all[q * hot_count + h, strip, :] for h in range(hot_count)]
                    for step in range(1, lanes):
                        target = at * lanes + lax.rem(g.lane + step, lanes)
                        value = pick(target, q, blocks)
                        if fused:
                            turn_buf[step - 1, q, strip, :] = value
                        else:
                            turn_buf[step - 1, q, :, strip] = value.T
                    if not fused:
                        s_all[rows, i * height + k * size:i * height + (k + 1) * size] = pick(g.row, q, blocks).T
                for step in range(1, lanes):
                    turn_copy(i, step, q).start()

    def turns(act):
        def one(q, carry):
            for i in range(ratio):
                _, home_lane = tile_place(g.col, i)
                act(i, q, home_lane)
            return carry

        lax.fori_loop(0, row_n, one, 0)

    def turn_came(i, q, home_lane):
        @pl.when(home_lane != g.lane)
        def _():
            turn_copy(i, 1, q).wait_recv()

    def turn_sent(i, q, home_lane):
        @pl.when(home_lane == g.lane)
        def _():
            for step in range(1, lanes):
                turn_copy(i, step, q).wait_send()

    if fused:
        stripe = x_buf.shape[2]
        stripes = width // stripe
        per_tile = height // stripe
        rows_at_once = height // 2
        share = -(-stripes // pieces)
        late = late_slot(at, line)
        take_wa = pltpu.make_async_copy(wa_hbm, wa, load_sem.at[0])
        early = line - 1
        first_early = jnp.where(late == 0, 1, 0)
        depth = pl.ds(pl.multiple_of(first_early * lanes * size, lanes * size), early * lanes * size)

        def band(n):
            return pl.ds(pl.multiple_of(n * stripe, stripe), stripe)

        def loads(n):
            turn_n = lax.rem(n, 2)
            return [
                pltpu.make_async_copy(x_hbm.at[:, band(n)], x_buf.at[turn_n], x_sem.at[turn_n]),
                pltpu.make_async_copy(start_hbm.at[:, band(n)], start_buf.at[turn_n], start_sem.at[turn_n]),
                pltpu.make_async_copy(wb_hbm.at[n // per_tile, band(lax.rem(n, per_tile)), :], wb_buf.at[turn_n], wb_sem.at[turn_n]),
            ]

        def acc_copy(n):
            return pltpu.make_async_copy(acc.at[:, band(n)], acc_out.at[:, band(n)], acc_sem.at[n])

        def beta_side(n, carry):
            tile, turn_n = n // per_tile, lax.rem(n, 2)

            @pl.when(n + 1 < stripes)
            def _():
                for copy in loads(n + 1):
                    copy.start()

            @pl.when(lax.rem(n, per_tile) == 0)
            def _():
                for q in range(row_n):
                    beta[:, q * size:(q + 1) * size] = c_all[q * hot_count + sel[g.col * ratio + tile, q]]

            for copy in loads(n):
                copy.wait()
            for k in range(2):
                rows = slice(k * rows_at_once, (k + 1) * rows_at_once)
                value = dot_t(beta[rows, :], wb_buf[turn_n])
                value = value + (rd_ref[rows, :] + cd_ref[:, band(n)] - center) * x_buf[turn_n, rows, :]
                acc[rows, band(n)] = value - start_buf[turn_n, rows, :] * (half_width / 2.0)
            return carry

        def alpha_side(n, carry):
            tile, inner = n // per_tile, lax.rem(n, per_tile)

            @pl.when(at != home)
            def _():
                for k in range(2):
                    rows = slice(k * rows_at_once, (k + 1) * rows_at_once)
                    acc[rows, band(n)] += jnp.dot(wa[rows, depth], s_all[depth, band(n)], preferred_element_type=jnp.float32)

            @pl.when(diag)
            def _():
                _, home_lane = tile_place(g.col, tile)

                @pl.when(home_lane == g.lane)
                def _():
                    for q in range(row_n):
                        st_buf[:, q * size:(q + 1) * size] = c_all[q * hot_count + sel[g.row, q], band(inner), :]

                @pl.when(home_lane != g.lane)
                def _():
                    for q in range(row_n):
                        st_buf[:, q * size:(q + 1) * size] = got[got_at(tile), q, band(inner), :]

                for k in range(2):
                    rows = slice(k * rows_at_once, (k + 1) * rows_at_once)
                    acc[rows, band(n)] += dot_t(wa[rows, :], st_buf[...])
            acc_copy(n).start()
            return carry

        def some_stripes(work, turn_n):
            lax.fori_loop(turn_n * share, jnp.minimum(turn_n * share + share, stripes), work, 0)

    per_step = -(-row_n // pieces)
    if fused:
        if leaves is not None:
            @pl.when(leaves)
            def _():
                for p in range(kept, pieces):
                    via_leave(p).start()

        lax.fori_loop(pieces, half, relay, 0)
        take_wa.start()
        for copy in loads(0):
            copy.start()
        lax.fori_loop(0, half, digest, 0)
    else:
        def held_rows(p, carry):
            @pl.when(up_ok & (up_first == False))
            def _():
                up_copy(at, p).start()

            @pl.when(down_ok & (down_first == False))
            def _():
                down_copy(at, p).start()
            return carry

        lax.fori_loop(0, pieces, relay, 0)
        lax.fori_loop(0, pieces, digest, 0)
        lax.fori_loop(0, pieces, ham_next, 0)
        if line > 2:
            far_steps(2)
        lax.fori_loop(0, pieces, held_rows, 0)
        lax.fori_loop(pieces, half, advance, 0)
        for s in range(3, line):
            far_steps(s)
    for step in range(first_step, g.chips):
        for b in range(block_n):
            slot = chip_slot(step) + b
            remote(cols_ref.at[b], c_all.at[slot], chip_send.at[step - 1, b], chip_recv.at[step - 1, b], g.other_chip(step)).wait_recv()
            if g.cores == 2:
                core_copy(step, b).start()

    take_cols.wait()
    if fused:
        take_chip.wait()
    if g.cores == 2:
        for step in range(g.chips):
            for b in range(block_n):
                core_came(step, b).wait_recv()
    if not fused:
        cd_out[...] = diag_ref[:, pl.ds(pl.multiple_of(g.col * width, width), width)]
        for k in range(height // size):
            strip = diag_ref[:, pl.ds(pl.multiple_of(g.row * height + k * size, size), size)]
            rd_out[k * size:(k + 1) * size, :] = jnp.broadcast_to(strip, (size, size)).T[:, :1]
        put_cols = pltpu.make_async_copy(c_all, c_out, own_sem.at[2])
        put_cols.start()
    else:
        take_wa.wait()

    def middle(n, carry):
        if leaves is not None:
            @pl.when((n < half + 2) & (at == far_before))
            def _():
                p = kept + lax.rem(n - half, 2)
                via_came(0, p).wait_recv()
                via_pass(p).start()

            @pl.when((n >= half) & (n < half + 2) & (at == far_end))
            def _():
                p = kept + lax.rem(n - half, 2)
                via_came(1, p).wait_recv()
                via_land(p).start()

        advance(n, carry)

        @pl.when(diag)
        def _():
            for u in range(per_step):
                q = (n - half) * per_step + u

                @pl.when(q < row_n)
                def _():
                    turn(q)
        if fused:
            some_stripes(beta_side, n - half)
        return carry

    def lanes_came(slot):
        def one(p, carry):
            for step in range(1, lanes):
                lane_came(step, slot, p).wait_recv()
            return carry

        @pl.when(at != home)
        def _():
            lax.fori_loop(0, pieces, one, 0)

    lax.fori_loop(half, half + pieces, middle, 0)
    if fused:
        for other in range(1, line):
            lanes_came(lax.rem(late + other, line))

        @pl.when(diag)
        def _():
            turns(turn_came)

        def ending(n, carry):
            advance(n, carry)
            some_stripes(alpha_side, n - half - pieces)
            return carry

        lax.fori_loop(half + pieces, pieces * line, ending, 0)
        lanes_came(late)

        @pl.when(diag)
        def _():
            s_all[pl.ds(pl.multiple_of(late * lanes * size, size), lanes * size), :] = jnp.zeros((lanes * size, width), s_all.dtype)

        put_s = pltpu.make_async_copy(s_all.at[pl.ds(pl.multiple_of(late * lanes * size, size), lanes * size), :], s_out, own_sem.at[5])
        put_s.start()
        put_s.wait()
        for n in range(stripes):
            acc_copy(n).wait()
    else:
        lax.fori_loop(half + pieces, pieces * line, advance, 0)
        for slot in range(line):
            lanes_came(slot)

        @pl.when(diag)
        def _():
            turns(turn_came)

        put_s = pltpu.make_async_copy(s_all, s_out, own_sem.at[5])
        put_s.start()
        put_s.wait()
        put_cols.wait()

    @pl.when(diag)
    def _():
        turns(turn_sent)

    def finish(n, carry):
        slot, p = n // pieces, lax.rem(n, pieces)

        @pl.when((slot <= at + 1 - first_step) & up_ok & via_up(slot, p))
        def _():
            up_copy(slot, p).wait_send()

        @pl.when((slot >= at - 1 + first_step) & down_ok & via_down(slot, p))
        def _():
            down_copy(slot, p).wait_send()

        @pl.when(at != home)
        def _():
            for step in range(1, lanes):
                lane_copy(step, slot, p).wait_send()
        return carry

    lax.fori_loop(0, line * pieces, finish, 0)
    if leaves is not None:
        for p in range(kept, pieces):
            @pl.when(leaves)
            def _():
                via_leave(p).wait_send()

            @pl.when(at == far_before)
            def _():
                via_pass(p).wait_send()

            @pl.when(at == far_end)
            def _():
                via_land(p).wait_send()
    for b in range(block_n):
        for step in range(first_step, g.chips):
            chip_copy(step, b).wait_send()
        if g.cores == 2:
            for step in range(g.chips):
                core_copy(step, b).wait_send()
    if not fused:
        for i in range(ratio):
            _, home_lane = tile_place(g.col, i)

            def settle(p, carry):
                ham_sends(i, p, lambda copy: copy.wait_send())
                if detour:
                    far_sends(i, p, lambda copy: copy.wait_send())

                @pl.when(home_lane != g.lane)
                def _():
                    ham_copies(i, p)[2][0].wait_recv()
                return carry

            lax.fori_loop(0, pieces, settle, 0)


def exchange(rows, cols, sel, row_n, col_n, ident, ham=None, diagonal=None, ahead=None, product=None):
    hot_count, size, width = rows.shape
    block_n, height = cols.shape[:2]
    ratio = row_n // col_n
    pieces = 4
    fused = product is not None
    line, lanes, chips, _ = layout(row_n, col_n)
    others = max(lanes - 1, 1)
    dma = pltpu.SemaphoreType.DMA
    vmem = lambda *shape: pltpu.VMEM(shape, jnp.bfloat16)
    anywhere = pl.BlockSpec(memory_space=pl.ANY)
    whole = pl.BlockSpec(memory_space=pltpu.VMEM)
    scratch = [
        vmem(line, hot_count, size, width),
        vmem(others, line, size, width),
        vmem(others, row_n, *((height, size) if fused else (size, height))),
        vmem(row_n * size, width),
        vmem(col_n * block_n, height, size),
        dma((6,)),
        dma((line, pieces)),
        dma((line, pieces)),
        dma((line, pieces)),
        dma((others, line, pieces)),
        dma((others, line, pieces)),
        dma((max(chips - 1, 1), block_n)),
        dma((max(chips - 1, 1), block_n)),
        dma((chips, block_n)),
        dma((chips, block_n)),
        dma((others, row_n)),
        dma((ratio, row_n)),
    ]
    args = [sel, rows, cols]
    in_specs = [pl.BlockSpec(memory_space=pltpu.SMEM), anywhere, anywhere]
    if fused:
        wa, wb, rd, cd, x, start = product
        stripe = 256 if height % 256 == 0 else size
        args += list(ahead) + [wa, wb, rd, cd, x, start]
        in_specs += [anywhere] * 5 + [whole] * 2 + [anywhere] * 2
        out_shape = [
            jax.ShapeDtypeStruct((lanes * size, width), jnp.bfloat16),
            jax.ShapeDtypeStruct((height, width), jnp.float32),
        ]
        out_specs = [anywhere] * 2
        scratch += [
            pltpu.VMEM((height, width), jnp.float32),
            vmem(*wa.shape),
            vmem(2, stripe, wb.shape[2]),
            pltpu.VMEM((2, height, stripe), jnp.float32),
            pltpu.VMEM((2, height, stripe), jnp.float32),
            vmem(pieces - pieces // 2, hot_count, size // pieces, width),
            vmem(height, row_n * size),
            vmem(stripe, row_n * size),
            vmem(got_slots(row_n, col_n), row_n, height, size),
            dma((2,)),
            dma((2,)),
            dma((2,)),
            dma((2,)),
            dma((width // stripe,)),
            dma((3, pieces)),
            dma((3, pieces)),
        ]
    else:
        args += [ham, diagonal[None, :]]
        in_specs += [anywhere, whole]
        out_shape = [
            jax.ShapeDtypeStruct((row_n * size, width), jnp.bfloat16),
            jax.ShapeDtypeStruct((col_n * block_n, height, size), jnp.bfloat16),
            jax.ShapeDtypeStruct((ratio,) + ham.shape, ham.dtype),
            jax.ShapeDtypeStruct((height, 1), jnp.float32),
            jax.ShapeDtypeStruct((1, width), jnp.float32),
        ]
        out_specs = [anywhere] * 3 + [whole] * 2
        scratch += [
            pltpu.VMEM(ham.shape, ham.dtype),
            pltpu.VMEM(ham.shape, ham.dtype),
            dma((1,)),
            dma((ratio, pieces)),
            dma((ratio, pieces)),
            dma((ratio, pieces)),
            dma((ratio, others, pieces)),
            dma((pieces,)),
            dma((pieces,)),
            dma((pieces,)),
        ]
    return pl.pallas_call(
        functools.partial(exchange_kernel, row_n, col_n, pieces, ham is not None, fused),
        out_shape=out_shape,
        in_specs=in_specs,
        out_specs=out_specs,
        scratch_shapes=scratch,
        compiler_params=pltpu.CompilerParams(collective_id=ident, has_side_effects=True, vmem_limit_bytes=VMEM_MOST),
    )(*args)


def last_kernel(place, acc_ref, wa_ref, s_ref, out_ref):
    acc = acc_ref[...] + jnp.dot(wa_ref[...], s_ref[...], preferred_element_type=jnp.float32)
    out_ref[...] = acc * (2.0 / half_width)


def last_step(place, acc, wa, s, row_n, col_n):
    height, width = acc.shape
    depth = s.shape[0]
    line, lanes, _, _ = layout(row_n, col_n)
    stripe = next(n for n in (512, 384, 256, width) if width % n == 0)
    grid_spec = pltpu.PrefetchScalarGridSpec(
        num_scalar_prefetch=1,
        grid=(width // stripe,),
        in_specs=[
            pl.BlockSpec((height, stripe), lambda n, place: (0, n)),
            pl.BlockSpec((height, depth), lambda n, place: (0, late_slot(place[0] // lanes, line))),
            pl.BlockSpec((depth, stripe), lambda n, place: (0, n)),
        ],
        out_specs=pl.BlockSpec((height, stripe), lambda n, place: (0, n)),
    )
    return pl.pallas_call(
        last_kernel,
        out_shape=jax.ShapeDtypeStruct(acc.shape, jnp.float32),
        grid_spec=grid_spec,
        compiler_params=pltpu.CompilerParams(vmem_limit_bytes=VMEM_LIMIT),
    )(place, acc, wa, s)


def hot_kernel(row_n, hot_count, place, hot, sel, *refs):
    refs = list(refs)

    def some(count):
        taken = refs[:count]
        del refs[:count]
        return taken

    wide = lambda blocks: jnp.concatenate(blocks, axis=1)
    wa_hot, x_rows, rd_hot = some(hot_count), some(hot_count), some(hot_count)
    b_hot = [some(row_n) for _ in range(hot_count)]
    s_ref, wb_ref, cd_ref = some(3)
    wa_ref, rd_ref = some(2)
    b_refs = some(row_n)
    s_hot, wb_hot, x_cols, cd_hot = some(hot_count), some(hot_count), some(hot_count), some(hot_count)
    rows_ref, cols_ref = refs
    scale = 1.0 / half_width

    def dot(a, b):
        return jnp.dot(a, b, preferred_element_type=jnp.float32)

    size = rows_ref.shape[1]
    acc = dot(jnp.concatenate([w[...] for w in wa_hot], axis=0), s_ref[...])
    beta = jnp.concatenate([wide([b[0] for b in blocks]) for blocks in b_hot], axis=0)
    acc = acc + dot_t(beta, wb_ref[0])
    for h in range(hot_count):
        value = acc[h * size:(h + 1) * size] + (rd_hot[h][...] + cd_ref[...] - center) * x_rows[h][...]
        rows_ref[h] = (value * scale).astype(rows_ref.dtype)
    acc = dot(wa_ref[...], wide([s[...] for s in s_hot]))
    acc = acc + dot_t(wide([b[0] for b in b_refs]), jnp.concatenate([w[0] for w in wb_hot], axis=0))
    for h in range(hot_count):
        value = acc[:, h * size:(h + 1) * size] + (rd_ref[...] + cd_hot[h][...] - center) * x_cols[h][...]
        cols_ref[h] = (value * scale).astype(cols_ref.dtype)


def hot_step(place, hot, sel, wa, s, wb, rd, cd, cols, x, row_n, ratio):
    height, width = x.shape
    size = cols.shape[-1]
    hot_count = hot.shape[1]
    tile_width = width // ratio
    stripe = tile_width // 2 if tile_width % 256 == 0 else size
    per_tile = tile_width // stripe
    blocks = tile_width // size
    depth = s.shape[0]

    def tile(n):
        return jnp.minimum(n // per_tile, ratio - 1)

    def hot_row(h, place, hot):
        return hot[place[0], h]

    def hot_col(h, n, place, hot):
        return hot[place[1] * ratio + tile(n), h]

    def source(q, n, place, sel):
        return q * hot_count + sel[place[1] * ratio + tile(n), q]

    spec = pl.BlockSpec
    each = range(hot_count)
    in_specs = [spec((size, depth), lambda n, place, hot, sel, h=h: (hot_row(h, place, hot), 0)) for h in each]
    in_specs += [spec((size, stripe), lambda n, place, hot, sel, h=h: (hot_row(h, place, hot), n)) for h in each]
    in_specs += [spec((size, 1), lambda n, place, hot, sel, h=h: (hot_row(h, place, hot), 0)) for h in each]
    in_specs += [spec((1, size, size), lambda n, place, hot, sel, h=h, q=q: (source(q, n, place, sel), hot_row(h, place, hot), 0))
                 for h in each for q in range(row_n)]
    in_specs += [
        spec((depth, stripe), lambda n, *_: (0, n)),
        spec((1, stripe, depth), lambda n, *_: (n // per_tile, n % per_tile, 0)),
        spec((1, stripe), lambda n, *_: (0, n)),
        spec((stripe, depth), lambda n, *_: (n % per_tile, 0)),
        spec((stripe, 1), lambda n, *_: (n % per_tile, 0)),
    ]
    in_specs += [spec((1, stripe, size), lambda n, place, hot, sel, q=q: (source(q, n, place, sel), n % per_tile, 0)) for q in range(row_n)]
    in_specs += [spec((depth, size), lambda n, place, hot, sel, h=h: (0, tile(n) * blocks + hot_col(h, n, place, hot))) for h in each]
    in_specs += [spec((1, size, depth), lambda n, place, hot, sel, h=h: (tile(n), hot_col(h, n, place, hot), 0)) for h in each]
    in_specs += [spec((stripe, size), lambda n, place, hot, sel, h=h: (n % per_tile, tile(n) * blocks + hot_col(h, n, place, hot))) for h in each]
    in_specs += [spec((1, size), lambda n, place, hot, sel, h=h: (0, tile(n) * blocks + hot_col(h, n, place, hot))) for h in each]
    args = [wa] * hot_count + [x] * hot_count + [rd] * hot_count + [cols] * (hot_count * row_n)
    args += [s, wb, cd, wa, rd] + [cols] * row_n + [s] * hot_count + [wb] * hot_count + [x] * hot_count + [cd] * hot_count
    grid_spec = pltpu.PrefetchScalarGridSpec(
        num_scalar_prefetch=3,
        grid=(width // stripe,),
        in_specs=in_specs,
        out_specs=[
            spec((hot_count, size, stripe), lambda n, *_: (0, 0, n)),
            spec((hot_count, stripe, size), lambda n, *_: (n // per_tile, n % per_tile, 0)),
        ],
    )
    return pl.pallas_call(
        functools.partial(hot_kernel, row_n, hot_count),
        out_shape=[
            jax.ShapeDtypeStruct((hot_count, size, width), jnp.bfloat16),
            jax.ShapeDtypeStruct((ratio * hot_count, height, size), jnp.bfloat16),
        ],
        grid_spec=grid_spec,
        compiler_params=pltpu.CompilerParams(vmem_limit_bytes=VMEM_LIMIT),
    )(place, hot, sel, *args)


def first_hops(rows, cols, row_n, col_n):
    line, lanes, chips, cores = layout(row_n, col_n)
    upward = [(r, r + lanes) for r in range(row_n - lanes)]
    below = lax.ppermute(rows, "row", upward)
    above = lax.ppermute(rows, "row", [(b, a) for a, b in upward])
    turn = [(c, (c // cores + 1) % chips * cores + c % cores) for c in range(col_n)]
    return [below, above, lax.ppermute(cols, "col", turn)]


def filter_kernel(source_count, row_chunk, place, sel, wa_ref, s_ref, wb_ref, rd_ref, cd_ref, *refs):
    b_refs = refs[:source_count]
    x_ref, out_ref = refs[source_count:]

    def chunk(i, carry):
        rows = pl.ds(pl.multiple_of(i * row_chunk, row_chunk), row_chunk)
        beta = jnp.concatenate([b[0, rows, :] for b in b_refs], axis=1)
        acc = jnp.dot(wa_ref[rows, :], s_ref[...], preferred_element_type=jnp.float32)
        acc = acc + dot_t(beta, wb_ref[0])
        acc = acc + (rd_ref[rows, :] + cd_ref[...] - center) * x_ref[rows, :]
        out_ref[rows, :] = acc * (1.0 / half_width)
        return carry

    lax.fori_loop(0, x_ref.shape[0] // row_chunk, chunk, 0)


def filter_step(place, sel, wa, s, wb, rd, cd, cols, x, row_n, ratio):
    height, width = x.shape
    size = cols.shape[-1]
    hot_count = cols.shape[0] // row_n
    tile_width = width // ratio
    stripe = next(n for n in (512, 384, 256, size) if tile_width % n == 0)
    per_tile = tile_width // stripe
    row_chunk = height // 2 if height % 256 == 0 else height

    def b_spec(q):
        return pl.BlockSpec(
            (1, height, size),
            lambda n, place, sel: (q * hot_count + sel[place[1] * ratio + jnp.minimum(n // per_tile, ratio - 1), q], 0, 0))

    striped = pl.BlockSpec((height, stripe), lambda n, *_: (0, n))
    in_specs = [
        pl.BlockSpec(wa.shape, lambda n, *_: (0, 0)),
        pl.BlockSpec((s.shape[0], stripe), lambda n, *_: (0, n)),
        pl.BlockSpec((1, stripe, wb.shape[2]), lambda n, *_: (n // per_tile, n % per_tile, 0)),
        pl.BlockSpec((height, 1), lambda n, *_: (0, 0)),
        pl.BlockSpec((1, stripe), lambda n, *_: (0, n)),
    ] + [b_spec(q) for q in range(row_n)] + [striped]
    args = [wa, s, wb, rd, cd] + [cols] * row_n + [x]
    grid_spec = pltpu.PrefetchScalarGridSpec(
        num_scalar_prefetch=2, grid=(width // stripe,), in_specs=in_specs, out_specs=striped)
    return pl.pallas_call(
        functools.partial(filter_kernel, row_n, row_chunk),
        out_shape=jax.ShapeDtypeStruct(x.shape, jnp.float32),
        grid_spec=grid_spec,
        cost_estimate=pl.CostEstimate(
            flops=4 * height * width * s.shape[0], bytes_accessed=4 * 3 * height * width, transcendentals=0),
        compiler_params=pltpu.CompilerParams(vmem_limit_bytes=VMEM_LIMIT),
    )(place, sel, *args)


def body(start_vector, ham_blocks, diagonal, pair_lists, pair_counts, hot_blocks, selection):
    row_n = lax.axis_size("row")
    col_n = lax.axis_size("col")
    ratio = row_n // col_n
    height, width = start_vector.shape
    size = ham_blocks.shape[1]
    place = jnp.stack([lax.axis_index("row"), lax.axis_index("col")]).astype(jnp.int32)
    shape = (height, row_n * size)
    rows, cols = pack(start_vector, place, hot_blocks, row_n, ratio, size)
    s, b, hams, rd, cd = exchange(rows, cols, selection, row_n, col_n, 0, ham=ham_blocks, diagonal=diagonal)
    wa = dense(ham_blocks[None], place, pair_lists, pair_counts, shape, lambda place, i: place[0])[0]
    wb = dense(hams, place, pair_lists, pair_counts, shape, lambda place, i: place[1] * ratio + i)
    rows, cols = hot_step(place, hot_blocks, selection, wa, s, wb, rd, cd, b, start_vector, row_n, ratio)
    ahead = first_hops(rows, cols, row_n, col_n)
    s, _ = lax.optimization_barrier((s, rows))
    first = filter_step(place, selection, wa, s, wb, rd, cd, b, start_vector, row_n, ratio)
    s, acc = exchange(rows, cols, selection, row_n, col_n, 1, ahead=ahead, product=(wa, wb, rd, cd, first, start_vector))
    return (first, last_step(place, acc, wa, s, row_n, col_n))


def solution(mesh):
    in_specs = (P("row", "col"), P("row", None, None), P(), P(), P(), P(), P())
    out_specs = (P("row", "col"), P("row", "col"))
    return jax.shard_map(body, mesh=mesh, in_specs=in_specs, out_specs=out_specs, check_vma=False)
```

```python
import functools

import jax
import jax.numpy as jnp
from jax import lax
from jax.experimental import pallas as pl
from jax.experimental.pallas import tpu as pltpu
from jax.sharding import PartitionSpec as P

center = 0.25
half_width = 2.5
VMEM_LIMIT = 60 * 1024 * 1024
VMEM_MOST = 67043328
MESH = pl.DeviceIdType.MESH


def dense_kernel(tile_of, place, pairs, counts, ham_ref, out_ref, acc):
    tile = tile_of(place, pl.program_id(0))
    size = ham_ref.shape[-1]
    acc[...] = jnp.zeros_like(acc)

    def add(slot, carry):
        source = pl.multiple_of(pairs[0, tile, slot] * size, size)
        target = pl.multiple_of(pairs[1, tile, slot] * size, size)
        acc[pl.ds(target, size), pl.ds(source, size)] += ham_ref[0, pairs[2, tile, slot]].astype(jnp.float32)
        return carry

    lax.fori_loop(0, counts[tile], add, 0)
    out_ref[0] = acc[...].astype(out_ref.dtype)


def dense(hams, place, pairs, counts, shape, tile_of):
    grid_spec = pltpu.PrefetchScalarGridSpec(
        num_scalar_prefetch=3,
        grid=(hams.shape[0],),
        in_specs=[pl.BlockSpec((1,) + hams.shape[1:], lambda i, *_: (i, 0, 0, 0))],
        out_specs=pl.BlockSpec((1,) + shape, lambda i, *_: (i, 0, 0)),
        scratch_shapes=[pltpu.VMEM(shape, jnp.float32)],
    )
    return pl.pallas_call(
        functools.partial(dense_kernel, tile_of),
        out_shape=jax.ShapeDtypeStruct((hams.shape[0],) + shape, jnp.bfloat16),
        grid_spec=grid_spec,
        compiler_params=pltpu.CompilerParams(vmem_limit_bytes=VMEM_LIMIT),
    )(place, pairs, counts, hams)


def dot_t(a, b):
    return lax.dot_general(a, b, (((1,), (1,)), ((), ())), preferred_element_type=jnp.float32)


def pack_kernel(place, hot, xr_ref, xc_ref, rows_ref, cols_ref):
    rows_ref[0] = xr_ref[...].astype(rows_ref.dtype)
    cols_ref[0] = xc_ref[...].astype(cols_ref.dtype)


def pack(x, place, hot, row_count, ratio, size):
    height, width = x.shape
    hot_count = hot.shape[1]
    blocks = width // (ratio * size)
    part = width // ratio

    def row_block(n, place, hot):
        n = jnp.minimum(n, ratio * hot_count - 1)
        return (hot[place[0], n // ratio], n % ratio)

    def col_block(n, place, hot):
        n = jnp.minimum(n, ratio * hot_count - 1)
        tile, which = n // hot_count, n % hot_count
        return (0, tile * blocks + hot[place[1] * ratio + tile, which])

    grid_spec = pltpu.PrefetchScalarGridSpec(
        num_scalar_prefetch=2,
        grid=(ratio * hot_count,),
        in_specs=[pl.BlockSpec((size, part), row_block), pl.BlockSpec((height, size), col_block)],
        out_specs=[
            pl.BlockSpec((1, size, part), lambda n, *_: (n // ratio, 0, n % ratio)),
            pl.BlockSpec((1, height, size), lambda n, *_: (n, 0, 0)),
        ],
    )
    return pl.pallas_call(
        pack_kernel,
        out_shape=[
            jax.ShapeDtypeStruct((hot_count, size, width), jnp.bfloat16),
            jax.ShapeDtypeStruct((ratio * hot_count, height, size), jnp.bfloat16),
        ],
        grid_spec=grid_spec,
    )(place, hot, x, x)


def layout(row_n, col_n):
    line = 1
    while 4 * line * line <= 2 * row_n:
        line *= 2
    cores = 2 if col_n % 2 == 0 else 1
    return line, row_n // line, col_n // cores, cores


class Grid:
    def __init__(self, row_n, col_n):
        self.line, self.lanes, self.chips, self.cores = layout(row_n, col_n)
        self.row_n, self.col_n = row_n, col_n
        row, col = lax.axis_index("row"), lax.axis_index("col")
        self.row, self.col = row, col
        self.at, self.lane = row // self.lanes, lax.rem(row, self.lanes)
        self.chip, self.core = col // self.cores, lax.rem(col, self.cores)

    def on_line(self, at):
        return (at * self.lanes + self.lane, self.col)

    def other_lane(self, step):
        return (self.at * self.lanes + lax.rem(self.lane + step, self.lanes), self.col)

    def other_chip(self, step):
        return (self.row, lax.rem(self.chip + step, self.chips) * self.cores + self.core)

    def other_core(self):
        return (self.row, self.chip * self.cores + lax.rem(self.core + 1, self.cores))


def remote(src, dst, send, recv, device):
    return pltpu.make_async_remote_copy(
        src_ref=src, dst_ref=dst, send_sem=send, recv_sem=recv, device_id=device, device_id_type=MESH)


def greet(g):
    barrier = pltpu.get_barrier_semaphore()
    up, down = g.at + 1 < g.line, g.at > 0

    def hello(device):
        pl.semaphore_signal(barrier, inc=1, device_id=device, device_id_type=MESH)

    @pl.when(up)
    def _():
        hello(g.on_line(g.at + 1))

    @pl.when(down)
    def _():
        hello(g.on_line(g.at - 1))

    for step in range(1, g.lanes):
        hello(g.other_lane(step))
    for step in range(1, g.chips):
        hello(g.other_chip(step))
    fixed = g.lanes - 1 + g.chips - 1
    if g.cores == 2:
        hello(g.other_core())
        fixed += 1
    pl.semaphore_wait(barrier, fixed + up.astype(jnp.int32) + down.astype(jnp.int32))


def got_slots(row_n, col_n):
    _, lanes, _, _ = layout(row_n, col_n)
    ratio = row_n // col_n
    return ratio if lanes > ratio > 1 else 1


def late_slot(at, line):
    return jnp.where(2 * at < line, line - 1, 0)


def exchange_kernel(row_n, col_n, pieces, with_ham, fused, sel, rows_ref, cols_ref, *refs):
    g = Grid(row_n, col_n)
    refs = list(refs)

    def some(count):
        taken = refs[:count]
        del refs[:count]
        return taken

    first_step = 2 if fused else 1
    if fused:
        below_ref, above_ref, chip_ref = some(3)
        side_refs = some(layout(row_n, col_n)[1] - 1)
        wa_hbm, wb_hbm, rd_ref, cd_ref, x_hbm, start_hbm, s_out, acc_out = some(8)
    else:
        ham_ref, diag_ref, s_out, c_out, h_out, rd_out, cd_out = some(7)
    held, lane_buf, turn_buf, s_all, c_all = some(5)
    own_sem, line_recv, up_send, down_send, lane_send, lane_recv = some(6)
    chip_send, chip_recv, core_send, core_recv, turn_send, turn_recv = some(6)
    if fused:
        acc, wa, wb_buf, x_buf, start_buf, via_buf, beta, st_buf, got, side_buf, load_sem, wb_sem, x_sem, start_sem, acc_sem, via_send, via_recv = some(17)
    else:
        ham_buf, far_buf, ham_sem, ham_recv, ham_up, ham_down, ham_lane, far_recv, far_send, far_chip = some(10)
        ham_rows = ham_ref.shape[0] // pieces
    ratio = row_n // col_n
    hot_count, size = rows_ref.shape[0], rows_ref.shape[1]
    height = cols_ref.shape[1]
    width = rows_ref.shape[2]
    piece = size // pieces
    block_n = cols_ref.shape[0]
    line, lanes, at = g.line, g.lanes, g.at

    home = (g.col * ratio) // lanes
    up_ok = (at + 1 < line) & ((home != line - 1) | (at + 1 != line - 1))
    down_ok = (at > 0) & ((home != 0) | (at - 1 != 0))
    deaf = (at == home) & ((at == 0) | (at == line - 1))
    far_base = jnp.where(at == 0, 2 * lanes, 0) if fused else 0
    far_count = (line - 2) * lanes if fused else row_n

    def chip_slot(step):
        return (lax.rem(g.chip - step + g.chips, g.chips) * g.cores + g.core) * block_n

    own_slot = g.col * block_n
    take = pltpu.make_async_copy(rows_ref, held.at[at], own_sem.at[0])
    take_cols = pltpu.make_async_copy(cols_ref, c_all.at[pl.ds(own_slot, block_n)], own_sem.at[1])
    take.start()
    take_cols.start()
    if fused:
        take_chip = pltpu.make_async_copy(chip_ref, c_all.at[pl.ds(chip_slot(1), block_n)], own_sem.at[2])
        take_chip.start()

        @pl.when(at > 0)
        def _():
            pltpu.make_async_copy(below_ref, held.at[at - 1], own_sem.at[3]).start()

        @pl.when(at + 1 < line)
        def _():
            pltpu.make_async_copy(above_ref, held.at[at + 1], own_sem.at[4]).start()
    else:
        take_ham = pltpu.make_async_copy(ham_ref, ham_buf, ham_sem.at[0])
        take_ham.start()
    greet(g)

    def chip_copy(step, b):
        return remote(cols_ref.at[b], c_all.at[own_slot + b], chip_send.at[step - 1, b], chip_recv.at[step - 1, b], g.other_chip(step))

    def core_copy(step, b):
        if step == 0:
            src, slot = cols_ref.at[b], own_slot + b
        else:
            slot = chip_slot(step) + b
            src = chip_ref.at[b] if fused and step == 1 else c_all.at[slot]
        return remote(src, c_all.at[slot], core_send.at[step, b], core_recv.at[step, b], g.other_core())

    for b in range(block_n):
        for step in range(first_step, g.chips):
            chip_copy(step, b).start()
    if g.cores == 2:
        for step in range(first_step):
            for b in range(block_n):
                core_copy(step, b).start()
    take.wait()
    if fused:
        @pl.when(at > 0)
        def _():
            pltpu.make_async_copy(below_ref, held.at[at - 1], own_sem.at[3]).wait()

        @pl.when(at + 1 < line)
        def _():
            pltpu.make_async_copy(above_ref, held.at[at + 1], own_sem.at[4]).wait()

    def part(slot, p):
        return held.at[slot, :, pl.ds(pl.multiple_of(p * piece, piece), piece), :]

    def up_copy(slot, p):
        return remote(part(slot, p), part(slot, p), up_send.at[slot, p], line_recv.at[slot, p], g.on_line(at + 1))

    def down_copy(slot, p):
        return remote(part(slot, p), part(slot, p), down_send.at[slot, p], line_recv.at[slot, p], g.on_line(at - 1))

    def s_rows(source, p):
        return pl.ds(pl.multiple_of(source * size + p * piece, piece), piece)

    def lane_copy(step, slot, p):
        rows = pl.ds(pl.multiple_of(p * piece, piece), piece)
        return remote(
            lane_buf.at[step - 1, slot, rows, :], s_all.at[s_rows(slot * lanes + g.lane, p), :],
            lane_send.at[step - 1, slot, p], lane_recv.at[step - 1, slot, p], g.other_lane(step))

    def lane_came(step, slot, p):
        rows = pl.ds(pl.multiple_of(p * piece, piece), piece)
        came = slot * lanes + lax.rem(g.lane - step + lanes, lanes)
        return remote(
            lane_buf.at[step - 1, slot, rows, :], s_all.at[s_rows(came, p), :],
            lane_send.at[step - 1, slot, p], lane_recv.at[step - 1, slot, p], g.other_lane(step))

    def pick(target, source, blocks):
        which = sel[target, source]
        value = blocks[0]
        for h in range(1, hot_count):
            value = jnp.where(which == h, blocks[h], value)
        return value

    def select(slot, p):
        source = slot * lanes + g.lane
        rows = pl.ds(pl.multiple_of(p * piece, piece), piece)
        blocks = [held[slot, h, rows, :] for h in range(hot_count)]

        @pl.when((slot != at) | (not fused))
        def _():
            for step in range(1, lanes):
                target = at * lanes + lax.rem(g.lane + step, lanes)
                lane_buf[step - 1, slot, rows, :] = pick(target, source, blocks)
                lane_copy(step, slot, p).start()

        s_all[s_rows(source, p), :] = pick(g.row, source, blocks)

    def tile_place(col, i):
        tile = col * ratio + i
        return tile // lanes, lax.rem(tile, lanes)

    detour = g.chips % 2 == 0 and g.chips > 1
    across = g.chips // 2
    end = jnp.where(2 * home < line, line - 1, 0)
    if not fused:
        def ham_part(ref, p):
            return ref.at[pl.ds(pl.multiple_of(p * ham_rows, ham_rows), ham_rows)]

        def ham_copies(i, p):
            here = ham_part(h_out.at[i], p)
            up = remote(here, here, ham_up.at[i, p], ham_recv.at[i, p], g.on_line(at + 1))
            down = remote(here, here, ham_down.at[i, p], ham_recv.at[i, p], g.on_line(at - 1))
            over = [remote(here, here, ham_lane.at[i, step - 1, p], ham_recv.at[i, p], g.other_lane(step))
                    for step in range(1, lanes)]
            return up, down, over

        def ham_sends(i, p, act):
            _, home_lane = tile_place(g.col, i)
            up, down, over = ham_copies(i, p)
            skip = end if detour else line

            @pl.when(home_lane == g.lane)
            def _():
                @pl.when((at >= home) & (at + 1 < line) & (at + 1 != skip))
                def _():
                    act(up)

                @pl.when((at <= home) & (at > 0) & (at - 1 != skip))
                def _():
                    act(down)

                for copy in over:
                    act(copy)

        if detour:
            far_col = lax.rem(g.chip + across, g.chips) * g.cores + g.core
            far_home = (far_col * ratio) // lanes
            far_end = jnp.where(2 * far_home < line, line - 1, 0)
            rising = far_end > far_home
            far_away = jnp.where(rising, at - far_home, far_home - at)

            def far_copies(i, p):
                here = ham_part(far_buf, p)
                way = jnp.where(rising, at + 1, at - 1)
                on = remote(here, here, far_send.at[p], far_recv.at[p], g.on_line(way))
                chip = remote(here, ham_part(h_out.at[i], p), far_chip.at[p], ham_recv.at[i, p], g.other_chip(across))
                return on, chip

            def far_sends(i, p, act):
                _, far_lane = tile_place(far_col, i)
                on, chip = far_copies(i, p)

                @pl.when((far_lane == g.lane) & (far_away >= 0))
                def _():
                    @pl.when(at != far_end)
                    def _():
                        act(on)

                    @pl.when(at == far_end)
                    def _():
                        act(chip)

        take_ham.wait()
        for i in range(ratio):
            _, home_lane = tile_place(g.col, i)

            @pl.when((home == at) & (home_lane == g.lane))
            def _():
                put = pltpu.make_async_copy(ham_buf, h_out.at[i], ham_sem.at[0])
                put.start()
                put.wait()

            if detour:
                _, far_lane = tile_place(far_col, i)

                @pl.when((far_home == at) & (far_lane == g.lane))
                def _():
                    put = pltpu.make_async_copy(ham_ref, far_buf, ham_sem.at[0])
                    put.start()
                    put.wait()

        def near_step(s, p):
            for i in range(ratio):
                _, home_lane = tile_place(g.col, i)
                away = jnp.where(at >= home, at - home, home - at)

                @pl.when((home_lane == g.lane) & (away == s))
                def _():
                    if s > 0:
                        ham_copies(i, p)[0].wait_recv()

                    ham_sends(i, p, lambda copy: copy.start())

        def far_step(s, p):
            for i in range(ratio if detour else 0):
                _, far_lane = tile_place(far_col, i)

                @pl.when((far_lane == g.lane) & (far_away == s))
                def _():
                    if s > 0:
                        far_copies(i, p)[0].wait_recv()

                    far_sends(i, p, lambda copy: copy.start())

        def far_steps(s):
            def one(p, carry):
                far_step(s, p)
                return carry

            lax.fori_loop(0, pieces, one, 0)

        if detour:
            held_back = (far_away > 0) & (at != far_end)
            up_first = (held_back & rising) == False
            down_first = (held_back & (rising == False)) == False
        else:
            up_first = down_first = at >= 0

        def ham_start(p, carry):
            near_step(0, p)
            far_step(0, p)
            return carry

        def ham_next(p, carry):
            near_step(1, p)
            far_step(1, p)
            return carry

        lax.fori_loop(0, pieces, ham_start, 0)

    if fused and detour and line > 2:
        climbs = end > home
        before = jnp.where(climbs, end - 1, end + 1)
        via_slot = jnp.where(climbs, end - 2, end + 2)
        leaves = at == before
        far_col = lax.rem(g.chip + across, g.chips) * g.cores + g.core
        far_home = (far_col * ratio) // lanes
        far_end = jnp.where(2 * far_home < line, line - 1, 0)
        far_before = jnp.where(far_end > far_home, far_end - 1, far_end + 1)
        far_slot = jnp.where(far_end > far_home, far_end - 2, far_end + 2)
        kept = pieces // 2

        def via_leave(p):
            return remote(part(via_slot, p), via_buf.at[p - kept], via_send.at[0, p - kept], via_recv.at[0, p - kept], g.other_chip(across))

        def via_pass(p):
            return remote(via_buf.at[p - kept], via_buf.at[p - kept], via_send.at[1, p - kept], via_recv.at[1, p - kept], g.on_line(far_end))

        def via_land(p):
            return remote(via_buf.at[p - kept], part(far_slot, p), via_send.at[2, p - kept], line_recv.at[far_slot, p], g.other_chip(across))

        def via_came(stage, p):
            there = g.other_chip(across) if stage == 0 else g.on_line(far_before)
            return remote(via_buf.at[p - kept], via_buf.at[p - kept], via_send.at[stage, p - kept], via_recv.at[stage, p - kept], there)

        def via_up(slot, p):
            return ((leaves & climbs & (slot == via_slot)) == False) | (p < kept)

        def via_down(slot, p):
            return ((leaves & (climbs == False) & (slot == via_slot)) == False) | (p < kept)
    else:
        leaves = None
        via_up = via_down = lambda slot, p: p >= 0

    half = pieces * (line // 2)

    def hears(s):
        quiet = (s == 0) | (deaf == False)
        return (at - s >= 0) & quiet, (at + s < line) & quiet

    if fused:
        up_first = down_first = at >= 0

    def relay(n, carry):
        s, p = n // pieces, lax.rem(n, pieces)
        hears_below, hears_above = hears(s)

        @pl.when(hears_below)
        def _():
            @pl.when(s >= first_step)
            def _():
                up_copy(at - s, p).wait_recv()

            @pl.when(up_ok & (s >= first_step - 1) & via_up(at - s, p) & ((s > 0) | up_first))
            def _():
                up_copy(at - s, p).start()

        @pl.when(hears_above)
        def _():
            @pl.when(s >= first_step)
            def _():
                down_copy(at + s, p).wait_recv()

            @pl.when(down_ok & (s >= first_step - 1) & via_down(at + s, p) & ((s > 0) | down_first))
            def _():
                down_copy(at + s, p).start()
        return carry

    def digest(n, carry):
        s, p = n // pieces, lax.rem(n, pieces)
        hears_below, hears_above = hears(s)

        if fused:
            hears_below = (at - s >= 0) & ((s < 2) | (deaf == False))
            hears_above = (at + s < line) & ((s < 2) | (deaf == False))
        else:
            hears_below, hears_above = hears_below & (deaf == False), hears_above & (deaf == False)

        @pl.when(hears_below)
        def _():
            select(at - s, p)

        @pl.when(hears_above & (s > 0))
        def _():
            select(at + s, p)
        return carry

    def advance(n, carry):
        relay(n, carry)
        if not fused:
            @pl.when((n >= half) & (n < half + pieces))
            def _():
                for s in range(2, line):
                    near_step(s, n - half)
        return digest(n, carry)

    def core_came(step, b):
        other = lax.rem(g.core + 1, g.cores)
        slot = (lax.rem(g.chip - step + g.chips, g.chips) * g.cores + other) * block_n + b
        return remote(cols_ref.at[b], c_all.at[slot], core_send.at[step, b], core_recv.at[step, b], g.other_core())

    def got_at(i):
        return i if got_slots(row_n, col_n) > 1 else 0

    def turn_copy(i, step, q):
        if fused:
            there = got.at[got_at(i), q]
        else:
            there = s_all.at[pl.ds(pl.multiple_of(q * size, size), size), i * height:(i + 1) * height]
        return remote(turn_buf.at[step - 1, q], there, turn_send.at[step - 1, q], turn_recv.at[i, q], g.other_lane(step))

    def turn(q):
        rows = pl.ds(pl.multiple_of(q * size, size), size)
        for i in range(ratio):
            _, home_lane = tile_place(g.col, i)

            @pl.when(home_lane == g.lane)
            def _():
                for k in range(height // size):
                    strip = slice(k * size, (k + 1) * size)
                    blocks = [c_all[q * hot_count + h, strip, :] for h in range(hot_count)]
                    for step in range(1, lanes):
                        target = at * lanes + lax.rem(g.lane + step, lanes)
                        value = pick(target, q, blocks)
                        if fused:
                            turn_buf[step - 1, q, strip, :] = value
                        else:
                            turn_buf[step - 1, q, :, strip] = value.astype(jnp.float32).T.astype(turn_buf.dtype)
                    if not fused:
                        s_all[rows, i * height + k * size:i * height + (k + 1) * size] = pick(g.row, q, blocks).astype(jnp.float32).T.astype(s_all.dtype)
                for step in range(1, lanes):
                    turn_copy(i, step, q).start()

    def turns(act):
        def one(q, carry):
            for i in range(ratio):
                _, home_lane = tile_place(g.col, i)
                act(i, q, home_lane)
            return carry

        lax.fori_loop(far_base, far_base + far_count, one, 0)

    def turn_came(i, q, home_lane):
        @pl.when(home_lane != g.lane)
        def _():
            turn_copy(i, 1, q).wait_recv()

    def turn_sent(i, q, home_lane):
        @pl.when(home_lane == g.lane)
        def _():
            for step in range(1, lanes):
                turn_copy(i, step, q).wait_send()

    if fused:
        stripe = x_buf.shape[2]
        stripes = width // stripe
        per_tile = height // stripe
        rows_at_once = height // 2
        share = -(-stripes // pieces)
        late = late_slot(at, line)
        take_wa = pltpu.make_async_copy(wa_hbm, wa, load_sem.at[0])
        early = line - 1
        first_early = jnp.where(late == 0, 1, 0)
        depth = pl.ds(pl.multiple_of(first_early * lanes * size, lanes * size), early * lanes * size)

        def band(n):
            return pl.ds(pl.multiple_of(n * stripe, stripe), stripe)

        def loads(n):
            turn_n = lax.rem(n, 2)
            return [
                pltpu.make_async_copy(x_hbm.at[:, band(n)], x_buf.at[turn_n], x_sem.at[turn_n]),
                pltpu.make_async_copy(start_hbm.at[:, band(n)], start_buf.at[turn_n], start_sem.at[turn_n]),
                pltpu.make_async_copy(wb_hbm.at[n // per_tile, band(lax.rem(n, per_tile)), :], wb_buf.at[turn_n], wb_sem.at[turn_n]),
            ]

        def acc_copy(n):
            return pltpu.make_async_copy(acc.at[:, band(n)], acc_out.at[:, band(n)], acc_sem.at[n])

        def beta_side(n, carry):
            tile, turn_n = n // per_tile, lax.rem(n, 2)

            @pl.when(n + 1 < stripes)
            def _():
                for copy in loads(n + 1):
                    copy.start()

            @pl.when(lax.rem(n, per_tile) == 0)
            def _():
                for q in range(row_n):
                    beta[:, q * size:(q + 1) * size] = c_all[q * hot_count + sel[g.col * ratio + tile, q]]

            for copy in loads(n):
                copy.wait()
            for k in range(2):
                rows = slice(k * rows_at_once, (k + 1) * rows_at_once)
                value = dot_t(beta[rows, :], wb_buf[turn_n])
                value = value + (rd_ref[rows, :] + cd_ref[:, band(n)] - center) * x_buf[turn_n, rows, :]
                acc[rows, band(n)] = value - start_buf[turn_n, rows, :] * (half_width / 2.0)
            return carry

        near_base = jnp.where(at == 0, 0, (line - 2) * lanes * size)
        near_depth = pl.ds(pl.multiple_of(near_base, lanes * size), 2 * lanes * size)
        far_depth = pl.ds(pl.multiple_of(far_base * size, lanes * size), far_count * size)

        def alpha_side(m, carry):
            n = jnp.where(deaf, lax.rem(m + g.lane * per_tile, stripes), m)
            tile, inner = n // per_tile, lax.rem(n, per_tile)

            @pl.when(deaf == False)
            def _():
                for k in range(2):
                    rows = slice(k * rows_at_once, (k + 1) * rows_at_once)
                    acc[rows, band(n)] += jnp.dot(wa[rows, depth], s_all[depth, band(n)], preferred_element_type=jnp.float32)

            @pl.when(deaf)
            def _():
                _, home_lane = tile_place(g.col, tile)

                @pl.when(home_lane == g.lane)
                def _():
                    for j in range(far_count):
                        q = far_base + j
                        st_buf[:, j * size:(j + 1) * size] = c_all[q * hot_count + sel[g.row, q], band(inner), :]

                @pl.when(home_lane != g.lane)
                def _():
                    @pl.when(inner == 0)
                    def _():
                        def come(q, carry):
                            turn_copy(tile, 1, q).wait_recv()
                            return carry

                        lax.fori_loop(far_base, far_base + far_count, come, 0)

                    for j in range(far_count):
                        st_buf[:, j * size:(j + 1) * size] = got[got_at(tile), far_base + j, band(inner), :]

                for k in range(2):
                    rows = slice(k * rows_at_once, (k + 1) * rows_at_once)
                    value = jnp.dot(wa[rows, near_depth], s_all[near_depth, band(n)], preferred_element_type=jnp.float32)
                    acc[rows, band(n)] += value + dot_t(wa[rows, far_depth], st_buf[...])
            acc_copy(n).start()
            return carry

        def some_stripes(work, turn_n):
            lax.fori_loop(turn_n * share, jnp.minimum(turn_n * share + share, stripes), work, 0)

    per_step = -(-row_n // pieces)
    if fused:
        if leaves is not None:
            @pl.when(leaves)
            def _():
                for p in range(kept, pieces):
                    via_leave(p).start()

        lax.fori_loop(pieces, half, relay, 0)
        take_sides = [pltpu.make_async_copy(side, side_buf.at[step], load_sem.at[1 + step]) for step, side in enumerate(side_refs)]
        for copy in take_sides:
            copy.start()
        lax.fori_loop(pieces, half, digest, 0)
        take_wa.start()
        for copy in loads(0):
            copy.start()
        lax.fori_loop(0, pieces, digest, 0)
        for copy in take_sides:
            copy.wait()

        def sides(p, carry):
            rows = pl.ds(pl.multiple_of(p * piece, piece), piece)
            for step in range(1, lanes):
                source = at * lanes + lax.rem(g.lane - step + lanes, lanes)
                blocks = [side_buf[step - 1, h, rows, :] for h in range(hot_count)]
                s_all[s_rows(source, p), :] = pick(g.row, source, blocks)
            return carry

        lax.fori_loop(0, pieces, sides, 0)
    else:
        def held_rows(p, carry):
            @pl.when(up_ok & (up_first == False))
            def _():
                up_copy(at, p).start()

            @pl.when(down_ok & (down_first == False))
            def _():
                down_copy(at, p).start()
            return carry

        lax.fori_loop(0, pieces, relay, 0)
        lax.fori_loop(0, pieces, digest, 0)
        lax.fori_loop(0, pieces, ham_next, 0)
        for s in range(2, line):
            far_steps(s)
        lax.fori_loop(0, pieces, held_rows, 0)
        lax.fori_loop(pieces, half, advance, 0)
    for step in range(first_step, g.chips):
        for b in range(block_n):
            slot = chip_slot(step) + b
            remote(cols_ref.at[b], c_all.at[slot], chip_send.at[step - 1, b], chip_recv.at[step - 1, b], g.other_chip(step)).wait_recv()
            if g.cores == 2:
                core_copy(step, b).start()

    take_cols.wait()
    if fused:
        take_chip.wait()
    if g.cores == 2:
        for step in range(g.chips):
            for b in range(block_n):
                core_came(step, b).wait_recv()
    if not fused:
        cd_out[...] = diag_ref[:, pl.ds(pl.multiple_of(g.col * width, width), width)]
        for k in range(height // size):
            strip = diag_ref[:, pl.ds(pl.multiple_of(g.row * height + k * size, size), size)]
            rd_out[k * size:(k + 1) * size, :] = jnp.broadcast_to(strip, (size, size)).T[:, :1]
        put_cols = pltpu.make_async_copy(c_all, c_out, own_sem.at[2])
        put_cols.start()
    else:
        take_wa.wait()

        @pl.when(deaf)
        def _():
            def turn_on(q, carry):
                turn(q)
                return carry

            lax.fori_loop(far_base, far_base + far_count, turn_on, 0)

    def middle(n, carry):
        if leaves is not None:
            @pl.when((n < half + 2) & (at == far_before))
            def _():
                p = kept + lax.rem(n - half, 2)
                via_came(0, p).wait_recv()
                via_pass(p).start()

            @pl.when((n >= half) & (n < half + 2) & (at == far_end))
            def _():
                p = kept + lax.rem(n - half, 2)
                via_came(1, p).wait_recv()
                via_land(p).start()

        advance(n, carry)
        if not fused:
            @pl.when(deaf)
            def _():
                for u in range(per_step):
                    q = (n - half) * per_step + u

                    @pl.when(q < row_n)
                    def _():
                        turn(q)
        if fused:
            some_stripes(beta_side, n - half)
        return carry

    def lanes_came(slot):
        def one(p, carry):
            for step in range(1, lanes):
                lane_came(step, slot, p).wait_recv()
            return carry

        near = (slot - at <= 1) & (at - slot <= 1) if fused else False
        away = slot != at if fused else True

        @pl.when(((deaf == False) | near) & away)
        def _():
            lax.fori_loop(0, pieces, one, 0)

    lax.fori_loop(half, half + pieces, middle, 0)
    if fused:
        for other in range(1, line):
            lanes_came(lax.rem(late + other, line))

        def ending(n, carry):
            advance(n, carry)
            some_stripes(alpha_side, n - half - pieces)
            return carry

        lax.fori_loop(half + pieces, pieces * line, ending, 0)
        lanes_came(late)

        @pl.when(deaf)
        def _():
            s_all[pl.ds(pl.multiple_of(late * lanes * size, size), lanes * size), :] = jnp.zeros((lanes * size, width), s_all.dtype)

        put_s = pltpu.make_async_copy(s_all.at[pl.ds(pl.multiple_of(late * lanes * size, size), lanes * size), :], s_out, own_sem.at[5])
        put_s.start()
        put_s.wait()
        for n in range(stripes):
            acc_copy(n).wait()
    else:
        lax.fori_loop(half + pieces, pieces * line, advance, 0)
        for slot in range(line):
            lanes_came(slot)

        @pl.when(deaf)
        def _():
            turns(turn_came)

        put_s = pltpu.make_async_copy(s_all, s_out, own_sem.at[5])
        put_s.start()
        put_s.wait()
        put_cols.wait()

    @pl.when(deaf)
    def _():
        turns(turn_sent)

    def finish(n, carry):
        slot, p = n // pieces, lax.rem(n, pieces)

        @pl.when((slot <= at + 1 - first_step) & up_ok & via_up(slot, p))
        def _():
            up_copy(slot, p).wait_send()

        @pl.when((slot >= at - 1 + first_step) & down_ok & via_down(slot, p))
        def _():
            down_copy(slot, p).wait_send()

        near = (slot - at <= 1) & (at - slot <= 1) if fused else False
        away = slot != at if fused else True

        @pl.when(((deaf == False) | near) & away)
        def _():
            for step in range(1, lanes):
                lane_copy(step, slot, p).wait_send()
        return carry

    lax.fori_loop(0, line * pieces, finish, 0)
    if leaves is not None:
        for p in range(kept, pieces):
            @pl.when(leaves)
            def _():
                via_leave(p).wait_send()

            @pl.when(at == far_before)
            def _():
                via_pass(p).wait_send()

            @pl.when(at == far_end)
            def _():
                via_land(p).wait_send()
    for b in range(block_n):
        for step in range(first_step, g.chips):
            chip_copy(step, b).wait_send()
        if g.cores == 2:
            for step in range(g.chips):
                core_copy(step, b).wait_send()
    if not fused:
        for i in range(ratio):
            _, home_lane = tile_place(g.col, i)

            def settle(p, carry):
                ham_sends(i, p, lambda copy: copy.wait_send())
                if detour:
                    far_sends(i, p, lambda copy: copy.wait_send())

                @pl.when(home_lane != g.lane)
                def _():
                    ham_copies(i, p)[2][0].wait_recv()
                return carry

            lax.fori_loop(0, pieces, settle, 0)


def exchange(rows, cols, sel, row_n, col_n, ident, ham=None, diagonal=None, ahead=None, product=None):
    hot_count, size, width = rows.shape
    block_n, height = cols.shape[:2]
    ratio = row_n // col_n
    pieces = 4
    fused = product is not None
    line, lanes, chips, _ = layout(row_n, col_n)
    others = max(lanes - 1, 1)
    dma = pltpu.SemaphoreType.DMA
    vmem = lambda *shape: pltpu.VMEM(shape, jnp.bfloat16)
    anywhere = pl.BlockSpec(memory_space=pl.ANY)
    whole = pl.BlockSpec(memory_space=pltpu.VMEM)
    scratch = [
        vmem(line, hot_count, size, width),
        vmem(others, line, size, width),
        vmem(others, row_n, *((height, size) if fused else (size, height))),
        vmem(row_n * size, width),
        vmem(col_n * block_n, height, size),
        dma((6,)),
        dma((line, pieces)),
        dma((line, pieces)),
        dma((line, pieces)),
        dma((others, line, pieces)),
        dma((others, line, pieces)),
        dma((max(chips - 1, 1), block_n)),
        dma((max(chips - 1, 1), block_n)),
        dma((chips, block_n)),
        dma((chips, block_n)),
        dma((others, row_n)),
        dma((ratio, row_n)),
    ]
    args = [sel, rows, cols]
    in_specs = [pl.BlockSpec(memory_space=pltpu.SMEM), anywhere, anywhere]
    if fused:
        wa, wb, rd, cd, x, start = product
        stripe = 256 if height % 256 == 0 else size
        args += list(ahead) + [wa, wb, rd, cd, x, start]
        in_specs += [anywhere] * (len(ahead) + 2) + [whole] * 2 + [anywhere] * 2
        out_shape = [
            jax.ShapeDtypeStruct((lanes * size, width), jnp.bfloat16),
            jax.ShapeDtypeStruct((height, width), jnp.float32),
        ]
        out_specs = [anywhere] * 2
        scratch += [
            pltpu.VMEM((height, width), jnp.float32),
            vmem(*wa.shape),
            vmem(2, stripe, wb.shape[2]),
            pltpu.VMEM((2, height, stripe), jnp.float32),
            pltpu.VMEM((2, height, stripe), jnp.float32),
            vmem(pieces - pieces // 2, hot_count, size // pieces, width),
            vmem(height, row_n * size),
            vmem(stripe, (line - 2) * lanes * size),
            vmem(got_slots(row_n, col_n), row_n, height, size),
            vmem(others, hot_count, size, width),
            dma((1 + others,)),
            dma((2,)),
            dma((2,)),
            dma((2,)),
            dma((width // stripe,)),
            dma((3, pieces)),
            dma((3, pieces)),
        ]
    else:
        args += [ham, diagonal[None, :]]
        in_specs += [anywhere, whole]
        out_shape = [
            jax.ShapeDtypeStruct((row_n * size, width), jnp.bfloat16),
            jax.ShapeDtypeStruct((col_n * block_n, height, size), jnp.bfloat16),
            jax.ShapeDtypeStruct((ratio,) + ham.shape, ham.dtype),
            jax.ShapeDtypeStruct((height, 1), jnp.float32),
            jax.ShapeDtypeStruct((1, width), jnp.float32),
        ]
        out_specs = [anywhere] * 3 + [whole] * 2
        scratch += [
            pltpu.VMEM(ham.shape, ham.dtype),
            pltpu.VMEM(ham.shape, ham.dtype),
            dma((1,)),
            dma((ratio, pieces)),
            dma((ratio, pieces)),
            dma((ratio, pieces)),
            dma((ratio, others, pieces)),
            dma((pieces,)),
            dma((pieces,)),
            dma((pieces,)),
        ]
    return pl.pallas_call(
        functools.partial(exchange_kernel, row_n, col_n, pieces, ham is not None, fused),
        out_shape=out_shape,
        in_specs=in_specs,
        out_specs=out_specs,
        scratch_shapes=scratch,
        compiler_params=pltpu.CompilerParams(collective_id=ident, has_side_effects=True, vmem_limit_bytes=VMEM_MOST),
    )(*args)


def last_kernel(place, acc_ref, wa_ref, s_ref, out_ref):
    acc = acc_ref[...] + jnp.dot(wa_ref[...], s_ref[...], preferred_element_type=jnp.float32)
    out_ref[...] = acc * (2.0 / half_width)


def last_step(place, acc, wa, s, row_n, col_n):
    height, width = acc.shape
    depth = s.shape[0]
    line, lanes, _, _ = layout(row_n, col_n)
    stripe = next(n for n in (512, 384, 256, width) if width % n == 0)
    grid_spec = pltpu.PrefetchScalarGridSpec(
        num_scalar_prefetch=1,
        grid=(width // stripe,),
        in_specs=[
            pl.BlockSpec((height, stripe), lambda n, place: (0, n)),
            pl.BlockSpec((height, depth), lambda n, place: (0, late_slot(place[0] // lanes, line))),
            pl.BlockSpec((depth, stripe), lambda n, place: (0, n)),
        ],
        out_specs=pl.BlockSpec((height, stripe), lambda n, place: (0, n)),
    )
    return pl.pallas_call(
        last_kernel,
        out_shape=jax.ShapeDtypeStruct(acc.shape, jnp.float32),
        grid_spec=grid_spec,
        compiler_params=pltpu.CompilerParams(vmem_limit_bytes=VMEM_LIMIT),
    )(place, acc, wa, s)


def hot_kernel(row_n, hot_count, place, hot, sel, *refs):
    refs = list(refs)

    def some(count):
        taken = refs[:count]
        del refs[:count]
        return taken

    wide = lambda blocks: jnp.concatenate(blocks, axis=1)
    wa_hot, x_rows, rd_hot = some(hot_count), some(hot_count), some(hot_count)
    b_hot = [some(row_n) for _ in range(hot_count)]
    s_ref, wb_ref, cd_ref = some(3)
    wa_ref, rd_ref = some(2)
    b_refs = some(row_n)
    s_hot, wb_hot, x_cols, cd_hot = some(hot_count), some(hot_count), some(hot_count), some(hot_count)
    rows_ref, cols_ref = refs
    scale = 1.0 / half_width

    def dot(a, b):
        return jnp.dot(a, b, preferred_element_type=jnp.float32)

    size = rows_ref.shape[1]
    acc = dot(jnp.concatenate([w[...] for w in wa_hot], axis=0), s_ref[...])
    beta = jnp.concatenate([wide([b[0] for b in blocks]) for blocks in b_hot], axis=0)
    acc = acc + dot_t(beta, wb_ref[0])
    for h in range(hot_count):
        value = acc[h * size:(h + 1) * size] + (rd_hot[h][...] + cd_ref[...] - center) * x_rows[h][...]
        rows_ref[h] = (value * scale).astype(rows_ref.dtype)
    acc = dot(wa_ref[...], wide([s[...] for s in s_hot]))
    acc = acc + dot_t(wide([b[0] for b in b_refs]), jnp.concatenate([w[0] for w in wb_hot], axis=0))
    for h in range(hot_count):
        value = acc[:, h * size:(h + 1) * size] + (rd_ref[...] + cd_hot[h][...] - center) * x_cols[h][...]
        cols_ref[h] = (value * scale).astype(cols_ref.dtype)


def hot_step(place, hot, sel, wa, s, wb, rd, cd, cols, x, row_n, ratio):
    height, width = x.shape
    size = cols.shape[-1]
    hot_count = hot.shape[1]
    tile_width = width // ratio
    stripe = tile_width // 2 if tile_width % 256 == 0 else size
    per_tile = tile_width // stripe
    blocks = tile_width // size
    depth = s.shape[0]

    def tile(n):
        return jnp.minimum(n // per_tile, ratio - 1)

    def hot_row(h, place, hot):
        return hot[place[0], h]

    def hot_col(h, n, place, hot):
        return hot[place[1] * ratio + tile(n), h]

    def source(q, n, place, sel):
        return q * hot_count + sel[place[1] * ratio + tile(n), q]

    spec = pl.BlockSpec
    each = range(hot_count)
    in_specs = [spec((size, depth), lambda n, place, hot, sel, h=h: (hot_row(h, place, hot), 0)) for h in each]
    in_specs += [spec((size, stripe), lambda n, place, hot, sel, h=h: (hot_row(h, place, hot), n)) for h in each]
    in_specs += [spec((size, 1), lambda n, place, hot, sel, h=h: (hot_row(h, place, hot), 0)) for h in each]
    in_specs += [spec((1, size, size), lambda n, place, hot, sel, h=h, q=q: (source(q, n, place, sel), hot_row(h, place, hot), 0))
                 for h in each for q in range(row_n)]
    in_specs += [
        spec((depth, stripe), lambda n, *_: (0, n)),
        spec((1, stripe, depth), lambda n, *_: (n // per_tile, n % per_tile, 0)),
        spec((1, stripe), lambda n, *_: (0, n)),
        spec((stripe, depth), lambda n, *_: (n % per_tile, 0)),
        spec((stripe, 1), lambda n, *_: (n % per_tile, 0)),
    ]
    in_specs += [spec((1, stripe, size), lambda n, place, hot, sel, q=q: (source(q, n, place, sel), n % per_tile, 0)) for q in range(row_n)]
    in_specs += [spec((depth, size), lambda n, place, hot, sel, h=h: (0, tile(n) * blocks + hot_col(h, n, place, hot))) for h in each]
    in_specs += [spec((1, size, depth), lambda n, place, hot, sel, h=h: (tile(n), hot_col(h, n, place, hot), 0)) for h in each]
    in_specs += [spec((stripe, size), lambda n, place, hot, sel, h=h: (n % per_tile, tile(n) * blocks + hot_col(h, n, place, hot))) for h in each]
    in_specs += [spec((1, size), lambda n, place, hot, sel, h=h: (0, tile(n) * blocks + hot_col(h, n, place, hot))) for h in each]
    args = [wa] * hot_count + [x] * hot_count + [rd] * hot_count + [cols] * (hot_count * row_n)
    args += [s, wb, cd, wa, rd] + [cols] * row_n + [s] * hot_count + [wb] * hot_count + [x] * hot_count + [cd] * hot_count
    grid_spec = pltpu.PrefetchScalarGridSpec(
        num_scalar_prefetch=3,
        grid=(width // stripe,),
        in_specs=in_specs,
        out_specs=[
            spec((hot_count, size, stripe), lambda n, *_: (0, 0, n)),
            spec((hot_count, stripe, size), lambda n, *_: (n // per_tile, n % per_tile, 0)),
        ],
    )
    return pl.pallas_call(
        functools.partial(hot_kernel, row_n, hot_count),
        out_shape=[
            jax.ShapeDtypeStruct((hot_count, size, width), jnp.bfloat16),
            jax.ShapeDtypeStruct((ratio * hot_count, height, size), jnp.bfloat16),
        ],
        grid_spec=grid_spec,
        compiler_params=pltpu.CompilerParams(vmem_limit_bytes=VMEM_LIMIT),
    )(place, hot, sel, *args)


def first_hops(rows, cols, row_n, col_n):
    line, lanes, chips, cores = layout(row_n, col_n)
    upward = [(r, r + lanes) for r in range(row_n - lanes)]
    below = lax.ppermute(rows, "row", upward)
    above = lax.ppermute(rows, "row", [(b, a) for a, b in upward])
    turn = [(c, (c // cores + 1) % chips * cores + c % cores) for c in range(col_n)]
    ahead = [below, above, lax.ppermute(cols, "col", turn)]
    for step in range(1, lanes):
        ahead.append(lax.ppermute(rows, "row", [(r, r // lanes * lanes + (r + step) % lanes) for r in range(row_n)]))
    return ahead


def filter_kernel(source_count, row_chunk, place, sel, wa_ref, s_ref, wb_ref, rd_ref, cd_ref, *refs):
    b_refs = refs[:source_count]
    x_ref, out_ref = refs[source_count:]

    def chunk(i, carry):
        rows = pl.ds(pl.multiple_of(i * row_chunk, row_chunk), row_chunk)
        beta = jnp.concatenate([b[0, rows, :] for b in b_refs], axis=1)
        acc = jnp.dot(wa_ref[rows, :], s_ref[...], preferred_element_type=jnp.float32)
        acc = acc + dot_t(beta, wb_ref[0])
        acc = acc + (rd_ref[rows, :] + cd_ref[...] - center) * x_ref[rows, :]
        out_ref[rows, :] = acc * (1.0 / half_width)
        return carry

    lax.fori_loop(0, x_ref.shape[0] // row_chunk, chunk, 0)


def filter_step(place, sel, wa, s, wb, rd, cd, cols, x, row_n, ratio):
    height, width = x.shape
    size = cols.shape[-1]
    hot_count = cols.shape[0] // row_n
    tile_width = width // ratio
    stripe = next(n for n in (512, 384, 256, size) if tile_width % n == 0)
    per_tile = tile_width // stripe
    row_chunk = height // 2 if height % 256 == 0 else height

    def b_spec(q):
        return pl.BlockSpec(
            (1, height, size),
            lambda n, place, sel: (q * hot_count + sel[place[1] * ratio + jnp.minimum(n // per_tile, ratio - 1), q], 0, 0))

    striped = pl.BlockSpec((height, stripe), lambda n, *_: (0, n))
    in_specs = [
        pl.BlockSpec(wa.shape, lambda n, *_: (0, 0)),
        pl.BlockSpec((s.shape[0], stripe), lambda n, *_: (0, n)),
        pl.BlockSpec((1, stripe, wb.shape[2]), lambda n, *_: (n // per_tile, n % per_tile, 0)),
        pl.BlockSpec((height, 1), lambda n, *_: (0, 0)),
        pl.BlockSpec((1, stripe), lambda n, *_: (0, n)),
    ] + [b_spec(q) for q in range(row_n)] + [striped]
    args = [wa, s, wb, rd, cd] + [cols] * row_n + [x]
    grid_spec = pltpu.PrefetchScalarGridSpec(
        num_scalar_prefetch=2, grid=(width // stripe,), in_specs=in_specs, out_specs=striped)
    return pl.pallas_call(
        functools.partial(filter_kernel, row_n, row_chunk),
        out_shape=jax.ShapeDtypeStruct(x.shape, jnp.float32),
        grid_spec=grid_spec,
        cost_estimate=pl.CostEstimate(
            flops=4 * height * width * s.shape[0], bytes_accessed=4 * 3 * height * width, transcendentals=0),
        compiler_params=pltpu.CompilerParams(vmem_limit_bytes=VMEM_LIMIT),
    )(place, sel, *args)


def body(start_vector, ham_blocks, diagonal, pair_lists, pair_counts, hot_blocks, selection):
    row_n = lax.axis_size("row")
    col_n = lax.axis_size("col")
    ratio = row_n // col_n
    height, width = start_vector.shape
    size = ham_blocks.shape[1]
    place = jnp.stack([lax.axis_index("row"), lax.axis_index("col")]).astype(jnp.int32)
    shape = (height, row_n * size)
    rows, cols = pack(start_vector, place, hot_blocks, row_n, ratio, size)
    s, b, hams, rd, cd = exchange(rows, cols, selection, row_n, col_n, 0, ham=ham_blocks, diagonal=diagonal)
    wa = dense(ham_blocks[None], place, pair_lists, pair_counts, shape, lambda place, i: place[0])[0]
    wb = dense(hams, place, pair_lists, pair_counts, shape, lambda place, i: place[1] * ratio + i)
    rows, cols = hot_step(place, hot_blocks, selection, wa, s, wb, rd, cd, b, start_vector, row_n, ratio)
    ahead = first_hops(rows, cols, row_n, col_n)
    s, _ = lax.optimization_barrier((s, rows))
    first = filter_step(place, selection, wa, s, wb, rd, cd, b, start_vector, row_n, ratio)
    s, acc = exchange(rows, cols, selection, row_n, col_n, 1, ahead=ahead, product=(wa, wb, rd, cd, first, start_vector))
    return (first, last_step(place, acc, wa, s, row_n, col_n))


def solution(mesh):
    in_specs = (P("row", "col"), P("row", None, None), P(), P(), P(), P(), P())
    out_specs = (P("row", "col"), P("row", "col"))
    return jax.shard_map(body, mesh=mesh, in_specs=in_specs, out_specs=out_specs, check_vma=False)
```

```python
import functools

import jax
import jax.numpy as jnp
from jax import lax
from jax.experimental import pallas as pl
from jax.experimental.pallas import tpu as pltpu
from jax.sharding import PartitionSpec as P

center = 0.25
half_width = 2.5
VMEM_LIMIT = 60 * 1024 * 1024
VMEM_MOST = 67043328
MESH = pl.DeviceIdType.MESH


def dense_kernel(tile_of, place, pairs, counts, ham_ref, out_ref, acc):
    tile = tile_of(place, pl.program_id(0))
    size = ham_ref.shape[-1]
    acc[...] = jnp.zeros_like(acc)

    def add(slot, carry):
        source = pl.multiple_of(pairs[0, tile, slot] * size, size)
        target = pl.multiple_of(pairs[1, tile, slot] * size, size)
        acc[pl.ds(target, size), pl.ds(source, size)] += ham_ref[0, pairs[2, tile, slot]].astype(jnp.float32)
        return carry

    lax.fori_loop(0, counts[tile], add, 0)
    out_ref[0] = acc[...].astype(out_ref.dtype)


def dense(hams, place, pairs, counts, shape, tile_of):
    grid_spec = pltpu.PrefetchScalarGridSpec(
        num_scalar_prefetch=3,
        grid=(hams.shape[0],),
        in_specs=[pl.BlockSpec((1,) + hams.shape[1:], lambda i, *_: (i, 0, 0, 0))],
        out_specs=pl.BlockSpec((1,) + shape, lambda i, *_: (i, 0, 0)),
        scratch_shapes=[pltpu.VMEM(shape, jnp.float32)],
    )
    return pl.pallas_call(
        functools.partial(dense_kernel, tile_of),
        out_shape=jax.ShapeDtypeStruct((hams.shape[0],) + shape, jnp.bfloat16),
        grid_spec=grid_spec,
        compiler_params=pltpu.CompilerParams(vmem_limit_bytes=VMEM_LIMIT),
    )(place, pairs, counts, hams)


def dot_t(a, b):
    return lax.dot_general(a, b, (((1,), (1,)), ((), ())), preferred_element_type=jnp.float32)


def pack_kernel(place, hot, xr_ref, xc_ref, rows_ref, cols_ref):
    rows_ref[0] = xr_ref[...].astype(rows_ref.dtype)
    cols_ref[0] = xc_ref[...].astype(cols_ref.dtype)


def pack(x, place, hot, row_count, ratio, size):
    height, width = x.shape
    hot_count = hot.shape[1]
    blocks = width // (ratio * size)
    part = width // ratio

    def row_block(n, place, hot):
        n = jnp.minimum(n, ratio * hot_count - 1)
        return (hot[place[0], n // ratio], n % ratio)

    def col_block(n, place, hot):
        n = jnp.minimum(n, ratio * hot_count - 1)
        tile, which = n // hot_count, n % hot_count
        return (0, tile * blocks + hot[place[1] * ratio + tile, which])

    grid_spec = pltpu.PrefetchScalarGridSpec(
        num_scalar_prefetch=2,
        grid=(ratio * hot_count,),
        in_specs=[pl.BlockSpec((size, part), row_block), pl.BlockSpec((height, size), col_block)],
        out_specs=[
            pl.BlockSpec((1, size, part), lambda n, *_: (n // ratio, 0, n % ratio)),
            pl.BlockSpec((1, height, size), lambda n, *_: (n, 0, 0)),
        ],
    )
    return pl.pallas_call(
        pack_kernel,
        out_shape=[
            jax.ShapeDtypeStruct((hot_count, size, width), jnp.bfloat16),
            jax.ShapeDtypeStruct((ratio * hot_count, height, size), jnp.bfloat16),
        ],
        grid_spec=grid_spec,
    )(place, hot, x, x)


def layout(row_n, col_n):
    line = 1
    while 4 * line * line <= 2 * row_n:
        line *= 2
    cores = 2 if col_n % 2 == 0 else 1
    return line, row_n // line, col_n // cores, cores


class Grid:
    def __init__(self, row_n, col_n):
        self.line, self.lanes, self.chips, self.cores = layout(row_n, col_n)
        self.row_n, self.col_n = row_n, col_n
        row, col = lax.axis_index("row"), lax.axis_index("col")
        self.row, self.col = row, col
        self.at, self.lane = row // self.lanes, lax.rem(row, self.lanes)
        self.chip, self.core = col // self.cores, lax.rem(col, self.cores)

    def on_line(self, at):
        return (at * self.lanes + self.lane, self.col)

    def other_lane(self, step):
        return (self.at * self.lanes + lax.rem(self.lane + step, self.lanes), self.col)

    def other_chip(self, step):
        return (self.row, lax.rem(self.chip + step, self.chips) * self.cores + self.core)

    def other_core(self):
        return (self.row, self.chip * self.cores + lax.rem(self.core + 1, self.cores))


def remote(src, dst, send, recv, device):
    return pltpu.make_async_remote_copy(
        src_ref=src, dst_ref=dst, send_sem=send, recv_sem=recv, device_id=device, device_id_type=MESH)


def greet(g):
    barrier = pltpu.get_barrier_semaphore()
    up, down = g.at + 1 < g.line, g.at > 0

    def hello(device):
        pl.semaphore_signal(barrier, inc=1, device_id=device, device_id_type=MESH)

    @pl.when(up)
    def _():
        hello(g.on_line(g.at + 1))

    @pl.when(down)
    def _():
        hello(g.on_line(g.at - 1))

    for step in range(1, g.lanes):
        hello(g.other_lane(step))
    for step in range(1, g.chips):
        hello(g.other_chip(step))
    fixed = g.lanes - 1 + g.chips - 1
    if g.cores == 2:
        hello(g.other_core())
        fixed += 1
    pl.semaphore_wait(barrier, fixed + up.astype(jnp.int32) + down.astype(jnp.int32))


def got_slots(row_n, col_n):
    _, lanes, _, _ = layout(row_n, col_n)
    ratio = row_n // col_n
    return ratio if lanes > ratio > 1 else 1


def late_slot(at, line):
    return jnp.where(2 * at < line, line - 1, 0)


def exchange_kernel(row_n, col_n, pieces, with_ham, fused, sel, rows_ref, cols_ref, *refs):
    g = Grid(row_n, col_n)
    refs = list(refs)

    def some(count):
        taken = refs[:count]
        del refs[:count]
        return taken

    first_step = 2 if fused else 1
    if fused:
        below_ref, above_ref, chip_ref = some(3)
        side_refs = some(layout(row_n, col_n)[1] - 1)
        wa_hbm, wb_hbm, rd_ref, cd_ref, x_hbm, start_hbm, s_out, acc_out = some(8)
    else:
        ham_ref, diag_ref, s_out, c_out, h_out, rd_out, cd_out = some(7)
    held, lane_buf, turn_buf, s_all, c_all = some(5)
    own_sem, line_recv, up_send, down_send, lane_send, lane_recv = some(6)
    chip_send, chip_recv, core_send, core_recv, turn_send, turn_recv = some(6)
    if fused:
        acc, wa, wb_buf, x_buf, start_buf, via_buf, beta, st_buf, got, side_buf, load_sem, wb_sem, x_sem, start_sem, acc_sem, via_send, via_recv = some(17)
    else:
        ham_buf, far_buf, ham_sem, ham_recv, ham_up, ham_down, ham_lane, far_recv, far_send, far_chip = some(10)
        ham_rows = ham_ref.shape[0] // pieces
    ratio = row_n // col_n
    hot_count, size = rows_ref.shape[0], rows_ref.shape[1]
    height = cols_ref.shape[1]
    width = rows_ref.shape[2]
    piece = size // pieces
    block_n = cols_ref.shape[0]
    line, lanes, at = g.line, g.lanes, g.at

    home = (g.col * ratio) // lanes
    up_ok = (at + 1 < line) & ((home != line - 1) | (at + 1 != line - 1))
    down_ok = (at > 0) & ((home != 0) | (at - 1 != 0))
    deaf = (at == home) & ((at == 0) | (at == line - 1))
    far_base = jnp.where(at == 0, first_step * lanes, 0)
    far_count = (line - first_step) * lanes

    def chip_slot(step):
        return (lax.rem(g.chip - step + g.chips, g.chips) * g.cores + g.core) * block_n

    own_slot = g.col * block_n
    own_chip = g.chip * g.cores * ratio
    take = pltpu.make_async_copy(rows_ref, held.at[at], own_sem.at[0])
    take_cols = pltpu.make_async_copy(cols_ref, c_all.at[pl.ds(own_slot, block_n)], own_sem.at[1])
    take.start()
    take_cols.start()
    if fused:
        take_chip = pltpu.make_async_copy(chip_ref, c_all.at[pl.ds(chip_slot(1), block_n)], own_sem.at[2])
        take_chip.start()

        @pl.when(at > 0)
        def _():
            pltpu.make_async_copy(below_ref, held.at[at - 1], own_sem.at[3]).start()

        @pl.when(at + 1 < line)
        def _():
            pltpu.make_async_copy(above_ref, held.at[at + 1], own_sem.at[4]).start()
    else:
        take_ham = pltpu.make_async_copy(ham_ref, ham_buf, ham_sem.at[0])
        take_ham.start()
    greet(g)

    def chip_copy(step, b):
        return remote(cols_ref.at[b], c_all.at[own_slot + b], chip_send.at[step - 1, b], chip_recv.at[step - 1, b], g.other_chip(step))

    def core_copy(step, b):
        if step == 0:
            src, slot = cols_ref.at[b], own_slot + b
        else:
            slot = chip_slot(step) + b
            src = chip_ref.at[b] if fused and step == 1 else c_all.at[slot]
        return remote(src, c_all.at[slot], core_send.at[step, b], core_recv.at[step, b], g.other_core())

    for b in range(block_n):
        for step in range(first_step, g.chips):
            chip_copy(step, b).start()
    if g.cores == 2:
        for step in range(first_step):
            for b in range(block_n):
                core_copy(step, b).start()
    take.wait()
    if fused:
        @pl.when(at > 0)
        def _():
            pltpu.make_async_copy(below_ref, held.at[at - 1], own_sem.at[3]).wait()

        @pl.when(at + 1 < line)
        def _():
            pltpu.make_async_copy(above_ref, held.at[at + 1], own_sem.at[4]).wait()

    def part(slot, p):
        return held.at[slot, :, pl.ds(pl.multiple_of(p * piece, piece), piece), :]

    def up_copy(slot, p):
        return remote(part(slot, p), part(slot, p), up_send.at[slot, p], line_recv.at[slot, p], g.on_line(at + 1))

    def down_copy(slot, p):
        return remote(part(slot, p), part(slot, p), down_send.at[slot, p], line_recv.at[slot, p], g.on_line(at - 1))

    def s_rows(source, p):
        return pl.ds(pl.multiple_of(source * size + p * piece, piece), piece)

    def lane_copy(step, slot, p):
        rows = pl.ds(pl.multiple_of(p * piece, piece), piece)
        return remote(
            lane_buf.at[step - 1, slot, rows, :], s_all.at[s_rows(slot * lanes + g.lane, p), :],
            lane_send.at[step - 1, slot, p], lane_recv.at[step - 1, slot, p], g.other_lane(step))

    def lane_came(step, slot, p):
        rows = pl.ds(pl.multiple_of(p * piece, piece), piece)
        came = slot * lanes + lax.rem(g.lane - step + lanes, lanes)
        return remote(
            lane_buf.at[step - 1, slot, rows, :], s_all.at[s_rows(came, p), :],
            lane_send.at[step - 1, slot, p], lane_recv.at[step - 1, slot, p], g.other_lane(step))

    def pick(target, source, blocks):
        which = sel[target, source]
        value = blocks[0]
        for h in range(1, hot_count):
            value = jnp.where(which == h, blocks[h], value)
        return value

    def select(slot, p):
        source = slot * lanes + g.lane
        rows = pl.ds(pl.multiple_of(p * piece, piece), piece)
        blocks = [held[slot, h, rows, :] for h in range(hot_count)]

        @pl.when((slot != at) | (not fused))
        def _():
            for step in range(1, lanes):
                target = at * lanes + lax.rem(g.lane + step, lanes)
                lane_buf[step - 1, slot, rows, :] = pick(target, source, blocks)
                lane_copy(step, slot, p).start()

        s_all[s_rows(source, p), :] = pick(g.row, source, blocks)

    def tile_place(col, i):
        tile = col * ratio + i
        return tile // lanes, lax.rem(tile, lanes)

    detour = g.chips % 2 == 0 and g.chips > 1
    across = g.chips // 2
    end = jnp.where(2 * home < line, line - 1, 0)
    if not fused:
        def ham_part(ref, p):
            return ref.at[pl.ds(pl.multiple_of(p * ham_rows, ham_rows), ham_rows)]

        def ham_copies(i, p):
            here = ham_part(h_out.at[i], p)
            up = remote(here, here, ham_up.at[i, p], ham_recv.at[i, p], g.on_line(at + 1))
            down = remote(here, here, ham_down.at[i, p], ham_recv.at[i, p], g.on_line(at - 1))
            over = [remote(here, here, ham_lane.at[i, step - 1, p], ham_recv.at[i, p], g.other_lane(step))
                    for step in range(1, lanes)]
            return up, down, over

        def ham_sends(i, p, act):
            _, home_lane = tile_place(g.col, i)
            up, down, over = ham_copies(i, p)
            skip = end if detour else line

            @pl.when(home_lane == g.lane)
            def _():
                @pl.when((at >= home) & (at + 1 < line) & (at + 1 != skip))
                def _():
                    act(up)

                @pl.when((at <= home) & (at > 0) & (at - 1 != skip))
                def _():
                    act(down)

                for copy in over:
                    act(copy)

        if detour:
            far_col = lax.rem(g.chip + across, g.chips) * g.cores + g.core
            far_home = (far_col * ratio) // lanes
            far_end = jnp.where(2 * far_home < line, line - 1, 0)
            rising = far_end > far_home
            far_away = jnp.where(rising, at - far_home, far_home - at)

            def far_copies(i, p):
                here = ham_part(far_buf, p)
                way = jnp.where(rising, at + 1, at - 1)
                on = remote(here, here, far_send.at[p], far_recv.at[p], g.on_line(way))
                chip = remote(here, ham_part(h_out.at[i], p), far_chip.at[p], ham_recv.at[i, p], g.other_chip(across))
                return on, chip

            def far_sends(i, p, act):
                _, far_lane = tile_place(far_col, i)
                on, chip = far_copies(i, p)

                @pl.when((far_lane == g.lane) & (far_away >= 0))
                def _():
                    @pl.when(at != far_end)
                    def _():
                        act(on)

                    @pl.when(at == far_end)
                    def _():
                        act(chip)

        take_ham.wait()
        for i in range(ratio):
            _, home_lane = tile_place(g.col, i)

            @pl.when((home == at) & (home_lane == g.lane))
            def _():
                put = pltpu.make_async_copy(ham_buf, h_out.at[i], ham_sem.at[0])
                put.start()
                put.wait()

            if detour:
                _, far_lane = tile_place(far_col, i)

                @pl.when((far_home == at) & (far_lane == g.lane))
                def _():
                    put = pltpu.make_async_copy(ham_ref, far_buf, ham_sem.at[0])
                    put.start()
                    put.wait()

        def near_step(s, p):
            for i in range(ratio):
                _, home_lane = tile_place(g.col, i)
                away = jnp.where(at >= home, at - home, home - at)

                @pl.when((home_lane == g.lane) & (away == s))
                def _():
                    if s > 0:
                        ham_copies(i, p)[0].wait_recv()

                    ham_sends(i, p, lambda copy: copy.start())

        def far_step(s, p):
            for i in range(ratio if detour else 0):
                _, far_lane = tile_place(far_col, i)

                @pl.when((far_lane == g.lane) & (far_away == s))
                def _():
                    if s > 0:
                        far_copies(i, p)[0].wait_recv()

                    far_sends(i, p, lambda copy: copy.start())

        def far_steps(s):
            def one(p, carry):
                far_step(s, p)
                return carry

            lax.fori_loop(0, pieces, one, 0)

        if detour:
            held_back = (far_away > 0) & (at != far_end)
            up_first = (held_back & rising) == False
            down_first = (held_back & (rising == False)) == False
        else:
            up_first = down_first = at >= 0

        def ham_start(p, carry):
            near_step(0, p)
            far_step(0, p)
            return carry

        def ham_next(p, carry):
            near_step(1, p)
            far_step(1, p)
            return carry

        lax.fori_loop(0, pieces, ham_start, 0)

    if fused and detour and line > 2:
        climbs = end > home
        before = jnp.where(climbs, end - 1, end + 1)
        via_slot = jnp.where(climbs, end - 2, end + 2)
        leaves = at == before
        far_col = lax.rem(g.chip + across, g.chips) * g.cores + g.core
        far_home = (far_col * ratio) // lanes
        far_end = jnp.where(2 * far_home < line, line - 1, 0)
        far_before = jnp.where(far_end > far_home, far_end - 1, far_end + 1)
        far_slot = jnp.where(far_end > far_home, far_end - 2, far_end + 2)
        kept = pieces // 2

        def via_leave(p):
            return remote(part(via_slot, p), via_buf.at[p - kept], via_send.at[0, p - kept], via_recv.at[0, p - kept], g.other_chip(across))

        def via_pass(p):
            return remote(via_buf.at[p - kept], via_buf.at[p - kept], via_send.at[1, p - kept], via_recv.at[1, p - kept], g.on_line(far_end))

        def via_land(p):
            return remote(via_buf.at[p - kept], part(far_slot, p), via_send.at[2, p - kept], line_recv.at[far_slot, p], g.other_chip(across))

        def via_came(stage, p):
            there = g.other_chip(across) if stage == 0 else g.on_line(far_before)
            return remote(via_buf.at[p - kept], via_buf.at[p - kept], via_send.at[stage, p - kept], via_recv.at[stage, p - kept], there)

        def via_up(slot, p):
            return ((leaves & climbs & (slot == via_slot)) == False) | (p < kept)

        def via_down(slot, p):
            return ((leaves & (climbs == False) & (slot == via_slot)) == False) | (p < kept)
    else:
        leaves = None
        via_up = via_down = lambda slot, p: p >= 0

    half = pieces * (line // 2)

    def hears(s):
        quiet = (s == 0) | (deaf == False)
        return (at - s >= 0) & quiet, (at + s < line) & quiet

    if fused:
        up_first = down_first = at >= 0

    def relay(n, carry):
        s, p = n // pieces, lax.rem(n, pieces)
        hears_below, hears_above = hears(s)

        @pl.when(hears_below)
        def _():
            @pl.when(s >= first_step)
            def _():
                up_copy(at - s, p).wait_recv()

            @pl.when(up_ok & (s >= first_step - 1) & via_up(at - s, p) & ((s > 0) | up_first))
            def _():
                up_copy(at - s, p).start()

        @pl.when(hears_above)
        def _():
            @pl.when(s >= first_step)
            def _():
                down_copy(at + s, p).wait_recv()

            @pl.when(down_ok & (s >= first_step - 1) & via_down(at + s, p) & ((s > 0) | down_first))
            def _():
                down_copy(at + s, p).start()
        return carry

    def digest(n, carry):
        s, p = n // pieces, lax.rem(n, pieces)
        hears_below = (at - s >= 0) & ((s < first_step) | (deaf == False))
        hears_above = (at + s < line) & ((s < first_step) | (deaf == False))

        @pl.when(hears_below)
        def _():
            select(at - s, p)

        @pl.when(hears_above & (s > 0))
        def _():
            select(at + s, p)
        return carry

    def advance(n, carry):
        relay(n, carry)
        if not fused:
            @pl.when((n >= half) & (n < half + pieces))
            def _():
                for s in range(2, line):
                    near_step(s, n - half)
        return digest(n, carry)

    def core_came(step, b):
        other = lax.rem(g.core + 1, g.cores)
        slot = (lax.rem(g.chip - step + g.chips, g.chips) * g.cores + other) * block_n + b
        return remote(cols_ref.at[b], c_all.at[slot], core_send.at[step, b], core_recv.at[step, b], g.other_core())

    def got_at(i):
        return i if got_slots(row_n, col_n) > 1 else 0

    def turn_copy(i, step, q):
        if fused:
            there = got.at[got_at(i), q]
        else:
            there = s_all.at[pl.ds(pl.multiple_of(q * size, size), size), i * height:(i + 1) * height]
        return remote(turn_buf.at[step - 1, q], there, turn_send.at[step - 1, q], turn_recv.at[i, q], g.other_lane(step))

    def turn(q):
        rows = pl.ds(pl.multiple_of(q * size, size), size)
        for i in range(ratio):
            _, home_lane = tile_place(g.col, i)

            @pl.when(home_lane == g.lane)
            def _():
                for k in range(height // size):
                    strip = slice(k * size, (k + 1) * size)
                    blocks = [c_all[q * hot_count + h, strip, :] for h in range(hot_count)]
                    for step in range(1, lanes):
                        target = at * lanes + lax.rem(g.lane + step, lanes)
                        value = pick(target, q, blocks)
                        if fused:
                            turn_buf[step - 1, q, strip, :] = value
                        else:
                            turn_buf[step - 1, q, :, strip] = value.astype(jnp.float32).T.astype(turn_buf.dtype)
                    if not fused:
                        s_all[rows, i * height + k * size:i * height + (k + 1) * size] = pick(g.row, q, blocks).astype(jnp.float32).T.astype(s_all.dtype)
                for step in range(1, lanes):
                    turn_copy(i, step, q).start()

    def turns(act):
        def one(q, carry):
            for i in range(ratio):
                _, home_lane = tile_place(g.col, i)
                act(i, q, home_lane)
            return carry

        lax.fori_loop(far_base, far_base + far_count, one, 0)

    def turn_came(i, q, home_lane):
        @pl.when(home_lane != g.lane)
        def _():
            turn_copy(i, 1, q).wait_recv()

    def turn_sent(i, q, home_lane):
        @pl.when(home_lane == g.lane)
        def _():
            for step in range(1, lanes):
                turn_copy(i, step, q).wait_send()

    if fused:
        stripe = x_buf.shape[2]
        stripes = width // stripe
        per_tile = height // stripe
        rows_at_once = height // 2
        share = -(-stripes // pieces)
        late = late_slot(at, line)
        take_wa = pltpu.make_async_copy(wa_hbm, wa, load_sem.at[0])
        early = line - 1
        first_early = jnp.where(late == 0, 1, 0)
        depth = pl.ds(pl.multiple_of(first_early * lanes * size, lanes * size), early * lanes * size)

        def band(n):
            return pl.ds(pl.multiple_of(n * stripe, stripe), stripe)

        def loads(n):
            turn_n = lax.rem(n, 2)
            return [
                pltpu.make_async_copy(x_hbm.at[:, band(n)], x_buf.at[turn_n], x_sem.at[turn_n]),
                pltpu.make_async_copy(start_hbm.at[:, band(n)], start_buf.at[turn_n], start_sem.at[turn_n]),
                pltpu.make_async_copy(wb_hbm.at[n // per_tile, band(lax.rem(n, per_tile)), :], wb_buf.at[turn_n], wb_sem.at[turn_n]),
            ]

        def acc_copy(n):
            return pltpu.make_async_copy(acc.at[:, band(n)], acc_out.at[:, band(n)], acc_sem.at[n])

        def beta_side(n, carry):
            tile, turn_n = n // per_tile, lax.rem(n, 2)

            @pl.when(n + 1 < stripes)
            def _():
                for copy in loads(n + 1):
                    copy.start()

            @pl.when(lax.rem(n, per_tile) == 0)
            def _():
                for q in range(row_n):
                    beta[:, q * size:(q + 1) * size] = c_all[q * hot_count + sel[g.col * ratio + tile, q]]

            for copy in loads(n):
                copy.wait()
            for k in range(2):
                rows = slice(k * rows_at_once, (k + 1) * rows_at_once)
                value = dot_t(beta[rows, :], wb_buf[turn_n])
                value = value + (rd_ref[rows, :] + cd_ref[:, band(n)] - center) * x_buf[turn_n, rows, :]
                acc[rows, band(n)] = value - start_buf[turn_n, rows, :] * (half_width / 2.0)
            return carry

        near_base = jnp.where(at == 0, 0, (line - 2) * lanes * size)
        near_depth = pl.ds(pl.multiple_of(near_base, lanes * size), 2 * lanes * size)
        far_depth = pl.ds(pl.multiple_of(far_base * size, lanes * size), far_count * size)

        def alpha_side(m, carry):
            n = jnp.where(deaf, lax.rem(m + g.lane * per_tile, stripes), m)
            tile, inner = n // per_tile, lax.rem(n, per_tile)

            @pl.when(deaf == False)
            def _():
                for k in range(2):
                    rows = slice(k * rows_at_once, (k + 1) * rows_at_once)
                    acc[rows, band(n)] += jnp.dot(wa[rows, depth], s_all[depth, band(n)], preferred_element_type=jnp.float32)

            @pl.when(deaf)
            def _():
                _, home_lane = tile_place(g.col, tile)

                @pl.when(home_lane == g.lane)
                def _():
                    for j in range(far_count):
                        q = far_base + j
                        st_buf[:, j * size:(j + 1) * size] = c_all[q * hot_count + sel[g.row, q], band(inner), :]

                @pl.when(home_lane != g.lane)
                def _():
                    @pl.when(inner == 0)
                    def _():
                        def come(q, carry):
                            turn_copy(tile, 1, q).wait_recv()
                            return carry

                        lax.fori_loop(far_base, far_base + far_count, come, 0)

                    for j in range(far_count):
                        st_buf[:, j * size:(j + 1) * size] = got[got_at(tile), far_base + j, band(inner), :]

                for k in range(2):
                    rows = slice(k * rows_at_once, (k + 1) * rows_at_once)
                    value = jnp.dot(wa[rows, near_depth], s_all[near_depth, band(n)], preferred_element_type=jnp.float32)
                    acc[rows, band(n)] += value + dot_t(wa[rows, far_depth], st_buf[...])
            acc_copy(n).start()
            return carry

        def some_stripes(work, turn_n):
            lax.fori_loop(turn_n * share, jnp.minimum(turn_n * share + share, stripes), work, 0)

    if fused:
        if leaves is not None:
            @pl.when(leaves)
            def _():
                for p in range(kept, pieces):
                    via_leave(p).start()

        lax.fori_loop(pieces, half, relay, 0)
        take_sides = [pltpu.make_async_copy(side, side_buf.at[step], load_sem.at[1 + step]) for step, side in enumerate(side_refs)]
        for copy in take_sides:
            copy.start()
        lax.fori_loop(pieces, half, digest, 0)
        take_wa.start()
        for copy in loads(0):
            copy.start()
        lax.fori_loop(0, pieces, digest, 0)
        for copy in take_sides:
            copy.wait()

        def sides(p, carry):
            rows = pl.ds(pl.multiple_of(p * piece, piece), piece)
            for step in range(1, lanes):
                source = at * lanes + lax.rem(g.lane - step + lanes, lanes)
                blocks = [side_buf[step - 1, h, rows, :] for h in range(hot_count)]
                s_all[s_rows(source, p), :] = pick(g.row, source, blocks)
            return carry

        lax.fori_loop(0, pieces, sides, 0)
    else:
        def held_rows(p, carry):
            @pl.when(up_ok & (up_first == False))
            def _():
                up_copy(at, p).start()

            @pl.when(down_ok & (down_first == False))
            def _():
                down_copy(at, p).start()
            return carry

        lax.fori_loop(0, pieces, relay, 0)
        lax.fori_loop(0, pieces, digest, 0)
        take_cols.wait()
        if g.cores == 2:
            for b in range(block_n):
                core_came(0, b).wait_recv()

        @pl.when(deaf)
        def _():
            def turn_early(q, carry):
                @pl.when(q // lanes != at)
                def _():
                    turn(q)
                return carry

            lax.fori_loop(own_chip, own_chip + g.cores * ratio, turn_early, 0)

        lax.fori_loop(0, pieces, ham_next, 0)
        for s in range(2, line):
            far_steps(s)
        lax.fori_loop(0, pieces, held_rows, 0)
        lax.fori_loop(pieces, half, advance, 0)
    for step in range(first_step, g.chips):
        for b in range(block_n):
            slot = chip_slot(step) + b
            remote(cols_ref.at[b], c_all.at[slot], chip_send.at[step - 1, b], chip_recv.at[step - 1, b], g.other_chip(step)).wait_recv()
            if g.cores == 2:
                core_copy(step, b).start()

    if fused:
        take_cols.wait()
        take_chip.wait()
    if g.cores == 2:
        for step in range(0 if fused else 1, g.chips):
            for b in range(block_n):
                core_came(step, b).wait_recv()
    if not fused:
        @pl.when(deaf)
        def _():
            def turn_rest(q, carry):
                @pl.when(q // (g.cores * ratio) != g.chip)
                def _():
                    turn(q)
                return carry

            lax.fori_loop(far_base, far_base + far_count, turn_rest, 0)

        cd_out[...] = diag_ref[:, pl.ds(pl.multiple_of(g.col * width, width), width)]
        for k in range(height // size):
            strip = diag_ref[:, pl.ds(pl.multiple_of(g.row * height + k * size, size), size)]
            rd_out[k * size:(k + 1) * size, :] = jnp.broadcast_to(strip, (size, size)).T[:, :1]
        put_cols = pltpu.make_async_copy(c_all, c_out, own_sem.at[2])
        put_cols.start()
    else:
        take_wa.wait()

        @pl.when(deaf)
        def _():
            def turn_on(q, carry):
                turn(q)
                return carry

            lax.fori_loop(far_base, far_base + far_count, turn_on, 0)

    def middle(n, carry):
        if leaves is not None:
            @pl.when((n < half + 2) & (at == far_before))
            def _():
                p = kept + lax.rem(n - half, 2)
                via_came(0, p).wait_recv()
                via_pass(p).start()

            @pl.when((n >= half) & (n < half + 2) & (at == far_end))
            def _():
                p = kept + lax.rem(n - half, 2)
                via_came(1, p).wait_recv()
                via_land(p).start()

        advance(n, carry)
        if fused:
            some_stripes(beta_side, n - half)
        return carry

    def lanes_came(slot):
        def one(p, carry):
            for step in range(1, lanes):
                lane_came(step, slot, p).wait_recv()
            return carry

        near = (slot - at < first_step) & (at - slot < first_step)
        away = slot != at if fused else True

        @pl.when(((deaf == False) | near) & away)
        def _():
            lax.fori_loop(0, pieces, one, 0)

    lax.fori_loop(half, half + pieces, middle, 0)
    if fused:
        for other in range(1, line):
            lanes_came(lax.rem(late + other, line))

        def ending(n, carry):
            advance(n, carry)
            some_stripes(alpha_side, n - half - pieces)
            return carry

        lax.fori_loop(half + pieces, pieces * line, ending, 0)
        lanes_came(late)

        @pl.when(deaf)
        def _():
            s_all[pl.ds(pl.multiple_of(late * lanes * size, size), lanes * size), :] = jnp.zeros((lanes * size, width), s_all.dtype)

        put_s = pltpu.make_async_copy(s_all.at[pl.ds(pl.multiple_of(late * lanes * size, size), lanes * size), :], s_out, own_sem.at[5])
        put_s.start()
        put_s.wait()
        for n in range(stripes):
            acc_copy(n).wait()
    else:
        lax.fori_loop(half + pieces, pieces * line, advance, 0)
        for slot in range(line):
            lanes_came(slot)

        @pl.when(deaf)
        def _():
            turns(turn_came)

        put_s = pltpu.make_async_copy(s_all, s_out, own_sem.at[5])
        put_s.start()
        put_s.wait()
        put_cols.wait()

    @pl.when(deaf)
    def _():
        turns(turn_sent)

    def finish(n, carry):
        slot, p = n // pieces, lax.rem(n, pieces)

        @pl.when((slot <= at + 1 - first_step) & up_ok & via_up(slot, p))
        def _():
            up_copy(slot, p).wait_send()

        @pl.when((slot >= at - 1 + first_step) & down_ok & via_down(slot, p))
        def _():
            down_copy(slot, p).wait_send()

        near = (slot - at < first_step) & (at - slot < first_step)
        away = slot != at if fused else True

        @pl.when(((deaf == False) | near) & away)
        def _():
            for step in range(1, lanes):
                lane_copy(step, slot, p).wait_send()
        return carry

    lax.fori_loop(0, line * pieces, finish, 0)
    if leaves is not None:
        for p in range(kept, pieces):
            @pl.when(leaves)
            def _():
                via_leave(p).wait_send()

            @pl.when(at == far_before)
            def _():
                via_pass(p).wait_send()

            @pl.when(at == far_end)
            def _():
                via_land(p).wait_send()
    for b in range(block_n):
        for step in range(first_step, g.chips):
            chip_copy(step, b).wait_send()
        if g.cores == 2:
            for step in range(g.chips):
                core_copy(step, b).wait_send()
    if not fused:
        for i in range(ratio):
            _, home_lane = tile_place(g.col, i)

            def settle(p, carry):
                ham_sends(i, p, lambda copy: copy.wait_send())
                if detour:
                    far_sends(i, p, lambda copy: copy.wait_send())

                @pl.when(home_lane != g.lane)
                def _():
                    ham_copies(i, p)[2][0].wait_recv()
                return carry

            lax.fori_loop(0, pieces, settle, 0)


def exchange(rows, cols, sel, row_n, col_n, ident, ham=None, diagonal=None, ahead=None, product=None):
    hot_count, size, width = rows.shape
    block_n, height = cols.shape[:2]
    ratio = row_n // col_n
    pieces = 4
    fused = product is not None
    line, lanes, chips, _ = layout(row_n, col_n)
    others = max(lanes - 1, 1)
    dma = pltpu.SemaphoreType.DMA
    vmem = lambda *shape: pltpu.VMEM(shape, jnp.bfloat16)
    anywhere = pl.BlockSpec(memory_space=pl.ANY)
    whole = pl.BlockSpec(memory_space=pltpu.VMEM)
    scratch = [
        vmem(line, hot_count, size, width),
        vmem(others, line, size, width),
        vmem(others, row_n, *((height, size) if fused else (size, height))),
        vmem(row_n * size, width),
        vmem(col_n * block_n, height, size),
        dma((6,)),
        dma((line, pieces)),
        dma((line, pieces)),
        dma((line, pieces)),
        dma((others, line, pieces)),
        dma((others, line, pieces)),
        dma((max(chips - 1, 1), block_n)),
        dma((max(chips - 1, 1), block_n)),
        dma((chips, block_n)),
        dma((chips, block_n)),
        dma((others, row_n)),
        dma((ratio, row_n)),
    ]
    args = [sel, rows, cols]
    in_specs = [pl.BlockSpec(memory_space=pltpu.SMEM), anywhere, anywhere]
    if fused:
        wa, wb, rd, cd, x, start = product
        stripe = 256 if height % 256 == 0 else size
        args += list(ahead) + [wa, wb, rd, cd, x, start]
        in_specs += [anywhere] * (len(ahead) + 2) + [whole] * 2 + [anywhere] * 2
        out_shape = [
            jax.ShapeDtypeStruct((lanes * size, width), jnp.bfloat16),
            jax.ShapeDtypeStruct((height, width), jnp.float32),
        ]
        out_specs = [anywhere] * 2
        scratch += [
            pltpu.VMEM((height, width), jnp.float32),
            vmem(*wa.shape),
            vmem(2, stripe, wb.shape[2]),
            pltpu.VMEM((2, height, stripe), jnp.float32),
            pltpu.VMEM((2, height, stripe), jnp.float32),
            vmem(pieces - pieces // 2, hot_count, size // pieces, width),
            vmem(height, row_n * size),
            vmem(stripe, (line - 2) * lanes * size),
            vmem(got_slots(row_n, col_n), row_n, height, size),
            vmem(others, hot_count, size, width),
            dma((1 + others,)),
            dma((2,)),
            dma((2,)),
            dma((2,)),
            dma((width // stripe,)),
            dma((3, pieces)),
            dma((3, pieces)),
        ]
    else:
        args += [ham, diagonal[None, :]]
        in_specs += [anywhere, whole]
        out_shape = [
            jax.ShapeDtypeStruct((row_n * size, width), jnp.bfloat16),
            jax.ShapeDtypeStruct((col_n * block_n, height, size), jnp.bfloat16),
            jax.ShapeDtypeStruct((ratio,) + ham.shape, ham.dtype),
            jax.ShapeDtypeStruct((height, 1), jnp.float32),
            jax.ShapeDtypeStruct((1, width), jnp.float32),
        ]
        out_specs = [anywhere] * 3 + [whole] * 2
        scratch += [
            pltpu.VMEM(ham.shape, ham.dtype),
            pltpu.VMEM(ham.shape, ham.dtype),
            dma((1,)),
            dma((ratio, pieces)),
            dma((ratio, pieces)),
            dma((ratio, pieces)),
            dma((ratio, others, pieces)),
            dma((pieces,)),
            dma((pieces,)),
            dma((pieces,)),
        ]
    return pl.pallas_call(
        functools.partial(exchange_kernel, row_n, col_n, pieces, ham is not None, fused),
        out_shape=out_shape,
        in_specs=in_specs,
        out_specs=out_specs,
        scratch_shapes=scratch,
        compiler_params=pltpu.CompilerParams(collective_id=ident, has_side_effects=True, vmem_limit_bytes=VMEM_MOST),
    )(*args)


def last_kernel(place, acc_ref, wa_ref, s_ref, out_ref):
    acc = acc_ref[...] + jnp.dot(wa_ref[...], s_ref[...], preferred_element_type=jnp.float32)
    out_ref[...] = acc * (2.0 / half_width)


def last_step(place, acc, wa, s, row_n, col_n):
    height, width = acc.shape
    depth = s.shape[0]
    line, lanes, _, _ = layout(row_n, col_n)
    stripe = next(n for n in (512, 384, 256, width) if width % n == 0)
    grid_spec = pltpu.PrefetchScalarGridSpec(
        num_scalar_prefetch=1,
        grid=(width // stripe,),
        in_specs=[
            pl.BlockSpec((height, stripe), lambda n, place: (0, n)),
            pl.BlockSpec((height, depth), lambda n, place: (0, late_slot(place[0] // lanes, line))),
            pl.BlockSpec((depth, stripe), lambda n, place: (0, n)),
        ],
        out_specs=pl.BlockSpec((height, stripe), lambda n, place: (0, n)),
    )
    return pl.pallas_call(
        last_kernel,
        out_shape=jax.ShapeDtypeStruct(acc.shape, jnp.float32),
        grid_spec=grid_spec,
        compiler_params=pltpu.CompilerParams(vmem_limit_bytes=VMEM_LIMIT),
    )(place, acc, wa, s)


def hot_kernel(row_n, hot_count, place, hot, sel, *refs):
    refs = list(refs)

    def some(count):
        taken = refs[:count]
        del refs[:count]
        return taken

    wide = lambda blocks: jnp.concatenate(blocks, axis=1)
    wa_hot, x_rows, rd_hot = some(hot_count), some(hot_count), some(hot_count)
    b_hot = [some(row_n) for _ in range(hot_count)]
    s_ref, wb_ref, cd_ref = some(3)
    wa_ref, rd_ref = some(2)
    b_refs = some(row_n)
    s_hot, wb_hot, x_cols, cd_hot = some(hot_count), some(hot_count), some(hot_count), some(hot_count)
    rows_ref, cols_ref = refs
    scale = 1.0 / half_width

    def dot(a, b):
        return jnp.dot(a, b, preferred_element_type=jnp.float32)

    size = rows_ref.shape[1]
    acc = dot(jnp.concatenate([w[...] for w in wa_hot], axis=0), s_ref[...])
    beta = jnp.concatenate([wide([b[0] for b in blocks]) for blocks in b_hot], axis=0)
    acc = acc + dot_t(beta, wb_ref[0])
    for h in range(hot_count):
        value = acc[h * size:(h + 1) * size] + (rd_hot[h][...] + cd_ref[...] - center) * x_rows[h][...]
        rows_ref[h] = (value * scale).astype(rows_ref.dtype)
    acc = dot(wa_ref[...], wide([s[...] for s in s_hot]))
    acc = acc + dot_t(wide([b[0] for b in b_refs]), jnp.concatenate([w[0] for w in wb_hot], axis=0))
    for h in range(hot_count):
        value = acc[:, h * size:(h + 1) * size] + (rd_ref[...] + cd_hot[h][...] - center) * x_cols[h][...]
        cols_ref[h] = (value * scale).astype(cols_ref.dtype)


def hot_step(place, hot, sel, wa, s, wb, rd, cd, cols, x, row_n, ratio):
    height, width = x.shape
    size = cols.shape[-1]
    hot_count = hot.shape[1]
    tile_width = width // ratio
    stripe = tile_width // 2 if tile_width % 256 == 0 else size
    per_tile = tile_width // stripe
    blocks = tile_width // size
    depth = s.shape[0]

    def tile(n):
        return jnp.minimum(n // per_tile, ratio - 1)

    def hot_row(h, place, hot):
        return hot[place[0], h]

    def hot_col(h, n, place, hot):
        return hot[place[1] * ratio + tile(n), h]

    def source(q, n, place, sel):
        return q * hot_count + sel[place[1] * ratio + tile(n), q]

    spec = pl.BlockSpec
    each = range(hot_count)
    in_specs = [spec((size, depth), lambda n, place, hot, sel, h=h: (hot_row(h, place, hot), 0)) for h in each]
    in_specs += [spec((size, stripe), lambda n, place, hot, sel, h=h: (hot_row(h, place, hot), n)) for h in each]
    in_specs += [spec((size, 1), lambda n, place, hot, sel, h=h: (hot_row(h, place, hot), 0)) for h in each]
    in_specs += [spec((1, size, size), lambda n, place, hot, sel, h=h, q=q: (source(q, n, place, sel), hot_row(h, place, hot), 0))
                 for h in each for q in range(row_n)]
    in_specs += [
        spec((depth, stripe), lambda n, *_: (0, n)),
        spec((1, stripe, depth), lambda n, *_: (n // per_tile, n % per_tile, 0)),
        spec((1, stripe), lambda n, *_: (0, n)),
        spec((stripe, depth), lambda n, *_: (n % per_tile, 0)),
        spec((stripe, 1), lambda n, *_: (n % per_tile, 0)),
    ]
    in_specs += [spec((1, stripe, size), lambda n, place, hot, sel, q=q: (source(q, n, place, sel), n % per_tile, 0)) for q in range(row_n)]
    in_specs += [spec((depth, size), lambda n, place, hot, sel, h=h: (0, tile(n) * blocks + hot_col(h, n, place, hot))) for h in each]
    in_specs += [spec((1, size, depth), lambda n, place, hot, sel, h=h: (tile(n), hot_col(h, n, place, hot), 0)) for h in each]
    in_specs += [spec((stripe, size), lambda n, place, hot, sel, h=h: (n % per_tile, tile(n) * blocks + hot_col(h, n, place, hot))) for h in each]
    in_specs += [spec((1, size), lambda n, place, hot, sel, h=h: (0, tile(n) * blocks + hot_col(h, n, place, hot))) for h in each]
    args = [wa] * hot_count + [x] * hot_count + [rd] * hot_count + [cols] * (hot_count * row_n)
    args += [s, wb, cd, wa, rd] + [cols] * row_n + [s] * hot_count + [wb] * hot_count + [x] * hot_count + [cd] * hot_count
    grid_spec = pltpu.PrefetchScalarGridSpec(
        num_scalar_prefetch=3,
        grid=(width // stripe,),
        in_specs=in_specs,
        out_specs=[
            spec((hot_count, size, stripe), lambda n, *_: (0, 0, n)),
            spec((hot_count, stripe, size), lambda n, *_: (n // per_tile, n % per_tile, 0)),
        ],
    )
    return pl.pallas_call(
        functools.partial(hot_kernel, row_n, hot_count),
        out_shape=[
            jax.ShapeDtypeStruct((hot_count, size, width), jnp.bfloat16),
            jax.ShapeDtypeStruct((ratio * hot_count, height, size), jnp.bfloat16),
        ],
        grid_spec=grid_spec,
        compiler_params=pltpu.CompilerParams(vmem_limit_bytes=VMEM_LIMIT),
    )(place, hot, sel, *args)


def first_hops(rows, cols, row_n, col_n):
    line, lanes, chips, cores = layout(row_n, col_n)
    upward = [(r, r + lanes) for r in range(row_n - lanes)]
    below = lax.ppermute(rows, "row", upward)
    above = lax.ppermute(rows, "row", [(b, a) for a, b in upward])
    turn = [(c, (c // cores + 1) % chips * cores + c % cores) for c in range(col_n)]
    ahead = [below, above, lax.ppermute(cols, "col", turn)]
    for step in range(1, lanes):
        ahead.append(lax.ppermute(rows, "row", [(r, r // lanes * lanes + (r + step) % lanes) for r in range(row_n)]))
    return ahead


def filter_kernel(source_count, row_chunk, place, sel, wa_ref, s_ref, wb_ref, rd_ref, cd_ref, *refs):
    b_refs = refs[:source_count]
    x_ref, out_ref = refs[source_count:]

    def chunk(i, carry):
        rows = pl.ds(pl.multiple_of(i * row_chunk, row_chunk), row_chunk)
        beta = jnp.concatenate([b[0, rows, :] for b in b_refs], axis=1)
        acc = jnp.dot(wa_ref[rows, :], s_ref[...], preferred_element_type=jnp.float32)
        acc = acc + dot_t(beta, wb_ref[0])
        acc = acc + (rd_ref[rows, :] + cd_ref[...] - center) * x_ref[rows, :]
        out_ref[rows, :] = acc * (1.0 / half_width)
        return carry

    lax.fori_loop(0, x_ref.shape[0] // row_chunk, chunk, 0)


def filter_step(place, sel, wa, s, wb, rd, cd, cols, x, row_n, ratio):
    height, width = x.shape
    size = cols.shape[-1]
    hot_count = cols.shape[0] // row_n
    tile_width = width // ratio
    stripe = next(n for n in (512, 384, 256, size) if tile_width % n == 0)
    per_tile = tile_width // stripe
    row_chunk = height // 2 if height % 256 == 0 else height

    def b_spec(q):
        return pl.BlockSpec(
            (1, height, size),
            lambda n, place, sel: (q * hot_count + sel[place[1] * ratio + jnp.minimum(n // per_tile, ratio - 1), q], 0, 0))

    striped = pl.BlockSpec((height, stripe), lambda n, *_: (0, n))
    in_specs = [
        pl.BlockSpec(wa.shape, lambda n, *_: (0, 0)),
        pl.BlockSpec((s.shape[0], stripe), lambda n, *_: (0, n)),
        pl.BlockSpec((1, stripe, wb.shape[2]), lambda n, *_: (n // per_tile, n % per_tile, 0)),
        pl.BlockSpec((height, 1), lambda n, *_: (0, 0)),
        pl.BlockSpec((1, stripe), lambda n, *_: (0, n)),
    ] + [b_spec(q) for q in range(row_n)] + [striped]
    args = [wa, s, wb, rd, cd] + [cols] * row_n + [x]
    grid_spec = pltpu.PrefetchScalarGridSpec(
        num_scalar_prefetch=2, grid=(width // stripe,), in_specs=in_specs, out_specs=striped)
    return pl.pallas_call(
        functools.partial(filter_kernel, row_n, row_chunk),
        out_shape=jax.ShapeDtypeStruct(x.shape, jnp.float32),
        grid_spec=grid_spec,
        cost_estimate=pl.CostEstimate(
            flops=4 * height * width * s.shape[0], bytes_accessed=4 * 3 * height * width, transcendentals=0),
        compiler_params=pltpu.CompilerParams(vmem_limit_bytes=VMEM_LIMIT),
    )(place, sel, *args)


def body(start_vector, ham_blocks, diagonal, pair_lists, pair_counts, hot_blocks, selection):
    row_n = lax.axis_size("row")
    col_n = lax.axis_size("col")
    ratio = row_n // col_n
    height, width = start_vector.shape
    size = ham_blocks.shape[1]
    place = jnp.stack([lax.axis_index("row"), lax.axis_index("col")]).astype(jnp.int32)
    shape = (height, row_n * size)
    rows, cols = pack(start_vector, place, hot_blocks, row_n, ratio, size)
    s, b, hams, rd, cd = exchange(rows, cols, selection, row_n, col_n, 0, ham=ham_blocks, diagonal=diagonal)
    wa = dense(ham_blocks[None], place, pair_lists, pair_counts, shape, lambda place, i: place[0])[0]
    wb = dense(hams, place, pair_lists, pair_counts, shape, lambda place, i: place[1] * ratio + i)
    rows, cols = hot_step(place, hot_blocks, selection, wa, s, wb, rd, cd, b, start_vector, row_n, ratio)
    ahead = first_hops(rows, cols, row_n, col_n)
    s, _ = lax.optimization_barrier((s, rows))
    first = filter_step(place, selection, wa, s, wb, rd, cd, b, start_vector, row_n, ratio)
    s, acc = exchange(rows, cols, selection, row_n, col_n, 1, ahead=ahead, product=(wa, wb, rd, cd, first, start_vector))
    return (first, last_step(place, acc, wa, s, row_n, col_n))


def solution(mesh):
    in_specs = (P("row", "col"), P("row", None, None), P(), P(), P(), P(), P())
    out_specs = (P("row", "col"), P("row", "col"))
    return jax.shard_map(body, mesh=mesh, in_specs=in_specs, out_specs=out_specs, check_vma=False)
```

```python
import functools

import jax
import jax.numpy as jnp
from jax import lax
from jax.experimental import pallas as pl
from jax.experimental.pallas import tpu as pltpu
from jax.sharding import PartitionSpec as P

center = 0.25
half_width = 2.5
VMEM_LIMIT = 60 * 1024 * 1024
VMEM_MOST = 67043328
MESH = pl.DeviceIdType.MESH


def dense_kernel(tile_of, place, pairs, counts, ham_ref, out_ref, acc):
    tile = tile_of(place, pl.program_id(0))
    size = ham_ref.shape[-1]
    acc[...] = jnp.zeros_like(acc)

    def add(slot, carry):
        source = pl.multiple_of(pairs[0, tile, slot] * size, size)
        target = pl.multiple_of(pairs[1, tile, slot] * size, size)
        acc[pl.ds(target, size), pl.ds(source, size)] += ham_ref[0, pairs[2, tile, slot]].astype(jnp.float32)
        return carry

    lax.fori_loop(0, counts[tile], add, 0)
    out_ref[0] = acc[...].astype(out_ref.dtype)


def dense(hams, place, pairs, counts, shape, tile_of):
    grid_spec = pltpu.PrefetchScalarGridSpec(
        num_scalar_prefetch=3,
        grid=(hams.shape[0],),
        in_specs=[pl.BlockSpec((1,) + hams.shape[1:], lambda i, *_: (i, 0, 0, 0))],
        out_specs=pl.BlockSpec((1,) + shape, lambda i, *_: (i, 0, 0)),
        scratch_shapes=[pltpu.VMEM(shape, jnp.float32)],
    )
    return pl.pallas_call(
        functools.partial(dense_kernel, tile_of),
        out_shape=jax.ShapeDtypeStruct((hams.shape[0],) + shape, jnp.bfloat16),
        grid_spec=grid_spec,
        compiler_params=pltpu.CompilerParams(vmem_limit_bytes=VMEM_LIMIT),
    )(place, pairs, counts, hams)


def dot_t(a, b):
    return lax.dot_general(a, b, (((1,), (1,)), ((), ())), preferred_element_type=jnp.float32)


def pack_kernel(place, hot, xr_ref, xc_ref, rows_ref, cols_ref):
    rows_ref[0] = xr_ref[...].astype(rows_ref.dtype)
    cols_ref[0] = xc_ref[...].astype(cols_ref.dtype)


def pack(x, place, hot, row_count, ratio, size):
    height, width = x.shape
    hot_count = hot.shape[1]
    blocks = width // (ratio * size)
    part = width // ratio

    def row_block(n, place, hot):
        n = jnp.minimum(n, ratio * hot_count - 1)
        return (hot[place[0], n // ratio], n % ratio)

    def col_block(n, place, hot):
        n = jnp.minimum(n, ratio * hot_count - 1)
        tile, which = n // hot_count, n % hot_count
        return (0, tile * blocks + hot[place[1] * ratio + tile, which])

    grid_spec = pltpu.PrefetchScalarGridSpec(
        num_scalar_prefetch=2,
        grid=(ratio * hot_count,),
        in_specs=[pl.BlockSpec((size, part), row_block), pl.BlockSpec((height, size), col_block)],
        out_specs=[
            pl.BlockSpec((1, size, part), lambda n, *_: (n // ratio, 0, n % ratio)),
            pl.BlockSpec((1, height, size), lambda n, *_: (n, 0, 0)),
        ],
    )
    return pl.pallas_call(
        pack_kernel,
        out_shape=[
            jax.ShapeDtypeStruct((hot_count, size, width), jnp.bfloat16),
            jax.ShapeDtypeStruct((ratio * hot_count, height, size), jnp.bfloat16),
        ],
        grid_spec=grid_spec,
    )(place, hot, x, x)


def layout(row_n, col_n):
    line = 1
    while 4 * line * line <= 2 * row_n:
        line *= 2
    cores = 2 if col_n % 2 == 0 else 1
    return line, row_n // line, col_n // cores, cores


class Grid:
    def __init__(self, row_n, col_n):
        self.line, self.lanes, self.chips, self.cores = layout(row_n, col_n)
        self.row_n, self.col_n = row_n, col_n
        row, col = lax.axis_index("row"), lax.axis_index("col")
        self.row, self.col = row, col
        self.at, self.lane = row // self.lanes, lax.rem(row, self.lanes)
        self.chip, self.core = col // self.cores, lax.rem(col, self.cores)

    def on_line(self, at):
        return (at * self.lanes + self.lane, self.col)

    def other_lane(self, step):
        return (self.at * self.lanes + lax.rem(self.lane + step, self.lanes), self.col)

    def other_chip(self, step):
        return (self.row, lax.rem(self.chip + step, self.chips) * self.cores + self.core)

    def other_core(self):
        return (self.row, self.chip * self.cores + lax.rem(self.core + 1, self.cores))


def remote(src, dst, send, recv, device):
    return pltpu.make_async_remote_copy(
        src_ref=src, dst_ref=dst, send_sem=send, recv_sem=recv, device_id=device, device_id_type=MESH)


def greet(g):
    barrier = pltpu.get_barrier_semaphore()
    up, down = g.at + 1 < g.line, g.at > 0

    def hello(device):
        pl.semaphore_signal(barrier, inc=1, device_id=device, device_id_type=MESH)

    @pl.when(up)
    def _():
        hello(g.on_line(g.at + 1))

    @pl.when(down)
    def _():
        hello(g.on_line(g.at - 1))

    for step in range(1, g.lanes):
        hello(g.other_lane(step))
    for step in range(1, g.chips):
        hello(g.other_chip(step))
    fixed = g.lanes - 1 + g.chips - 1
    if g.cores == 2:
        hello(g.other_core())
        fixed += 1
    pl.semaphore_wait(barrier, fixed + up.astype(jnp.int32) + down.astype(jnp.int32))


def got_slots(row_n, col_n):
    _, lanes, _, _ = layout(row_n, col_n)
    ratio = row_n // col_n
    return ratio if lanes > ratio > 1 else 1


def late_slot(at, line):
    return jnp.where(2 * at < line, line - 1, 0)


def exchange_kernel(row_n, col_n, pieces, with_ham, fused, sel, rows_ref, cols_ref, *refs):
    g = Grid(row_n, col_n)
    refs = list(refs)

    def some(count):
        taken = refs[:count]
        del refs[:count]
        return taken

    first_step = 2 if fused else 1
    if fused:
        below_ref, above_ref, chip_ref = some(3)
        side_refs = some(layout(row_n, col_n)[1] - 1)
        wa_hbm, wb_hbm, rd_ref, cd_ref, x_hbm, start_hbm, s_out, acc_out = some(8)
    else:
        ham_ref, diag_ref, s_out, c_out, h_out, rd_out, cd_out = some(7)
    held, lane_buf, turn_buf, s_all, c_all = some(5)
    own_sem, line_recv, up_send, down_send, lane_send, lane_recv = some(6)
    chip_send, chip_recv, core_send, core_recv, turn_send, turn_recv = some(6)
    if fused:
        acc, wa, wb_buf, x_buf, start_buf, via_buf, beta, st_buf, got, side_buf, load_sem, wb_sem, x_sem, start_sem, acc_sem, via_send, via_recv = some(17)
    else:
        ham_buf, far_buf, ham_sem, ham_recv, ham_up, ham_down, ham_lane, far_recv, far_send, far_chip = some(10)
        ham_rows = ham_ref.shape[0] // pieces
    ratio = row_n // col_n
    hot_count, size = rows_ref.shape[0], rows_ref.shape[1]
    height = cols_ref.shape[1]
    width = rows_ref.shape[2]
    piece = size // pieces
    block_n = cols_ref.shape[0]
    line, lanes, at = g.line, g.lanes, g.at

    home = (g.col * ratio) // lanes
    up_ok = (at + 1 < line) & ((home != line - 1) | (at + 1 != line - 1))
    down_ok = (at > 0) & ((home != 0) | (at - 1 != 0))
    deaf = (at == home) & ((at == 0) | (at == line - 1))
    far_base = jnp.where(at == 0, first_step * lanes, 0)
    far_count = (line - first_step) * lanes

    def chip_slot(step):
        return (lax.rem(g.chip - step + g.chips, g.chips) * g.cores + g.core) * block_n

    own_slot = g.col * block_n
    own_chip = g.chip * g.cores * ratio
    take = pltpu.make_async_copy(rows_ref, held.at[at], own_sem.at[0])
    take_cols = pltpu.make_async_copy(cols_ref, c_all.at[pl.ds(own_slot, block_n)], own_sem.at[1])
    take.start()
    take_cols.start()
    if fused:
        take_chip = pltpu.make_async_copy(chip_ref, c_all.at[pl.ds(chip_slot(1), block_n)], own_sem.at[2])
        take_chip.start()

        @pl.when(at > 0)
        def _():
            pltpu.make_async_copy(below_ref, held.at[at - 1], own_sem.at[3]).start()

        @pl.when(at + 1 < line)
        def _():
            pltpu.make_async_copy(above_ref, held.at[at + 1], own_sem.at[4]).start()
    else:
        take_ham = pltpu.make_async_copy(ham_ref, ham_buf, ham_sem.at[0])
        take_ham.start()
    greet(g)

    def chip_copy(step, b):
        return remote(cols_ref.at[b], c_all.at[own_slot + b], chip_send.at[step - 1, b], chip_recv.at[step - 1, b], g.other_chip(step))

    def core_copy(step, b):
        if step == 0:
            src, slot = cols_ref.at[b], own_slot + b
        else:
            slot = chip_slot(step) + b
            src = chip_ref.at[b] if fused and step == 1 else c_all.at[slot]
        return remote(src, c_all.at[slot], core_send.at[step, b], core_recv.at[step, b], g.other_core())

    for b in range(block_n):
        for step in range(first_step, g.chips):
            chip_copy(step, b).start()
    if g.cores == 2:
        for step in range(first_step):
            for b in range(block_n):
                core_copy(step, b).start()
    take.wait()
    if fused:
        @pl.when(at > 0)
        def _():
            pltpu.make_async_copy(below_ref, held.at[at - 1], own_sem.at[3]).wait()

        @pl.when(at + 1 < line)
        def _():
            pltpu.make_async_copy(above_ref, held.at[at + 1], own_sem.at[4]).wait()

    def part(slot, p):
        return held.at[slot, :, pl.ds(pl.multiple_of(p * piece, piece), piece), :]

    def up_copy(slot, p):
        return remote(part(slot, p), part(slot, p), up_send.at[slot, p], line_recv.at[slot, p], g.on_line(at + 1))

    def down_copy(slot, p):
        return remote(part(slot, p), part(slot, p), down_send.at[slot, p], line_recv.at[slot, p], g.on_line(at - 1))

    def s_rows(source, p):
        return pl.ds(pl.multiple_of(source * size + p * piece, piece), piece)

    def lane_copy(step, slot, p):
        rows = pl.ds(pl.multiple_of(p * piece, piece), piece)
        return remote(
            lane_buf.at[step - 1, slot, rows, :], s_all.at[s_rows(slot * lanes + g.lane, p), :],
            lane_send.at[step - 1, slot, p], lane_recv.at[step - 1, slot, p], g.other_lane(step))

    def lane_came(step, slot, p):
        rows = pl.ds(pl.multiple_of(p * piece, piece), piece)
        came = slot * lanes + lax.rem(g.lane - step + lanes, lanes)
        return remote(
            lane_buf.at[step - 1, slot, rows, :], s_all.at[s_rows(came, p), :],
            lane_send.at[step - 1, slot, p], lane_recv.at[step - 1, slot, p], g.other_lane(step))

    def pick(target, source, blocks):
        which = sel[target, source]
        value = blocks[0]
        for h in range(1, hot_count):
            value = jnp.where(which == h, blocks[h], value)
        return value

    def select(slot, p):
        source = slot * lanes + g.lane
        rows = pl.ds(pl.multiple_of(p * piece, piece), piece)
        blocks = [held[slot, h, rows, :] for h in range(hot_count)]

        @pl.when((slot != at) | (not fused))
        def _():
            for step in range(1, lanes):
                target = at * lanes + lax.rem(g.lane + step, lanes)
                lane_buf[step - 1, slot, rows, :] = pick(target, source, blocks)
                lane_copy(step, slot, p).start()

        s_all[s_rows(source, p), :] = pick(g.row, source, blocks)

    def tile_place(col, i):
        tile = col * ratio + i
        return tile // lanes, lax.rem(tile, lanes)

    detour = g.chips % 2 == 0 and g.chips > 1
    across = g.chips // 2
    end = jnp.where(2 * home < line, line - 1, 0)
    if not fused:
        def ham_part(ref, p):
            return ref.at[pl.ds(pl.multiple_of(p * ham_rows, ham_rows), ham_rows)]

        def ham_copies(i, p):
            here = ham_part(h_out.at[i], p)
            up = remote(here, here, ham_up.at[i, p], ham_recv.at[i, p], g.on_line(at + 1))
            down = remote(here, here, ham_down.at[i, p], ham_recv.at[i, p], g.on_line(at - 1))
            over = [remote(here, here, ham_lane.at[i, step - 1, p], ham_recv.at[i, p], g.other_lane(step))
                    for step in range(1, lanes)]
            return up, down, over

        def ham_sends(i, p, act):
            _, home_lane = tile_place(g.col, i)
            up, down, over = ham_copies(i, p)
            skip = end if detour else line

            @pl.when(home_lane == g.lane)
            def _():
                @pl.when((at >= home) & (at + 1 < line) & (at + 1 != skip))
                def _():
                    act(up)

                @pl.when((at <= home) & (at > 0) & (at - 1 != skip))
                def _():
                    act(down)

                for copy in over:
                    act(copy)

        if detour:
            far_col = lax.rem(g.chip + across, g.chips) * g.cores + g.core
            far_home = (far_col * ratio) // lanes
            far_end = jnp.where(2 * far_home < line, line - 1, 0)
            rising = far_end > far_home
            far_away = jnp.where(rising, at - far_home, far_home - at)

            def far_copies(i, p):
                here = ham_part(far_buf, p)
                way = jnp.where(rising, at + 1, at - 1)
                on = remote(here, here, far_send.at[p], far_recv.at[p], g.on_line(way))
                chip = remote(here, ham_part(h_out.at[i], p), far_chip.at[p], ham_recv.at[i, p], g.other_chip(across))
                return on, chip

            def far_sends(i, p, act):
                _, far_lane = tile_place(far_col, i)
                on, chip = far_copies(i, p)

                @pl.when((far_lane == g.lane) & (far_away >= 0))
                def _():
                    @pl.when(at != far_end)
                    def _():
                        act(on)

                    @pl.when(at == far_end)
                    def _():
                        act(chip)

        take_ham.wait()
        for i in range(ratio):
            _, home_lane = tile_place(g.col, i)

            @pl.when((home == at) & (home_lane == g.lane))
            def _():
                put = pltpu.make_async_copy(ham_buf, h_out.at[i], ham_sem.at[0])
                put.start()
                put.wait()

            if detour:
                _, far_lane = tile_place(far_col, i)

                @pl.when((far_home == at) & (far_lane == g.lane))
                def _():
                    put = pltpu.make_async_copy(ham_ref, far_buf, ham_sem.at[0])
                    put.start()
                    put.wait()

        def near_step(s, p):
            for i in range(ratio):
                _, home_lane = tile_place(g.col, i)
                away = jnp.where(at >= home, at - home, home - at)

                @pl.when((home_lane == g.lane) & (away == s))
                def _():
                    if s > 0:
                        ham_copies(i, p)[0].wait_recv()

                    ham_sends(i, p, lambda copy: copy.start())

        def far_step(s, p):
            for i in range(ratio if detour else 0):
                _, far_lane = tile_place(far_col, i)

                @pl.when((far_lane == g.lane) & (far_away == s))
                def _():
                    if s > 0:
                        far_copies(i, p)[0].wait_recv()

                    far_sends(i, p, lambda copy: copy.start())

        def far_steps(s):
            def one(p, carry):
                far_step(s, p)
                return carry

            lax.fori_loop(0, pieces, one, 0)

        if detour:
            held_back = (far_away > 0) & (at != far_end)
            up_first = (held_back & rising) == False
            down_first = (held_back & (rising == False)) == False
        else:
            up_first = down_first = at >= 0

        def ham_start(p, carry):
            near_step(0, p)
            far_step(0, p)
            return carry

        def ham_next(p, carry):
            near_step(1, p)
            far_step(1, p)
            return carry

        lax.fori_loop(0, pieces, ham_start, 0)

    if fused and detour and line > 2:
        climbs = end > home
        before = jnp.where(climbs, end - 1, end + 1)
        via_slot = jnp.where(climbs, end - 2, end + 2)
        leaves = at == before
        far_col = lax.rem(g.chip + across, g.chips) * g.cores + g.core
        far_home = (far_col * ratio) // lanes
        far_end = jnp.where(2 * far_home < line, line - 1, 0)
        far_before = jnp.where(far_end > far_home, far_end - 1, far_end + 1)
        far_slot = jnp.where(far_end > far_home, far_end - 2, far_end + 2)
        kept = pieces * 3 // 4

        def via_leave(p):
            return remote(part(via_slot, p), via_buf.at[p - kept], via_send.at[0, p - kept], via_recv.at[0, p - kept], g.other_chip(across))

        def via_pass(p):
            return remote(via_buf.at[p - kept], via_buf.at[p - kept], via_send.at[1, p - kept], via_recv.at[1, p - kept], g.on_line(far_end))

        def via_land(p):
            return remote(via_buf.at[p - kept], part(far_slot, p), via_send.at[2, p - kept], line_recv.at[far_slot, p], g.other_chip(across))

        def via_came(stage, p):
            there = g.other_chip(across) if stage == 0 else g.on_line(far_before)
            return remote(via_buf.at[p - kept], via_buf.at[p - kept], via_send.at[stage, p - kept], via_recv.at[stage, p - kept], there)

        def via_up(slot, p):
            return ((leaves & climbs & (slot == via_slot)) == False) | (p < kept)

        def via_down(slot, p):
            return ((leaves & (climbs == False) & (slot == via_slot)) == False) | (p < kept)
    else:
        leaves = None
        via_up = via_down = lambda slot, p: p >= 0

    half = pieces * (line // 2)

    def hears(s):
        quiet = (s == 0) | (deaf == False)
        return (at - s >= 0) & quiet, (at + s < line) & quiet

    if fused:
        up_first = down_first = at >= 0

    def relay(n, carry):
        s, p = n // pieces, lax.rem(n, pieces)
        hears_below, hears_above = hears(s)

        @pl.when(hears_below)
        def _():
            @pl.when(s >= first_step)
            def _():
                up_copy(at - s, p).wait_recv()

            @pl.when(up_ok & (s >= first_step - 1) & via_up(at - s, p) & ((s > 0) | up_first))
            def _():
                up_copy(at - s, p).start()

        @pl.when(hears_above)
        def _():
            @pl.when(s >= first_step)
            def _():
                down_copy(at + s, p).wait_recv()

            @pl.when(down_ok & (s >= first_step - 1) & via_down(at + s, p) & ((s > 0) | down_first))
            def _():
                down_copy(at + s, p).start()
        return carry

    def digest(n, carry):
        s, p = n // pieces, lax.rem(n, pieces)
        hears_below = (at - s >= 0) & ((s < first_step) | (deaf == False))
        hears_above = (at + s < line) & ((s < first_step) | (deaf == False))

        @pl.when(hears_below)
        def _():
            select(at - s, p)

        @pl.when(hears_above & (s > 0))
        def _():
            select(at + s, p)
        return carry

    def advance(n, carry):
        relay(n, carry)
        if not fused:
            @pl.when((n >= half) & (n < half + pieces))
            def _():
                for s in range(2, line):
                    near_step(s, n - half)
        return digest(n, carry)

    def core_came(step, b):
        other = lax.rem(g.core + 1, g.cores)
        slot = (lax.rem(g.chip - step + g.chips, g.chips) * g.cores + other) * block_n + b
        return remote(cols_ref.at[b], c_all.at[slot], core_send.at[step, b], core_recv.at[step, b], g.other_core())

    def got_at(i):
        return i if got_slots(row_n, col_n) > 1 else 0

    def turn_copy(i, step, q):
        if fused:
            there = got.at[got_at(i), q]
        else:
            there = s_all.at[pl.ds(pl.multiple_of(q * size, size), size), i * height:(i + 1) * height]
        return remote(turn_buf.at[step - 1, q], there, turn_send.at[step - 1, q], turn_recv.at[i, q], g.other_lane(step))

    def turn(q):
        rows = pl.ds(pl.multiple_of(q * size, size), size)
        for i in range(ratio):
            _, home_lane = tile_place(g.col, i)

            @pl.when(home_lane == g.lane)
            def _():
                for k in range(height // size):
                    strip = slice(k * size, (k + 1) * size)
                    blocks = [c_all[q * hot_count + h, strip, :] for h in range(hot_count)]
                    for step in range(1, lanes):
                        target = at * lanes + lax.rem(g.lane + step, lanes)
                        value = pick(target, q, blocks)
                        if fused:
                            turn_buf[step - 1, q, strip, :] = value
                        else:
                            turn_buf[step - 1, q, :, strip] = value.astype(jnp.float32).T.astype(turn_buf.dtype)
                    if not fused:
                        s_all[rows, i * height + k * size:i * height + (k + 1) * size] = pick(g.row, q, blocks).astype(jnp.float32).T.astype(s_all.dtype)
                for step in range(1, lanes):
                    turn_copy(i, step, q).start()

    def turns(act):
        def one(q, carry):
            for i in range(ratio):
                _, home_lane = tile_place(g.col, i)
                act(i, q, home_lane)
            return carry

        lax.fori_loop(far_base, far_base + far_count, one, 0)

    def turn_came(i, q, home_lane):
        @pl.when(home_lane != g.lane)
        def _():
            turn_copy(i, 1, q).wait_recv()

    def turn_sent(i, q, home_lane):
        @pl.when(home_lane == g.lane)
        def _():
            for step in range(1, lanes):
                turn_copy(i, step, q).wait_send()

    if fused:
        stripe = x_buf.shape[2]
        stripes = width // stripe
        per_tile = height // stripe
        rows_at_once = height // 2
        share = -(-stripes // pieces)
        late = late_slot(at, line)
        take_wa = pltpu.make_async_copy(wa_hbm, wa, load_sem.at[0])
        early = line - 1
        first_early = jnp.where(late == 0, 1, 0)
        depth = pl.ds(pl.multiple_of(first_early * lanes * size, lanes * size), early * lanes * size)

        def band(n):
            return pl.ds(pl.multiple_of(n * stripe, stripe), stripe)

        def loads(n):
            turn_n = lax.rem(n, 2)
            return [
                pltpu.make_async_copy(x_hbm.at[:, band(n)], x_buf.at[turn_n], x_sem.at[turn_n]),
                pltpu.make_async_copy(start_hbm.at[:, band(n)], start_buf.at[turn_n], start_sem.at[turn_n]),
                pltpu.make_async_copy(wb_hbm.at[n // per_tile, band(lax.rem(n, per_tile)), :], wb_buf.at[turn_n], wb_sem.at[turn_n]),
            ]

        def acc_copy(n):
            return pltpu.make_async_copy(acc.at[:, band(n)], acc_out.at[:, band(n)], acc_sem.at[n])

        def beta_side(n, carry):
            tile, turn_n = n // per_tile, lax.rem(n, 2)

            @pl.when(n + 1 < stripes)
            def _():
                for copy in loads(n + 1):
                    copy.start()

            @pl.when(lax.rem(n, per_tile) == 0)
            def _():
                for q in range(row_n):
                    beta[:, q * size:(q + 1) * size] = c_all[q * hot_count + sel[g.col * ratio + tile, q]]

            for copy in loads(n):
                copy.wait()
            for k in range(2):
                rows = slice(k * rows_at_once, (k + 1) * rows_at_once)
                value = dot_t(beta[rows, :], wb_buf[turn_n])
                value = value + (rd_ref[rows, :] + cd_ref[:, band(n)] - center) * x_buf[turn_n, rows, :]
                acc[rows, band(n)] = value - start_buf[turn_n, rows, :] * (half_width / 2.0)
            return carry

        near_base = jnp.where(at == 0, 0, (line - 2) * lanes * size)
        near_depth = pl.ds(pl.multiple_of(near_base, lanes * size), 2 * lanes * size)
        far_depth = pl.ds(pl.multiple_of(far_base * size, lanes * size), far_count * size)

        def alpha_side(m, carry):
            n = jnp.where(deaf, lax.rem(m + g.lane * per_tile, stripes), m)
            tile, inner = n // per_tile, lax.rem(n, per_tile)

            @pl.when(deaf == False)
            def _():
                for k in range(2):
                    rows = slice(k * rows_at_once, (k + 1) * rows_at_once)
                    acc[rows, band(n)] += jnp.dot(wa[rows, depth], s_all[depth, band(n)], preferred_element_type=jnp.float32)

            @pl.when(deaf)
            def _():
                _, home_lane = tile_place(g.col, tile)

                @pl.when(home_lane == g.lane)
                def _():
                    for j in range(far_count):
                        q = far_base + j
                        st_buf[:, j * size:(j + 1) * size] = c_all[q * hot_count + sel[g.row, q], band(inner), :]

                @pl.when(home_lane != g.lane)
                def _():
                    @pl.when(inner == 0)
                    def _():
                        def come(q, carry):
                            turn_copy(tile, 1, q).wait_recv()
                            return carry

                        lax.fori_loop(far_base, far_base + far_count, come, 0)

                    for j in range(far_count):
                        st_buf[:, j * size:(j + 1) * size] = got[got_at(tile), far_base + j, band(inner), :]

                for k in range(2):
                    rows = slice(k * rows_at_once, (k + 1) * rows_at_once)
                    value = jnp.dot(wa[rows, near_depth], s_all[near_depth, band(n)], preferred_element_type=jnp.float32)
                    acc[rows, band(n)] += value + dot_t(wa[rows, far_depth], st_buf[...])
            acc_copy(n).start()
            return carry

        def some_stripes(work, turn_n):
            lax.fori_loop(turn_n * share, jnp.minimum(turn_n * share + share, stripes), work, 0)

    if fused:
        if leaves is not None:
            @pl.when(leaves)
            def _():
                for p in range(kept, pieces):
                    via_leave(p).start()

        lax.fori_loop(pieces, half, relay, 0)
        take_sides = [pltpu.make_async_copy(side, side_buf.at[step], load_sem.at[1 + step]) for step, side in enumerate(side_refs)]
        for copy in take_sides:
            copy.start()
        lax.fori_loop(pieces, half, digest, 0)
        take_wa.start()
        for copy in loads(0):
            copy.start()
        lax.fori_loop(0, pieces, digest, 0)
        for copy in take_sides:
            copy.wait()

        def sides(p, carry):
            rows = pl.ds(pl.multiple_of(p * piece, piece), piece)
            for step in range(1, lanes):
                source = at * lanes + lax.rem(g.lane - step + lanes, lanes)
                blocks = [side_buf[step - 1, h, rows, :] for h in range(hot_count)]
                s_all[s_rows(source, p), :] = pick(g.row, source, blocks)
            return carry

        lax.fori_loop(0, pieces, sides, 0)
    else:
        def held_rows(p, carry):
            @pl.when(up_ok & (up_first == False))
            def _():
                up_copy(at, p).start()

            @pl.when(down_ok & (down_first == False))
            def _():
                down_copy(at, p).start()
            return carry

        lax.fori_loop(0, pieces, relay, 0)
        lax.fori_loop(0, pieces, digest, 0)
        take_cols.wait()
        if g.cores == 2:
            for b in range(block_n):
                core_came(0, b).wait_recv()

        @pl.when(deaf)
        def _():
            def turn_early(q, carry):
                @pl.when(q // lanes != at)
                def _():
                    turn(q)
                return carry

            lax.fori_loop(own_chip, own_chip + g.cores * ratio, turn_early, 0)

        lax.fori_loop(0, pieces, ham_next, 0)
        for s in range(2, line):
            far_steps(s)
        lax.fori_loop(0, pieces, held_rows, 0)
        lax.fori_loop(pieces, half, advance, 0)
    for step in range(first_step, g.chips):
        for b in range(block_n):
            slot = chip_slot(step) + b
            remote(cols_ref.at[b], c_all.at[slot], chip_send.at[step - 1, b], chip_recv.at[step - 1, b], g.other_chip(step)).wait_recv()
            if g.cores == 2:
                core_copy(step, b).start()

    if fused:
        take_cols.wait()
        take_chip.wait()
    if g.cores == 2:
        for step in range(0 if fused else 1, g.chips):
            for b in range(block_n):
                core_came(step, b).wait_recv()
    if not fused:
        @pl.when(deaf)
        def _():
            def turn_rest(q, carry):
                @pl.when(q // (g.cores * ratio) != g.chip)
                def _():
                    turn(q)
                return carry

            lax.fori_loop(far_base, far_base + far_count, turn_rest, 0)

        cd_out[...] = diag_ref[:, pl.ds(pl.multiple_of(g.col * width, width), width)]
        for k in range(height // size):
            strip = diag_ref[:, pl.ds(pl.multiple_of(g.row * height + k * size, size), size)]
            rd_out[k * size:(k + 1) * size, :] = jnp.broadcast_to(strip, (size, size)).T[:, :1]
        put_cols = pltpu.make_async_copy(c_all, c_out, own_sem.at[2])
        put_cols.start()
    else:
        take_wa.wait()

        @pl.when(deaf)
        def _():
            def turn_on(q, carry):
                turn(q)
                return carry

            lax.fori_loop(far_base, far_base + far_count, turn_on, 0)

    def middle(n, carry):
        if fused:
            some_stripes(beta_side, n - half)
        if leaves is not None:
            via_p = kept + jnp.minimum(n - half, pieces - kept - 1)

            @pl.when((n < half + pieces - kept) & (at == far_before))
            def _():
                p = via_p
                via_came(0, p).wait_recv()
                via_pass(p).start()

            @pl.when((n < half + pieces - kept) & (at == far_end))
            def _():
                p = via_p
                via_came(1, p).wait_recv()
                via_land(p).start()

        return advance(n, carry)

    def lanes_came(slot):
        def one(p, carry):
            for step in range(1, lanes):
                lane_came(step, slot, p).wait_recv()
            return carry

        near = (slot - at < first_step) & (at - slot < first_step)
        away = slot != at if fused else True

        @pl.when(((deaf == False) | near) & away)
        def _():
            lax.fori_loop(0, pieces, one, 0)

    lax.fori_loop(half, half + pieces, middle, 0)
    if fused:
        for other in range(1, line):
            lanes_came(lax.rem(late + other, line))

        def ending(n, carry):
            some_stripes(alpha_side, n - half - pieces)
            return advance(n, carry)

        lax.fori_loop(half + pieces, pieces * line, ending, 0)
        lanes_came(late)

        @pl.when(deaf)
        def _():
            s_all[pl.ds(pl.multiple_of(late * lanes * size, size), lanes * size), :] = jnp.zeros((lanes * size, width), s_all.dtype)

        put_s = pltpu.make_async_copy(s_all.at[pl.ds(pl.multiple_of(late * lanes * size, size), lanes * size), :], s_out, own_sem.at[5])
        put_s.start()
        put_s.wait()
        for n in range(stripes):
            acc_copy(n).wait()
    else:
        lax.fori_loop(half + pieces, pieces * line, advance, 0)
        for slot in range(line):
            lanes_came(slot)

        @pl.when(deaf)
        def _():
            turns(turn_came)

        put_s = pltpu.make_async_copy(s_all, s_out, own_sem.at[5])
        put_s.start()
        put_s.wait()
        put_cols.wait()

    @pl.when(deaf)
    def _():
        turns(turn_sent)

    def finish(n, carry):
        slot, p = n // pieces, lax.rem(n, pieces)

        @pl.when((slot <= at + 1 - first_step) & up_ok & via_up(slot, p))
        def _():
            up_copy(slot, p).wait_send()

        @pl.when((slot >= at - 1 + first_step) & down_ok & via_down(slot, p))
        def _():
            down_copy(slot, p).wait_send()

        near = (slot - at < first_step) & (at - slot < first_step)
        away = slot != at if fused else True

        @pl.when(((deaf == False) | near) & away)
        def _():
            for step in range(1, lanes):
                lane_copy(step, slot, p).wait_send()
        return carry

    lax.fori_loop(0, line * pieces, finish, 0)
    if leaves is not None:
        for p in range(kept, pieces):
            @pl.when(leaves)
            def _():
                via_leave(p).wait_send()

            @pl.when(at == far_before)
            def _():
                via_pass(p).wait_send()

            @pl.when(at == far_end)
            def _():
                via_land(p).wait_send()
    for b in range(block_n):
        for step in range(first_step, g.chips):
            chip_copy(step, b).wait_send()
        if g.cores == 2:
            for step in range(g.chips):
                core_copy(step, b).wait_send()
    if not fused:
        for i in range(ratio):
            _, home_lane = tile_place(g.col, i)

            def settle(p, carry):
                ham_sends(i, p, lambda copy: copy.wait_send())
                if detour:
                    far_sends(i, p, lambda copy: copy.wait_send())

                @pl.when(home_lane != g.lane)
                def _():
                    ham_copies(i, p)[2][0].wait_recv()
                return carry

            lax.fori_loop(0, pieces, settle, 0)


def exchange(rows, cols, sel, row_n, col_n, ident, ham=None, diagonal=None, ahead=None, product=None):
    hot_count, size, width = rows.shape
    block_n, height = cols.shape[:2]
    ratio = row_n // col_n
    pieces = 8
    fused = product is not None
    line, lanes, chips, _ = layout(row_n, col_n)
    others = max(lanes - 1, 1)
    dma = pltpu.SemaphoreType.DMA
    vmem = lambda *shape: pltpu.VMEM(shape, jnp.bfloat16)
    anywhere = pl.BlockSpec(memory_space=pl.ANY)
    whole = pl.BlockSpec(memory_space=pltpu.VMEM)
    scratch = [
        vmem(line, hot_count, size, width),
        vmem(others, line, size, width),
        vmem(others, row_n, *((height, size) if fused else (size, height))),
        vmem(row_n * size, width),
        vmem(col_n * block_n, height, size),
        dma((6,)),
        dma((line, pieces)),
        dma((line, pieces)),
        dma((line, pieces)),
        dma((others, line, pieces)),
        dma((others, line, pieces)),
        dma((max(chips - 1, 1), block_n)),
        dma((max(chips - 1, 1), block_n)),
        dma((chips, block_n)),
        dma((chips, block_n)),
        dma((others, row_n)),
        dma((ratio, row_n)),
    ]
    args = [sel, rows, cols]
    in_specs = [pl.BlockSpec(memory_space=pltpu.SMEM), anywhere, anywhere]
    if fused:
        wa, wb, rd, cd, x, start = product
        stripe = 256 if height % 256 == 0 else size
        args += list(ahead) + [wa, wb, rd, cd, x, start]
        in_specs += [anywhere] * (len(ahead) + 2) + [whole] * 2 + [anywhere] * 2
        out_shape = [
            jax.ShapeDtypeStruct((lanes * size, width), jnp.bfloat16),
            jax.ShapeDtypeStruct((height, width), jnp.float32),
        ]
        out_specs = [anywhere] * 2
        scratch += [
            pltpu.VMEM((height, width), jnp.float32),
            vmem(*wa.shape),
            vmem(2, stripe, wb.shape[2]),
            pltpu.VMEM((2, height, stripe), jnp.float32),
            pltpu.VMEM((2, height, stripe), jnp.float32),
            vmem(pieces - pieces * 3 // 4, hot_count, size // pieces, width),
            vmem(height, row_n * size),
            vmem(stripe, (line - 2) * lanes * size),
            vmem(got_slots(row_n, col_n), row_n, height, size),
            vmem(others, hot_count, size, width),
            dma((1 + others,)),
            dma((2,)),
            dma((2,)),
            dma((2,)),
            dma((width // stripe,)),
            dma((3, pieces)),
            dma((3, pieces)),
        ]
    else:
        args += [ham, diagonal[None, :]]
        in_specs += [anywhere, whole]
        out_shape = [
            jax.ShapeDtypeStruct((row_n * size, width), jnp.bfloat16),
            jax.ShapeDtypeStruct((col_n * block_n, height, size), jnp.bfloat16),
            jax.ShapeDtypeStruct((ratio,) + ham.shape, ham.dtype),
            jax.ShapeDtypeStruct((height, 1), jnp.float32),
            jax.ShapeDtypeStruct((1, width), jnp.float32),
        ]
        out_specs = [anywhere] * 3 + [whole] * 2
        scratch += [
            pltpu.VMEM(ham.shape, ham.dtype),
            pltpu.VMEM(ham.shape, ham.dtype),
            dma((1,)),
            dma((ratio, pieces)),
            dma((ratio, pieces)),
            dma((ratio, pieces)),
            dma((ratio, others, pieces)),
            dma((pieces,)),
            dma((pieces,)),
            dma((pieces,)),
        ]
    return pl.pallas_call(
        functools.partial(exchange_kernel, row_n, col_n, pieces, ham is not None, fused),
        out_shape=out_shape,
        in_specs=in_specs,
        out_specs=out_specs,
        scratch_shapes=scratch,
        compiler_params=pltpu.CompilerParams(collective_id=ident, has_side_effects=True, vmem_limit_bytes=VMEM_MOST),
    )(*args)


def last_kernel(place, acc_ref, wa_ref, s_ref, out_ref):
    acc = acc_ref[...] + jnp.dot(wa_ref[...], s_ref[...], preferred_element_type=jnp.float32)
    out_ref[...] = acc * (2.0 / half_width)


def last_step(place, acc, wa, s, row_n, col_n):
    height, width = acc.shape
    depth = s.shape[0]
    line, lanes, _, _ = layout(row_n, col_n)
    stripe = next(n for n in (512, 384, 256, width) if width % n == 0)
    grid_spec = pltpu.PrefetchScalarGridSpec(
        num_scalar_prefetch=1,
        grid=(width // stripe,),
        in_specs=[
            pl.BlockSpec((height, stripe), lambda n, place: (0, n)),
            pl.BlockSpec((height, depth), lambda n, place: (0, late_slot(place[0] // lanes, line))),
            pl.BlockSpec((depth, stripe), lambda n, place: (0, n)),
        ],
        out_specs=pl.BlockSpec((height, stripe), lambda n, place: (0, n)),
    )
    return pl.pallas_call(
        last_kernel,
        out_shape=jax.ShapeDtypeStruct(acc.shape, jnp.float32),
        grid_spec=grid_spec,
        compiler_params=pltpu.CompilerParams(vmem_limit_bytes=VMEM_LIMIT),
    )(place, acc, wa, s)


def hot_kernel(row_n, hot_count, place, hot, sel, *refs):
    refs = list(refs)

    def some(count):
        taken = refs[:count]
        del refs[:count]
        return taken

    wide = lambda blocks: jnp.concatenate(blocks, axis=1)
    wa_hot, x_rows, rd_hot = some(hot_count), some(hot_count), some(hot_count)
    b_hot = [some(row_n) for _ in range(hot_count)]
    s_ref, wb_ref, cd_ref = some(3)
    wa_ref, rd_ref = some(2)
    b_refs = some(row_n)
    s_hot, wb_hot, x_cols, cd_hot = some(hot_count), some(hot_count), some(hot_count), some(hot_count)
    rows_ref, cols_ref = refs
    scale = 1.0 / half_width

    def dot(a, b):
        return jnp.dot(a, b, preferred_element_type=jnp.float32)

    size = rows_ref.shape[1]
    acc = dot(jnp.concatenate([w[...] for w in wa_hot], axis=0), s_ref[...])
    beta = jnp.concatenate([wide([b[0] for b in blocks]) for blocks in b_hot], axis=0)
    acc = acc + dot_t(beta, wb_ref[0])
    for h in range(hot_count):
        value = acc[h * size:(h + 1) * size] + (rd_hot[h][...] + cd_ref[...] - center) * x_rows[h][...]
        rows_ref[h] = (value * scale).astype(rows_ref.dtype)
    acc = dot(wa_ref[...], wide([s[...] for s in s_hot]))
    acc = acc + dot_t(wide([b[0] for b in b_refs]), jnp.concatenate([w[0] for w in wb_hot], axis=0))
    for h in range(hot_count):
        value = acc[:, h * size:(h + 1) * size] + (rd_ref[...] + cd_hot[h][...] - center) * x_cols[h][...]
        cols_ref[h] = (value * scale).astype(cols_ref.dtype)


def hot_step(place, hot, sel, wa, s, wb, rd, cd, cols, x, row_n, ratio):
    height, width = x.shape
    size = cols.shape[-1]
    hot_count = hot.shape[1]
    tile_width = width // ratio
    stripe = tile_width // 2 if tile_width % 256 == 0 else size
    per_tile = tile_width // stripe
    blocks = tile_width // size
    depth = s.shape[0]

    def tile(n):
        return jnp.minimum(n // per_tile, ratio - 1)

    def hot_row(h, place, hot):
        return hot[place[0], h]

    def hot_col(h, n, place, hot):
        return hot[place[1] * ratio + tile(n), h]

    def source(q, n, place, sel):
        return q * hot_count + sel[place[1] * ratio + tile(n), q]

    spec = pl.BlockSpec
    each = range(hot_count)
    in_specs = [spec((size, depth), lambda n, place, hot, sel, h=h: (hot_row(h, place, hot), 0)) for h in each]
    in_specs += [spec((size, stripe), lambda n, place, hot, sel, h=h: (hot_row(h, place, hot), n)) for h in each]
    in_specs += [spec((size, 1), lambda n, place, hot, sel, h=h: (hot_row(h, place, hot), 0)) for h in each]
    in_specs += [spec((1, size, size), lambda n, place, hot, sel, h=h, q=q: (source(q, n, place, sel), hot_row(h, place, hot), 0))
                 for h in each for q in range(row_n)]
    in_specs += [
        spec((depth, stripe), lambda n, *_: (0, n)),
        spec((1, stripe, depth), lambda n, *_: (n // per_tile, n % per_tile, 0)),
        spec((1, stripe), lambda n, *_: (0, n)),
        spec((stripe, depth), lambda n, *_: (n % per_tile, 0)),
        spec((stripe, 1), lambda n, *_: (n % per_tile, 0)),
    ]
    in_specs += [spec((1, stripe, size), lambda n, place, hot, sel, q=q: (source(q, n, place, sel), n % per_tile, 0)) for q in range(row_n)]
    in_specs += [spec((depth, size), lambda n, place, hot, sel, h=h: (0, tile(n) * blocks + hot_col(h, n, place, hot))) for h in each]
    in_specs += [spec((1, size, depth), lambda n, place, hot, sel, h=h: (tile(n), hot_col(h, n, place, hot), 0)) for h in each]
    in_specs += [spec((stripe, size), lambda n, place, hot, sel, h=h: (n % per_tile, tile(n) * blocks + hot_col(h, n, place, hot))) for h in each]
    in_specs += [spec((1, size), lambda n, place, hot, sel, h=h: (0, tile(n) * blocks + hot_col(h, n, place, hot))) for h in each]
    args = [wa] * hot_count + [x] * hot_count + [rd] * hot_count + [cols] * (hot_count * row_n)
    args += [s, wb, cd, wa, rd] + [cols] * row_n + [s] * hot_count + [wb] * hot_count + [x] * hot_count + [cd] * hot_count
    grid_spec = pltpu.PrefetchScalarGridSpec(
        num_scalar_prefetch=3,
        grid=(width // stripe,),
        in_specs=in_specs,
        out_specs=[
            spec((hot_count, size, stripe), lambda n, *_: (0, 0, n)),
            spec((hot_count, stripe, size), lambda n, *_: (n // per_tile, n % per_tile, 0)),
        ],
    )
    return pl.pallas_call(
        functools.partial(hot_kernel, row_n, hot_count),
        out_shape=[
            jax.ShapeDtypeStruct((hot_count, size, width), jnp.bfloat16),
            jax.ShapeDtypeStruct((ratio * hot_count, height, size), jnp.bfloat16),
        ],
        grid_spec=grid_spec,
        compiler_params=pltpu.CompilerParams(vmem_limit_bytes=VMEM_LIMIT),
    )(place, hot, sel, *args)


def first_hops(rows, cols, row_n, col_n):
    line, lanes, chips, cores = layout(row_n, col_n)
    upward = [(r, r + lanes) for r in range(row_n - lanes)]
    below = lax.ppermute(rows, "row", upward)
    above = lax.ppermute(rows, "row", [(b, a) for a, b in upward])
    turn = [(c, (c // cores + 1) % chips * cores + c % cores) for c in range(col_n)]
    ahead = [below, above, lax.ppermute(cols, "col", turn)]
    for step in range(1, lanes):
        ahead.append(lax.ppermute(rows, "row", [(r, r // lanes * lanes + (r + step) % lanes) for r in range(row_n)]))
    return ahead


def filter_kernel(source_count, row_chunk, place, sel, wa_ref, s_ref, wb_ref, rd_ref, cd_ref, *refs):
    b_refs = refs[:source_count]
    x_ref, out_ref = refs[source_count:]

    def chunk(i, carry):
        rows = pl.ds(pl.multiple_of(i * row_chunk, row_chunk), row_chunk)
        beta = jnp.concatenate([b[0, rows, :] for b in b_refs], axis=1)
        acc = jnp.dot(wa_ref[rows, :], s_ref[...], preferred_element_type=jnp.float32)
        acc = acc + dot_t(beta, wb_ref[0])
        acc = acc + (rd_ref[rows, :] + cd_ref[...] - center) * x_ref[rows, :]
        out_ref[rows, :] = acc * (1.0 / half_width)
        return carry

    lax.fori_loop(0, x_ref.shape[0] // row_chunk, chunk, 0)


def filter_step(place, sel, wa, s, wb, rd, cd, cols, x, row_n, ratio):
    height, width = x.shape
    size = cols.shape[-1]
    hot_count = cols.shape[0] // row_n
    tile_width = width // ratio
    stripe = next(n for n in (512, 384, 256, size) if tile_width % n == 0)
    per_tile = tile_width // stripe
    row_chunk = height // 2 if height % 256 == 0 else height

    def b_spec(q):
        return pl.BlockSpec(
            (1, height, size),
            lambda n, place, sel: (q * hot_count + sel[place[1] * ratio + jnp.minimum(n // per_tile, ratio - 1), q], 0, 0))

    striped = pl.BlockSpec((height, stripe), lambda n, *_: (0, n))
    in_specs = [
        pl.BlockSpec(wa.shape, lambda n, *_: (0, 0)),
        pl.BlockSpec((s.shape[0], stripe), lambda n, *_: (0, n)),
        pl.BlockSpec((1, stripe, wb.shape[2]), lambda n, *_: (n // per_tile, n % per_tile, 0)),
        pl.BlockSpec((height, 1), lambda n, *_: (0, 0)),
        pl.BlockSpec((1, stripe), lambda n, *_: (0, n)),
    ] + [b_spec(q) for q in range(row_n)] + [striped]
    args = [wa, s, wb, rd, cd] + [cols] * row_n + [x]
    grid_spec = pltpu.PrefetchScalarGridSpec(
        num_scalar_prefetch=2, grid=(width // stripe,), in_specs=in_specs, out_specs=striped)
    return pl.pallas_call(
        functools.partial(filter_kernel, row_n, row_chunk),
        out_shape=jax.ShapeDtypeStruct(x.shape, jnp.float32),
        grid_spec=grid_spec,
        cost_estimate=pl.CostEstimate(
            flops=4 * height * width * s.shape[0], bytes_accessed=4 * 3 * height * width, transcendentals=0),
        compiler_params=pltpu.CompilerParams(vmem_limit_bytes=VMEM_LIMIT),
    )(place, sel, *args)


def body(start_vector, ham_blocks, diagonal, pair_lists, pair_counts, hot_blocks, selection):
    row_n = lax.axis_size("row")
    col_n = lax.axis_size("col")
    ratio = row_n // col_n
    height, width = start_vector.shape
    size = ham_blocks.shape[1]
    place = jnp.stack([lax.axis_index("row"), lax.axis_index("col")]).astype(jnp.int32)
    shape = (height, row_n * size)
    rows, cols = pack(start_vector, place, hot_blocks, row_n, ratio, size)
    s, b, hams, rd, cd = exchange(rows, cols, selection, row_n, col_n, 0, ham=ham_blocks, diagonal=diagonal)
    wa = dense(ham_blocks[None], place, pair_lists, pair_counts, shape, lambda place, i: place[0])[0]
    wb = dense(hams, place, pair_lists, pair_counts, shape, lambda place, i: place[1] * ratio + i)
    rows, cols = hot_step(place, hot_blocks, selection, wa, s, wb, rd, cd, b, start_vector, row_n, ratio)
    ahead = first_hops(rows, cols, row_n, col_n)
    s, _ = lax.optimization_barrier((s, rows))
    first = filter_step(place, selection, wa, s, wb, rd, cd, b, start_vector, row_n, ratio)
    s, acc = exchange(rows, cols, selection, row_n, col_n, 1, ahead=ahead, product=(wa, wb, rd, cd, first, start_vector))
    return (first, last_step(place, acc, wa, s, row_n, col_n))


def solution(mesh):
    in_specs = (P("row", "col"), P("row", None, None), P(), P(), P(), P(), P())
    out_specs = (P("row", "col"), P("row", "col"))
    return jax.shard_map(body, mesh=mesh, in_specs=in_specs, out_specs=out_specs, check_vma=False)
```

```python
import functools

import jax
import jax.numpy as jnp
from jax import lax
from jax.experimental import pallas as pl
from jax.experimental.pallas import tpu as pltpu
from jax.sharding import PartitionSpec as P

center = 0.25
half_width = 2.5
VMEM_LIMIT = 60 * 1024 * 1024
VMEM_MOST = 67043328
MESH = pl.DeviceIdType.MESH


def dense_kernel(tile_of, place, pairs, counts, ham_ref, out_ref, acc):
    tile = tile_of(place, pl.program_id(0))
    size = ham_ref.shape[-1]
    acc[...] = jnp.zeros_like(acc)

    def add(slot, carry):
        source = pl.multiple_of(pairs[0, tile, slot] * size, size)
        target = pl.multiple_of(pairs[1, tile, slot] * size, size)
        acc[pl.ds(target, size), pl.ds(source, size)] += ham_ref[0, pairs[2, tile, slot]].astype(jnp.float32)
        return carry

    lax.fori_loop(0, counts[tile], add, 0)
    out_ref[0] = acc[...].astype(out_ref.dtype)


def dense(hams, place, pairs, counts, shape, tile_of):
    grid_spec = pltpu.PrefetchScalarGridSpec(
        num_scalar_prefetch=3,
        grid=(hams.shape[0],),
        in_specs=[pl.BlockSpec((1,) + hams.shape[1:], lambda i, *_: (i, 0, 0, 0))],
        out_specs=pl.BlockSpec((1,) + shape, lambda i, *_: (i, 0, 0)),
        scratch_shapes=[pltpu.VMEM(shape, jnp.float32)],
    )
    return pl.pallas_call(
        functools.partial(dense_kernel, tile_of),
        out_shape=jax.ShapeDtypeStruct((hams.shape[0],) + shape, jnp.bfloat16),
        grid_spec=grid_spec,
        compiler_params=pltpu.CompilerParams(vmem_limit_bytes=VMEM_LIMIT),
    )(place, pairs, counts, hams)


def dot_t(a, b):
    return lax.dot_general(a, b, (((1,), (1,)), ((), ())), preferred_element_type=jnp.float32)


def pack_kernel(place, hot, xr_ref, xc_ref, rows_ref, cols_ref):
    rows_ref[0] = xr_ref[...].astype(rows_ref.dtype)
    cols_ref[0] = xc_ref[...].astype(cols_ref.dtype)


def pack(x, place, hot, row_count, ratio, size):
    height, width = x.shape
    hot_count = hot.shape[1]
    blocks = width // (ratio * size)
    part = width // ratio

    def row_block(n, place, hot):
        n = jnp.minimum(n, ratio * hot_count - 1)
        return (hot[place[0], n // ratio], n % ratio)

    def col_block(n, place, hot):
        n = jnp.minimum(n, ratio * hot_count - 1)
        tile, which = n // hot_count, n % hot_count
        return (0, tile * blocks + hot[place[1] * ratio + tile, which])

    grid_spec = pltpu.PrefetchScalarGridSpec(
        num_scalar_prefetch=2,
        grid=(ratio * hot_count,),
        in_specs=[pl.BlockSpec((size, part), row_block), pl.BlockSpec((height, size), col_block)],
        out_specs=[
            pl.BlockSpec((1, size, part), lambda n, *_: (n // ratio, 0, n % ratio)),
            pl.BlockSpec((1, height, size), lambda n, *_: (n, 0, 0)),
        ],
    )
    return pl.pallas_call(
        pack_kernel,
        out_shape=[
            jax.ShapeDtypeStruct((hot_count, size, width), jnp.bfloat16),
            jax.ShapeDtypeStruct((ratio * hot_count, height, size), jnp.bfloat16),
        ],
        grid_spec=grid_spec,
    )(place, hot, x, x)


def layout(row_n, col_n):
    line = 1
    while 4 * line * line <= 2 * row_n:
        line *= 2
    cores = 2 if col_n % 2 == 0 else 1
    return line, row_n // line, col_n // cores, cores


class Grid:
    def __init__(self, row_n, col_n):
        self.line, self.lanes, self.chips, self.cores = layout(row_n, col_n)
        self.row_n, self.col_n = row_n, col_n
        row, col = lax.axis_index("row"), lax.axis_index("col")
        self.row, self.col = row, col
        self.at, self.lane = row // self.lanes, lax.rem(row, self.lanes)
        self.chip, self.core = col // self.cores, lax.rem(col, self.cores)

    def on_line(self, at):
        return (at * self.lanes + self.lane, self.col)

    def other_lane(self, step):
        return (self.at * self.lanes + lax.rem(self.lane + step, self.lanes), self.col)

    def other_chip(self, step):
        return (self.row, lax.rem(self.chip + step, self.chips) * self.cores + self.core)

    def other_core(self):
        return (self.row, self.chip * self.cores + lax.rem(self.core + 1, self.cores))


def remote(src, dst, send, recv, device):
    return pltpu.make_async_remote_copy(
        src_ref=src, dst_ref=dst, send_sem=send, recv_sem=recv, device_id=device, device_id_type=MESH)


def greet(g):
    barrier = pltpu.get_barrier_semaphore()
    up, down = g.at + 1 < g.line, g.at > 0

    def hello(device):
        pl.semaphore_signal(barrier, inc=1, device_id=device, device_id_type=MESH)

    @pl.when(up)
    def _():
        hello(g.on_line(g.at + 1))

    @pl.when(down)
    def _():
        hello(g.on_line(g.at - 1))

    for step in range(1, g.lanes):
        hello(g.other_lane(step))
    for step in range(1, g.chips):
        hello(g.other_chip(step))
    fixed = g.lanes - 1 + g.chips - 1
    if g.cores == 2:
        hello(g.other_core())
        fixed += 1
    pl.semaphore_wait(barrier, fixed + up.astype(jnp.int32) + down.astype(jnp.int32))


def got_slots(row_n, col_n):
    _, lanes, _, _ = layout(row_n, col_n)
    ratio = row_n // col_n
    return ratio if lanes > ratio > 1 else 1


def late_slot(at, line):
    return jnp.where(2 * at < line, line - 1, 0)


def exchange_kernel(row_n, col_n, pieces, with_ham, fused, sel, rows_ref, cols_ref, *refs):
    g = Grid(row_n, col_n)
    refs = list(refs)

    def some(count):
        taken = refs[:count]
        del refs[:count]
        return taken

    first_step = 2 if fused else 1
    if fused:
        below_ref, above_ref, chip_ref = some(3)
        side_refs = some(layout(row_n, col_n)[1] - 1)
        wa_hbm, wb_hbm, rd_ref, cd_ref, x_hbm, start_hbm, s_out, acc_out = some(8)
    else:
        ham_ref, diag_ref, s_out, c_out, h_out, rd_out, cd_out = some(7)
    held, lane_buf, turn_buf, s_all, c_all = some(5)
    own_sem, line_recv, up_send, down_send, lane_send, lane_recv = some(6)
    chip_send, chip_recv, core_send, core_recv, turn_send, turn_recv = some(6)
    if fused:
        acc, wa, wb_buf, x_buf, start_buf, via_buf, beta, st_buf, got, side_buf, load_sem, wb_sem, x_sem, start_sem, acc_sem, via_send, via_recv = some(17)
    else:
        ham_buf, far_buf, ham_sem, ham_recv, ham_up, ham_down, ham_lane, far_recv, far_send, far_chip = some(10)
        ham_rows = ham_ref.shape[0] // pieces
    ratio = row_n // col_n
    hot_count, size = rows_ref.shape[0], rows_ref.shape[1]
    height = cols_ref.shape[1]
    width = rows_ref.shape[2]
    piece = size // pieces
    block_n = cols_ref.shape[0]
    line, lanes, at = g.line, g.lanes, g.at

    home = (g.col * ratio) // lanes
    up_ok = (at + 1 < line) & ((home != line - 1) | (at + 1 != line - 1))
    down_ok = (at > 0) & ((home != 0) | (at - 1 != 0))
    deaf = (at == home) & ((at == 0) | (at == line - 1))
    far_base = jnp.where(at == 0, first_step * lanes, 0)
    far_count = (line - first_step) * lanes

    def chip_slot(step):
        return (lax.rem(g.chip - step + g.chips, g.chips) * g.cores + g.core) * block_n

    own_slot = g.col * block_n
    own_chip = g.chip * g.cores * ratio
    take = pltpu.make_async_copy(rows_ref, held.at[at], own_sem.at[0])
    take_cols = pltpu.make_async_copy(cols_ref, c_all.at[pl.ds(own_slot, block_n)], own_sem.at[1])
    take.start()
    take_cols.start()
    if fused:
        take_chip = pltpu.make_async_copy(chip_ref, c_all.at[pl.ds(chip_slot(1), block_n)], own_sem.at[2])
        take_chip.start()

        @pl.when(at > 0)
        def _():
            pltpu.make_async_copy(below_ref, held.at[at - 1], own_sem.at[3]).start()

        @pl.when(at + 1 < line)
        def _():
            pltpu.make_async_copy(above_ref, held.at[at + 1], own_sem.at[4]).start()
    else:
        take_ham = pltpu.make_async_copy(ham_ref, ham_buf, ham_sem.at[0])
        take_ham.start()
    greet(g)

    def chip_copy(step, b):
        return remote(cols_ref.at[b], c_all.at[own_slot + b], chip_send.at[step - 1, b], chip_recv.at[step - 1, b], g.other_chip(step))

    def core_copy(step, b):
        if step == 0:
            src, slot = cols_ref.at[b], own_slot + b
        else:
            slot = chip_slot(step) + b
            src = chip_ref.at[b] if fused and step == 1 else c_all.at[slot]
        return remote(src, c_all.at[slot], core_send.at[step, b], core_recv.at[step, b], g.other_core())

    for b in range(block_n):
        for step in range(first_step, g.chips):
            chip_copy(step, b).start()
    if g.cores == 2:
        for step in range(first_step):
            for b in range(block_n):
                core_copy(step, b).start()
    take.wait()
    if fused:
        @pl.when(at > 0)
        def _():
            pltpu.make_async_copy(below_ref, held.at[at - 1], own_sem.at[3]).wait()

        @pl.when(at + 1 < line)
        def _():
            pltpu.make_async_copy(above_ref, held.at[at + 1], own_sem.at[4]).wait()

    def part(slot, p):
        return held.at[slot, :, pl.ds(pl.multiple_of(p * piece, piece), piece), :]

    def up_copy(slot, p):
        return remote(part(slot, p), part(slot, p), up_send.at[slot, p], line_recv.at[slot, p], g.on_line(at + 1))

    def down_copy(slot, p):
        return remote(part(slot, p), part(slot, p), down_send.at[slot, p], line_recv.at[slot, p], g.on_line(at - 1))

    def s_rows(source, p):
        return pl.ds(pl.multiple_of(source * size + p * piece, piece), piece)

    def lane_copy(step, slot, p):
        rows = pl.ds(pl.multiple_of(p * piece, piece), piece)
        return remote(
            lane_buf.at[step - 1, slot, rows, :], s_all.at[s_rows(slot * lanes + g.lane, p), :],
            lane_send.at[step - 1, slot, p], lane_recv.at[step - 1, slot, p], g.other_lane(step))

    def lane_came(step, slot, p):
        rows = pl.ds(pl.multiple_of(p * piece, piece), piece)
        came = slot * lanes + lax.rem(g.lane - step + lanes, lanes)
        return remote(
            lane_buf.at[step - 1, slot, rows, :], s_all.at[s_rows(came, p), :],
            lane_send.at[step - 1, slot, p], lane_recv.at[step - 1, slot, p], g.other_lane(step))

    def pick(target, source, blocks):
        which = sel[target, source]
        value = blocks[0]
        for h in range(1, hot_count):
            value = jnp.where(which == h, blocks[h], value)
        return value

    def select(slot, p):
        source = slot * lanes + g.lane
        rows = pl.ds(pl.multiple_of(p * piece, piece), piece)
        blocks = [held[slot, h, rows, :] for h in range(hot_count)]

        @pl.when((slot != at) | (not fused))
        def _():
            for step in range(1, lanes):
                target = at * lanes + lax.rem(g.lane + step, lanes)
                lane_buf[step - 1, slot, rows, :] = pick(target, source, blocks)
                lane_copy(step, slot, p).start()

        s_all[s_rows(source, p), :] = pick(g.row, source, blocks)

    def tile_place(col, i):
        tile = col * ratio + i
        return tile // lanes, lax.rem(tile, lanes)

    detour = g.chips % 2 == 0 and g.chips > 1
    across = g.chips // 2
    end = jnp.where(2 * home < line, line - 1, 0)
    if not fused:
        def ham_part(ref, p):
            return ref.at[pl.ds(pl.multiple_of(p * ham_rows, ham_rows), ham_rows)]

        def ham_copies(i, p):
            here = ham_part(h_out.at[i], p)
            up = remote(here, here, ham_up.at[i, p], ham_recv.at[i, p], g.on_line(at + 1))
            down = remote(here, here, ham_down.at[i, p], ham_recv.at[i, p], g.on_line(at - 1))
            over = [remote(here, here, ham_lane.at[i, step - 1, p], ham_recv.at[i, p], g.other_lane(step))
                    for step in range(1, lanes)]
            return up, down, over

        def ham_sends(i, p, act):
            _, home_lane = tile_place(g.col, i)
            up, down, over = ham_copies(i, p)
            skip = end if detour else line

            @pl.when(home_lane == g.lane)
            def _():
                @pl.when((at >= home) & (at + 1 < line) & (at + 1 != skip))
                def _():
                    act(up)

                @pl.when((at <= home) & (at > 0) & (at - 1 != skip))
                def _():
                    act(down)

                for copy in over:
                    act(copy)

        if detour:
            far_col = lax.rem(g.chip + across, g.chips) * g.cores + g.core
            far_home = (far_col * ratio) // lanes
            far_end = jnp.where(2 * far_home < line, line - 1, 0)
            rising = far_end > far_home
            far_away = jnp.where(rising, at - far_home, far_home - at)

            def far_copies(i, p):
                here = ham_part(far_buf, p)
                way = jnp.where(rising, at + 1, at - 1)
                on = remote(here, here, far_send.at[p], far_recv.at[p], g.on_line(way))
                chip = remote(here, ham_part(h_out.at[i], p), far_chip.at[p], ham_recv.at[i, p], g.other_chip(across))
                return on, chip

            def far_sends(i, p, act):
                _, far_lane = tile_place(far_col, i)
                on, chip = far_copies(i, p)

                @pl.when((far_lane == g.lane) & (far_away >= 0))
                def _():
                    @pl.when(at != far_end)
                    def _():
                        act(on)

                    @pl.when(at == far_end)
                    def _():
                        act(chip)

        take_ham.wait()
        for i in range(ratio):
            _, home_lane = tile_place(g.col, i)

            @pl.when((home == at) & (home_lane == g.lane))
            def _():
                put = pltpu.make_async_copy(ham_buf, h_out.at[i], ham_sem.at[0])
                put.start()
                put.wait()

            if detour:
                _, far_lane = tile_place(far_col, i)

                @pl.when((far_home == at) & (far_lane == g.lane))
                def _():
                    put = pltpu.make_async_copy(ham_ref, far_buf, ham_sem.at[0])
                    put.start()
                    put.wait()

        def near_step(s, p):
            for i in range(ratio):
                _, home_lane = tile_place(g.col, i)
                away = jnp.where(at >= home, at - home, home - at)

                @pl.when((home_lane == g.lane) & (away == s))
                def _():
                    if s > 0:
                        ham_copies(i, p)[0].wait_recv()

                    ham_sends(i, p, lambda copy: copy.start())

        def far_step(s, p):
            for i in range(ratio if detour else 0):
                _, far_lane = tile_place(far_col, i)

                @pl.when((far_lane == g.lane) & (far_away == s))
                def _():
                    if s > 0:
                        far_copies(i, p)[0].wait_recv()

                    far_sends(i, p, lambda copy: copy.start())

        def far_steps(s):
            def one(p, carry):
                far_step(s, p)
                return carry

            lax.fori_loop(0, pieces, one, 0)

        if detour:
            held_back = (far_away > 0) & (at != far_end)
            up_first = (held_back & rising) == False
            down_first = (held_back & (rising == False)) == False
        else:
            up_first = down_first = at >= 0

        def ham_start(p, carry):
            near_step(0, p)
            far_step(0, p)
            return carry

        def ham_next(p, carry):
            near_step(1, p)
            far_step(1, p)
            return carry

        lax.fori_loop(0, pieces, ham_start, 0)

    if fused and detour and line > 2:
        climbs = end > home
        before = jnp.where(climbs, end - 1, end + 1)
        via_slot = jnp.where(climbs, end - 2, end + 2)
        leaves = at == before
        far_col = lax.rem(g.chip + across, g.chips) * g.cores + g.core
        far_home = (far_col * ratio) // lanes
        far_end = jnp.where(2 * far_home < line, line - 1, 0)
        far_before = jnp.where(far_end > far_home, far_end - 1, far_end + 1)
        far_slot = jnp.where(far_end > far_home, far_end - 2, far_end + 2)
        kept = pieces * 3 // 4

        def via_leave(p):
            return remote(part(via_slot, p), via_buf.at[p - kept], via_send.at[0, p - kept], via_recv.at[0, p - kept], g.other_chip(across))

        def via_pass(p):
            return remote(via_buf.at[p - kept], via_buf.at[p - kept], via_send.at[1, p - kept], via_recv.at[1, p - kept], g.on_line(far_end))

        def via_land(p):
            return remote(via_buf.at[p - kept], part(far_slot, p), via_send.at[2, p - kept], line_recv.at[far_slot, p], g.other_chip(across))

        def via_came(stage, p):
            there = g.other_chip(across) if stage == 0 else g.on_line(far_before)
            return remote(via_buf.at[p - kept], via_buf.at[p - kept], via_send.at[stage, p - kept], via_recv.at[stage, p - kept], there)

        def via_up(slot, p):
            return ((leaves & climbs & (slot == via_slot)) == False) | (p < kept)

        def via_down(slot, p):
            return ((leaves & (climbs == False) & (slot == via_slot)) == False) | (p < kept)
    else:
        leaves = None
        via_up = via_down = lambda slot, p: p >= 0

    half = pieces * (line // 2)

    def hears(s):
        quiet = (s == 0) | (deaf == False)
        return (at - s >= 0) & quiet, (at + s < line) & quiet

    if fused:
        up_first = down_first = at >= 0

    def relay(n, carry):
        s, p = n // pieces, lax.rem(n, pieces)
        hears_below, hears_above = hears(s)

        @pl.when(hears_below)
        def _():
            @pl.when(s >= first_step)
            def _():
                up_copy(at - s, p).wait_recv()

            @pl.when(up_ok & (s >= first_step - 1) & via_up(at - s, p) & ((s > 0) | up_first))
            def _():
                up_copy(at - s, p).start()

        @pl.when(hears_above)
        def _():
            @pl.when(s >= first_step)
            def _():
                down_copy(at + s, p).wait_recv()

            @pl.when(down_ok & (s >= first_step - 1) & via_down(at + s, p) & ((s > 0) | down_first))
            def _():
                down_copy(at + s, p).start()
        return carry

    def digest(n, carry):
        s, p = n // pieces, lax.rem(n, pieces)
        hears_below = (at - s >= 0) & ((s < first_step) | (deaf == False))
        hears_above = (at + s < line) & ((s < first_step) | (deaf == False))

        @pl.when(hears_below)
        def _():
            select(at - s, p)

        @pl.when(hears_above & (s > 0))
        def _():
            select(at + s, p)
        return carry

    def advance(n, carry):
        relay(n, carry)
        if not fused:
            @pl.when((n >= half) & (n < half + pieces))
            def _():
                for s in range(2, line):
                    near_step(s, n - half)
        return digest(n, carry)

    def core_came(step, b):
        other = lax.rem(g.core + 1, g.cores)
        slot = (lax.rem(g.chip - step + g.chips, g.chips) * g.cores + other) * block_n + b
        return remote(cols_ref.at[b], c_all.at[slot], core_send.at[step, b], core_recv.at[step, b], g.other_core())

    def got_at(i):
        return i if got_slots(row_n, col_n) > 1 else 0

    def turn_copy(i, step, q):
        if fused:
            there = got.at[got_at(i), q]
        else:
            there = s_all.at[pl.ds(pl.multiple_of(q * size, size), size), i * height:(i + 1) * height]
        return remote(turn_buf.at[step - 1, q], there, turn_send.at[step - 1, q], turn_recv.at[i, q], g.other_lane(step))

    def turn(q):
        rows = pl.ds(pl.multiple_of(q * size, size), size)
        for i in range(ratio):
            _, home_lane = tile_place(g.col, i)

            @pl.when(home_lane == g.lane)
            def _():
                for k in range(height // size):
                    strip = slice(k * size, (k + 1) * size)
                    blocks = [c_all[q * hot_count + h, strip, :] for h in range(hot_count)]
                    for step in range(1, lanes):
                        target = at * lanes + lax.rem(g.lane + step, lanes)
                        value = pick(target, q, blocks)
                        if fused:
                            turn_buf[step - 1, q, strip, :] = value
                        else:
                            turn_buf[step - 1, q, :, strip] = value.astype(jnp.float32).T.astype(turn_buf.dtype)
                    if not fused:
                        s_all[rows, i * height + k * size:i * height + (k + 1) * size] = pick(g.row, q, blocks).astype(jnp.float32).T.astype(s_all.dtype)
                for step in range(1, lanes):
                    turn_copy(i, step, q).start()

    def turns(act):
        def one(q, carry):
            for i in range(ratio):
                _, home_lane = tile_place(g.col, i)
                act(i, q, home_lane)
            return carry

        lax.fori_loop(far_base, far_base + far_count, one, 0)

    def turn_came(i, q, home_lane):
        @pl.when(home_lane != g.lane)
        def _():
            turn_copy(i, 1, q).wait_recv()

    def turn_sent(i, q, home_lane):
        @pl.when(home_lane == g.lane)
        def _():
            for step in range(1, lanes):
                turn_copy(i, step, q).wait_send()

    if fused:
        stripe = x_buf.shape[2]
        stripes = width // stripe
        per_tile = height // stripe
        rows_at_once = height // 2
        share = -(-stripes // pieces)
        late = late_slot(at, line)
        take_wa = pltpu.make_async_copy(wa_hbm, wa, load_sem.at[0])
        early = line - 1
        first_early = jnp.where(late == 0, 1, 0)
        depth = pl.ds(pl.multiple_of(first_early * lanes * size, lanes * size), early * lanes * size)

        def band(n):
            return pl.ds(pl.multiple_of(n * stripe, stripe), stripe)

        def loads(n):
            turn_n = lax.rem(n, 2)
            return [
                pltpu.make_async_copy(x_hbm.at[:, band(n)], x_buf.at[turn_n], x_sem.at[turn_n]),
                pltpu.make_async_copy(start_hbm.at[:, band(n)], start_buf.at[turn_n], start_sem.at[turn_n]),
                pltpu.make_async_copy(wb_hbm.at[n // per_tile, band(lax.rem(n, per_tile)), :], wb_buf.at[turn_n], wb_sem.at[turn_n]),
            ]

        def acc_copy(n):
            return pltpu.make_async_copy(acc.at[:, band(n)], acc_out.at[:, band(n)], acc_sem.at[n])

        def beta_side(n, carry):
            tile, turn_n = n // per_tile, lax.rem(n, 2)

            @pl.when(n + 1 < stripes)
            def _():
                for copy in loads(n + 1):
                    copy.start()

            @pl.when(lax.rem(n, per_tile) == 0)
            def _():
                for q in range(row_n):
                    beta[:, q * size:(q + 1) * size] = c_all[q * hot_count + sel[g.col * ratio + tile, q]]

            for copy in loads(n):
                copy.wait()
            for k in range(2):
                rows = slice(k * rows_at_once, (k + 1) * rows_at_once)
                value = dot_t(beta[rows, :], wb_buf[turn_n])
                value = value + (rd_ref[rows, :] + cd_ref[:, band(n)] - center) * x_buf[turn_n, rows, :]
                acc[rows, band(n)] = value - start_buf[turn_n, rows, :] * (half_width / 2.0)
            return carry

        near_base = jnp.where(at == 0, 0, (line - 2) * lanes * size)
        near_depth = pl.ds(pl.multiple_of(near_base, lanes * size), 2 * lanes * size)
        far_depth = pl.ds(pl.multiple_of(far_base * size, lanes * size), far_count * size)

        def alpha_side(m, carry):
            n = jnp.where(deaf, lax.rem(m + g.lane * per_tile, stripes), m)
            tile, inner = n // per_tile, lax.rem(n, per_tile)

            @pl.when(deaf == False)
            def _():
                for k in range(2):
                    rows = slice(k * rows_at_once, (k + 1) * rows_at_once)
                    acc[rows, band(n)] += jnp.dot(wa[rows, depth], s_all[depth, band(n)], preferred_element_type=jnp.float32)

            @pl.when(deaf)
            def _():
                _, home_lane = tile_place(g.col, tile)

                @pl.when(home_lane == g.lane)
                def _():
                    for j in range(far_count):
                        q = far_base + j
                        st_buf[:, j * size:(j + 1) * size] = c_all[q * hot_count + sel[g.row, q], band(inner), :]

                @pl.when(home_lane != g.lane)
                def _():
                    @pl.when(inner == 0)
                    def _():
                        def come(q, carry):
                            turn_copy(tile, 1, q).wait_recv()
                            return carry

                        lax.fori_loop(far_base, far_base + far_count, come, 0)

                    for j in range(far_count):
                        st_buf[:, j * size:(j + 1) * size] = got[got_at(tile), far_base + j, band(inner), :]

                for k in range(2):
                    rows = slice(k * rows_at_once, (k + 1) * rows_at_once)
                    value = jnp.dot(wa[rows, near_depth], s_all[near_depth, band(n)], preferred_element_type=jnp.float32)
                    acc[rows, band(n)] += value + dot_t(wa[rows, far_depth], st_buf[...])
            acc_copy(n).start()
            return carry

        def some_stripes(work, turn_n, share=share):
            lax.fori_loop(turn_n * share, jnp.minimum(turn_n * share + share, stripes), work, 0)

    if fused:
        if leaves is not None:
            @pl.when(leaves)
            def _():
                for p in range(kept, pieces):
                    via_leave(p).start()

        lax.fori_loop(pieces, half, relay, 0)
        take_sides = [pltpu.make_async_copy(side, side_buf.at[step], load_sem.at[1 + step]) for step, side in enumerate(side_refs)]
        for copy in take_sides:
            copy.start()
        lax.fori_loop(pieces, half, digest, 0)
        take_wa.start()
        for copy in loads(0):
            copy.start()
        lax.fori_loop(0, pieces, digest, 0)
        for copy in take_sides:
            copy.wait()

        def sides(p, carry):
            rows = pl.ds(pl.multiple_of(p * piece, piece), piece)
            for step in range(1, lanes):
                source = at * lanes + lax.rem(g.lane - step + lanes, lanes)
                blocks = [side_buf[step - 1, h, rows, :] for h in range(hot_count)]
                s_all[s_rows(source, p), :] = pick(g.row, source, blocks)
            return carry

        lax.fori_loop(0, pieces, sides, 0)
    else:
        def held_rows(p, carry):
            @pl.when(up_ok & (up_first == False))
            def _():
                up_copy(at, p).start()

            @pl.when(down_ok & (down_first == False))
            def _():
                down_copy(at, p).start()
            return carry

        lax.fori_loop(0, pieces, relay, 0)
        lax.fori_loop(0, pieces, digest, 0)
        take_cols.wait()
        if g.cores == 2:
            for b in range(block_n):
                core_came(0, b).wait_recv()

        @pl.when(deaf)
        def _():
            def turn_early(q, carry):
                @pl.when(q // lanes != at)
                def _():
                    turn(q)
                return carry

            lax.fori_loop(own_chip, own_chip + g.cores * ratio, turn_early, 0)

        lax.fori_loop(0, pieces, ham_next, 0)
        for s in range(2, line):
            far_steps(s)
        lax.fori_loop(0, pieces, held_rows, 0)
        lax.fori_loop(pieces, half, advance, 0)
    for step in range(first_step, g.chips):
        for b in range(block_n):
            slot = chip_slot(step) + b
            remote(cols_ref.at[b], c_all.at[slot], chip_send.at[step - 1, b], chip_recv.at[step - 1, b], g.other_chip(step)).wait_recv()
            if g.cores == 2:
                core_copy(step, b).start()

    if fused:
        take_cols.wait()
        take_chip.wait()
    if g.cores == 2:
        for step in range(0 if fused else 1, g.chips):
            for b in range(block_n):
                core_came(step, b).wait_recv()
    if not fused:
        @pl.when(deaf)
        def _():
            def turn_rest(q, carry):
                @pl.when(q // (g.cores * ratio) != g.chip)
                def _():
                    turn(q)
                return carry

            lax.fori_loop(far_base, far_base + far_count, turn_rest, 0)

        cd_out[...] = diag_ref[:, pl.ds(pl.multiple_of(g.col * width, width), width)]
        for k in range(height // size):
            strip = diag_ref[:, pl.ds(pl.multiple_of(g.row * height + k * size, size), size)]
            rd_out[k * size:(k + 1) * size, :] = jnp.broadcast_to(strip, (size, size)).T[:, :1]
        put_cols = pltpu.make_async_copy(c_all, c_out, own_sem.at[2])
        put_cols.start()
    else:
        take_wa.wait()

        @pl.when(deaf)
        def _():
            def turn_on(q, carry):
                turn(q)
                return carry

            lax.fori_loop(far_base, far_base + far_count, turn_on, 0)

    def middle(n, carry):
        if fused:
            some_stripes(beta_side, n - half)
        if leaves is not None:
            via_p = kept + jnp.minimum(n - half, pieces - kept - 1)

            @pl.when((n < half + pieces - kept) & (at == far_before))
            def _():
                p = via_p
                via_came(0, p).wait_recv()
                via_pass(p).start()

            @pl.when((n < half + pieces - kept) & (at == far_end))
            def _():
                p = via_p
                via_came(1, p).wait_recv()
                via_land(p).start()

        return advance(n, carry)

    def lanes_came(slot):
        def one(p, carry):
            for step in range(1, lanes):
                lane_came(step, slot, p).wait_recv()
            return carry

        near = (slot - at < first_step) & (at - slot < first_step)
        away = slot != at if fused else True

        @pl.when(((deaf == False) | near) & away)
        def _():
            lax.fori_loop(0, pieces, one, 0)

    lax.fori_loop(half, half + pieces, middle, 0)
    if fused:
        for other in range(1, line):
            lanes_came(lax.rem(late + other, line))

        def ending(turn_n, carry):
            for u in range(2):
                advance(half + pieces + 2 * turn_n + u, carry)
            some_stripes(alpha_side, turn_n, -(-stripes // (pieces // 2)))
            return carry

        lax.fori_loop(0, (pieces * line - half - pieces) // 2, ending, 0)
        lanes_came(late)

        @pl.when(deaf)
        def _():
            s_all[pl.ds(pl.multiple_of(late * lanes * size, size), lanes * size), :] = jnp.zeros((lanes * size, width), s_all.dtype)

        put_s = pltpu.make_async_copy(s_all.at[pl.ds(pl.multiple_of(late * lanes * size, size), lanes * size), :], s_out, own_sem.at[5])
        put_s.start()
        put_s.wait()
        for n in range(stripes):
            acc_copy(n).wait()
    else:
        lax.fori_loop(half + pieces, pieces * line, advance, 0)
        for slot in range(line):
            lanes_came(slot)

        @pl.when(deaf)
        def _():
            turns(turn_came)

        put_s = pltpu.make_async_copy(s_all, s_out, own_sem.at[5])
        put_s.start()
        put_s.wait()
        put_cols.wait()

    @pl.when(deaf)
    def _():
        turns(turn_sent)

    def finish(n, carry):
        slot, p = n // pieces, lax.rem(n, pieces)

        @pl.when((slot <= at + 1 - first_step) & up_ok & via_up(slot, p))
        def _():
            up_copy(slot, p).wait_send()

        @pl.when((slot >= at - 1 + first_step) & down_ok & via_down(slot, p))
        def _():
            down_copy(slot, p).wait_send()

        near = (slot - at < first_step) & (at - slot < first_step)
        away = slot != at if fused else True

        @pl.when(((deaf == False) | near) & away)
        def _():
            for step in range(1, lanes):
                lane_copy(step, slot, p).wait_send()
        return carry

    lax.fori_loop(0, line * pieces, finish, 0)
    if leaves is not None:
        for p in range(kept, pieces):
            @pl.when(leaves)
            def _():
                via_leave(p).wait_send()

            @pl.when(at == far_before)
            def _():
                via_pass(p).wait_send()

            @pl.when(at == far_end)
            def _():
                via_land(p).wait_send()
    for b in range(block_n):
        for step in range(first_step, g.chips):
            chip_copy(step, b).wait_send()
        if g.cores == 2:
            for step in range(g.chips):
                core_copy(step, b).wait_send()
    if not fused:
        for i in range(ratio):
            _, home_lane = tile_place(g.col, i)

            def settle(p, carry):
                ham_sends(i, p, lambda copy: copy.wait_send())
                if detour:
                    far_sends(i, p, lambda copy: copy.wait_send())

                @pl.when(home_lane != g.lane)
                def _():
                    ham_copies(i, p)[2][0].wait_recv()
                return carry

            lax.fori_loop(0, pieces, settle, 0)


def exchange(rows, cols, sel, row_n, col_n, ident, ham=None, diagonal=None, ahead=None, product=None):
    hot_count, size, width = rows.shape
    block_n, height = cols.shape[:2]
    ratio = row_n // col_n
    pieces = 8
    fused = product is not None
    line, lanes, chips, _ = layout(row_n, col_n)
    others = max(lanes - 1, 1)
    dma = pltpu.SemaphoreType.DMA
    vmem = lambda *shape: pltpu.VMEM(shape, jnp.bfloat16)
    anywhere = pl.BlockSpec(memory_space=pl.ANY)
    whole = pl.BlockSpec(memory_space=pltpu.VMEM)
    scratch = [
        vmem(line, hot_count, size, width),
        vmem(others, line, size, width),
        vmem(others, row_n, *((height, size) if fused else (size, height))),
        vmem(row_n * size, width),
        vmem(col_n * block_n, height, size),
        dma((6,)),
        dma((line, pieces)),
        dma((line, pieces)),
        dma((line, pieces)),
        dma((others, line, pieces)),
        dma((others, line, pieces)),
        dma((max(chips - 1, 1), block_n)),
        dma((max(chips - 1, 1), block_n)),
        dma((chips, block_n)),
        dma((chips, block_n)),
        dma((others, row_n)),
        dma((ratio, row_n)),
    ]
    args = [sel, rows, cols]
    in_specs = [pl.BlockSpec(memory_space=pltpu.SMEM), anywhere, anywhere]
    if fused:
        wa, wb, rd, cd, x, start = product
        stripe = 256 if height % 256 == 0 else size
        args += list(ahead) + [wa, wb, rd, cd, x, start]
        in_specs += [anywhere] * (len(ahead) + 2) + [whole] * 2 + [anywhere] * 2
        out_shape = [
            jax.ShapeDtypeStruct((lanes * size, width), jnp.bfloat16),
            jax.ShapeDtypeStruct((height, width), jnp.float32),
        ]
        out_specs = [anywhere] * 2
        scratch += [
            pltpu.VMEM((height, width), jnp.float32),
            vmem(*wa.shape),
            vmem(2, stripe, wb.shape[2]),
            pltpu.VMEM((2, height, stripe), jnp.float32),
            pltpu.VMEM((2, height, stripe), jnp.float32),
            vmem(pieces - pieces * 3 // 4, hot_count, size // pieces, width),
            vmem(height, row_n * size),
            vmem(stripe, (line - 2) * lanes * size),
            vmem(got_slots(row_n, col_n), row_n, height, size),
            vmem(others, hot_count, size, width),
            dma((1 + others,)),
            dma((2,)),
            dma((2,)),
            dma((2,)),
            dma((width // stripe,)),
            dma((3, pieces)),
            dma((3, pieces)),
        ]
    else:
        args += [ham, diagonal[None, :]]
        in_specs += [anywhere, whole]
        out_shape = [
            jax.ShapeDtypeStruct((row_n * size, width), jnp.bfloat16),
            jax.ShapeDtypeStruct((col_n * block_n, height, size), jnp.bfloat16),
            jax.ShapeDtypeStruct((ratio,) + ham.shape, ham.dtype),
            jax.ShapeDtypeStruct((height, 1), jnp.float32),
            jax.ShapeDtypeStruct((1, width), jnp.float32),
        ]
        out_specs = [anywhere] * 3 + [whole] * 2
        scratch += [
            pltpu.VMEM(ham.shape, ham.dtype),
            pltpu.VMEM(ham.shape, ham.dtype),
            dma((1,)),
            dma((ratio, pieces)),
            dma((ratio, pieces)),
            dma((ratio, pieces)),
            dma((ratio, others, pieces)),
            dma((pieces,)),
            dma((pieces,)),
            dma((pieces,)),
        ]
    return pl.pallas_call(
        functools.partial(exchange_kernel, row_n, col_n, pieces, ham is not None, fused),
        out_shape=out_shape,
        in_specs=in_specs,
        out_specs=out_specs,
        scratch_shapes=scratch,
        compiler_params=pltpu.CompilerParams(collective_id=ident, has_side_effects=True, vmem_limit_bytes=VMEM_MOST),
    )(*args)


def last_kernel(place, acc_ref, wa_ref, s_ref, out_ref):
    acc = acc_ref[...] + jnp.dot(wa_ref[...], s_ref[...], preferred_element_type=jnp.float32)
    out_ref[...] = acc * (2.0 / half_width)


def last_step(place, acc, wa, s, row_n, col_n):
    height, width = acc.shape
    depth = s.shape[0]
    line, lanes, _, _ = layout(row_n, col_n)
    stripe = next(n for n in (512, 384, 256, width) if width % n == 0)
    grid_spec = pltpu.PrefetchScalarGridSpec(
        num_scalar_prefetch=1,
        grid=(width // stripe,),
        in_specs=[
            pl.BlockSpec((height, stripe), lambda n, place: (0, n)),
            pl.BlockSpec((height, depth), lambda n, place: (0, late_slot(place[0] // lanes, line))),
            pl.BlockSpec((depth, stripe), lambda n, place: (0, n)),
        ],
        out_specs=pl.BlockSpec((height, stripe), lambda n, place: (0, n)),
    )
    return pl.pallas_call(
        last_kernel,
        out_shape=jax.ShapeDtypeStruct(acc.shape, jnp.float32),
        grid_spec=grid_spec,
        compiler_params=pltpu.CompilerParams(vmem_limit_bytes=VMEM_LIMIT),
    )(place, acc, wa, s)


def hot_kernel(row_n, hot_count, place, hot, sel, *refs):
    refs = list(refs)

    def some(count):
        taken = refs[:count]
        del refs[:count]
        return taken

    wide = lambda blocks: jnp.concatenate(blocks, axis=1)
    wa_hot, x_rows, rd_hot = some(hot_count), some(hot_count), some(hot_count)
    b_hot = [some(row_n) for _ in range(hot_count)]
    s_ref, wb_ref, cd_ref = some(3)
    wa_ref, rd_ref = some(2)
    b_refs = some(row_n)
    s_hot, wb_hot, x_cols, cd_hot = some(hot_count), some(hot_count), some(hot_count), some(hot_count)
    rows_ref, cols_ref = refs
    scale = 1.0 / half_width

    def dot(a, b):
        return jnp.dot(a, b, preferred_element_type=jnp.float32)

    size = rows_ref.shape[1]
    acc = dot(jnp.concatenate([w[...] for w in wa_hot], axis=0), s_ref[...])
    beta = jnp.concatenate([wide([b[0] for b in blocks]) for blocks in b_hot], axis=0)
    acc = acc + dot_t(beta, wb_ref[0])
    for h in range(hot_count):
        value = acc[h * size:(h + 1) * size] + (rd_hot[h][...] + cd_ref[...] - center) * x_rows[h][...]
        rows_ref[h] = (value * scale).astype(rows_ref.dtype)
    acc = dot(wa_ref[...], wide([s[...] for s in s_hot]))
    acc = acc + dot_t(wide([b[0] for b in b_refs]), jnp.concatenate([w[0] for w in wb_hot], axis=0))
    for h in range(hot_count):
        value = acc[:, h * size:(h + 1) * size] + (rd_ref[...] + cd_hot[h][...] - center) * x_cols[h][...]
        cols_ref[h] = (value * scale).astype(cols_ref.dtype)


def hot_step(place, hot, sel, wa, s, wb, rd, cd, cols, x, row_n, ratio):
    height, width = x.shape
    size = cols.shape[-1]
    hot_count = hot.shape[1]
    tile_width = width // ratio
    stripe = tile_width
    per_tile = tile_width // stripe
    blocks = tile_width // size
    depth = s.shape[0]

    def tile(n):
        return jnp.minimum(n // per_tile, ratio - 1)

    def hot_row(h, place, hot):
        return hot[place[0], h]

    def hot_col(h, n, place, hot):
        return hot[place[1] * ratio + tile(n), h]

    def source(q, n, place, sel):
        return q * hot_count + sel[place[1] * ratio + tile(n), q]

    spec = pl.BlockSpec
    each = range(hot_count)
    in_specs = [spec((size, depth), lambda n, place, hot, sel, h=h: (hot_row(h, place, hot), 0)) for h in each]
    in_specs += [spec((size, stripe), lambda n, place, hot, sel, h=h: (hot_row(h, place, hot), n)) for h in each]
    in_specs += [spec((size, 1), lambda n, place, hot, sel, h=h: (hot_row(h, place, hot), 0)) for h in each]
    in_specs += [spec((1, size, size), lambda n, place, hot, sel, h=h, q=q: (source(q, n, place, sel), hot_row(h, place, hot), 0))
                 for h in each for q in range(row_n)]
    in_specs += [
        spec((depth, stripe), lambda n, *_: (0, n)),
        spec((1, stripe, depth), lambda n, *_: (n // per_tile, n % per_tile, 0)),
        spec((1, stripe), lambda n, *_: (0, n)),
        spec((stripe, depth), lambda n, *_: (n % per_tile, 0)),
        spec((stripe, 1), lambda n, *_: (n % per_tile, 0)),
    ]
    in_specs += [spec((1, stripe, size), lambda n, place, hot, sel, q=q: (source(q, n, place, sel), n % per_tile, 0)) for q in range(row_n)]
    in_specs += [spec((depth, size), lambda n, place, hot, sel, h=h: (0, tile(n) * blocks + hot_col(h, n, place, hot))) for h in each]
    in_specs += [spec((1, size, depth), lambda n, place, hot, sel, h=h: (tile(n), hot_col(h, n, place, hot), 0)) for h in each]
    in_specs += [spec((stripe, size), lambda n, place, hot, sel, h=h: (n % per_tile, tile(n) * blocks + hot_col(h, n, place, hot))) for h in each]
    in_specs += [spec((1, size), lambda n, place, hot, sel, h=h: (0, tile(n) * blocks + hot_col(h, n, place, hot))) for h in each]
    args = [wa] * hot_count + [x] * hot_count + [rd] * hot_count + [cols] * (hot_count * row_n)
    args += [s, wb, cd, wa, rd] + [cols] * row_n + [s] * hot_count + [wb] * hot_count + [x] * hot_count + [cd] * hot_count
    grid_spec = pltpu.PrefetchScalarGridSpec(
        num_scalar_prefetch=3,
        grid=(width // stripe,),
        in_specs=in_specs,
        out_specs=[
            spec((hot_count, size, stripe), lambda n, *_: (0, 0, n)),
            spec((hot_count, stripe, size), lambda n, *_: (n // per_tile, n % per_tile, 0)),
        ],
    )
    return pl.pallas_call(
        functools.partial(hot_kernel, row_n, hot_count),
        out_shape=[
            jax.ShapeDtypeStruct((hot_count, size, width), jnp.bfloat16),
            jax.ShapeDtypeStruct((ratio * hot_count, height, size), jnp.bfloat16),
        ],
        grid_spec=grid_spec,
        compiler_params=pltpu.CompilerParams(vmem_limit_bytes=VMEM_LIMIT),
    )(place, hot, sel, *args)


def first_hops(rows, cols, row_n, col_n):
    line, lanes, chips, cores = layout(row_n, col_n)
    upward = [(r, r + lanes) for r in range(row_n - lanes)]
    below = lax.ppermute(rows, "row", upward)
    above = lax.ppermute(rows, "row", [(b, a) for a, b in upward])
    turn = [(c, (c // cores + 1) % chips * cores + c % cores) for c in range(col_n)]
    ahead = [below, above, lax.ppermute(cols, "col", turn)]
    for step in range(1, lanes):
        ahead.append(lax.ppermute(rows, "row", [(r, r // lanes * lanes + (r + step) % lanes) for r in range(row_n)]))
    return ahead


def filter_kernel(source_count, row_chunk, place, sel, wa_ref, s_ref, wb_ref, rd_ref, cd_ref, *refs):
    b_refs = refs[:source_count]
    x_ref, out_ref = refs[source_count:]

    def chunk(i, carry):
        rows = pl.ds(pl.multiple_of(i * row_chunk, row_chunk), row_chunk)
        beta = jnp.concatenate([b[0, rows, :] for b in b_refs], axis=1)
        acc = jnp.dot(wa_ref[rows, :], s_ref[...], preferred_element_type=jnp.float32)
        acc = acc + dot_t(beta, wb_ref[0])
        acc = acc + (rd_ref[rows, :] + cd_ref[...] - center) * x_ref[rows, :]
        out_ref[rows, :] = acc * (1.0 / half_width)
        return carry

    lax.fori_loop(0, x_ref.shape[0] // row_chunk, chunk, 0)


def filter_step(place, sel, wa, s, wb, rd, cd, cols, x, row_n, ratio):
    height, width = x.shape
    size = cols.shape[-1]
    hot_count = cols.shape[0] // row_n
    tile_width = width // ratio
    stripe = next(n for n in (512, 384, 256, size) if tile_width % n == 0)
    per_tile = tile_width // stripe
    row_chunk = height // 2 if height % 256 == 0 else height

    def b_spec(q):
        return pl.BlockSpec(
            (1, height, size),
            lambda n, place, sel: (q * hot_count + sel[place[1] * ratio + jnp.minimum(n // per_tile, ratio - 1), q], 0, 0))

    striped = pl.BlockSpec((height, stripe), lambda n, *_: (0, n))
    in_specs = [
        pl.BlockSpec(wa.shape, lambda n, *_: (0, 0)),
        pl.BlockSpec((s.shape[0], stripe), lambda n, *_: (0, n)),
        pl.BlockSpec((1, stripe, wb.shape[2]), lambda n, *_: (n // per_tile, n % per_tile, 0)),
        pl.BlockSpec((height, 1), lambda n, *_: (0, 0)),
        pl.BlockSpec((1, stripe), lambda n, *_: (0, n)),
    ] + [b_spec(q) for q in range(row_n)] + [striped]
    args = [wa, s, wb, rd, cd] + [cols] * row_n + [x]
    grid_spec = pltpu.PrefetchScalarGridSpec(
        num_scalar_prefetch=2, grid=(width // stripe,), in_specs=in_specs, out_specs=striped)
    return pl.pallas_call(
        functools.partial(filter_kernel, row_n, row_chunk),
        out_shape=jax.ShapeDtypeStruct(x.shape, jnp.float32),
        grid_spec=grid_spec,
        cost_estimate=pl.CostEstimate(
            flops=4 * height * width * s.shape[0], bytes_accessed=4 * 3 * height * width, transcendentals=0),
        compiler_params=pltpu.CompilerParams(vmem_limit_bytes=VMEM_LIMIT),
    )(place, sel, *args)


def body(start_vector, ham_blocks, diagonal, pair_lists, pair_counts, hot_blocks, selection):
    row_n = lax.axis_size("row")
    col_n = lax.axis_size("col")
    ratio = row_n // col_n
    height, width = start_vector.shape
    size = ham_blocks.shape[1]
    place = jnp.stack([lax.axis_index("row"), lax.axis_index("col")]).astype(jnp.int32)
    shape = (height, row_n * size)
    rows, cols = pack(start_vector, place, hot_blocks, row_n, ratio, size)
    s, b, hams, rd, cd = exchange(rows, cols, selection, row_n, col_n, 0, ham=ham_blocks, diagonal=diagonal)
    wa = dense(ham_blocks[None], place, pair_lists, pair_counts, shape, lambda place, i: place[0])[0]
    wb = dense(hams, place, pair_lists, pair_counts, shape, lambda place, i: place[1] * ratio + i)
    rows, cols = hot_step(place, hot_blocks, selection, wa, s, wb, rd, cd, b, start_vector, row_n, ratio)
    ahead = first_hops(rows, cols, row_n, col_n)
    s, _ = lax.optimization_barrier((s, rows))
    first = filter_step(place, selection, wa, s, wb, rd, cd, b, start_vector, row_n, ratio)
    s, acc = exchange(rows, cols, selection, row_n, col_n, 1, ahead=ahead, product=(wa, wb, rd, cd, first, start_vector))
    return (first, last_step(place, acc, wa, s, row_n, col_n))


def solution(mesh):
    in_specs = (P("row", "col"), P("row", None, None), P(), P(), P(), P(), P())
    out_specs = (P("row", "col"), P("row", "col"))
    return jax.shard_map(body, mesh=mesh, in_specs=in_specs, out_specs=out_specs, check_vma=False)
```

```python
import functools

import jax
import jax.numpy as jnp
from jax import lax
from jax.experimental import pallas as pl
from jax.experimental.pallas import tpu as pltpu
from jax.sharding import PartitionSpec as P

center = 0.25
half_width = 2.5
VMEM_LIMIT = 60 * 1024 * 1024
VMEM_MOST = 67043328
MESH = pl.DeviceIdType.MESH


def dense_kernel(tile_of, place, pairs, counts, ham_ref, out_ref, acc):
    tile = tile_of(place, pl.program_id(0))
    size = ham_ref.shape[-1]
    acc[...] = jnp.zeros_like(acc)

    def add(slot, carry):
        source = pl.multiple_of(pairs[0, tile, slot] * size, size)
        target = pl.multiple_of(pairs[1, tile, slot] * size, size)
        acc[pl.ds(target, size), pl.ds(source, size)] += ham_ref[0, pairs[2, tile, slot]].astype(jnp.float32)
        return carry

    lax.fori_loop(0, counts[tile], add, 0)
    out_ref[0] = acc[...].astype(out_ref.dtype)


def dense(hams, place, pairs, counts, shape, tile_of):
    grid_spec = pltpu.PrefetchScalarGridSpec(
        num_scalar_prefetch=3,
        grid=(hams.shape[0],),
        in_specs=[pl.BlockSpec((1,) + hams.shape[1:], lambda i, *_: (i, 0, 0, 0))],
        out_specs=pl.BlockSpec((1,) + shape, lambda i, *_: (i, 0, 0)),
        scratch_shapes=[pltpu.VMEM(shape, jnp.float32)],
    )
    return pl.pallas_call(
        functools.partial(dense_kernel, tile_of),
        out_shape=jax.ShapeDtypeStruct((hams.shape[0],) + shape, jnp.bfloat16),
        grid_spec=grid_spec,
        compiler_params=pltpu.CompilerParams(vmem_limit_bytes=VMEM_LIMIT),
    )(place, pairs, counts, hams)


def dot_t(a, b):
    return lax.dot_general(a, b, (((1,), (1,)), ((), ())), preferred_element_type=jnp.float32)


def pack_kernel(place, hot, xr_ref, xc_ref, rows_ref, cols_ref):
    rows_ref[0] = xr_ref[...].astype(rows_ref.dtype)
    cols_ref[0] = xc_ref[...].astype(cols_ref.dtype)


def pack(x, place, hot, row_count, ratio, size):
    height, width = x.shape
    hot_count = hot.shape[0]
    blocks = width // (ratio * size)
    part = width // ratio

    def row_block(n, place, hot):
        n = jnp.minimum(n, ratio * hot_count - 1)
        return (hot[n // ratio, place[0]], n % ratio)

    def col_block(n, place, hot):
        n = jnp.minimum(n, ratio * hot_count - 1)
        tile, which = n // hot_count, n % hot_count
        return (0, tile * blocks + hot[which, place[1] * ratio + tile])

    grid_spec = pltpu.PrefetchScalarGridSpec(
        num_scalar_prefetch=2,
        grid=(ratio * hot_count,),
        in_specs=[pl.BlockSpec((size, part), row_block), pl.BlockSpec((height, size), col_block)],
        out_specs=[
            pl.BlockSpec((1, size, part), lambda n, *_: (n // ratio, 0, n % ratio)),
            pl.BlockSpec((1, height, size), lambda n, *_: (n, 0, 0)),
        ],
    )
    return pl.pallas_call(
        pack_kernel,
        out_shape=[
            jax.ShapeDtypeStruct((hot_count, size, width), jnp.bfloat16),
            jax.ShapeDtypeStruct((ratio * hot_count, height, size), jnp.bfloat16),
        ],
        grid_spec=grid_spec,
    )(place, hot, x, x)


def layout(row_n, col_n):
    line = 1
    while 4 * line * line <= 2 * row_n:
        line *= 2
    cores = 2 if col_n % 2 == 0 else 1
    return line, row_n // line, col_n // cores, cores


class Grid:
    def __init__(self, row_n, col_n):
        self.line, self.lanes, self.chips, self.cores = layout(row_n, col_n)
        self.row_n, self.col_n = row_n, col_n
        row, col = lax.axis_index("row"), lax.axis_index("col")
        self.row, self.col = row, col
        self.at, self.lane = row // self.lanes, lax.rem(row, self.lanes)
        self.chip, self.core = col // self.cores, lax.rem(col, self.cores)

    def on_line(self, at):
        return (at * self.lanes + self.lane, self.col)

    def other_lane(self, step):
        return (self.at * self.lanes + lax.rem(self.lane + step, self.lanes), self.col)

    def other_chip(self, step):
        return (self.row, lax.rem(self.chip + step, self.chips) * self.cores + self.core)

    def other_core(self):
        return (self.row, self.chip * self.cores + lax.rem(self.core + 1, self.cores))


def remote(src, dst, send, recv, device):
    return pltpu.make_async_remote_copy(
        src_ref=src, dst_ref=dst, send_sem=send, recv_sem=recv, device_id=device, device_id_type=MESH)


def greet(g):
    barrier = pltpu.get_barrier_semaphore()
    up, down = g.at + 1 < g.line, g.at > 0

    def hello(device):
        pl.semaphore_signal(barrier, inc=1, device_id=device, device_id_type=MESH)

    @pl.when(up)
    def _():
        hello(g.on_line(g.at + 1))

    @pl.when(down)
    def _():
        hello(g.on_line(g.at - 1))

    for step in range(1, g.lanes):
        hello(g.other_lane(step))
    for step in range(1, g.chips):
        hello(g.other_chip(step))
    fixed = g.lanes - 1 + g.chips - 1
    if g.cores == 2:
        hello(g.other_core())
        fixed += 1
    pl.semaphore_wait(barrier, fixed + up.astype(jnp.int32) + down.astype(jnp.int32))


def got_slots(row_n, col_n):
    _, lanes, _, _ = layout(row_n, col_n)
    ratio = row_n // col_n
    return ratio if lanes > ratio > 1 else 1


def late_slot(at, line):
    return jnp.where(2 * at < line, line - 1, 0)


def exchange_kernel(row_n, col_n, pieces, with_ham, fused, sel, rows_ref, cols_ref, *refs):
    g = Grid(row_n, col_n)
    refs = list(refs)

    def some(count):
        taken = refs[:count]
        del refs[:count]
        return taken

    first_step = 2 if fused else 1
    if fused:
        below_ref, above_ref, chip_ref = some(3)
        side_refs = some(layout(row_n, col_n)[1] - 1)
        w_hbm, rd_ref, cd_ref, x_hbm, start_hbm, s_out, acc_out = some(7)
    else:
        ham_ref, diag_ref, s_out, c_out, h_out, rd_out, cd_out = some(7)
    held, lane_buf, turn_buf, s_all, c_all = some(5)
    own_sem, line_recv, up_send, down_send, lane_send, lane_recv = some(6)
    chip_send, chip_recv, core_send, core_recv, turn_send, turn_recv = some(6)
    if fused:
        acc, wa, wb_buf, x_buf, start_buf, via_buf, beta, st_buf, got, side_buf, load_sem, wb_sem, x_sem, start_sem, acc_sem, via_send, via_recv = some(17)
    else:
        ham_buf, far_buf, ham_sem, ham_recv, ham_up, ham_down, ham_lane, far_recv, far_send, far_chip = some(10)
        ham_rows = ham_ref.shape[0] // pieces
    ratio = row_n // col_n
    hot_count, size = rows_ref.shape[0], rows_ref.shape[1]
    height = cols_ref.shape[1]
    width = rows_ref.shape[2]
    piece = size // pieces
    block_n = cols_ref.shape[0]
    line, lanes, at = g.line, g.lanes, g.at

    home = (g.col * ratio) // lanes
    up_ok = (at + 1 < line) & ((home != line - 1) | (at + 1 != line - 1))
    down_ok = (at > 0) & ((home != 0) | (at - 1 != 0))
    deaf = (at == home) & ((at == 0) | (at == line - 1))
    far_base = jnp.where(at == 0, first_step * lanes, 0)
    far_count = (line - first_step) * lanes

    def chip_slot(step):
        return (lax.rem(g.chip - step + g.chips, g.chips) * g.cores + g.core) * block_n

    own_slot = g.col * block_n
    own_chip = g.chip * g.cores * ratio
    take = pltpu.make_async_copy(rows_ref, held.at[at], own_sem.at[0])
    take_cols = pltpu.make_async_copy(cols_ref, c_all.at[pl.ds(own_slot, block_n)], own_sem.at[1])
    take.start()
    take_cols.start()
    if fused:
        take_chip = pltpu.make_async_copy(chip_ref, c_all.at[pl.ds(chip_slot(1), block_n)], own_sem.at[2])
        take_chip.start()

        @pl.when(at > 0)
        def _():
            pltpu.make_async_copy(below_ref, held.at[at - 1], own_sem.at[3]).start()

        @pl.when(at + 1 < line)
        def _():
            pltpu.make_async_copy(above_ref, held.at[at + 1], own_sem.at[4]).start()
    else:
        take_ham = pltpu.make_async_copy(ham_ref, ham_buf, ham_sem.at[0])
        take_ham.start()
    greet(g)

    def chip_copy(step, b):
        return remote(cols_ref.at[b], c_all.at[own_slot + b], chip_send.at[step - 1, b], chip_recv.at[step - 1, b], g.other_chip(step))

    def core_copy(step, b):
        if step == 0:
            src, slot = cols_ref.at[b], own_slot + b
        else:
            slot = chip_slot(step) + b
            src = chip_ref.at[b] if fused and step == 1 else c_all.at[slot]
        return remote(src, c_all.at[slot], core_send.at[step, b], core_recv.at[step, b], g.other_core())

    for b in range(block_n):
        for step in range(first_step, g.chips):
            chip_copy(step, b).start()
    if g.cores == 2:
        for step in range(first_step):
            for b in range(block_n):
                core_copy(step, b).start()
    take.wait()
    if fused:
        @pl.when(at > 0)
        def _():
            pltpu.make_async_copy(below_ref, held.at[at - 1], own_sem.at[3]).wait()

        @pl.when(at + 1 < line)
        def _():
            pltpu.make_async_copy(above_ref, held.at[at + 1], own_sem.at[4]).wait()

    def part(slot, p):
        return held.at[slot, :, pl.ds(pl.multiple_of(p * piece, piece), piece), :]

    def up_copy(slot, p):
        return remote(part(slot, p), part(slot, p), up_send.at[slot, p], line_recv.at[slot, p], g.on_line(at + 1))

    def down_copy(slot, p):
        return remote(part(slot, p), part(slot, p), down_send.at[slot, p], line_recv.at[slot, p], g.on_line(at - 1))

    def s_rows(source, p):
        return pl.ds(pl.multiple_of(source * size + p * piece, piece), piece)

    def lane_copy(step, slot, p):
        rows = pl.ds(pl.multiple_of(p * piece, piece), piece)
        return remote(
            lane_buf.at[step - 1, slot, rows, :], s_all.at[s_rows(slot * lanes + g.lane, p), :],
            lane_send.at[step - 1, slot, p], lane_recv.at[step - 1, slot, p], g.other_lane(step))

    def lane_came(step, slot, p):
        rows = pl.ds(pl.multiple_of(p * piece, piece), piece)
        came = slot * lanes + lax.rem(g.lane - step + lanes, lanes)
        return remote(
            lane_buf.at[step - 1, slot, rows, :], s_all.at[s_rows(came, p), :],
            lane_send.at[step - 1, slot, p], lane_recv.at[step - 1, slot, p], g.other_lane(step))

    def pick(target, source, blocks):
        which = sel[target, source]
        value = blocks[0]
        for h in range(1, hot_count):
            value = jnp.where(which == h, blocks[h], value)
        return value

    def select(slot, p):
        source = slot * lanes + g.lane
        rows = pl.ds(pl.multiple_of(p * piece, piece), piece)
        blocks = [held[slot, h, rows, :] for h in range(hot_count)]

        @pl.when((slot != at) | (not fused))
        def _():
            for step in range(1, lanes):
                target = at * lanes + lax.rem(g.lane + step, lanes)
                lane_buf[step - 1, slot, rows, :] = pick(target, source, blocks)
                lane_copy(step, slot, p).start()

        s_all[s_rows(source, p), :] = pick(g.row, source, blocks)

    def tile_place(col, i):
        tile = col * ratio + i
        return tile // lanes, lax.rem(tile, lanes)

    detour = g.chips % 2 == 0 and g.chips > 1
    across = g.chips // 2
    end = jnp.where(2 * home < line, line - 1, 0)
    if not fused:
        def ham_part(ref, p):
            return ref.at[pl.ds(pl.multiple_of(p * ham_rows, ham_rows), ham_rows)]

        def ham_copies(i, p):
            here = ham_part(h_out.at[i], p)
            up = remote(here, here, ham_up.at[i, p], ham_recv.at[i, p], g.on_line(at + 1))
            down = remote(here, here, ham_down.at[i, p], ham_recv.at[i, p], g.on_line(at - 1))
            over = [remote(here, here, ham_lane.at[i, step - 1, p], ham_recv.at[i, p], g.other_lane(step))
                    for step in range(1, lanes)]
            return up, down, over

        def ham_sends(i, p, act):
            _, home_lane = tile_place(g.col, i)
            up, down, over = ham_copies(i, p)
            skip = end if detour else line

            @pl.when(home_lane == g.lane)
            def _():
                @pl.when((at >= home) & (at + 1 < line) & (at + 1 != skip))
                def _():
                    act(up)

                @pl.when((at <= home) & (at > 0) & (at - 1 != skip))
                def _():
                    act(down)

                for copy in over:
                    act(copy)

        if detour:
            far_col = lax.rem(g.chip + across, g.chips) * g.cores + g.core
            far_home = (far_col * ratio) // lanes
            far_end = jnp.where(2 * far_home < line, line - 1, 0)
            rising = far_end > far_home
            far_away = jnp.where(rising, at - far_home, far_home - at)

            def far_copies(i, p):
                here = ham_part(far_buf, p)
                way = jnp.where(rising, at + 1, at - 1)
                on = remote(here, here, far_send.at[p], far_recv.at[p], g.on_line(way))
                chip = remote(here, ham_part(h_out.at[i], p), far_chip.at[p], ham_recv.at[i, p], g.other_chip(across))
                return on, chip

            def far_sends(i, p, act):
                _, far_lane = tile_place(far_col, i)
                on, chip = far_copies(i, p)

                @pl.when((far_lane == g.lane) & (far_away >= 0))
                def _():
                    @pl.when(at != far_end)
                    def _():
                        act(on)

                    @pl.when(at == far_end)
                    def _():
                        act(chip)

        take_ham.wait()
        put_own = pltpu.make_async_copy(ham_buf, h_out.at[ratio], ham_sem.at[1])
        put_own.start()
        for i in range(ratio):
            _, home_lane = tile_place(g.col, i)

            @pl.when((home == at) & (home_lane == g.lane))
            def _():
                put = pltpu.make_async_copy(ham_buf, h_out.at[i], ham_sem.at[0])
                put.start()
                put.wait()

            if detour:
                _, far_lane = tile_place(far_col, i)

                @pl.when((far_home == at) & (far_lane == g.lane))
                def _():
                    put = pltpu.make_async_copy(ham_ref, far_buf, ham_sem.at[0])
                    put.start()
                    put.wait()

        def near_step(s, p):
            for i in range(ratio):
                _, home_lane = tile_place(g.col, i)
                away = jnp.where(at >= home, at - home, home - at)

                @pl.when((home_lane == g.lane) & (away == s))
                def _():
                    if s > 0:
                        ham_copies(i, p)[0].wait_recv()

                    ham_sends(i, p, lambda copy: copy.start())

        def far_step(s, p):
            for i in range(ratio if detour else 0):
                _, far_lane = tile_place(far_col, i)

                @pl.when((far_lane == g.lane) & (far_away == s))
                def _():
                    if s > 0:
                        far_copies(i, p)[0].wait_recv()

                    far_sends(i, p, lambda copy: copy.start())

        def far_steps(s):
            def one(p, carry):
                far_step(s, p)
                return carry

            lax.fori_loop(0, pieces, one, 0)

        if detour:
            held_back = (far_away > 0) & (at != far_end)
            up_first = (held_back & rising) == False
            down_first = (held_back & (rising == False)) == False
        else:
            up_first = down_first = at >= 0

        def ham_start(p, carry):
            near_step(0, p)
            far_step(0, p)
            return carry

        def ham_next(p, carry):
            near_step(1, p)
            far_step(1, p)
            return carry

        lax.fori_loop(0, pieces, ham_start, 0)

    if fused and detour and line > 2:
        climbs = end > home
        before = jnp.where(climbs, end - 1, end + 1)
        via_slot = jnp.where(climbs, end - 2, end + 2)
        leaves = at == before
        far_col = lax.rem(g.chip + across, g.chips) * g.cores + g.core
        far_home = (far_col * ratio) // lanes
        far_end = jnp.where(2 * far_home < line, line - 1, 0)
        far_before = jnp.where(far_end > far_home, far_end - 1, far_end + 1)
        far_slot = jnp.where(far_end > far_home, far_end - 2, far_end + 2)
        kept = pieces * 3 // 4

        def via_leave(p):
            return remote(part(via_slot, p), via_buf.at[p - kept], via_send.at[0, p - kept], via_recv.at[0, p - kept], g.other_chip(across))

        def via_pass(p):
            return remote(via_buf.at[p - kept], via_buf.at[p - kept], via_send.at[1, p - kept], via_recv.at[1, p - kept], g.on_line(far_end))

        def via_land(p):
            return remote(via_buf.at[p - kept], part(far_slot, p), via_send.at[2, p - kept], line_recv.at[far_slot, p], g.other_chip(across))

        def via_came(stage, p):
            there = g.other_chip(across) if stage == 0 else g.on_line(far_before)
            return remote(via_buf.at[p - kept], via_buf.at[p - kept], via_send.at[stage, p - kept], via_recv.at[stage, p - kept], there)

        def via_up(slot, p):
            return ((leaves & climbs & (slot == via_slot)) == False) | (p < kept)

        def via_down(slot, p):
            return ((leaves & (climbs == False) & (slot == via_slot)) == False) | (p < kept)
    else:
        leaves = None
        via_up = via_down = lambda slot, p: p >= 0

    half = pieces * (line // 2)

    def hears(s):
        quiet = (s == 0) | (deaf == False)
        return (at - s >= 0) & quiet, (at + s < line) & quiet

    if fused:
        up_first = down_first = at >= 0

    def relay(n, carry):
        s, p = n // pieces, lax.rem(n, pieces)
        hears_below, hears_above = hears(s)

        @pl.when(hears_below)
        def _():
            @pl.when(s >= first_step)
            def _():
                up_copy(at - s, p).wait_recv()

            @pl.when(up_ok & (s >= first_step - 1) & via_up(at - s, p) & ((s > 0) | up_first))
            def _():
                up_copy(at - s, p).start()

        @pl.when(hears_above)
        def _():
            @pl.when(s >= first_step)
            def _():
                down_copy(at + s, p).wait_recv()

            @pl.when(down_ok & (s >= first_step - 1) & via_down(at + s, p) & ((s > 0) | down_first))
            def _():
                down_copy(at + s, p).start()
        return carry

    def digest(n, carry):
        s, p = n // pieces, lax.rem(n, pieces)
        hears_below = (at - s >= 0) & ((s < first_step) | (deaf == False))
        hears_above = (at + s < line) & ((s < first_step) | (deaf == False))

        @pl.when(hears_below)
        def _():
            select(at - s, p)

        @pl.when(hears_above & (s > 0))
        def _():
            select(at + s, p)
        return carry

    def advance(n, carry):
        relay(n, carry)
        if not fused:
            @pl.when((n >= half) & (n < half + pieces))
            def _():
                for s in range(2, line):
                    near_step(s, n - half)
        return digest(n, carry)

    def core_came(step, b):
        other = lax.rem(g.core + 1, g.cores)
        slot = (lax.rem(g.chip - step + g.chips, g.chips) * g.cores + other) * block_n + b
        return remote(cols_ref.at[b], c_all.at[slot], core_send.at[step, b], core_recv.at[step, b], g.other_core())

    def got_at(i):
        return i if got_slots(row_n, col_n) > 1 else 0

    def turn_copy(i, step, q):
        if fused:
            there = got.at[got_at(i), q]
        else:
            there = s_all.at[pl.ds(pl.multiple_of(q * size, size), size), i * height:(i + 1) * height]
        return remote(turn_buf.at[step - 1, q], there, turn_send.at[step - 1, q], turn_recv.at[i, q], g.other_lane(step))

    def turn(q):
        rows = pl.ds(pl.multiple_of(q * size, size), size)
        for i in range(ratio):
            _, home_lane = tile_place(g.col, i)

            @pl.when(home_lane == g.lane)
            def _():
                for k in range(height // size):
                    strip = slice(k * size, (k + 1) * size)
                    blocks = [c_all[q * hot_count + h, strip, :] for h in range(hot_count)]
                    for step in range(1, lanes):
                        target = at * lanes + lax.rem(g.lane + step, lanes)
                        value = pick(target, q, blocks)
                        if fused:
                            turn_buf[step - 1, q, strip, :] = value
                        else:
                            turn_buf[step - 1, q, :, strip] = value.astype(jnp.float32).T.astype(turn_buf.dtype)
                    if not fused:
                        s_all[rows, i * height + k * size:i * height + (k + 1) * size] = pick(g.row, q, blocks).astype(jnp.float32).T.astype(s_all.dtype)
                for step in range(1, lanes):
                    turn_copy(i, step, q).start()

    def turns(act):
        def one(q, carry):
            for i in range(ratio):
                _, home_lane = tile_place(g.col, i)
                act(i, q, home_lane)
            return carry

        lax.fori_loop(far_base, far_base + far_count, one, 0)

    def turn_came(i, q, home_lane):
        @pl.when(home_lane != g.lane)
        def _():
            turn_copy(i, 1, q).wait_recv()

    def turn_sent(i, q, home_lane):
        @pl.when(home_lane == g.lane)
        def _():
            for step in range(1, lanes):
                turn_copy(i, step, q).wait_send()

    if fused:
        stripe = x_buf.shape[2]
        stripes = width // stripe
        per_tile = height // stripe
        rows_at_once = height // 2
        share = -(-stripes // pieces)
        late = late_slot(at, line)
        take_wa = pltpu.make_async_copy(w_hbm.at[ratio], wa, load_sem.at[0])
        early = line - 1
        first_early = jnp.where(late == 0, 1, 0)
        depth = pl.ds(pl.multiple_of(first_early * lanes * size, lanes * size), early * lanes * size)

        def band(n):
            return pl.ds(pl.multiple_of(n * stripe, stripe), stripe)

        def loads(n):
            turn_n = lax.rem(n, 2)
            return [
                pltpu.make_async_copy(x_hbm.at[:, band(n)], x_buf.at[turn_n], x_sem.at[turn_n]),
                pltpu.make_async_copy(start_hbm.at[:, band(n)], start_buf.at[turn_n], start_sem.at[turn_n]),
                pltpu.make_async_copy(w_hbm.at[n // per_tile, band(lax.rem(n, per_tile)), :], wb_buf.at[turn_n], wb_sem.at[turn_n]),
            ]

        def acc_copy(n):
            return pltpu.make_async_copy(acc.at[:, band(n)], acc_out.at[:, band(n)], acc_sem.at[n])

        def beta_side(n, carry):
            tile, turn_n = n // per_tile, lax.rem(n, 2)

            @pl.when(n + 1 < stripes)
            def _():
                for copy in loads(n + 1):
                    copy.start()

            @pl.when(lax.rem(n, per_tile) == 0)
            def _():
                for q in range(row_n):
                    beta[:, q * size:(q + 1) * size] = c_all[q * hot_count + sel[g.col * ratio + tile, q]]

            for copy in loads(n):
                copy.wait()
            for k in range(2):
                rows = slice(k * rows_at_once, (k + 1) * rows_at_once)
                value = dot_t(beta[rows, :], wb_buf[turn_n])
                value = value + (rd_ref[rows, :] + cd_ref[:, band(n)] - center) * x_buf[turn_n, rows, :]
                acc[rows, band(n)] = value - start_buf[turn_n, rows, :] * (half_width / 2.0)
            return carry

        near_base = jnp.where(at == 0, 0, (line - 2) * lanes * size)
        near_depth = pl.ds(pl.multiple_of(near_base, lanes * size), 2 * lanes * size)
        far_depth = pl.ds(pl.multiple_of(far_base * size, lanes * size), far_count * size)

        def alpha_side(m, carry):
            n = jnp.where(deaf, lax.rem(m + g.lane * per_tile, stripes), m)
            tile, inner = n // per_tile, lax.rem(n, per_tile)

            @pl.when(deaf == False)
            def _():
                for k in range(2):
                    rows = slice(k * rows_at_once, (k + 1) * rows_at_once)
                    acc[rows, band(n)] += jnp.dot(wa[rows, depth], s_all[depth, band(n)], preferred_element_type=jnp.float32)

            @pl.when(deaf)
            def _():
                _, home_lane = tile_place(g.col, tile)

                @pl.when(home_lane == g.lane)
                def _():
                    for j in range(far_count):
                        q = far_base + j
                        st_buf[:, j * size:(j + 1) * size] = c_all[q * hot_count + sel[g.row, q], band(inner), :]

                @pl.when(home_lane != g.lane)
                def _():
                    @pl.when(inner == 0)
                    def _():
                        def come(q, carry):
                            turn_copy(tile, 1, q).wait_recv()
                            return carry

                        lax.fori_loop(far_base, far_base + far_count, come, 0)

                    for j in range(far_count):
                        st_buf[:, j * size:(j + 1) * size] = got[got_at(tile), far_base + j, band(inner), :]

                for k in range(2):
                    rows = slice(k * rows_at_once, (k + 1) * rows_at_once)
                    value = jnp.dot(wa[rows, near_depth], s_all[near_depth, band(n)], preferred_element_type=jnp.float32)
                    acc[rows, band(n)] += value + dot_t(wa[rows, far_depth], st_buf[...])
            acc_copy(n).start()
            return carry

        def some_stripes(work, turn_n, share=share):
            lax.fori_loop(turn_n * share, jnp.minimum(turn_n * share + share, stripes), work, 0)

    if fused:
        if leaves is not None:
            @pl.when(leaves)
            def _():
                for p in range(kept, pieces):
                    via_leave(p).start()

        lax.fori_loop(pieces, half, relay, 0)
        take_sides = [pltpu.make_async_copy(side, side_buf.at[step], load_sem.at[1 + step]) for step, side in enumerate(side_refs)]
        for copy in take_sides:
            copy.start()
        lax.fori_loop(pieces, half, digest, 0)
        take_wa.start()
        for copy in loads(0):
            copy.start()
        lax.fori_loop(0, pieces, digest, 0)
        for copy in take_sides:
            copy.wait()

        def sides(p, carry):
            rows = pl.ds(pl.multiple_of(p * piece, piece), piece)
            for step in range(1, lanes):
                source = at * lanes + lax.rem(g.lane - step + lanes, lanes)
                blocks = [side_buf[step - 1, h, rows, :] for h in range(hot_count)]
                s_all[s_rows(source, p), :] = pick(g.row, source, blocks)
            return carry

        lax.fori_loop(0, pieces, sides, 0)
    else:
        def held_rows(p, carry):
            @pl.when(up_ok & (up_first == False))
            def _():
                up_copy(at, p).start()

            @pl.when(down_ok & (down_first == False))
            def _():
                down_copy(at, p).start()
            return carry

        lax.fori_loop(0, pieces, relay, 0)
        lax.fori_loop(0, pieces, digest, 0)
        take_cols.wait()
        if g.cores == 2:
            for b in range(block_n):
                core_came(0, b).wait_recv()

        @pl.when(deaf)
        def _():
            def turn_early(q, carry):
                @pl.when(q // lanes != at)
                def _():
                    turn(q)
                return carry

            lax.fori_loop(own_chip, own_chip + g.cores * ratio, turn_early, 0)

        lax.fori_loop(0, pieces, ham_next, 0)
        for s in range(2, line):
            far_steps(s)
        lax.fori_loop(0, pieces, held_rows, 0)
        lax.fori_loop(pieces, half, advance, 0)
    for step in range(first_step, g.chips):
        for b in range(block_n):
            slot = chip_slot(step) + b
            remote(cols_ref.at[b], c_all.at[slot], chip_send.at[step - 1, b], chip_recv.at[step - 1, b], g.other_chip(step)).wait_recv()
            if g.cores == 2:
                core_copy(step, b).start()

    if fused:
        take_cols.wait()
        take_chip.wait()
    if g.cores == 2:
        for step in range(0 if fused else 1, g.chips):
            for b in range(block_n):
                core_came(step, b).wait_recv()
    if not fused:
        @pl.when(deaf)
        def _():
            def turn_rest(q, carry):
                @pl.when(q // (g.cores * ratio) != g.chip)
                def _():
                    turn(q)
                return carry

            lax.fori_loop(far_base, far_base + far_count, turn_rest, 0)

        cd_out[...] = diag_ref[:, pl.ds(pl.multiple_of(g.col * width, width), width)]
        for k in range(height // size):
            strip = diag_ref[:, pl.ds(pl.multiple_of(g.row * height + k * size, size), size)]
            rd_out[k * size:(k + 1) * size, :] = jnp.broadcast_to(strip, (size, size)).T[:, :1]
        put_cols = pltpu.make_async_copy(c_all, c_out, own_sem.at[2])
        put_cols.start()
    else:
        take_wa.wait()

        @pl.when(deaf)
        def _():
            def turn_on(q, carry):
                turn(q)
                return carry

            lax.fori_loop(far_base, far_base + far_count, turn_on, 0)

    def middle(n, carry):
        if fused:
            some_stripes(beta_side, n - half)
        if leaves is not None:
            via_p = kept + jnp.minimum(n - half, pieces - kept - 1)

            @pl.when((n < half + pieces - kept) & (at == far_before))
            def _():
                p = via_p
                via_came(0, p).wait_recv()
                via_pass(p).start()

            @pl.when((n < half + pieces - kept) & (at == far_end))
            def _():
                p = via_p
                via_came(1, p).wait_recv()
                via_land(p).start()

        return advance(n, carry)

    def lanes_came(slot):
        def one(p, carry):
            for step in range(1, lanes):
                lane_came(step, slot, p).wait_recv()
            return carry

        near = (slot - at < first_step) & (at - slot < first_step)
        away = slot != at if fused else True

        @pl.when(((deaf == False) | near) & away)
        def _():
            lax.fori_loop(0, pieces, one, 0)

    lax.fori_loop(half, half + pieces, middle, 0)
    if fused:
        for other in range(1, line):
            lanes_came(lax.rem(late + other, line))

        def ending(turn_n, carry):
            for u in range(2):
                advance(half + pieces + 2 * turn_n + u, carry)
            some_stripes(alpha_side, turn_n, -(-stripes // (pieces // 2)))
            return carry

        lax.fori_loop(0, (pieces * line - half - pieces) // 2, ending, 0)
        lanes_came(late)

        @pl.when(deaf)
        def _():
            s_all[pl.ds(pl.multiple_of(late * lanes * size, size), lanes * size), :] = jnp.zeros((lanes * size, width), s_all.dtype)

        put_s = pltpu.make_async_copy(s_all.at[pl.ds(pl.multiple_of(late * lanes * size, size), lanes * size), :], s_out, own_sem.at[5])
        put_s.start()
        put_s.wait()
        for n in range(stripes):
            acc_copy(n).wait()
    else:
        lax.fori_loop(half + pieces, pieces * line, advance, 0)
        for slot in range(line):
            lanes_came(slot)

        @pl.when(deaf)
        def _():
            turns(turn_came)

        put_s = pltpu.make_async_copy(s_all, s_out, own_sem.at[5])
        put_s.start()
        put_s.wait()
        put_cols.wait()

    @pl.when(deaf)
    def _():
        turns(turn_sent)

    def finish(n, carry):
        slot, p = n // pieces, lax.rem(n, pieces)

        @pl.when((slot <= at + 1 - first_step) & up_ok & via_up(slot, p))
        def _():
            up_copy(slot, p).wait_send()

        @pl.when((slot >= at - 1 + first_step) & down_ok & via_down(slot, p))
        def _():
            down_copy(slot, p).wait_send()

        near = (slot - at < first_step) & (at - slot < first_step)
        away = slot != at if fused else True

        @pl.when(((deaf == False) | near) & away)
        def _():
            for step in range(1, lanes):
                lane_copy(step, slot, p).wait_send()
        return carry

    lax.fori_loop(0, line * pieces, finish, 0)
    if leaves is not None:
        for p in range(kept, pieces):
            @pl.when(leaves)
            def _():
                via_leave(p).wait_send()

            @pl.when(at == far_before)
            def _():
                via_pass(p).wait_send()

            @pl.when(at == far_end)
            def _():
                via_land(p).wait_send()
    for b in range(block_n):
        for step in range(first_step, g.chips):
            chip_copy(step, b).wait_send()
        if g.cores == 2:
            for step in range(g.chips):
                core_copy(step, b).wait_send()
    if not fused:
        put_own.wait()
        for i in range(ratio):
            _, home_lane = tile_place(g.col, i)

            def settle(p, carry):
                ham_sends(i, p, lambda copy: copy.wait_send())
                if detour:
                    far_sends(i, p, lambda copy: copy.wait_send())

                @pl.when(home_lane != g.lane)
                def _():
                    ham_copies(i, p)[2][0].wait_recv()
                return carry

            lax.fori_loop(0, pieces, settle, 0)


def exchange(rows, cols, sel, row_n, col_n, ident, ham=None, diagonal=None, ahead=None, product=None):
    hot_count, size, width = rows.shape
    block_n, height = cols.shape[:2]
    ratio = row_n // col_n
    pieces = 8
    fused = product is not None
    line, lanes, chips, _ = layout(row_n, col_n)
    others = max(lanes - 1, 1)
    dma = pltpu.SemaphoreType.DMA
    vmem = lambda *shape: pltpu.VMEM(shape, jnp.bfloat16)
    anywhere = pl.BlockSpec(memory_space=pl.ANY)
    whole = pl.BlockSpec(memory_space=pltpu.VMEM)
    scratch = [
        vmem(line, hot_count, size, width),
        vmem(others, line, size, width),
        vmem(others, row_n, *((height, size) if fused else (size, height))),
        vmem(row_n * size, width),
        vmem(col_n * block_n, height, size),
        dma((6,)),
        dma((line, pieces)),
        dma((line, pieces)),
        dma((line, pieces)),
        dma((others, line, pieces)),
        dma((others, line, pieces)),
        dma((max(chips - 1, 1), block_n)),
        dma((max(chips - 1, 1), block_n)),
        dma((chips, block_n)),
        dma((chips, block_n)),
        dma((others, row_n)),
        dma((ratio, row_n)),
    ]
    args = [sel, rows, cols]
    in_specs = [pl.BlockSpec(memory_space=pltpu.SMEM), anywhere, anywhere]
    if fused:
        w, rd, cd, x, start = product
        stripe = 256 if height % 256 == 0 else size
        args += list(ahead) + [w, rd, cd, x, start]
        in_specs += [anywhere] * (len(ahead) + 1) + [whole] * 2 + [anywhere] * 2
        out_shape = [
            jax.ShapeDtypeStruct((lanes * size, width), jnp.bfloat16),
            jax.ShapeDtypeStruct((height, width), jnp.float32),
        ]
        out_specs = [anywhere] * 2
        scratch += [
            pltpu.VMEM((height, width), jnp.float32),
            vmem(*w.shape[1:]),
            vmem(2, stripe, w.shape[2]),
            pltpu.VMEM((2, height, stripe), jnp.float32),
            pltpu.VMEM((2, height, stripe), jnp.float32),
            vmem(pieces - pieces * 3 // 4, hot_count, size // pieces, width),
            vmem(height, row_n * size),
            vmem(stripe, (line - 2) * lanes * size),
            vmem(got_slots(row_n, col_n), row_n, height, size),
            vmem(others, hot_count, size, width),
            dma((1 + others,)),
            dma((2,)),
            dma((2,)),
            dma((2,)),
            dma((width // stripe,)),
            dma((3, pieces)),
            dma((3, pieces)),
        ]
    else:
        args += [ham, diagonal[None, :]]
        in_specs += [anywhere, whole]
        out_shape = [
            jax.ShapeDtypeStruct((row_n * size, width), jnp.bfloat16),
            jax.ShapeDtypeStruct((col_n * block_n, height, size), jnp.bfloat16),
            jax.ShapeDtypeStruct((ratio + 1,) + ham.shape, ham.dtype),
            jax.ShapeDtypeStruct((height, 1), jnp.float32),
            jax.ShapeDtypeStruct((1, width), jnp.float32),
        ]
        out_specs = [anywhere] * 3 + [whole] * 2
        scratch += [
            pltpu.VMEM(ham.shape, ham.dtype),
            pltpu.VMEM(ham.shape, ham.dtype),
            dma((2,)),
            dma((ratio, pieces)),
            dma((ratio, pieces)),
            dma((ratio, pieces)),
            dma((ratio, others, pieces)),
            dma((pieces,)),
            dma((pieces,)),
            dma((pieces,)),
        ]
    return pl.pallas_call(
        functools.partial(exchange_kernel, row_n, col_n, pieces, ham is not None, fused),
        out_shape=out_shape,
        in_specs=in_specs,
        out_specs=out_specs,
        scratch_shapes=scratch,
        compiler_params=pltpu.CompilerParams(collective_id=ident, has_side_effects=True, vmem_limit_bytes=VMEM_MOST),
    )(*args)


def last_kernel(place, acc_ref, wa_ref, s_ref, out_ref):
    acc = acc_ref[...] + jnp.dot(wa_ref[...], s_ref[...], preferred_element_type=jnp.float32)
    out_ref[...] = acc * (2.0 / half_width)


def last_step(place, acc, w, s, row_n, col_n):
    height, width = acc.shape
    depth = s.shape[0]
    line, lanes, _, _ = layout(row_n, col_n)
    stripe = next(n for n in (512, 384, 256, width) if width % n == 0)
    grid_spec = pltpu.PrefetchScalarGridSpec(
        num_scalar_prefetch=1,
        grid=(width // stripe,),
        in_specs=[
            pl.BlockSpec((height, stripe), lambda n, place: (0, n)),
            pl.BlockSpec((None, height, depth), lambda n, place: (row_n // col_n, 0, late_slot(place[0] // lanes, line))),
            pl.BlockSpec((depth, stripe), lambda n, place: (0, n)),
        ],
        out_specs=pl.BlockSpec((height, stripe), lambda n, place: (0, n)),
    )
    return pl.pallas_call(
        last_kernel,
        out_shape=jax.ShapeDtypeStruct(acc.shape, jnp.float32),
        grid_spec=grid_spec,
        compiler_params=pltpu.CompilerParams(vmem_limit_bytes=VMEM_LIMIT),
    )(place, acc, w, s)


def hot_kernel(row_n, hot_count, place, hot, sel, *refs):
    refs = list(refs)

    def some(count):
        taken = refs[:count]
        del refs[:count]
        return taken

    wide = lambda blocks: jnp.concatenate(blocks, axis=1)
    wa_hot, x_rows, rd_hot = some(hot_count), some(hot_count), some(hot_count)
    b_hot = [some(row_n) for _ in range(hot_count)]
    s_ref, wb_ref, cd_ref = some(3)
    wa_ref, rd_ref = some(2)
    b_refs = some(row_n)
    s_hot, wb_hot, x_cols, cd_hot = some(hot_count), some(hot_count), some(hot_count), some(hot_count)
    rows_ref, cols_ref = refs
    scale = 1.0 / half_width

    def dot(a, b):
        return jnp.dot(a, b, preferred_element_type=jnp.float32)

    size = rows_ref.shape[1]
    acc = dot(jnp.concatenate([w[...] for w in wa_hot], axis=0), s_ref[...])
    beta = jnp.concatenate([wide([b[0] for b in blocks]) for blocks in b_hot], axis=0)
    acc = acc + dot_t(beta, wb_ref[0])
    for h in range(hot_count):
        value = acc[h * size:(h + 1) * size] + (rd_hot[h][...] + cd_ref[...] - center) * x_rows[h][...]
        rows_ref[h] = (value * scale).astype(rows_ref.dtype)
    acc = dot(wa_ref[...], wide([s[...] for s in s_hot]))
    acc = acc + dot_t(wide([b[0] for b in b_refs]), jnp.concatenate([w[0] for w in wb_hot], axis=0))
    for h in range(hot_count):
        value = acc[:, h * size:(h + 1) * size] + (rd_ref[...] + cd_hot[h][...] - center) * x_cols[h][...]
        cols_ref[h] = (value * scale).astype(cols_ref.dtype)


def hot_step(place, hot, sel, w, s, rd, cd, cols, x, row_n, ratio):
    height, width = x.shape
    size = cols.shape[-1]
    hot_count = hot.shape[0]
    tile_width = width // ratio
    stripe = tile_width
    per_tile = tile_width // stripe
    blocks = tile_width // size
    depth = s.shape[0]

    def tile(n):
        return jnp.minimum(n // per_tile, ratio - 1)

    def hot_row(h, place, hot):
        return hot[h, place[0]]

    def hot_col(h, n, place, hot):
        return hot[h, place[1] * ratio + tile(n)]

    def source(q, n, place, sel):
        return q * hot_count + sel[place[1] * ratio + tile(n), q]

    spec = pl.BlockSpec
    each = range(hot_count)
    in_specs = [spec((None, size, depth), lambda n, place, hot, sel, h=h: (ratio, hot_row(h, place, hot), 0)) for h in each]
    in_specs += [spec((size, stripe), lambda n, place, hot, sel, h=h: (hot_row(h, place, hot), n)) for h in each]
    in_specs += [spec((size, 1), lambda n, place, hot, sel, h=h: (hot_row(h, place, hot), 0)) for h in each]
    in_specs += [spec((1, size, size), lambda n, place, hot, sel, h=h, q=q: (source(q, n, place, sel), hot_row(h, place, hot), 0))
                 for h in each for q in range(row_n)]
    in_specs += [
        spec((depth, stripe), lambda n, *_: (0, n)),
        spec((1, stripe, depth), lambda n, *_: (n // per_tile, n % per_tile, 0)),
        spec((1, stripe), lambda n, *_: (0, n)),
        spec((None, stripe, depth), lambda n, *_: (ratio, n % per_tile, 0)),
        spec((stripe, 1), lambda n, *_: (n % per_tile, 0)),
    ]
    in_specs += [spec((1, stripe, size), lambda n, place, hot, sel, q=q: (source(q, n, place, sel), n % per_tile, 0)) for q in range(row_n)]
    in_specs += [spec((depth, size), lambda n, place, hot, sel, h=h: (0, tile(n) * blocks + hot_col(h, n, place, hot))) for h in each]
    in_specs += [spec((1, size, depth), lambda n, place, hot, sel, h=h: (tile(n), hot_col(h, n, place, hot), 0)) for h in each]
    in_specs += [spec((stripe, size), lambda n, place, hot, sel, h=h: (n % per_tile, tile(n) * blocks + hot_col(h, n, place, hot))) for h in each]
    in_specs += [spec((1, size), lambda n, place, hot, sel, h=h: (0, tile(n) * blocks + hot_col(h, n, place, hot))) for h in each]
    args = [w] * hot_count + [x] * hot_count + [rd] * hot_count + [cols] * (hot_count * row_n)
    args += [s, w, cd, w, rd] + [cols] * row_n + [s] * hot_count + [w] * hot_count + [x] * hot_count + [cd] * hot_count
    grid_spec = pltpu.PrefetchScalarGridSpec(
        num_scalar_prefetch=3,
        grid=(width // stripe,),
        in_specs=in_specs,
        out_specs=[
            spec((hot_count, size, stripe), lambda n, *_: (0, 0, n)),
            spec((hot_count, stripe, size), lambda n, *_: (n // per_tile, n % per_tile, 0)),
        ],
    )
    return pl.pallas_call(
        functools.partial(hot_kernel, row_n, hot_count),
        out_shape=[
            jax.ShapeDtypeStruct((hot_count, size, width), jnp.bfloat16),
            jax.ShapeDtypeStruct((ratio * hot_count, height, size), jnp.bfloat16),
        ],
        grid_spec=grid_spec,
        compiler_params=pltpu.CompilerParams(vmem_limit_bytes=VMEM_LIMIT),
    )(place, hot, sel, *args)


def first_hops(rows, cols, row_n, col_n):
    line, lanes, chips, cores = layout(row_n, col_n)
    upward = [(r, r + lanes) for r in range(row_n - lanes)]
    below = lax.ppermute(rows, "row", upward)
    above = lax.ppermute(rows, "row", [(b, a) for a, b in upward])
    turn = [(c, (c // cores + 1) % chips * cores + c % cores) for c in range(col_n)]
    ahead = [below, above, lax.ppermute(cols, "col", turn)]
    for step in range(1, lanes):
        ahead.append(lax.ppermute(rows, "row", [(r, r // lanes * lanes + (r + step) % lanes) for r in range(row_n)]))
    return ahead


def filter_kernel(source_count, row_chunk, place, sel, wa_ref, s_ref, wb_ref, rd_ref, cd_ref, *refs):
    b_refs = refs[:source_count]
    x_ref, out_ref = refs[source_count:]

    def chunk(i, carry):
        rows = pl.ds(pl.multiple_of(i * row_chunk, row_chunk), row_chunk)
        beta = jnp.concatenate([b[0, rows, :] for b in b_refs], axis=1)
        acc = jnp.dot(wa_ref[rows, :], s_ref[...], preferred_element_type=jnp.float32)
        acc = acc + dot_t(beta, wb_ref[0])
        acc = acc + (rd_ref[rows, :] + cd_ref[...] - center) * x_ref[rows, :]
        out_ref[rows, :] = acc * (1.0 / half_width)
        return carry

    lax.fori_loop(0, x_ref.shape[0] // row_chunk, chunk, 0)


def filter_step(place, sel, w, s, rd, cd, cols, x, row_n, ratio):
    height, width = x.shape
    size = cols.shape[-1]
    hot_count = cols.shape[0] // row_n
    tile_width = width // ratio
    stripe = next(n for n in (512, 384, 256, size) if tile_width % n == 0)
    per_tile = tile_width // stripe
    row_chunk = height // 2 if height % 256 == 0 else height

    def b_spec(q):
        return pl.BlockSpec(
            (1, height, size),
            lambda n, place, sel: (q * hot_count + sel[place[1] * ratio + jnp.minimum(n // per_tile, ratio - 1), q], 0, 0))

    striped = pl.BlockSpec((height, stripe), lambda n, *_: (0, n))
    in_specs = [
        pl.BlockSpec((None,) + w.shape[1:], lambda n, *_: (ratio, 0, 0)),
        pl.BlockSpec((s.shape[0], stripe), lambda n, *_: (0, n)),
        pl.BlockSpec((1, stripe, w.shape[2]), lambda n, *_: (n // per_tile, n % per_tile, 0)),
        pl.BlockSpec((height, 1), lambda n, *_: (0, 0)),
        pl.BlockSpec((1, stripe), lambda n, *_: (0, n)),
    ] + [b_spec(q) for q in range(row_n)] + [striped]
    args = [w, s, w, rd, cd] + [cols] * row_n + [x]
    grid_spec = pltpu.PrefetchScalarGridSpec(
        num_scalar_prefetch=2, grid=(width // stripe,), in_specs=in_specs, out_specs=striped)
    return pl.pallas_call(
        functools.partial(filter_kernel, row_n, row_chunk),
        out_shape=jax.ShapeDtypeStruct(x.shape, jnp.float32),
        grid_spec=grid_spec,
        cost_estimate=pl.CostEstimate(
            flops=4 * height * width * s.shape[0], bytes_accessed=4 * 3 * height * width, transcendentals=0),
        compiler_params=pltpu.CompilerParams(vmem_limit_bytes=VMEM_LIMIT),
    )(place, sel, *args)


def body(start_vector, ham_blocks, diagonal, pair_lists, pair_counts, hot_blocks, selection):
    row_n = lax.axis_size("row")
    col_n = lax.axis_size("col")
    ratio = row_n // col_n
    height, width = start_vector.shape
    size = ham_blocks.shape[1]
    place = jnp.stack([lax.axis_index("row"), lax.axis_index("col")]).astype(jnp.int32)
    shape = (height, row_n * size)
    hot = hot_blocks.T
    rows, cols = pack(start_vector, place, hot, row_n, ratio, size)
    s, b, hams, rd, cd = exchange(rows, cols, selection, row_n, col_n, 0, ham=ham_blocks, diagonal=diagonal)
    w = dense(hams, place, pair_lists, pair_counts, shape, lambda place, i: jnp.where(i < ratio, place[1] * ratio + i, place[0]))
    rows, cols = hot_step(place, hot, selection, w, s, rd, cd, b, start_vector, row_n, ratio)
    ahead = first_hops(rows, cols, row_n, col_n)
    s, _ = lax.optimization_barrier((s, rows))
    first = filter_step(place, selection, w, s, rd, cd, b, start_vector, row_n, ratio)
    s, acc = exchange(rows, cols, selection, row_n, col_n, 1, ahead=ahead, product=(w, rd, cd, first, start_vector))
    return (first, last_step(place, acc, w, s, row_n, col_n))


def solution(mesh):
    in_specs = (P("row", "col"), P("row", None, None), P(), P(), P(), P(), P())
    out_specs = (P("row", "col"), P("row", "col"))
    return jax.shard_map(body, mesh=mesh, in_specs=in_specs, out_specs=out_specs, check_vma=False)
```
